32 devices in a mesh: dp: 8 (over y, x, core), mp: 4 (over z).
Axes of the slice: x: 2, y: 2, z: 4, core: 2. Of those that a mesh axis runs over, the one named last changes fastest.
Arguments:
- tokens: bfloat16 [16384, 1024], P(('dp', 'mp')), may hold values from -6 to 6
- segments: int32 [16384], P('dp'), may hold values from 0 to 68, as said below
- ln1_gain: bfloat16 [1024], replicated, may hold values from 0.5 to 1.5
- ln1_bias: bfloat16 [1024], replicated, may hold values from -1.75 to 1.75
- w_query: bfloat16 [1024, 1024], P(None, 'mp'), may hold values from -0.1875 to 0.1875
- b_query: bfloat16 [1024], P('mp'), may hold values from -3 to 3
- w_key: bfloat16 [1024, 1024], P(None, 'mp'), may hold values from -0.1875 to 0.1875
- w_value: bfloat16 [1024, 1024], P(None, 'mp'), may hold values from -0.1875 to 0.1875
- b_value: bfloat16 [1024], P('mp'), may hold values from -3 to 3
- w_out: bfloat16 [1024, 1024], P('mp'), may hold values from -0.5 to 0.5
- b_out: bfloat16 [1024], replicated, may hold values from -1.75 to 1.75
- ln2_gain: bfloat16 [1024], replicated, may hold values from 0.5 to 1.5
- ln2_bias: bfloat16 [1024], replicated, may hold values from -1.75 to 1.75
- w_up: bfloat16 [1024, 4096], P(None, 'mp'), may hold values from -0.1875 to 0.1875
- b_up: bfloat16 [4096], P('mp'), may hold values from -3 to 3
- w_down: bfloat16 [4096, 1024], P('mp'), may hold values from -0.09375 to 0.09375
- b_down: bfloat16 [1024], replicated, may hold values from -1.75 to 1.75
- cotangent: bfloat16 [16384, 1024], P(('dp', 'mp')), may hold values from -6 to 6
Outputs:
- output: bfloat16 [16384, 1024], P(('dp', 'mp'))
- grad_tokens: float32 [16384, 1024], P(('dp', 'mp'))
- grad_ln1_gain: float32 [1024], replicated
- grad_ln1_bias: float32 [1024], replicated
- grad_w_query: float32 [1024, 1024], P(None, 'mp')
- grad_b_query: float32 [1024], P('mp')
- grad_w_key: float32 [1024, 1024], P(None, 'mp')
- grad_w_value: float32 [1024, 1024], P(None, 'mp')
- grad_b_value: float32 [1024], P('mp')
- grad_w_out: float32 [1024, 1024], P('mp')
- grad_b_out: float32 [1024], replicated
- grad_ln2_gain: float32 [1024], replicated
- grad_ln2_bias: float32 [1024], replicated
- grad_w_up: float32 [1024, 4096], P(None, 'mp')
- grad_b_up: float32 [4096], P('mp')
- grad_w_down: float32 [4096, 1024], P('mp')
- grad_b_down: float32 [1024], replicated
The draws below stay inside these ranges and needn't reach their ends.
Inputs may be any that keep to these rules, and one draw needn't show every extreme that they name: `segments`: within each group of 2048 rows the ids start at 0 and rise by one from image to image, so an image's patches are consecutive rows. Small images have 30 to 48 patches; in some groups, and always in at least one, the first image has exactly 900 patches; in at least one other group every image has exactly 30 patches; the last image of a group may have fewer patches. No image has more than 900 patches.
All inputs are finite; a program needn't handle non-finite values.
Results may differ from the reference program's by a relative error of at most 0.019.
Values may be sent and summed in bfloat16 or wider, within the bound.
A program may use at most 128 MiB of HBM per device.

```python
import jax
import jax.numpy as jnp
from jax import lax

D = 1024
HEADS = 16
HEAD_DIM = 64
FF = 4096
ROWS = 2048
LONGEST = 900
SMALL_LO = 30
SMALL_HI = 48
TOKENS = 16384


def draw_segments(key, part):
    blocks = TOKENS // ROWS
    coin_key, pick_key, size_key = jax.random.split(key, 3)
    block_index = jnp.arange(blocks)
    chosen = jax.random.randint(pick_key, (), 0, blocks)
    dense = block_index == (chosen + 1) % blocks
    holders = jax.random.randint(coin_key, (blocks,), 0, 4) == 0
    holders = jnp.logical_and(holders, jnp.logical_not(dense))
    holders = jnp.logical_or(holders, block_index == chosen)
    offset = jnp.where(holders, LONGEST, 0).astype(jnp.int32)
    slot_count = ROWS // SMALL_LO + 1
    image_sizes = jax.random.randint(size_key, (blocks, slot_count), SMALL_LO, SMALL_HI + 1)
    image_sizes = jnp.where(dense[:, None], SMALL_LO, image_sizes).astype(jnp.int32)
    image_ends = offset[:, None] + jnp.cumsum(image_sizes, axis=1)
    positions = jnp.arange(ROWS)
    passed = jnp.sum((image_ends[:, None, :] <= positions[None, :, None]).astype(jnp.int32), axis=2)
    segment_ids = jnp.where(positions[None, :] < offset[:, None], 0, passed + holders.astype(jnp.int32)[:, None])
    return segment_ids.reshape(TOKENS).astype(jnp.int32)


def level_of(key, dims, cuts, least, top_value):
    def one(dim, blocks):
        steps = jax.random.uniform(jax.random.fold_in(jax.random.fold_in(key, 6), dim), (blocks,), jnp.float32, least / len(cuts), top_value / len(cuts))
        return jnp.repeat(jnp.exp(steps), dims[dim] // blocks).reshape((-1,) + (1,) * (len(dims) - dim - 1))

    loudness = one(*cuts[0])
    for cut in cuts[1:]:
        loudness = loudness * one(*cut)
    return loudness


def normal_values(key, shape, scale, reach, cuts=(), kind=jnp.bfloat16):
    gain = level_of(key, shape, cuts, -0.22, 0.18) if cuts else 1.0
    values = jax.random.normal(key, shape, jnp.float32) * scale * gain
    return jnp.minimum(jnp.maximum(values, -reach), reach).astype(kind)


def setup_inputs(seed: int = 0) -> dict:
    key_list = jax.random.split(jax.random.key(seed), 19)
    tokens = normal_values(key_list[0], (TOKENS, D), 1.0, 6.0, ((0, 32),))
    segments = draw_segments(jax.random.fold_in(key_list[18], 71), 0)
    ln1_gain = jnp.clip(1.0 + 0.1 * jax.random.normal(key_list[2], (D,), jnp.float32), 0.5, 1.5).astype(jnp.bfloat16)
    ln1_bias = normal_values(key_list[3], (D,), 0.3, 1.75)
    w_query = normal_values(key_list[4], (D, D), D ** -0.5, 0.1875, ((1, 4),))
    b_query = normal_values(key_list[5], (D,), 0.5, 3.0, ((0, 4),))
    w_key = normal_values(key_list[6], (D, D), D ** -0.5, 0.1875, ((1, 4),))
    w_value = normal_values(key_list[7], (D, D), D ** -0.5, 0.1875, ((1, 4),))
    b_value = normal_values(key_list[8], (D,), 0.5, 3.0, ((0, 4),))
    w_out = normal_values(key_list[9], (D, D), (D // 8) ** -0.5, 0.5, ((0, 4),))
    b_out = normal_values(key_list[10], (D,), 0.3, 1.75)
    ln2_gain = jnp.clip(1.0 + 0.1 * jax.random.normal(key_list[11], (D,), jnp.float32), 0.5, 1.5).astype(jnp.bfloat16)
    ln2_bias = normal_values(key_list[12], (D,), 0.3, 1.75)
    w_up = normal_values(key_list[13], (D, FF), D ** -0.5, 0.1875, ((1, 4),))
    b_up = normal_values(key_list[14], (FF,), 0.5, 3.0, ((0, 4),))
    w_down = normal_values(key_list[15], (FF, D), FF ** -0.5, 0.09375, ((0, 4),))
    b_down = normal_values(key_list[16], (D,), 0.3, 1.75)
    cotangent = normal_values(key_list[17], (TOKENS, D), 1.0, 6.0, ((0, 32),))
    return {"tokens": tokens, "segments": segments, "ln1_gain": ln1_gain, "ln1_bias": ln1_bias, "w_query": w_query, "b_query": b_query, "w_key": w_key, "w_value": w_value, "b_value": b_value, "w_out": w_out, "b_out": b_out, "ln2_gain": ln2_gain, "ln2_bias": ln2_bias, "w_up": w_up, "b_up": b_up, "w_down": w_down, "b_down": b_down, "cotangent": cotangent}


@jax.custom_vjp
def low(v):
    return lax.optimization_barrier(v.astype(jnp.bfloat16)).astype(jnp.float32)

@jax.custom_vjp
def low_back(v):
    return v

def low_keep(v):
    return (low(v), None)

def low_pass(kept, grad):
    return (grad,)

def back_keep(v):
    return (v, None)

def back_low(kept, grad):
    return (low(grad),)
low.defvjp(low_keep, low_pass)
low_back.defvjp(back_keep, back_low)
epsilon = 1e-06
minus_big = -1e+30
highest = lax.Precision.HIGHEST

def product(left, right):
    return jnp.dot(left, right, precision=highest, preferred_element_type=jnp.float32)

def layer_norm(values, gain_vec, bias_vec):
    average = lax.optimization_barrier(jnp.mean(values, axis=-1, keepdims=True))
    centered = values - average
    spread = lax.optimization_barrier(jnp.mean(centered * centered, axis=-1, keepdims=True))
    return centered * lax.rsqrt(spread + epsilon) * gain_vec + bias_vec

def attention(query, keys, values, segment_ids):
    all_rows = query.shape[0]
    block_rows = min(512, all_rows)
    score_scale = HEAD_DIM ** (-0.5)
    keys_heads = keys.reshape(all_rows, HEADS, HEAD_DIM)
    values_heads = values.reshape(all_rows, HEADS, HEAD_DIM)

    def one_block(pieces):
        query_block, segment_block = pieces
        raw_scores = jnp.einsum('qhd,khd->hqk', query_block, keys_heads, precision=highest) * score_scale
        raw_scores = low_back(raw_scores)
        same_image = (segment_block[:, None] == segment_ids[None, :])[None]
        masked = jnp.where(same_image, raw_scores, minus_big)
        probabilities = jax.nn.softmax(masked, axis=2)
        return jnp.einsum('hqk,khd->qhd', low(probabilities), values_heads, precision=highest)
    block_count = all_rows // block_rows
    blocks_out = lax.map(jax.checkpoint(one_block), (query.reshape(block_count, block_rows, HEADS, HEAD_DIM), segment_ids.reshape(block_count, block_rows)))
    return blocks_out.reshape(all_rows, HEADS * HEAD_DIM)

def group_forward(weights, group_tokens, group_segments):
    ln1_gain, ln1_bias, w_query, b_query, w_key, w_value, b_value, w_out, b_out, ln2_gain, ln2_bias, w_up, b_up, w_down, b_down = weights
    normed_one = low(layer_norm(group_tokens, ln1_gain, ln1_bias))
    query = low_back(low(product(normed_one, w_query) + b_query))
    keys = low_back(low(product(normed_one, w_key)))
    values = low_back(low(product(normed_one, w_value) + b_value))
    attn = low_back(low(attention(query, keys, values, group_segments)))
    branch = low_back(product(attn, w_out))
    hidden_one = group_tokens + branch + b_out
    normed_two = low(layer_norm(hidden_one, ln2_gain, ln2_bias))
    upper = low_back(product(normed_two, w_up) + b_up)
    active = low(jax.nn.gelu(upper, approximate=False))
    mixed = low_back(product(active, w_down))
    return hidden_one + mixed + b_down

def reference(tokens, segments, ln1_gain, ln1_bias, w_query, b_query, w_key, w_value, b_value, w_out, b_out, ln2_gain, ln2_bias, w_up, b_up, w_down, b_down, cotangent):
    params = tuple((weight_arg.astype(jnp.float32) for weight_arg in (ln1_gain, ln1_bias, w_query, b_query, w_key, w_value, b_value, w_out, b_out, ln2_gain, ln2_bias, w_up, b_up, w_down, b_down)))
    group_total = TOKENS // ROWS
    segment_groups = segments.reshape(group_total, ROWS)

    def forward(weights, inputs):
        token_groups = inputs.reshape(group_total, ROWS, D)
        group_outs = lax.map(lambda group_pair: group_forward(weights, group_pair[0], group_pair[1]), (token_groups, segment_groups))
        return group_outs.reshape(TOKENS, D)
    result, pullback = jax.vjp(forward, params, tokens.astype(jnp.float32))
    grad_params, grad_tokens = pullback(cotangent.astype(jnp.float32))
    g_ln1_gain, g_ln1_bias, g_w_query, g_b_query, g_w_key, g_w_value, g_b_value, g_w_out, g_b_out, g_ln2_gain, g_ln2_bias, g_w_up, g_b_up, g_w_down, g_b_down = grad_params
    return (result.astype(jnp.bfloat16), grad_tokens, g_ln1_gain, g_ln1_bias, g_w_query, g_b_query, g_w_key, g_w_value, g_b_value, g_w_out, g_b_out, g_ln2_gain, g_ln2_bias, g_w_up, g_b_up, g_w_down, g_b_down)
```

```python
import functools

import jax
import jax.numpy as jnp
from jax import lax
from jax.experimental import pallas as pl
from jax.experimental.pallas import tpu as pltpu
from jax.sharding import PartitionSpec as P

HEAD_DIM = 64
LONGEST = 900
HALO = 64
PAIR = 128
EPS = 1e-06
NEG = -1e30
VMEM = 60 * 1024 * 1024
F32 = jnp.float32
BF16 = jnp.bfloat16


def dot_nn(a, b):
    return lax.dot_general(a, b, (((1,), (0,)), ((), ())), preferred_element_type=F32)


def dot_nt(a, b):
    return lax.dot_general(a, b, (((1,), (1,)), ((), ())), preferred_element_type=F32)


def dot_tn(a, b):
    return lax.dot_general(a, b, (((0,), (0,)), ((), ())), preferred_element_type=F32)


def barrier(*xs):
    return lax.optimization_barrier(xs)


def params(*sem, **kw):
    return pltpu.CompilerParams(dimension_semantics=sem, vmem_limit_bytes=VMEM, **kw)


def norm_rows(x):
    mean = jnp.mean(x, axis=1, keepdims=True)
    cent = x - mean
    inv = lax.rsqrt(jnp.mean(cent * cent, axis=1, keepdims=True) + EPS)
    return cent * inv, inv


def qkv_call(n1w, packed, b_q, b_v, own, rows, cw):
    n, dm, _ = packed.shape
    win = n1w.shape[0]

    def body(x_ref, w_ref, bq_ref, bv_ref, q_ref, k_ref, v_ref):
        x = x_ref[...]
        q_ref[0] = (dot_nn(x[own : own + rows], w_ref[0, :, 0:cw]) + bq_ref[0].astype(F32)).astype(BF16)
        k_ref[0] = dot_nn(x, w_ref[0, :, cw : 2 * cw]).astype(BF16)
        v_ref[0] = (dot_nn(x, w_ref[0, :, 2 * cw : 3 * cw]) + bv_ref[0].astype(F32)).astype(BF16)

    return pl.pallas_call(
        body,
        grid=(n,),
        in_specs=[
            pl.BlockSpec((win, dm), lambda d: (0, 0)),
            pl.BlockSpec((1, dm, 4 * cw), lambda d: (d, 0, 0)),
            pl.BlockSpec((1, 1, cw), lambda d: (d, 0, 0)),
            pl.BlockSpec((1, 1, cw), lambda d: (d, 0, 0)),
        ],
        out_specs=[
            pl.BlockSpec((1, rows, cw), lambda d: (d, 0, 0)),
            pl.BlockSpec((1, win, cw), lambda d: (d, 0, 0)),
            pl.BlockSpec((1, win, cw), lambda d: (d, 0, 0)),
        ],
        out_shape=[
            jax.ShapeDtypeStruct((n, rows, cw), BF16),
            jax.ShapeDtypeStruct((n, win, cw), BF16),
            jax.ShapeDtypeStruct((n, win, cw), BF16),
        ],
        compiler_params=params("arbitrary"),
        cost_estimate=pl.CostEstimate(
            flops=2 * n * dm * cw * (rows + 2 * win), bytes_accessed=2 * (n * dm * 4 * cw + win * dm), transcendentals=0
        ),
    )(n1w, packed, b_q[:, None, :], b_v[:, None, :])


def blocks_of(rows, own, win, big):
    if big:
        step = min(256, rows)
        return [(s, step, 0, win) for s in range(0, rows, step)]
    return [(s, 128, own + s - 128, 384) for s in range(0, rows, 128)]


def attn_fwd_call(is_big, q, k, v, qseg, kseg, own):
    n, rows, cw = q.shape
    win = k.shape[1]
    pairs = cw // PAIR

    def work(big, q_ref, k_ref, v_ref, qs_ref, ks_ref, o_ref, l_ref):
        for qs, qn, ks, kn in blocks_of(rows, own, win, big):
            mask = qs_ref[qs : qs + qn, :] == ks_ref[:, ks : ks + kn]
            for h in range(2):
                lanes = slice(h * HEAD_DIM, (h + 1) * HEAD_DIM)
                qh = q_ref[0, qs : qs + qn, lanes] * BF16(HEAD_DIM**-0.5)
                s = jnp.where(mask, dot_nt(qh, k_ref[0, ks : ks + kn, lanes]), NEG)
                top = jnp.max(s, axis=1, keepdims=True)
                p = jnp.exp(s - top)
                total = jnp.sum(p, axis=1, keepdims=True)
                o = dot_nn(p.astype(BF16), v_ref[0, ks : ks + kn, lanes])
                o_ref[0, qs : qs + qn, lanes] = (o / total).astype(BF16)
                l_ref[0, qs : qs + qn, h : h + 1] = top + jnp.log(total)

    def body(big_ref, *refs):
        @pl.when(big_ref[0] == 1)
        def _():
            work(True, *refs)

        @pl.when(big_ref[0] == 0)
        def _():
            work(False, *refs)

    return pl.pallas_call(
        body,
        grid_spec=pltpu.PrefetchScalarGridSpec(
            num_scalar_prefetch=1,
            grid=(n, pairs),
            in_specs=[
                pl.BlockSpec((1, rows, PAIR), lambda d, p, *_: (d, 0, p)),
                pl.BlockSpec((1, win, PAIR), lambda d, p, *_: (d, 0, p)),
                pl.BlockSpec((1, win, PAIR), lambda d, p, *_: (d, 0, p)),
                pl.BlockSpec((rows, 1), lambda d, p, *_: (0, 0)),
                pl.BlockSpec((1, win), lambda d, p, *_: (0, 0)),
            ],
            out_specs=[
                pl.BlockSpec((1, rows, PAIR), lambda d, p, *_: (d, 0, p)),
                pl.BlockSpec((1, rows, 2), lambda d, p, *_: (d * pairs + p, 0, 0)),
            ],
        ),
        out_shape=[
            jax.ShapeDtypeStruct((n, rows, cw), BF16),
            jax.ShapeDtypeStruct((n * pairs, rows, 2), F32),
        ],
        compiler_params=params("arbitrary", "arbitrary"),
        cost_estimate=pl.CostEstimate(
            flops=16 * n * rows * win * cw, bytes_accessed=2 * n * cw * (2 * rows + 2 * win), transcendentals=n * rows * win * 4
        ),
    )(is_big, q, k, v, qseg, kseg)


def attn_bwd_call(info, q, k, v, attn, gattn, lse, qseg, kseg, own):
    n, rows, cw = q.shape
    win = k.shape[1]
    pairs = cw // PAIR
    scale = HEAD_DIM**-0.5

    def work(big, q_ref, k_ref, v_ref, a_ref, g_ref, l_ref, qs_ref, ks_ref, dq_ref, dk_ref, dv_ref, dkt, dvt):
        if not big:
            dkt[...] = jnp.zeros_like(dkt)
            dvt[...] = jnp.zeros_like(dvt)
        for i, (qs, qn, ks, kn) in enumerate(blocks_of(rows, own, win, big)):
            mask = qs_ref[qs : qs + qn, :] == ks_ref[:, ks : ks + kn]
            for h in range(2):
                lanes = slice(h * HEAD_DIM, (h + 1) * HEAD_DIM)
                qh = q_ref[0, qs : qs + qn, lanes] * BF16(scale)
                kh = k_ref[0, ks : ks + kn, lanes]
                gh = g_ref[0, qs : qs + qn, lanes]
                s = jnp.where(mask, dot_nt(qh, kh) - l_ref[0, qs : qs + qn, h : h + 1], NEG)
                p = jnp.exp(s)
                dp = dot_nt(gh, v_ref[0, ks : ks + kn, lanes])
                delta = jnp.sum(
                    gh.astype(F32) * a_ref[0, qs : qs + qn, lanes].astype(F32), axis=1, keepdims=True
                )
                ds = (p * (dp - delta)).astype(BF16)
                dq_ref[0, qs : qs + qn, lanes] = (dot_nn(ds, kh) * scale).astype(BF16)
                dk = dot_tn(qh, ds)
                dv = dot_tn(gh, p.astype(BF16))
                if big and i == 0:
                    dkt[lanes, :] = dk
                    dvt[lanes, :] = dv
                else:
                    dkt[lanes, ks : ks + kn] += dk
                    dvt[lanes, ks : ks + kn] += dv
        dk_ref[0] = dkt[...].T.astype(BF16)
        dv_ref[0] = dvt[...].T.astype(BF16)

    def body(info_ref, *refs):
        @pl.when(info_ref[0] == 1)
        def _():
            work(True, *refs)

        @pl.when(info_ref[0] == 0)
        def _():
            work(False, *refs)

    if pairs > 1:

        def put(d, p, info):
            rel = lax.bitwise_xor(p // (pairs // 2), info[1])
            return (rel, 0, d * (pairs // 2) + p % (pairs // 2))

        half_shape = (2, rows, n * cw // 2)
        half_win = (2, win, n * cw // 2)
    else:

        def put(d, p, info):
            return (0, 0, d)

        half_shape = (1, rows, n * cw)
        half_win = (1, win, n * cw)
    return pl.pallas_call(
        body,
        grid_spec=pltpu.PrefetchScalarGridSpec(
            num_scalar_prefetch=1,
            grid=(n, pairs),
            in_specs=[
                pl.BlockSpec((1, rows, PAIR), lambda d, p, *_: (d, 0, p)),
                pl.BlockSpec((1, win, PAIR), lambda d, p, *_: (d, 0, p)),
                pl.BlockSpec((1, win, PAIR), lambda d, p, *_: (d, 0, p)),
                pl.BlockSpec((1, rows, PAIR), lambda d, p, *_: (d, 0, p)),
                pl.BlockSpec((1, rows, PAIR), lambda d, p, *_: (d, 0, p)),
                pl.BlockSpec((1, rows, 2), lambda d, p, *_: (d * pairs + p, 0, 0)),
                pl.BlockSpec((rows, 1), lambda d, p, *_: (0, 0)),
                pl.BlockSpec((1, win), lambda d, p, *_: (0, 0)),
            ],
            out_specs=[
                pl.BlockSpec((1, rows, PAIR), put),
                pl.BlockSpec((1, win, PAIR), put),
                pl.BlockSpec((1, win, PAIR), put),
            ],
            scratch_shapes=[pltpu.VMEM((PAIR, win), F32), pltpu.VMEM((PAIR, win), F32)],
        ),
        out_shape=[
            jax.ShapeDtypeStruct(half_shape, BF16),
            jax.ShapeDtypeStruct(half_win, BF16),
            jax.ShapeDtypeStruct(half_win, BF16),
        ],
        compiler_params=params("arbitrary", "arbitrary"),
        cost_estimate=pl.CostEstimate(
            flops=40 * n * rows * win * cw, bytes_accessed=2 * n * cw * (4 * rows + 4 * win), transcendentals=n * rows * win * 4
        ),
    )(info, q, k, v, attn, gattn, lse, qseg, kseg)


def out_call(attn, packed, resid, b_out, gain, bias):
    n, rows, cw = attn.shape
    dm = packed.shape[1]

    def body(a_ref, w_ref, x_ref, bo_ref, g_ref, b_ref, h_ref, n_ref):
        d = pl.program_id(0)
        part = dot_nt(a_ref[0], w_ref[0])

        @pl.when(d == 0)
        def _():
            h_ref[...] = part + x_ref[...].astype(F32) + bo_ref[...].astype(F32)

        @pl.when(d > 0)
        def _():
            h_ref[...] += part

        @pl.when(d == n - 1)
        def _():
            hat, _ = norm_rows(h_ref[...])
            n_ref[...] = (hat * g_ref[...].astype(F32) + b_ref[...].astype(F32)).astype(BF16)

    full = lambda d: (0, 0)
    return pl.pallas_call(
        body,
        grid=(n,),
        in_specs=[
            pl.BlockSpec((1, rows, cw), lambda d: (d, 0, 0)),
            pl.BlockSpec((1, dm, cw), lambda d: (d, 0, 3)),
            pl.BlockSpec((rows, dm), full),
            pl.BlockSpec((1, dm), full),
            pl.BlockSpec((1, dm), full),
            pl.BlockSpec((1, dm), full),
        ],
        out_specs=[pl.BlockSpec((rows, dm), full), pl.BlockSpec((rows, dm), full)],
        out_shape=[jax.ShapeDtypeStruct((rows, dm), F32), jax.ShapeDtypeStruct((rows, dm), BF16)],
        compiler_params=params("arbitrary"),
        cost_estimate=pl.CostEstimate(flops=2 * n * rows * cw * dm, bytes_accessed=2 * n * dm * cw, transcendentals=0),
    )(attn, packed, resid, b_out[None], gain[None], bias[None])


def up_call(n2, w_up, b_up):
    rows, dm = n2.shape
    ff = w_up.shape[1]
    tile = 512

    def body(x_ref, w_ref, b_ref, a_ref, s_ref):
        u = dot_nn(x_ref[...], w_ref[...]) + b_ref[...].astype(F32)
        cdf = 0.5 * (1.0 + lax.erf(u * 0.7071067811865476))
        a_ref[...] = (u * cdf).astype(BF16)
        s_ref[...] = (cdf + u * jnp.exp(-0.5 * u * u) * 0.3989422804014327).astype(BF16)

    return pl.pallas_call(
        body,
        grid=(ff // tile,),
        in_specs=[
            pl.BlockSpec((rows, dm), lambda t: (0, 0)),
            pl.BlockSpec((dm, tile), lambda t: (0, t)),
            pl.BlockSpec((1, tile), lambda t: (0, t)),
        ],
        out_specs=[pl.BlockSpec((rows, tile), lambda t: (0, t)), pl.BlockSpec((rows, tile), lambda t: (0, t))],
        out_shape=[jax.ShapeDtypeStruct((rows, ff), BF16), jax.ShapeDtypeStruct((rows, ff), BF16)],
        compiler_params=params("arbitrary"),
        cost_estimate=pl.CostEstimate(flops=2 * rows * dm * ff, bytes_accessed=2 * dm * ff, transcendentals=2 * rows * ff),
    )(n2, w_up, b_up[None])


def norm1_back_call(dq, dk, dv, packed, info, own):
    halves, rows, _ = dq.shape
    n, dm, four = packed.shape
    cw = four // 4
    win = dk.shape[1]
    width = cw // halves

    def body(info_ref, dq_ref, dk_ref, dv_ref, wq_ref, wk_ref, wv_ref, o_ref, h_ref, t_ref, acc):
        step = pl.program_id(0)
        part = dot_nt(dk_ref[0], wk_ref[0]) + dot_nt(dv_ref[0], wv_ref[0])
        mine = dot_nt(dq_ref[0], wq_ref[0])

        @pl.when(step == 0)
        def _():
            acc[...] = part

        @pl.when(step > 0)
        def _():
            acc[...] += part

        acc[own : own + rows, :] += mine

        @pl.when(step == n * halves - 1)
        def _():
            o_ref[...] = acc[own : own + rows, :]
            h_ref[...] = acc[0:own, :].astype(BF16)
            t_ref[...] = acc[own + rows : own + rows + HALO, :].astype(BF16)

    def grad_map(s, info):
        return (s // n, 0, s % n)

    def weight_map(which):
        def f(s, info):
            part = lax.bitwise_xor(s // n, info[1]) if halves > 1 else 0
            return (s % n, 0, which * halves + part)

        return f

    full = lambda s, info: (0, 0)
    return pl.pallas_call(
        body,
        grid_spec=pltpu.PrefetchScalarGridSpec(
            num_scalar_prefetch=1,
            grid=(n * halves,),
            in_specs=[
                pl.BlockSpec((1, rows, width), grad_map),
                pl.BlockSpec((1, win, width), grad_map),
                pl.BlockSpec((1, win, width), grad_map),
                pl.BlockSpec((1, dm, width), weight_map(0)),
                pl.BlockSpec((1, dm, width), weight_map(1)),
                pl.BlockSpec((1, dm, width), weight_map(2)),
            ],
            out_specs=[
                pl.BlockSpec((rows, dm), full),
                pl.BlockSpec((own, dm), full),
                pl.BlockSpec((HALO, dm), full),
            ],
            scratch_shapes=[pltpu.VMEM((win, dm), F32)],
        ),
        out_shape=[
            jax.ShapeDtypeStruct((rows, dm), F32),
            jax.ShapeDtypeStruct((own, dm), BF16),
            jax.ShapeDtypeStruct((HALO, dm), BF16),
        ],
        compiler_params=params("arbitrary"),
        cost_estimate=pl.CostEstimate(
            flops=2 * n * cw * dm * (rows + 2 * win), bytes_accessed=2 * n * cw * (3 * dm + rows + 2 * win), transcendentals=0
        ),
    )(info, dq, dk, dv, packed, packed, packed)


def swap(v, bit):
    return lax.ppermute(v, "dp", [(i, i ^ bit) for i in range(8)])


def plane_spread(v, axis):
    half = v.shape[axis] // 2
    first = lambda a: lax.slice_in_dim(a, 0, half, axis=axis)
    second = lambda a: lax.slice_in_dim(a, half, 2 * half, axis=axis)
    by_x = swap(v, 2)
    by_y = swap(v, 4)
    diag_a = swap(first(by_x), 4)
    diag_b = swap(second(by_y), 2)
    own = [v, by_x, by_y, diag_a, diag_b]
    return own + [swap(a, 1) for a in own]


def gather_shards(shard, me, after=None):
    step = shard.shape[0] // 8
    piece = lax.dynamic_slice_in_dim(shard, me * step, step, axis=0)
    if after is not None:
        piece, _ = barrier(piece, after)
    got = [lax.ppermute(piece, "mp", [((i + d) % 4, i) for i in range(4)]) for d in (1, 2, 3)]
    stack = jnp.stack(got)
    return stack, plane_spread(stack, 1)


def assemble(idx, shard, parts, mode):
    rows, cols = shard.shape
    step = rows // 8
    half = step // 2

    def body(idx_ref, l_ref, *refs):
        ins, out = refs[:-1], refs[-1]
        o = pl.program_id(0)

        def put(d, a, b, x):
            if mode == "stack":
                out[d, 0, a:b, :] = x
            elif mode == "rows":
                out[0, 0, d, 0, a:b, :] = x
            else:
                for j in range(2):
                    rel = lax.bitwise_xor(j, idx_ref[0])
                    for ab in range(2):
                        at = pl.multiple_of(rel * (cols * 2) + ab * cols + d * (cols // 4), 128)
                        src = (2 * j + ab) * (cols // 4)
                        out[a:b, pl.ds(at, cols // 4)] = x[:, src : src + cols // 4]

        put(0, 0, step, l_ref[...])
        for off in range(8):
            base = 5 * (off & 1)

            @pl.when(o == off)
            def _():
                for d in range(3):
                    if off // 2 < 3:
                        put(d + 1, 0, step, ins[base + off // 2][d])
                    else:
                        put(d + 1, 0, half, ins[base + 3][d])
                        put(d + 1, half, step, ins[base + 4][d])

    if mode == "stack":
        shape = (4, 8, step, cols)
        out_spec = pl.BlockSpec((4, 1, step, cols), lambda o, idx: (0, idx[1 + o], 0, 0))
        final = (4, rows, cols)
    elif mode == "rows":
        shape = (2, 2, 4, 2, step, cols)
        out_spec = pl.BlockSpec(
            (1, 1, 4, 1, step, cols),
            lambda o, idx: (
                lax.bitwise_xor(idx[1 + o] // 4, idx[0]),
                lax.rem(idx[1 + o] // 2, 2),
                0,
                lax.rem(idx[1 + o], 2),
                0,
                0,
            ),
        )
        final = (4 * rows, cols)
    else:
        shape = (rows, 4 * cols)
        out_spec = pl.BlockSpec((step, 4 * cols), lambda o, idx: (idx[1 + o], 0))
        final = shape
    once = pl.Buffered(1)
    in_specs = [pl.BlockSpec((step, cols), lambda o, idx: (idx[1 + o], 0))]
    for a in parts:
        in_specs.append(pl.BlockSpec(a.shape, lambda o, idx: (0, 0, 0), pipeline_mode=once))
    out = pl.pallas_call(
        body,
        grid_spec=pltpu.PrefetchScalarGridSpec(
            num_scalar_prefetch=1, grid=(8,), in_specs=in_specs, out_specs=out_spec
        ),
        out_shape=jax.ShapeDtypeStruct(shape, BF16),
        compiler_params=params("arbitrary"),
        cost_estimate=pl.CostEstimate(flops=0, bytes_accessed=16 * rows * cols, transcendentals=0),
    )(idx, shard, *parts)
    return out.reshape(final)


def reduce_grad(a, b, y, x):
    rows, cols = a.shape
    half, quarter = rows // 2, rows // 4
    w = cols // 4

    def cut(v, at, size):
        return lax.dynamic_slice_in_dim(v, at * size, size, axis=0)

    def add(u, v):
        return (u.astype(F32) + v.astype(F32)).astype(BF16)

    a1 = swap(cut(a, 1 - x, half), 2)
    b1 = swap(cut(b, 1 - y, half), 4)
    a = add(cut(a, x, half), a1)
    b = add(cut(b, y, half), b1)
    a2 = swap(cut(a, 1 - y, quarter), 4)
    b2 = swap(cut(b, 1 - x, quarter), 2)
    both = jnp.concatenate([add(cut(a, y, quarter), a2), add(cut(b, x, quarter), b2)], axis=0)
    total = both[:, :w].astype(F32)
    for d in (1, 2, 3):
        got = lax.ppermute(both[:, d * w : (d + 1) * w], "mp", [(i, (i + d) % 4) for i in range(4)])
        total = total + got.astype(F32)
    return plane_spread(total.astype(BF16), 0)


def place_grads(coords, parts, mode):
    two_q, w = parts[0].shape
    q = two_q // 2
    dm = 4 * q

    def body(c_ref, *refs):
        ins, outs = refs[:10], refs[10:]
        for off in range(8):
            y = lax.bitwise_xor(c_ref[0], off >> 2)
            x = lax.bitwise_xor(c_ref[1], (off >> 1) & 1)
            k = lax.bitwise_xor(c_ref[2], off & 1)
            base = 5 * (off & 1)
            for part in range(2):
                if off // 2 < 3:
                    val = ins[base + off // 2][part * q : (part + 1) * q, :]
                else:
                    val = ins[base + 3 + part][...]
                val = val.astype(F32)
                rows = pl.ds(pl.multiple_of((x * 2 + y if part == 0 else y * 2 + x) * q, q), q)
                if mode == "up":
                    outs[0][rows, pl.ds(pl.multiple_of((k * 2 + part) * w, w), w)] = val
                elif mode == "down":
                    outs[0][pl.ds(pl.multiple_of((k * 2 + part) * w, w), w), rows] = val.T
                else:
                    at = pl.ds(pl.multiple_of(k * (w // 2), w // 2), w // 2)
                    if part == 0:
                        outs[0][rows, at] = val[:, : w // 2]
                        outs[1][rows, at] = val[:, w // 2 :]
                    else:
                        outs[2][rows, at] = val[:, : w // 2]
                        outs[3][at, rows] = val[:, w // 2 :].T

    if mode == "up":
        shapes = [(dm, 4 * w)]
    elif mode == "down":
        shapes = [(4 * w, dm)]
    else:
        shapes = [(dm, w), (dm, w), (dm, w), (w, dm)]
    return pl.pallas_call(
        body,
        in_specs=[pl.BlockSpec(memory_space=pltpu.SMEM)] + [pl.BlockSpec(memory_space=pltpu.VMEM)] * 10,
        out_specs=[pl.BlockSpec(memory_space=pltpu.VMEM)] * len(shapes),
        out_shape=[jax.ShapeDtypeStruct(s, F32) for s in shapes],
        compiler_params=pltpu.CompilerParams(vmem_limit_bytes=VMEM),
        cost_estimate=pl.CostEstimate(flops=0, bytes_accessed=6 * 4 * dm * w, transcendentals=0),
    )(coords, *parts)


def relative(stack, z):
    return jnp.roll(stack, -z, axis=0)


def core_first(v, core, axis):
    return jnp.where(core == 0, v, jnp.flip(v, axis))


def gather_any(shard, z, core, mode):
    mp = lax.axis_size("mp")
    whole = relative(lax.all_gather(shard, "mp", axis=0, tiled=False), z)
    if mode == "stack":
        return whole
    if mode == "rows":
        v = whole.reshape(mp, 2, 2, shard.shape[0] // 4, shard.shape[1])
        v = core_first(v.transpose(1, 2, 0, 3, 4), core, 0)
        return v.reshape(mp * shard.shape[0], shard.shape[1])
    v = whole.reshape(mp, shard.shape[0], 2, 2, shard.shape[1] // 4).transpose(1, 2, 3, 0, 4)
    return core_first(v, core, 1).reshape(shard.shape[0], mp * shard.shape[1])


def reduce_any(half, z, core):
    mp = lax.axis_size("mp")
    zero = jnp.zeros_like(half)
    v = jnp.stack([jnp.where(core == 0, half, zero), jnp.where(core == 1, half, zero)], axis=1)
    v = jnp.roll(jnp.moveaxis(v, 3, 0), z, axis=0).astype(BF16)
    v = lax.psum_scatter(v, "mp", scatter_dimension=0, tiled=True)[0]
    return lax.psum(v.astype(BF16), "dp").astype(F32)


def local(
    tokens,
    segments,
    ln1_gain,
    ln1_bias,
    w_query,
    b_query,
    w_key,
    w_value,
    b_value,
    w_out,
    b_out,
    ln2_gain,
    ln2_bias,
    w_up,
    b_up,
    w_down,
    b_down,
    cotangent,
):
    rows, dm = tokens.shape
    cw = w_query.shape[1]
    ffw = w_up.shape[1]
    mp = lax.axis_size("mp")
    dp = lax.axis_size("dp")
    fast = mp == 4 and dp == 8 and rows % 128 == 0
    z = lax.axis_index("mp")
    me = lax.axis_index("dp")
    core = lax.rem(me, 2)
    x = lax.rem(me // 2, 2)
    y = me // 4
    f32 = lambda v: v.astype(F32)

    near = -(-LONGEST // rows)
    own = (near - 1) * rows
    win = own + rows + 2 * HALO
    halo = [
        lax.ppermute(tokens, "mp", [((i + j) % near, i) for i in range(near)]) for j in range(1, near)
    ]
    before = lax.ppermute(tokens[-HALO:], "mp", [(i - 1, i) for i in range(near, mp)])
    behind = lax.ppermute(tokens[:HALO], "mp", [(i + 1, i) for i in range(near - 1, mp - 1)])
    small_vec = jnp.concatenate([b_query, b_value, b_up])
    if fast:
        vecs = [small_vec] + [
            lax.ppermute(small_vec, "mp", [((i + d) % mp, i) for i in range(mp)]) for d in range(1, mp)
        ]
        vecs = jnp.stack(vecs)
    else:
        vecs = relative(lax.all_gather(small_vec, "mp", axis=0, tiled=False), z)
    bq_all, bv_all = vecs[:, :cw], vecs[:, cw : 2 * cw]
    bu_all = vecs[:, 2 * cw :].reshape(mp, 2, 2, ffw // 4).transpose(1, 2, 0, 3)
    bu_all = core_first(bu_all, core, 0).reshape(mp * ffw)

    is_near = z < near
    seg_parts = [
        jnp.where(is_near, lax.dynamic_slice_in_dim(segments, lax.rem(z + j, near) * rows, rows), -1)
        for j in range(1, near)
    ]
    seg_own = lax.dynamic_slice_in_dim(segments, z * rows, rows)
    seg_prev = lax.dynamic_slice_in_dim(segments, jnp.maximum(z * rows - HALO, 0), HALO)
    seg_next = lax.dynamic_slice_in_dim(segments, jnp.minimum((z + 1) * rows, segments.shape[0] - HALO), HALO)
    seg_far = jnp.concatenate(seg_parts)
    seg_far = jnp.concatenate([seg_far[:-HALO], jnp.where(is_near, seg_far[-HALO:], seg_prev)])
    has_next = jnp.logical_and(z >= near - 1, z < mp - 1)
    seg_win = jnp.concatenate(
        [seg_far, seg_own, jnp.where(has_next, seg_next, -1), jnp.full((HALO,), -1, segments.dtype)]
    )
    kseg, qseg = seg_win[None, :], seg_own[:, None]
    info = jnp.stack([is_near.astype(jnp.int32), core]).astype(jnp.int32)

    pack = jnp.concatenate([w_query, w_key, w_value, w_out.T], axis=1)
    if fast:
        idx = jnp.concatenate([core[None], jnp.bitwise_xor(me, jnp.arange(8, dtype=jnp.int32))]).astype(jnp.int32)
        mark1, parts1 = gather_shards(pack, me)
        mark2, parts2 = gather_shards(w_up, me, mark1)
        _, parts3 = gather_shards(w_down, me, mark2)
        packed = assemble(idx, pack, parts1, "stack")
        up_all = assemble(idx, w_up, parts2, "cols")
        down_all = assemble(idx, w_down, parts3, "rows")
    else:
        packed = gather_any(pack, z, core, "stack")
        up_all = gather_any(w_up, z, core, "cols")
        down_all = gather_any(w_down, z, core, "rows")

    far = jnp.concatenate(halo, axis=0)
    far = jnp.concatenate([far[:-HALO], far[-HALO:] + before], axis=0)
    tok_win = jnp.concatenate([far, tokens, behind, jnp.zeros((HALO, dm), tokens.dtype)], axis=0)
    hat_win, inv_win = norm_rows(f32(tok_win))
    n1w = (hat_win * f32(ln1_gain) + f32(ln1_bias)).astype(BF16)
    q, k, v = qkv_call(n1w, packed, bq_all, bv_all, own, rows, cw)
    attn, lse = attn_fwd_call(info, q, k, v, qseg, kseg, own)
    hidden, n2 = out_call(attn, packed, tokens, b_out, ln2_gain, ln2_bias)
    active, slope = up_call(n2, up_all, bu_all)
    output = (hidden + dot_nn(active, down_all) + f32(b_down)).astype(BF16)

    other = lambda v: lax.ppermute(v, "dp", [(i, i ^ 1) for i in range(dp)])
    hw = mp * ffw // 2
    cot_o = other(cotangent)
    act_o = other(active[:, hw:])
    gout = f32(cotangent)

    def pair_grad(left, right, left_o, right_o):
        return (dot_tn(left, right) + dot_tn(left_o, right_o)).astype(BF16)

    gd_a = pair_grad(cotangent, active[:, : hw // 2], cot_o, act_o[:, : hw // 2])
    gd_b = pair_grad(cotangent, active[:, hw // 2 : hw], cot_o, act_o[:, hw // 2 :])
    g_upper = (dot_nt(cotangent, down_all) * f32(slope)).astype(BF16)
    n2_o = other(n2)
    gup_o = other(g_upper[:, hw:])
    gu_a = pair_grad(n2, g_upper[:, : hw // 2], n2_o, gup_o[:, : hw // 2])
    gu_b = pair_grad(n2, g_upper[:, hw // 2 : hw], n2_o, gup_o[:, hw // 2 :])
    g_b_up = jnp.sum(f32(g_upper), axis=0)
    g_n2 = dot_nt(g_upper, up_all)
    hat2, inv2 = norm_rows(hidden)

    def norm_back(g, hat, inv, gain):
        gg = g * gain
        first = jnp.mean(gg, axis=1, keepdims=True)
        second = jnp.mean(gg * hat, axis=1, keepdims=True)
        return inv * (gg - first - hat * second), jnp.sum(g * hat, axis=0), jnp.sum(g, axis=0)

    g_hidden, g_gain2, g_bias2 = norm_back(g_n2, hat2, inv2, f32(ln2_gain))
    g_hidden = g_hidden + gout
    ghb = g_hidden.astype(BF16)

    g_attn = jnp.stack([dot_nn(ghb, packed[d, :, 3 * cw :]).astype(BF16) for d in range(mp)])
    dq, dk, dv = attn_bwd_call(info, q, k, v, attn, g_attn, lse, qseg, kseg, own)
    halves = dq.shape[0]
    g_own, g_far, g_next = norm1_back_call(dq, dk, dv, packed, info, own)
    back = g_own
    for j in range(1, near):
        part = g_far[(j - 1) * rows : j * rows]
        back = back + f32(lax.ppermute(part, "mp", [(i, (i + j) % near) for i in range(near)]))
    to_prev = f32(lax.ppermute(g_far[-HALO:], "mp", [(i, i - 1) for i in range(near, mp)]))
    to_next = f32(lax.ppermute(g_next, "mp", [(i, i + 1) for i in range(near - 1, mp - 1)]))
    back = jnp.concatenate([back[:HALO] + to_next, back[HALO:-HALO], back[-HALO:] + to_prev], axis=0)
    hat1 = hat_win[own : own + rows]
    inv1 = inv_win[own : own + rows]
    g_in, g_gain1, g_bias1 = norm_back(back, hat1, inv1, f32(ln1_gain))
    g_tokens = g_in + g_hidden

    n1 = n1w[own : own + rows]
    if fast:
        n1w_o = other(n1w)
        ghb_o = other(ghb)
        attn_h = attn.reshape(mp, rows, 2, cw // 2).transpose(2, 1, 0, 3).reshape(2, rows, mp * cw // 2)
        attn_m = lax.dynamic_index_in_dim(attn_h, core, 0, keepdims=False)
        attn_t = lax.dynamic_index_in_dim(attn_h, 1 - core, 0, keepdims=False)
        dq_o, dk_o, dv_o, at_o = other(dq[1]), other(dk[1]), other(dv[1]), other(attn_t)
        n1_o = n1w_o[own : own + rows]
        half = cw // 2
        by_shard = lambda v: v.reshape(dm, mp, half)
        gq = by_shard(pair_grad(n1, dq[0], n1_o, dq_o))
        gk = by_shard(pair_grad(n1w, dk[0], n1w_o, dk_o))
        gv = by_shard(pair_grad(n1w, dv[0], n1w_o, dv_o))
        go = by_shard(pair_grad(ghb, attn_m, ghb_o, at_o))
        gp_a = jnp.concatenate([gq, gk], axis=2).reshape(dm, mp * cw)
        gp_b = jnp.concatenate([gv, go], axis=2).reshape(dm, mp * cw)
        coords = jnp.stack([y, x, core]).astype(jnp.int32)
        (g_w_down,) = place_grads(coords, reduce_grad(gd_a, gd_b, y, x), "down")
        (g_w_up,) = place_grads(coords, reduce_grad(gu_a, gu_b, y, x), "up")
        g_w_query, g_w_key, g_w_value, g_w_out = place_grads(coords, reduce_grad(gp_a, gp_b, y, x), "pack")
    else:
        two = lambda a, b: jnp.stack([a, b], axis=1).reshape(dm, 2, mp, ffw // 4)
        g_w_up = reduce_any(two(gu_a, gu_b), z, core).reshape(dm, ffw)
        g_w_down = reduce_any(two(gd_a, gd_b), z, core).reshape(dm, ffw).T

        def whole_grad(left, right, name=None):
            v = dot_tn(left, right).astype(BF16).reshape(dm, mp, cw)
            v = jnp.roll(jnp.moveaxis(v, 1, 0), z, axis=0)
            v = lax.psum_scatter(v, "mp", scatter_dimension=0, tiled=True)[0]
            return lax.psum(v, "dp").astype(F32)

        def whole(v):
            if halves == 1:
                return v[0]
            v = v.reshape(2, v.shape[1], mp, cw // 2).transpose(1, 2, 0, 3)
            return core_first(v, core, 2).reshape(v.shape[0], mp * cw)

        g_w_query = whole_grad(n1, whole(dq))
        g_w_key = whole_grad(n1w, whole(dk))
        g_w_value = whole_grad(n1w, whole(dv))
        g_w_out = whole_grad(ghb, attn.transpose(1, 0, 2).reshape(rows, mp * cw)).T

    def shards(v, width):
        if v.shape[0] == 2:
            v = core_first(v.reshape(2, mp, width // 2), core, 0).transpose(1, 0, 2)
        return jnp.roll(v.reshape(mp, width), z, axis=0).reshape(mp * width)

    gbq = shards(jnp.sum(f32(dq), axis=1), cw)
    gbv = shards(jnp.sum(f32(dv), axis=1), cw)
    gbu = core_first(g_b_up.reshape(2, 2, mp, ffw // 4), core, 0).transpose(2, 0, 1, 3)
    gbu = jnp.roll(gbu.reshape(mp, ffw), z, axis=0).reshape(-1)
    vec = jnp.concatenate(
        [g_gain1, g_bias1, jnp.sum(g_hidden, axis=0), g_gain2, g_bias2, jnp.sum(gout, axis=0), gbq, gbv, gbu]
    )
    vec = lax.psum(vec, ("dp", "mp"))
    g_gain1, g_bias1, g_b_out, g_gain2, g_bias2, g_b_down = (vec[i * dm : (i + 1) * dm] for i in range(6))
    at = 6 * dm
    g_b_query = lax.dynamic_slice_in_dim(vec, at + z * cw, cw)
    g_b_value = lax.dynamic_slice_in_dim(vec, at + mp * cw + z * cw, cw)
    g_b_up = lax.dynamic_slice_in_dim(vec, at + 2 * mp * cw + z * ffw, ffw)
    return (
        output,
        g_tokens,
        g_gain1,
        g_bias1,
        g_w_query,
        g_b_query,
        g_w_key,
        g_w_value,
        g_b_value,
        g_w_out,
        g_b_out,
        g_gain2,
        g_bias2,
        g_w_up,
        g_b_up,
        g_w_down,
        g_b_down,
    )


def solution(mesh):
    in_specs = (
        P(("dp", "mp"), None),
        P("dp"),
        P(),
        P(),
        P(None, "mp"),
        P("mp"),
        P(None, "mp"),
        P(None, "mp"),
        P("mp"),
        P("mp", None),
        P(),
        P(),
        P(),
        P(None, "mp"),
        P("mp"),
        P("mp", None),
        P(),
        P(("dp", "mp"), None),
    )
    out_specs = (
        P(("dp", "mp"), None),
        P(("dp", "mp"), None),
        P(),
        P(),
        P(None, "mp"),
        P("mp"),
        P(None, "mp"),
        P(None, "mp"),
        P("mp"),
        P("mp", None),
        P(),
        P(),
        P(),
        P(None, "mp"),
        P("mp"),
        P("mp", None),
        P(),
    )
    return jax.shard_map(local, mesh=mesh, in_specs=in_specs, out_specs=out_specs, check_vma=False)
```

```python
import functools

import jax
import jax.numpy as jnp
from jax import lax
from jax.experimental import pallas as pl
from jax.experimental.pallas import tpu as pltpu
from jax.sharding import PartitionSpec as P

HEAD_DIM = 64
LONGEST = 900
HALO = 64
PAIR = 128
EPS = 1e-06
NEG = -1e30
VMEM = 60 * 1024 * 1024
F32 = jnp.float32
BF16 = jnp.bfloat16


def dot_nn(a, b):
    return lax.dot_general(a, b, (((1,), (0,)), ((), ())), preferred_element_type=F32)


def dot_nt(a, b):
    return lax.dot_general(a, b, (((1,), (1,)), ((), ())), preferred_element_type=F32)


def dot_tn(a, b):
    return lax.dot_general(a, b, (((0,), (0,)), ((), ())), preferred_element_type=F32)


def barrier(*xs):
    return lax.optimization_barrier(xs)


def params(*sem, **kw):
    return pltpu.CompilerParams(dimension_semantics=sem, vmem_limit_bytes=VMEM, **kw)


def norm_rows(x):
    mean = jnp.mean(x, axis=1, keepdims=True)
    cent = x - mean
    inv = lax.rsqrt(jnp.mean(cent * cent, axis=1, keepdims=True) + EPS)
    return cent * inv, inv


def qkv_call(n1w, packed, b_q, b_v, own, rows, cw):
    n, dm, _ = packed.shape
    win = n1w.shape[0]

    def body(x_ref, w_ref, bq_ref, bv_ref, q_ref, k_ref, v_ref):
        x = x_ref[...]
        q_ref[0] = (dot_nn(x[own : own + rows], w_ref[0, :, 0:cw]) + bq_ref[0].astype(F32)).astype(BF16)
        k_ref[0] = dot_nn(x, w_ref[0, :, cw : 2 * cw]).astype(BF16)
        v_ref[0] = (dot_nn(x, w_ref[0, :, 2 * cw : 3 * cw]) + bv_ref[0].astype(F32)).astype(BF16)

    return pl.pallas_call(
        body,
        grid=(n,),
        in_specs=[
            pl.BlockSpec((win, dm), lambda d: (0, 0)),
            pl.BlockSpec((1, dm, 4 * cw), lambda d: (d, 0, 0)),
            pl.BlockSpec((1, 1, cw), lambda d: (d, 0, 0)),
            pl.BlockSpec((1, 1, cw), lambda d: (d, 0, 0)),
        ],
        out_specs=[
            pl.BlockSpec((1, rows, cw), lambda d: (d, 0, 0)),
            pl.BlockSpec((1, win, cw), lambda d: (d, 0, 0)),
            pl.BlockSpec((1, win, cw), lambda d: (d, 0, 0)),
        ],
        out_shape=[
            jax.ShapeDtypeStruct((n, rows, cw), BF16),
            jax.ShapeDtypeStruct((n, win, cw), BF16),
            jax.ShapeDtypeStruct((n, win, cw), BF16),
        ],
        compiler_params=params("arbitrary"),
        cost_estimate=pl.CostEstimate(
            flops=2 * n * dm * cw * (rows + 2 * win), bytes_accessed=2 * (n * dm * 4 * cw + win * dm), transcendentals=0
        ),
    )(n1w, packed, b_q[:, None, :], b_v[:, None, :])


def blocks_of(rows, own, win, big):
    if big:
        step = min(256, rows)
        return [(s, step, 0, win) for s in range(0, rows, step)]
    return [(s, 128, own + s - 128, 384) for s in range(0, rows, 128)]


def attn_fwd_call(is_big, q, k, v, qseg, kseg, own):
    n, rows, cw = q.shape
    win = k.shape[1]
    pairs = cw // PAIR

    def work(big, q_ref, k_ref, v_ref, qs_ref, ks_ref, o_ref, l_ref):
        for qs, qn, ks, kn in blocks_of(rows, own, win, big):
            mask = qs_ref[qs : qs + qn, :] == ks_ref[:, ks : ks + kn]
            for h in range(2):
                lanes = slice(h * HEAD_DIM, (h + 1) * HEAD_DIM)
                qh = q_ref[0, qs : qs + qn, lanes] * BF16(HEAD_DIM**-0.5)
                s = jnp.where(mask, dot_nt(qh, k_ref[0, ks : ks + kn, lanes]), NEG)
                top = jnp.max(s, axis=1, keepdims=True)
                p = jnp.exp(s - top)
                total = jnp.sum(p, axis=1, keepdims=True)
                o = dot_nn(p.astype(BF16), v_ref[0, ks : ks + kn, lanes])
                o_ref[0, qs : qs + qn, lanes] = (o / total).astype(BF16)
                l_ref[0, qs : qs + qn, h : h + 1] = top + jnp.log(total)

    def body(big_ref, *refs):
        @pl.when(big_ref[0] == 1)
        def _():
            work(True, *refs)

        @pl.when(big_ref[0] == 0)
        def _():
            work(False, *refs)

    return pl.pallas_call(
        body,
        grid_spec=pltpu.PrefetchScalarGridSpec(
            num_scalar_prefetch=1,
            grid=(n, pairs),
            in_specs=[
                pl.BlockSpec((1, rows, PAIR), lambda d, p, *_: (d, 0, p)),
                pl.BlockSpec((1, win, PAIR), lambda d, p, *_: (d, 0, p)),
                pl.BlockSpec((1, win, PAIR), lambda d, p, *_: (d, 0, p)),
                pl.BlockSpec((rows, 1), lambda d, p, *_: (0, 0)),
                pl.BlockSpec((1, win), lambda d, p, *_: (0, 0)),
            ],
            out_specs=[
                pl.BlockSpec((1, rows, PAIR), lambda d, p, *_: (d, 0, p)),
                pl.BlockSpec((1, rows, 2), lambda d, p, *_: (d * pairs + p, 0, 0)),
            ],
        ),
        out_shape=[
            jax.ShapeDtypeStruct((n, rows, cw), BF16),
            jax.ShapeDtypeStruct((n * pairs, rows, 2), F32),
        ],
        compiler_params=params("arbitrary", "arbitrary"),
        cost_estimate=pl.CostEstimate(
            flops=16 * n * rows * win * cw, bytes_accessed=2 * n * cw * (2 * rows + 2 * win), transcendentals=n * rows * win * 4
        ),
    )(is_big, q, k, v, qseg, kseg)


def attn_bwd_call(info, q, k, v, attn, gattn, lse, qseg, kseg, own):
    n, rows, cw = q.shape
    win = k.shape[1]
    pairs = cw // PAIR
    scale = HEAD_DIM**-0.5

    def work(big, q_ref, k_ref, v_ref, a_ref, g_ref, l_ref, qs_ref, ks_ref, dq_ref, dk_ref, dv_ref, dkt, dvt):
        if not big:
            dkt[...] = jnp.zeros_like(dkt)
            dvt[...] = jnp.zeros_like(dvt)
        for i, (qs, qn, ks, kn) in enumerate(blocks_of(rows, own, win, big)):
            mask = qs_ref[qs : qs + qn, :] == ks_ref[:, ks : ks + kn]
            for h in range(2):
                lanes = slice(h * HEAD_DIM, (h + 1) * HEAD_DIM)
                qh = q_ref[0, qs : qs + qn, lanes] * BF16(scale)
                kh = k_ref[0, ks : ks + kn, lanes]
                gh = g_ref[0, qs : qs + qn, lanes]
                s = jnp.where(mask, dot_nt(qh, kh) - l_ref[0, qs : qs + qn, h : h + 1], NEG)
                p = jnp.exp(s)
                dp = dot_nt(gh, v_ref[0, ks : ks + kn, lanes])
                delta = jnp.sum(
                    gh.astype(F32) * a_ref[0, qs : qs + qn, lanes].astype(F32), axis=1, keepdims=True
                )
                ds = (p * (dp - delta)).astype(BF16)
                dq_ref[0, qs : qs + qn, lanes] = (dot_nn(ds, kh) * scale).astype(BF16)
                dk = dot_tn(qh, ds)
                dv = dot_tn(gh, p.astype(BF16))
                if big and i == 0:
                    dkt[lanes, :] = dk
                    dvt[lanes, :] = dv
                else:
                    dkt[lanes, ks : ks + kn] += dk
                    dvt[lanes, ks : ks + kn] += dv
        dk_ref[0] = dkt[...].T.astype(BF16)
        dv_ref[0] = dvt[...].T.astype(BF16)

    def body(info_ref, *refs):
        @pl.when(info_ref[0] == 1)
        def _():
            work(True, *refs)

        @pl.when(info_ref[0] == 0)
        def _():
            work(False, *refs)

    if pairs > 1:

        def put(d, p, info):
            rel = lax.bitwise_xor(p // (pairs // 2), info[1])
            return (rel, 0, d * (pairs // 2) + p % (pairs // 2))

        half_shape = (2, rows, n * cw // 2)
        half_win = (2, win, n * cw // 2)
    else:

        def put(d, p, info):
            return (0, 0, d)

        half_shape = (1, rows, n * cw)
        half_win = (1, win, n * cw)
    return pl.pallas_call(
        body,
        grid_spec=pltpu.PrefetchScalarGridSpec(
            num_scalar_prefetch=1,
            grid=(n, pairs),
            in_specs=[
                pl.BlockSpec((1, rows, PAIR), lambda d, p, *_: (d, 0, p)),
                pl.BlockSpec((1, win, PAIR), lambda d, p, *_: (d, 0, p)),
                pl.BlockSpec((1, win, PAIR), lambda d, p, *_: (d, 0, p)),
                pl.BlockSpec((1, rows, PAIR), lambda d, p, *_: (d, 0, p)),
                pl.BlockSpec((1, rows, PAIR), lambda d, p, *_: (d, 0, p)),
                pl.BlockSpec((1, rows, 2), lambda d, p, *_: (d * pairs + p, 0, 0)),
                pl.BlockSpec((rows, 1), lambda d, p, *_: (0, 0)),
                pl.BlockSpec((1, win), lambda d, p, *_: (0, 0)),
            ],
            out_specs=[
                pl.BlockSpec((1, rows, PAIR), put),
                pl.BlockSpec((1, win, PAIR), put),
                pl.BlockSpec((1, win, PAIR), put),
            ],
            scratch_shapes=[pltpu.VMEM((PAIR, win), F32), pltpu.VMEM((PAIR, win), F32)],
        ),
        out_shape=[
            jax.ShapeDtypeStruct(half_shape, BF16),
            jax.ShapeDtypeStruct(half_win, BF16),
            jax.ShapeDtypeStruct(half_win, BF16),
        ],
        compiler_params=params("arbitrary", "arbitrary"),
        cost_estimate=pl.CostEstimate(
            flops=40 * n * rows * win * cw, bytes_accessed=2 * n * cw * (4 * rows + 4 * win), transcendentals=n * rows * win * 4
        ),
    )(info, q, k, v, attn, gattn, lse, qseg, kseg)


def out_call(attn, packed, resid, b_out, gain, bias):
    n, rows, cw = attn.shape
    dm = packed.shape[1]

    def body(a_ref, w_ref, x_ref, bo_ref, g_ref, b_ref, h_ref, n_ref):
        d = pl.program_id(0)
        part = dot_nt(a_ref[0], w_ref[0])

        @pl.when(d == 0)
        def _():
            h_ref[...] = part + x_ref[...].astype(F32) + bo_ref[...].astype(F32)

        @pl.when(d > 0)
        def _():
            h_ref[...] += part

        @pl.when(d == n - 1)
        def _():
            hat, _ = norm_rows(h_ref[...])
            n_ref[...] = (hat * g_ref[...].astype(F32) + b_ref[...].astype(F32)).astype(BF16)

    full = lambda d: (0, 0)
    return pl.pallas_call(
        body,
        grid=(n,),
        in_specs=[
            pl.BlockSpec((1, rows, cw), lambda d: (d, 0, 0)),
            pl.BlockSpec((1, dm, cw), lambda d: (d, 0, 3)),
            pl.BlockSpec((rows, dm), full),
            pl.BlockSpec((1, dm), full),
            pl.BlockSpec((1, dm), full),
            pl.BlockSpec((1, dm), full),
        ],
        out_specs=[pl.BlockSpec((rows, dm), full), pl.BlockSpec((rows, dm), full)],
        out_shape=[jax.ShapeDtypeStruct((rows, dm), F32), jax.ShapeDtypeStruct((rows, dm), BF16)],
        compiler_params=params("arbitrary"),
        cost_estimate=pl.CostEstimate(flops=2 * n * rows * cw * dm, bytes_accessed=2 * n * dm * cw, transcendentals=0),
    )(attn, packed, resid, b_out[None], gain[None], bias[None])


def ffn_call(core, n2, hidden, cot, w_up, w_down, b_up, b_down, halves):
    rows, dm = n2.shape
    n, _, ffw = w_up.shape
    tile = ffw // halves

    def body(core_ref, x_ref, h_ref, c_ref, wu_ref, wd_ref, bu_ref, bd_ref, o_ref, gn_ref, a_ref, gu_ref, gb_ref, acc):
        t = pl.program_id(0)
        u = dot_nn(x_ref[...], wu_ref[0]) + bu_ref[...].astype(F32)
        cdf = 0.5 * (1.0 + lax.erf(u * 0.7071067811865476))
        act = (u * cdf).astype(BF16)
        slope = cdf + u * jnp.exp(-0.5 * u * u) * 0.3989422804014327
        a_ref[...] = act
        grad = dot_nt(c_ref[...], wd_ref[0]) * slope
        gu = grad.astype(BF16)
        gu_ref[...] = gu
        gb_ref[...] = jnp.sum(gu.astype(F32), axis=0, keepdims=True)
        out = dot_nn(act, wd_ref[0])
        gn = dot_nt(gu, wu_ref[0])

        @pl.when(t == 0)
        def _():
            acc[...] = h_ref[...] + bd_ref[...].astype(F32) + out
            gn_ref[...] = gn

        @pl.when(t > 0)
        def _():
            acc[...] += out
            gn_ref[...] += gn

        @pl.when(t == n * halves - 1)
        def _():
            o_ref[...] = acc[...].astype(BF16)

    full = lambda t, c: (0, 0)

    def part(t, c):
        return lax.bitwise_xor(t // n, c[0]) if halves > 1 else 0

    return pl.pallas_call(
        body,
        grid_spec=pltpu.PrefetchScalarGridSpec(
            num_scalar_prefetch=1,
            grid=(n * halves,),
            in_specs=[
                pl.BlockSpec((rows, dm), full),
                pl.BlockSpec((rows, dm), full),
                pl.BlockSpec((rows, dm), full),
                pl.BlockSpec((1, dm, tile), lambda t, c: (t % n, 0, part(t, c))),
                pl.BlockSpec((1, tile, dm), lambda t, c: (t % n, part(t, c), 0)),
                pl.BlockSpec((1, tile), lambda t, c: (0, t)),
                pl.BlockSpec((1, dm), full),
            ],
            out_specs=[
                pl.BlockSpec((rows, dm), full),
                pl.BlockSpec((rows, dm), full),
                pl.BlockSpec((rows, tile), lambda t, c: (0, t)),
                pl.BlockSpec((rows, tile), lambda t, c: (0, t)),
                pl.BlockSpec((1, tile), lambda t, c: (0, t)),
            ],
            scratch_shapes=[pltpu.VMEM((rows, dm), F32)],
        ),
        out_shape=[
            jax.ShapeDtypeStruct((rows, dm), BF16),
            jax.ShapeDtypeStruct((rows, dm), F32),
            jax.ShapeDtypeStruct((rows, n * ffw), BF16),
            jax.ShapeDtypeStruct((rows, n * ffw), BF16),
            jax.ShapeDtypeStruct((1, n * ffw), F32),
        ],
        compiler_params=params("arbitrary"),
        cost_estimate=pl.CostEstimate(
            flops=8 * rows * dm * n * ffw, bytes_accessed=4 * n * dm * ffw, transcendentals=2 * rows * n * ffw
        ),
    )(core, n2, hidden, cot, w_up, w_down, b_up[None], b_down[None])


def norm1_back_call(dq, dk, dv, packed, info, own):
    halves, rows, _ = dq.shape
    n, dm, four = packed.shape
    cw = four // 4
    win = dk.shape[1]
    width = cw // halves

    def body(info_ref, dq_ref, dk_ref, dv_ref, w_ref, o_ref, h_ref, t_ref, acc):
        step = pl.program_id(0)

        def weight(which, j):
            at = lax.bitwise_xor(j, info_ref[1]) if halves > 1 else 0
            return w_ref[0, :, pl.ds(pl.multiple_of(which * cw + at * width, width), width)]

        left = jnp.concatenate([r[j] for r in (dk_ref, dv_ref) for j in range(halves)], axis=1)
        right = jnp.concatenate([weight(m, j) for m in (1, 2) for j in range(halves)], axis=1)
        part = dot_nt(left, right)
        left = jnp.concatenate([dq_ref[j] for j in range(halves)], axis=1)
        right = jnp.concatenate([weight(0, j) for j in range(halves)], axis=1)
        mine = dot_nt(left, right)

        @pl.when(step == 0)
        def _():
            acc[...] = part

        @pl.when(step > 0)
        def _():
            acc[...] += part

        acc[own : own + rows, :] += mine

        @pl.when(step == n - 1)
        def _():
            o_ref[...] = acc[own : own + rows, :]
            h_ref[...] = acc[0:own, :].astype(BF16)
            t_ref[...] = acc[own + rows : own + rows + HALO, :].astype(BF16)

    full = lambda s, info: (0, 0)
    return pl.pallas_call(
        body,
        grid_spec=pltpu.PrefetchScalarGridSpec(
            num_scalar_prefetch=1,
            grid=(n,),
            in_specs=[
                pl.BlockSpec((halves, rows, width), lambda s, info: (0, 0, s)),
                pl.BlockSpec((halves, win, width), lambda s, info: (0, 0, s)),
                pl.BlockSpec((halves, win, width), lambda s, info: (0, 0, s)),
                pl.BlockSpec((1, dm, four), lambda s, info: (s, 0, 0)),
            ],
            out_specs=[
                pl.BlockSpec((rows, dm), full),
                pl.BlockSpec((own, dm), full),
                pl.BlockSpec((HALO, dm), full),
            ],
            scratch_shapes=[pltpu.VMEM((win, dm), F32)],
        ),
        out_shape=[
            jax.ShapeDtypeStruct((rows, dm), F32),
            jax.ShapeDtypeStruct((own, dm), BF16),
            jax.ShapeDtypeStruct((HALO, dm), BF16),
        ],
        compiler_params=params("arbitrary"),
        cost_estimate=pl.CostEstimate(
            flops=2 * n * cw * dm * (rows + 2 * win), bytes_accessed=2 * n * cw * (3 * dm + rows + 2 * win), transcendentals=0
        ),
    )(info, dq, dk, dv, packed)


MESH = pl.DeviceIdType.MESH


class Place:
    def __init__(self):
        self.me = lax.axis_index("dp")
        self.z = lax.axis_index("mp")
        self.k = lax.rem(self.me, 2)
        self.x = lax.rem(self.me // 2, 2)
        self.y = self.me // 4
        self.me_k = self.me + 1 - 2 * self.k
        self.me_x = self.me + 2 - 4 * self.x
        self.me_y = self.me + 4 - 8 * self.y
        self.me_xy = self.me_x + 4 - 8 * self.y
        self.core = {"dp": self.me_k, "mp": self.z}
        self.by_x = {"dp": self.me_x, "mp": self.z}
        self.by_y = {"dp": self.me_y, "mp": self.z}

    def along(self, d):
        return {"dp": self.me, "mp": lax.rem(self.z + d, 4)}

    def meet(self):
        sem = pltpu.get_barrier_semaphore()
        for dev in (self.core, self.by_x, self.by_y, self.along(1), self.along(2), self.along(3)):
            pl.semaphore_signal(sem, inc=1, device_id=dev, device_id_type=MESH)
        pl.semaphore_wait(sem, 6)


class Wire:
    def __init__(self, send, recv):
        self.send, self.recv = send, recv
        self.open = []

    def start(self, slot, src, dst, dev):
        copy = pltpu.make_async_remote_copy(
            src_ref=src, dst_ref=dst, send_sem=self.send.at[slot], recv_sem=self.recv.at[slot],
            device_id=dev, device_id_type=MESH,
        )
        copy.start()
        self.open.append(copy)

    def landed(self, slot, ref, dev):
        pltpu.make_async_remote_copy(
            src_ref=ref, dst_ref=ref, send_sem=self.send.at[slot], recv_sem=self.recv.at[slot],
            device_id=dev, device_id_type=MESH,
        ).wait_recv()

    def drain(self):
        for copy in self.open:
            copy.wait_send()


def gather_steps(place, wire, base, shard, whole):
    step = shard.shape[0] // 8
    half = step // 2

    def rows(who, at=0, size=step):
        return pl.ds(pl.multiple_of(who * step + at, half), size)

    def slot(d, kind):
        return base + (d - 1) * 9 + kind

    def begin():
        for d in (1, 2, 3):
            wire.start(slot(d, 0), shard.at[rows(place.me)], whole.at[d, rows(place.me)], place.along(4 - d))

    def first(d):
        mine = whole.at[d, rows(place.me)]
        wire.landed(slot(d, 0), mine, place.along(d))
        wire.start(slot(d, 2), mine, mine, place.by_x)
        wire.start(slot(d, 3), mine, mine, place.by_y)
        wire.start(slot(d, 1), mine, mine, place.core)

    def second(d):
        got = whole.at[d, rows(place.me_x)]
        wire.landed(slot(d, 2), got, place.by_x)
        part = whole.at[d, rows(place.me_x, 0, half)]
        wire.start(slot(d, 4), part, part, place.by_y)
        wire.start(slot(d, 6), got, got, place.core)
        got = whole.at[d, rows(place.me_y)]
        wire.landed(slot(d, 3), got, place.by_y)
        part = whole.at[d, rows(place.me_y, half, half)]
        wire.start(slot(d, 5), part, part, place.by_x)
        wire.start(slot(d, 7), got, got, place.core)

    def third(d):
        wire.landed(slot(d, 4), whole.at[d, rows(place.me_xy, 0, half)], place.by_y)
        wire.landed(slot(d, 5), whole.at[d, rows(place.me_xy, half, half)], place.by_x)
        got = whole.at[d, rows(place.me_xy)]
        wire.start(slot(d, 8), got, got, place.core)

    def finish():
        flip = 1 - 2 * place.k
        for d in (1, 2, 3):
            for kind, who in ((1, place.me), (6, place.me_x), (7, place.me_y), (8, place.me_xy)):
                wire.landed(slot(d, kind), whole.at[d, rows(who + flip)], place.core)

    return begin, first, second, third, finish


def gather_call(shards):
    count = len(shards)

    def body(*refs):
        ins, outs = refs[:count], refs[count : 2 * count]
        send, recv, local_sem = refs[2 * count :]
        place = Place()
        wire = Wire(send, recv)
        copies = [pltpu.make_async_copy(ins[g], outs[g].at[0], local_sem.at[g]) for g in range(count)]
        place.meet()
        groups = [gather_steps(place, wire, g * 27, ins[g], outs[g]) for g in range(count)]
        for begin, *_ in groups:
            begin()
        for c in copies:
            c.start()
        order = [(g, d) for g in range(count) for d in (1, 3, 2)]
        for i in range(len(order) + 2):
            for lag in range(3):
                if 0 <= i - lag < len(order):
                    g, d = order[i - lag]
                    groups[g][1 + lag](d)
        for *_, finish in groups:
            finish()
        for c in copies:
            c.wait()
        wire.drain()

    return pl.pallas_call(
        body,
        in_specs=[pl.BlockSpec(memory_space=pltpu.VMEM)] * count,
        out_specs=[pl.BlockSpec(memory_space=pl.ANY)] * count,
        out_shape=[jax.ShapeDtypeStruct((4,) + s.shape, s.dtype) for s in shards],
        scratch_shapes=[
            pltpu.SemaphoreType.DMA((27 * count,)),
            pltpu.SemaphoreType.DMA((27 * count,)),
            pltpu.SemaphoreType.DMA((count,)),
        ],
        compiler_params=pltpu.CompilerParams(collective_id=0, has_side_effects=True, vmem_limit_bytes=VMEM),
    )(*shards)


class Reduce:
    SLOTS = 32

    @staticmethod
    def scratch(dm, w):
        q = dm // 4
        e = q // 2
        return [
            pltpu.VMEM((4, q, w), BF16),
            pltpu.VMEM((4, q, w), BF16),
            pltpu.VMEM((4, e, w), BF16),
            pltpu.VMEM((4, e, w), BF16),
            pltpu.VMEM((4, e, w), BF16),
            pltpu.VMEM((4, e, w), BF16),
            pltpu.VMEM((4, q, w), BF16),
            pltpu.VMEM((3, q, w), BF16),
            pltpu.SemaphoreType.DMA((Reduce.SLOTS,)),
            pltpu.SemaphoreType.DMA((Reduce.SLOTS,)),
        ]

    def __init__(self, place, grad, landing, scratch):
        self.place, self.g, self.f = place, grad, landing
        self.ra1, self.rb1, self.ra2, self.rb2, self.sa, self.sb, self.t, self.zb = scratch[:8]
        self.wire = Wire(scratch[8], scratch[9])
        self.q = grad.shape[0] // 4
        self.e = self.q // 2
        self.w = grad.shape[1] // 4

    def at(self, base, big, small=None):
        start = base * 2 * self.q + big * self.q + (0 if small is None else small * self.e)
        return pl.ds(pl.multiple_of(start, self.e), self.q if small is None else self.e)

    def eighth(self, small):
        return pl.ds(pl.multiple_of(small * self.e, self.e), self.e)

    def cols(self, d):
        return slice(d * self.w, (d + 1) * self.w)

    def one(self, d):
        p, wire = self.place, self.wire
        wire.start(d, self.g.at[self.at(0, 1 - p.x), self.cols(d)], self.ra1.at[d], p.by_x)
        wire.start(4 + d, self.g.at[self.at(1, 1 - p.y), self.cols(d)], self.rb1.at[d], p.by_y)

    def two(self, d):
        p, wire, c = self.place, self.wire, self.cols(d)
        wire.landed(d, self.ra1.at[d], p.by_x)
        self.sa[d] = (
            self.g[self.at(0, p.x, 1 - p.y), c].astype(F32) + self.ra1[d, self.eighth(1 - p.y), :].astype(F32)
        ).astype(BF16)
        wire.start(8 + d, self.sa.at[d], self.ra2.at[d], p.by_y)
        wire.landed(4 + d, self.rb1.at[d], p.by_y)
        self.sb[d] = (
            self.g[self.at(1, p.y, 1 - p.x), c].astype(F32) + self.rb1[d, self.eighth(1 - p.x), :].astype(F32)
        ).astype(BF16)
        wire.start(12 + d, self.sb.at[d], self.rb2.at[d], p.by_x)

    def three(self, d):
        p, wire, c, e = self.place, self.wire, self.cols(d), self.e
        wire.landed(8 + d, self.ra2.at[d], p.by_y)
        wire.landed(12 + d, self.rb2.at[d], p.by_x)
        up = (
            self.g[self.at(0, p.x, p.y), c].astype(F32)
            + self.ra1[d, self.eighth(p.y), :].astype(F32)
            + self.ra2[d].astype(F32)
        )
        low = (
            self.g[self.at(1, p.y, p.x), c].astype(F32)
            + self.rb1[d, self.eighth(p.x), :].astype(F32)
            + self.rb2[d].astype(F32)
        )
        if d:
            self.t[d, 0:e] = up.astype(BF16)
            self.t[d, e : 2 * e] = low.astype(BF16)
            wire.start(16 + d, self.t.at[d], self.zb.at[d - 1], p.along(d))
        else:
            for s in (1, 2, 3):
                wire.landed(16 + s, self.zb.at[s - 1], p.along(4 - s))
                up = up + self.zb[s - 1, 0:e].astype(F32)
                low = low + self.zb[s - 1, e : 2 * e].astype(F32)
            self.f[0, 0:e] = up.astype(BF16)
            self.f[0, e : 2 * e] = low.astype(BF16)
            wire.start(20, self.f.at[0], self.f.at[2], p.by_x)
            wire.start(21, self.f.at[0], self.f.at[4], p.by_y)
            wire.start(22, self.f.at[0], self.f.at[1], p.core)

    def four(self):
        p, wire, e = self.place, self.wire, self.e
        wire.landed(20, self.f.at[2], p.by_x)
        wire.start(23, self.f.at[2, 0:e], self.f.at[6, 0:e], p.by_y)
        wire.start(25, self.f.at[2], self.f.at[3], p.core)
        wire.landed(21, self.f.at[4], p.by_y)
        wire.start(24, self.f.at[4, e : 2 * e], self.f.at[6, e : 2 * e], p.by_x)
        wire.start(26, self.f.at[4], self.f.at[5], p.core)

    def five(self):
        p, wire, e = self.place, self.wire, self.e
        wire.landed(23, self.f.at[6, 0:e], p.by_y)
        wire.landed(24, self.f.at[6, e : 2 * e], p.by_x)
        wire.start(27, self.f.at[6], self.f.at[7], p.core)

    def six(self):
        for slot, to in ((22, 1), (25, 3), (26, 5), (27, 7)):
            self.wire.landed(slot, self.f.at[to], self.place.core)
        self.wire.drain()

    def steps(self):
        out = [functools.partial(self.one, d) for d in (1, 2, 3, 0)]
        lagged = [(self.two, d) for d in (1, 2, 3, 0)]
        last = [(self.three, d) for d in (1, 2, 3, 0)]
        for i in range(6):
            if i < 4:
                out.append(functools.partial(*lagged[i]))
            if i >= 1 and i - 1 < 4:
                out.append(functools.partial(*last[i - 1]))
        return out + [self.four, self.five, self.six]


def reduce_call(grads, cid):
    count = len(grads)
    dm, cols = grads[0].shape
    w = cols // 4
    each = len(Reduce.scratch(dm, w))

    def body(*refs):
        ins, outs, scr = refs[:count], refs[count : 2 * count], refs[2 * count :]
        place = Place()
        place.meet()
        todo = [Reduce(place, ins[i], outs[i], scr[each * i : each * (i + 1)]).steps() for i in range(count)]
        for steps in todo:
            for s in steps[:4]:
                s()
        tails = [steps[4:] for steps in todo]
        if count == 1:
            order = tails[0]
        else:
            a, b = tails
            order = a[:-4] + b[:-4] + [a[-4], a[-3], b[-4], a[-2], b[-3], a[-1], b[-2], b[-1]]
        for s in order:
            s()

    return pl.pallas_call(
        body,
        in_specs=[pl.BlockSpec(memory_space=pltpu.VMEM)] * count,
        out_specs=[pl.BlockSpec(memory_space=pltpu.VMEM)] * count,
        out_shape=[jax.ShapeDtypeStruct((8, dm // 4, w), BF16) for _ in grads],
        scratch_shapes=Reduce.scratch(dm, w) * count,
        compiler_params=pltpu.CompilerParams(collective_id=cid, has_side_effects=True, vmem_limit_bytes=VMEM),
    )(*grads)


def place_grads(coords, done, mode):
    _, q, w = done.shape
    e = q // 2
    dm = 4 * q
    lanes = w // 4

    def body(c_ref, f_ref, *outs):
        for off in range(8):
            y = lax.bitwise_xor(c_ref[0], off >> 2)
            x = lax.bitwise_xor(c_ref[1], (off >> 1) & 1)
            k = lax.bitwise_xor(c_ref[2], off & 1)
            for part in range(2):
                val = f_ref[off, part * e : (part + 1) * e, :].astype(F32)
                block = x * 2 + y if part == 0 else 4 + y * 2 + x
                rows = pl.ds(pl.multiple_of(block * e, e), e)
                if mode == "up":
                    outs[0][rows, pl.ds(pl.multiple_of(k * w, w), w)] = val
                elif mode == "down":
                    outs[0][pl.ds(pl.multiple_of(k * w, w), w), rows] = val.T
                else:
                    at = pl.ds(pl.multiple_of(k * lanes, lanes), lanes)
                    for m in range(3):
                        outs[m][rows, at] = val[:, m * lanes : (m + 1) * lanes]
                    outs[3][at, rows] = val[:, 3 * lanes :].T

    if mode == "up":
        shapes = [(dm, 2 * w)]
    elif mode == "down":
        shapes = [(2 * w, dm)]
    else:
        shapes = [(dm, w // 2)] * 3 + [(w // 2, dm)]
    return pl.pallas_call(
        body,
        in_specs=[pl.BlockSpec(memory_space=pltpu.SMEM), pl.BlockSpec(memory_space=pltpu.VMEM)],
        out_specs=[pl.BlockSpec(memory_space=pltpu.VMEM)] * len(shapes),
        out_shape=[jax.ShapeDtypeStruct(s, F32) for s in shapes],
        compiler_params=pltpu.CompilerParams(vmem_limit_bytes=VMEM),
        cost_estimate=pl.CostEstimate(flops=0, bytes_accessed=12 * dm * w, transcendentals=0),
    )(coords, done)


def relative(stack, z):
    return jnp.roll(stack, -z, axis=0)


def core_first(v, core, axis):
    return jnp.where(core == 0, v, jnp.flip(v, axis))


def gather_any(shard, z):
    return relative(lax.all_gather(shard, "mp", axis=0, tiled=False), z)


def reduce_any(half, z, core):
    zero = jnp.zeros_like(half)
    v = jnp.stack([jnp.where(core == 0, half, zero), jnp.where(core == 1, half, zero)], axis=2)
    v = jnp.roll(jnp.moveaxis(v, 1, 0), z, axis=0)
    v = lax.psum_scatter(v, "mp", scatter_dimension=0, tiled=True)[0]
    return lax.psum(v, "dp").astype(F32).reshape(half.shape[0], -1)


def local(
    tokens,
    segments,
    ln1_gain,
    ln1_bias,
    w_query,
    b_query,
    w_key,
    w_value,
    b_value,
    w_out,
    b_out,
    ln2_gain,
    ln2_bias,
    w_up,
    b_up,
    w_down,
    b_down,
    cotangent,
):
    rows, dm = tokens.shape
    cw = w_query.shape[1]
    ffw = w_up.shape[1]
    mp = lax.axis_size("mp")
    dp = lax.axis_size("dp")
    fast = mp == 4 and dp == 8 and rows % 128 == 0
    z = lax.axis_index("mp")
    me = lax.axis_index("dp")
    core = lax.rem(me, 2)
    x = lax.rem(me // 2, 2)
    y = me // 4
    f32 = lambda v: v.astype(F32)

    near = -(-LONGEST // rows)
    own = (near - 1) * rows
    win = own + rows + 2 * HALO
    halo = [
        lax.ppermute(tokens, "mp", [((i + j) % near, i) for i in range(near)]) for j in range(1, near)
    ]
    before = lax.ppermute(tokens[-HALO:], "mp", [(i - 1, i) for i in range(near, mp)])
    behind = lax.ppermute(tokens[:HALO], "mp", [(i + 1, i) for i in range(near - 1, mp - 1)])
    small_vec = jnp.concatenate([b_query, b_value, b_up])
    if fast:
        vecs = [small_vec] + [
            lax.ppermute(small_vec, "mp", [((i + d) % mp, i) for i in range(mp)]) for d in range(1, mp)
        ]
        vecs = jnp.stack(vecs)
    else:
        vecs = relative(lax.all_gather(small_vec, "mp", axis=0, tiled=False), z)
    bq_all, bv_all = vecs[:, :cw], vecs[:, cw : 2 * cw]
    bu_all = vecs[:, 2 * cw :].reshape(mp, 2, ffw // 2).transpose(1, 0, 2)
    bu_all = core_first(bu_all, core, 0).reshape(mp * ffw)

    is_near = z < near
    seg_parts = [
        jnp.where(is_near, lax.dynamic_slice_in_dim(segments, lax.rem(z + j, near) * rows, rows), -1)
        for j in range(1, near)
    ]
    seg_own = lax.dynamic_slice_in_dim(segments, z * rows, rows)
    seg_prev = lax.dynamic_slice_in_dim(segments, jnp.maximum(z * rows - HALO, 0), HALO)
    seg_next = lax.dynamic_slice_in_dim(segments, jnp.minimum((z + 1) * rows, segments.shape[0] - HALO), HALO)
    seg_far = jnp.concatenate(seg_parts)
    seg_far = jnp.concatenate([seg_far[:-HALO], jnp.where(is_near, seg_far[-HALO:], seg_prev)])
    has_next = jnp.logical_and(z >= near - 1, z < mp - 1)
    seg_win = jnp.concatenate(
        [seg_far, seg_own, jnp.where(has_next, seg_next, -1), jnp.full((HALO,), -1, segments.dtype)]
    )
    kseg, qseg = seg_win[None, :], seg_own[:, None]
    info = jnp.stack([is_near.astype(jnp.int32), core]).astype(jnp.int32)

    pack = jnp.concatenate([w_query, w_key, w_value, w_out.T], axis=1)
    if fast:
        packed, up_all, down_all = gather_call([pack, w_up, w_down])
    else:
        packed, up_all, down_all = (gather_any(w, z) for w in (pack, w_up, w_down))

    far = jnp.concatenate(halo, axis=0)
    far = jnp.concatenate([far[:-HALO], far[-HALO:] + before], axis=0)
    tok_win = jnp.concatenate([far, tokens, behind, jnp.zeros((HALO, dm), tokens.dtype)], axis=0)
    hat_win, inv_win = norm_rows(f32(tok_win))
    n1w = (hat_win * f32(ln1_gain) + f32(ln1_bias)).astype(BF16)
    q, k, v = qkv_call(n1w, packed, bq_all, bv_all, own, rows, cw)
    attn, lse = attn_fwd_call(info, q, k, v, qseg, kseg, own)
    hidden, n2 = out_call(attn, packed, tokens, b_out, ln2_gain, ln2_bias)
    output, g_n2, active, g_upper, g_b_up = ffn_call(
        info[1:], n2, hidden, cotangent, up_all, down_all, bu_all, b_down, 2
    )

    other = lambda v: lax.ppermute(v, "dp", [(i, i - i % 2 + (i + 1) % 2) for i in range(dp)])
    hw = mp * ffw // 2
    cot_o = other(cotangent)
    act_o = other(active[:, hw:])
    n2_o = other(n2)
    gup_o = other(g_upper[:, hw:])
    gout = f32(cotangent)

    def pair_grad(left, right, left_o, right_o):
        return (dot_tn(left, right) + dot_tn(left_o, right_o)).astype(BF16)

    gd = pair_grad(cotangent, active[:, :hw], cot_o, act_o)
    gu = pair_grad(n2, g_upper[:, :hw], n2_o, gup_o)
    hat2, inv2 = norm_rows(hidden)

    def norm_back(g, hat, inv, gain):
        gg = g * gain
        first = jnp.mean(gg, axis=1, keepdims=True)
        second = jnp.mean(gg * hat, axis=1, keepdims=True)
        return inv * (gg - first - hat * second), jnp.sum(g * hat, axis=0), jnp.sum(g, axis=0)

    g_hidden, g_gain2, g_bias2 = norm_back(g_n2, hat2, inv2, f32(ln2_gain))
    g_hidden = g_hidden + gout
    ghb = g_hidden.astype(BF16)

    g_attn = jnp.stack([dot_nn(ghb, packed[d, :, 3 * cw :]).astype(BF16) for d in range(mp)])
    dq, dk, dv = attn_bwd_call(info, q, k, v, attn, g_attn, lse, qseg, kseg, own)
    halves = dq.shape[0]
    g_own, g_far, g_next = norm1_back_call(dq, dk, dv, packed, info, own)
    back = g_own
    for j in range(1, near):
        part = g_far[(j - 1) * rows : j * rows]
        back = back + f32(lax.ppermute(part, "mp", [(i, (i + j) % near) for i in range(near)]))
    to_prev = f32(lax.ppermute(g_far[-HALO:], "mp", [(i, i - 1) for i in range(near, mp)]))
    to_next = f32(lax.ppermute(g_next, "mp", [(i, i + 1) for i in range(near - 1, mp - 1)]))
    back = jnp.concatenate([back[:HALO] + to_next, back[HALO:-HALO], back[-HALO:] + to_prev], axis=0)
    hat1 = hat_win[own : own + rows]
    inv1 = inv_win[own : own + rows]
    g_in, g_gain1, g_bias1 = norm_back(back, hat1, inv1, f32(ln1_gain))
    g_tokens = g_in + g_hidden

    n1 = n1w[own : own + rows]
    if fast:
        n1w_o = other(n1w)
        ghb_o = other(ghb)
        attn_h = attn.reshape(mp, rows, 2, cw // 2).transpose(2, 1, 0, 3).reshape(2, rows, mp * cw // 2)
        attn_m = lax.dynamic_index_in_dim(attn_h, core, 0, keepdims=False)
        attn_t = lax.dynamic_index_in_dim(attn_h, 1 - core, 0, keepdims=False)
        dq_o, dk_o, dv_o, at_o = other(dq[1]), other(dk[1]), other(dv[1]), other(attn_t)
        n1_o = n1w_o[own : own + rows]
        half = cw // 2
        gs = [
            pair_grad(n1, dq[0], n1_o, dq_o),
            pair_grad(n1w, dk[0], n1w_o, dk_o),
            pair_grad(n1w, dv[0], n1w_o, dv_o),
            pair_grad(ghb, attn_m, ghb_o, at_o),
        ]
        gp = jnp.concatenate([g[:, d * half : (d + 1) * half] for d in range(mp) for g in gs], axis=1)
        coords = jnp.stack([y, x, core]).astype(jnp.int32)
        done_d, done_u = reduce_call([gd, gu], 1)
        (done_p,) = reduce_call([gp], 2)
        (g_w_down,) = place_grads(coords, done_d, "down")
        (g_w_up,) = place_grads(coords, done_u, "up")
        g_w_query, g_w_key, g_w_value, g_w_out = place_grads(coords, done_p, "pack")
    else:
        g_w_up = reduce_any(gu.reshape(dm, mp, ffw // 2), z, core)
        g_w_down = reduce_any(gd.reshape(dm, mp, ffw // 2), z, core).T

        def whole_grad(left, right, name=None):
            v = dot_tn(left, right).astype(BF16).reshape(dm, mp, cw)
            v = jnp.roll(jnp.moveaxis(v, 1, 0), z, axis=0)
            v = lax.psum_scatter(v, "mp", scatter_dimension=0, tiled=True)[0]
            return lax.psum(v, "dp").astype(F32)

        def whole(v):
            if halves == 1:
                return v[0]
            v = v.reshape(2, v.shape[1], mp, cw // 2).transpose(1, 2, 0, 3)
            return core_first(v, core, 2).reshape(v.shape[0], mp * cw)

        g_w_query = whole_grad(n1, whole(dq))
        g_w_key = whole_grad(n1w, whole(dk))
        g_w_value = whole_grad(n1w, whole(dv))
        g_w_out = whole_grad(ghb, attn.transpose(1, 0, 2).reshape(rows, mp * cw)).T

    def shards(v, width):
        if v.shape[0] == 2:
            v = core_first(v.reshape(2, mp, width // 2), core, 0).transpose(1, 0, 2)
        return jnp.roll(v.reshape(mp, width), z, axis=0).reshape(mp * width)

    gbq = shards(jnp.sum(f32(dq), axis=1), cw)
    gbv = shards(jnp.sum(f32(dv), axis=1), cw)
    gbu = core_first(g_b_up.reshape(2, mp, ffw // 2), core, 0).transpose(1, 0, 2)
    gbu = jnp.roll(gbu.reshape(mp, ffw), z, axis=0).reshape(-1)
    vec = jnp.concatenate(
        [g_gain1, g_bias1, jnp.sum(g_hidden, axis=0), g_gain2, g_bias2, jnp.sum(gout, axis=0), gbq, gbv, gbu]
    )
    vec = lax.psum(vec, ("dp", "mp"))
    g_gain1, g_bias1, g_b_out, g_gain2, g_bias2, g_b_down = (vec[i * dm : (i + 1) * dm] for i in range(6))
    at = 6 * dm
    g_b_query = lax.dynamic_slice_in_dim(vec, at + z * cw, cw)
    g_b_value = lax.dynamic_slice_in_dim(vec, at + mp * cw + z * cw, cw)
    g_b_up = lax.dynamic_slice_in_dim(vec, at + 2 * mp * cw + z * ffw, ffw)
    return (
        output,
        g_tokens,
        g_gain1,
        g_bias1,
        g_w_query,
        g_b_query,
        g_w_key,
        g_w_value,
        g_b_value,
        g_w_out,
        g_b_out,
        g_gain2,
        g_bias2,
        g_w_up,
        g_b_up,
        g_w_down,
        g_b_down,
    )


def solution(mesh):
    in_specs = (
        P(("dp", "mp"), None),
        P("dp"),
        P(),
        P(),
        P(None, "mp"),
        P("mp"),
        P(None, "mp"),
        P(None, "mp"),
        P("mp"),
        P("mp", None),
        P(),
        P(),
        P(),
        P(None, "mp"),
        P("mp"),
        P("mp", None),
        P(),
        P(("dp", "mp"), None),
    )
    out_specs = (
        P(("dp", "mp"), None),
        P(("dp", "mp"), None),
        P(),
        P(),
        P(None, "mp"),
        P("mp"),
        P(None, "mp"),
        P(None, "mp"),
        P("mp"),
        P("mp", None),
        P(),
        P(),
        P(),
        P(None, "mp"),
        P("mp"),
        P("mp", None),
        P(),
    )
    return jax.shard_map(local, mesh=mesh, in_specs=in_specs, out_specs=out_specs, check_vma=False)
```

```python
import functools

import jax
import jax.numpy as jnp
from jax import lax
from jax.experimental import pallas as pl
from jax.experimental.pallas import tpu as pltpu
from jax.sharding import PartitionSpec as P

HEAD_DIM = 64
LONGEST = 900
HALO = 64
PAIR = 128
EPS = 1e-06
NEG = -1e30
VMEM = 60 * 1024 * 1024
VMEM_ALL = 67043328
F32 = jnp.float32
BF16 = jnp.bfloat16


def dot_nn(a, b):
    return lax.dot_general(a, b, (((1,), (0,)), ((), ())), preferred_element_type=F32)


def dot_nt(a, b):
    return lax.dot_general(a, b, (((1,), (1,)), ((), ())), preferred_element_type=F32)


def dot_tn(a, b):
    return lax.dot_general(a, b, (((0,), (0,)), ((), ())), preferred_element_type=F32)


def barrier(*xs):
    return lax.optimization_barrier(xs)


def params(*sem, **kw):
    return pltpu.CompilerParams(dimension_semantics=sem, vmem_limit_bytes=VMEM, **kw)


def norm_rows(x):
    mean = jnp.mean(x, axis=1, keepdims=True)
    cent = x - mean
    inv = lax.rsqrt(jnp.mean(cent * cent, axis=1, keepdims=True) + EPS)
    return cent * inv, inv


def qkv_call(n1w, packed, b_q, b_v, own, rows, cw):
    n, dm, _ = packed.shape
    win = n1w.shape[0]

    def body(x_ref, w_ref, bq_ref, bv_ref, q_ref, k_ref, v_ref):
        x = x_ref[...]
        q_ref[0] = (dot_nn(x[own : own + rows], w_ref[0, :, 0:cw]) + bq_ref[0].astype(F32)).astype(BF16)
        k_ref[0] = dot_nn(x, w_ref[0, :, cw : 2 * cw]).astype(BF16)
        v_ref[0] = (dot_nn(x, w_ref[0, :, 2 * cw : 3 * cw]) + bv_ref[0].astype(F32)).astype(BF16)

    return pl.pallas_call(
        body,
        grid=(n,),
        in_specs=[
            pl.BlockSpec((win, dm), lambda d: (0, 0)),
            pl.BlockSpec((1, dm, 4 * cw), lambda d: (d, 0, 0)),
            pl.BlockSpec((1, 1, cw), lambda d: (d, 0, 0)),
            pl.BlockSpec((1, 1, cw), lambda d: (d, 0, 0)),
        ],
        out_specs=[
            pl.BlockSpec((1, rows, cw), lambda d: (d, 0, 0)),
            pl.BlockSpec((1, win, cw), lambda d: (d, 0, 0)),
            pl.BlockSpec((1, win, cw), lambda d: (d, 0, 0)),
        ],
        out_shape=[
            jax.ShapeDtypeStruct((n, rows, cw), BF16),
            jax.ShapeDtypeStruct((n, win, cw), BF16),
            jax.ShapeDtypeStruct((n, win, cw), BF16),
        ],
        compiler_params=params("arbitrary"),
        cost_estimate=pl.CostEstimate(
            flops=2 * n * dm * cw * (rows + 2 * win), bytes_accessed=2 * (n * dm * 4 * cw + win * dm), transcendentals=0
        ),
    )(n1w, packed, b_q[:, None, :], b_v[:, None, :])


def blocks_of(rows, own, win, big):
    if big:
        step = min(256, rows)
        return [(s, step, 0, win) for s in range(0, rows, step)]
    return [(s, 128, own + s - 128, 384) for s in range(0, rows, 128)]


def attn_fwd_call(is_big, q, k, v, qseg, kseg, own):
    n, rows, cw = q.shape
    win = k.shape[1]
    pairs = cw // PAIR

    def work(big, q_ref, k_ref, v_ref, qs_ref, ks_ref, o_ref, l_ref):
        for qs, qn, ks, kn in blocks_of(rows, own, win, big):
            mask = qs_ref[qs : qs + qn, :] == ks_ref[:, ks : ks + kn]
            for h in range(2):
                lanes = slice(h * HEAD_DIM, (h + 1) * HEAD_DIM)
                qh = q_ref[0, qs : qs + qn, lanes] * BF16(HEAD_DIM**-0.5)
                s = jnp.where(mask, dot_nt(qh, k_ref[0, ks : ks + kn, lanes]), NEG)
                top = jnp.max(s, axis=1, keepdims=True)
                p = jnp.exp(s - top)
                total = jnp.sum(p, axis=1, keepdims=True)
                o = dot_nn(p.astype(BF16), v_ref[0, ks : ks + kn, lanes])
                o_ref[0, qs : qs + qn, lanes] = (o / total).astype(BF16)
                l_ref[0, qs : qs + qn, h : h + 1] = top + jnp.log(total)

    def body(big_ref, *refs):
        @pl.when(big_ref[0] == 1)
        def _():
            work(True, *refs)

        @pl.when(big_ref[0] == 0)
        def _():
            work(False, *refs)

    return pl.pallas_call(
        body,
        grid_spec=pltpu.PrefetchScalarGridSpec(
            num_scalar_prefetch=1,
            grid=(n, pairs),
            in_specs=[
                pl.BlockSpec((1, rows, PAIR), lambda d, p, *_: (d, 0, p)),
                pl.BlockSpec((1, win, PAIR), lambda d, p, *_: (d, 0, p)),
                pl.BlockSpec((1, win, PAIR), lambda d, p, *_: (d, 0, p)),
                pl.BlockSpec((rows, 1), lambda d, p, *_: (0, 0)),
                pl.BlockSpec((1, win), lambda d, p, *_: (0, 0)),
            ],
            out_specs=[
                pl.BlockSpec((1, rows, PAIR), lambda d, p, *_: (d, 0, p)),
                pl.BlockSpec((1, rows, 2), lambda d, p, *_: (d * pairs + p, 0, 0)),
            ],
        ),
        out_shape=[
            jax.ShapeDtypeStruct((n, rows, cw), BF16),
            jax.ShapeDtypeStruct((n * pairs, rows, 2), F32),
        ],
        compiler_params=params("arbitrary", "arbitrary"),
        cost_estimate=pl.CostEstimate(
            flops=16 * n * rows * win * cw, bytes_accessed=2 * n * cw * (2 * rows + 2 * win), transcendentals=n * rows * win * 4
        ),
    )(is_big, q, k, v, qseg, kseg)


def attn_bwd_call(info, q, k, v, attn, gattn, lse, qseg, kseg, own):
    n, rows, cw = q.shape
    win = k.shape[1]
    pairs = cw // PAIR
    scale = HEAD_DIM**-0.5

    def work(big, q_ref, k_ref, v_ref, a_ref, g_ref, l_ref, qs_ref, ks_ref, dq_ref, dk_ref, dv_ref, dkt, dvt):
        if not big:
            dkt[...] = jnp.zeros_like(dkt)
            dvt[...] = jnp.zeros_like(dvt)
        for i, (qs, qn, ks, kn) in enumerate(blocks_of(rows, own, win, big)):
            mask = qs_ref[qs : qs + qn, :] == ks_ref[:, ks : ks + kn]
            for h in range(2):
                lanes = slice(h * HEAD_DIM, (h + 1) * HEAD_DIM)
                qh = q_ref[0, qs : qs + qn, lanes] * BF16(scale)
                kh = k_ref[0, ks : ks + kn, lanes]
                gh = g_ref[0, qs : qs + qn, lanes]
                s = jnp.where(mask, dot_nt(qh, kh) - l_ref[0, qs : qs + qn, h : h + 1], NEG)
                p = jnp.exp(s)
                dp = dot_nt(gh, v_ref[0, ks : ks + kn, lanes])
                delta = jnp.sum(
                    gh.astype(F32) * a_ref[0, qs : qs + qn, lanes].astype(F32), axis=1, keepdims=True
                )
                ds = (p * (dp - delta)).astype(BF16)
                dq_ref[0, qs : qs + qn, lanes] = (dot_nn(ds, kh) * scale).astype(BF16)
                dk = dot_tn(qh, ds)
                dv = dot_tn(gh, p.astype(BF16))
                if big and i == 0:
                    dkt[lanes, :] = dk
                    dvt[lanes, :] = dv
                else:
                    dkt[lanes, ks : ks + kn] += dk
                    dvt[lanes, ks : ks + kn] += dv
        dk_ref[0] = dkt[...].T.astype(BF16)
        dv_ref[0] = dvt[...].T.astype(BF16)

    def body(info_ref, *refs):
        @pl.when(info_ref[0] == 1)
        def _():
            work(True, *refs)

        @pl.when(info_ref[0] == 0)
        def _():
            work(False, *refs)

    if pairs > 1:

        def put(d, p, info):
            rel = lax.bitwise_xor(p // (pairs // 2), info[1])
            return (rel, 0, d * (pairs // 2) + p % (pairs // 2))

        half_shape = (2, rows, n * cw // 2)
        half_win = (2, win, n * cw // 2)
    else:

        def put(d, p, info):
            return (0, 0, d)

        half_shape = (1, rows, n * cw)
        half_win = (1, win, n * cw)
    return pl.pallas_call(
        body,
        grid_spec=pltpu.PrefetchScalarGridSpec(
            num_scalar_prefetch=1,
            grid=(n, pairs),
            in_specs=[
                pl.BlockSpec((1, rows, PAIR), lambda d, p, *_: (d, 0, p)),
                pl.BlockSpec((1, win, PAIR), lambda d, p, *_: (d, 0, p)),
                pl.BlockSpec((1, win, PAIR), lambda d, p, *_: (d, 0, p)),
                pl.BlockSpec((1, rows, PAIR), lambda d, p, *_: (d, 0, p)),
                pl.BlockSpec((1, rows, PAIR), lambda d, p, *_: (d, 0, p)),
                pl.BlockSpec((1, rows, 2), lambda d, p, *_: (d * pairs + p, 0, 0)),
                pl.BlockSpec((rows, 1), lambda d, p, *_: (0, 0)),
                pl.BlockSpec((1, win), lambda d, p, *_: (0, 0)),
            ],
            out_specs=[
                pl.BlockSpec((1, rows, PAIR), put),
                pl.BlockSpec((1, win, PAIR), put),
                pl.BlockSpec((1, win, PAIR), put),
            ],
            scratch_shapes=[pltpu.VMEM((PAIR, win), F32), pltpu.VMEM((PAIR, win), F32)],
        ),
        out_shape=[
            jax.ShapeDtypeStruct(half_shape, BF16),
            jax.ShapeDtypeStruct(half_win, BF16),
            jax.ShapeDtypeStruct(half_win, BF16),
        ],
        compiler_params=params("arbitrary", "arbitrary"),
        cost_estimate=pl.CostEstimate(
            flops=40 * n * rows * win * cw, bytes_accessed=2 * n * cw * (4 * rows + 4 * win), transcendentals=n * rows * win * 4
        ),
    )(info, q, k, v, attn, gattn, lse, qseg, kseg)


def out_call(attn, packed, resid, b_out, gain, bias):
    n, rows, cw = attn.shape
    dm = packed.shape[1]

    def body(a_ref, w_ref, x_ref, bo_ref, g_ref, b_ref, h_ref, n_ref):
        d = pl.program_id(0)
        part = dot_nt(a_ref[0], w_ref[0])

        @pl.when(d == 0)
        def _():
            h_ref[...] = part + x_ref[...].astype(F32) + bo_ref[...].astype(F32)

        @pl.when(d > 0)
        def _():
            h_ref[...] += part

        @pl.when(d == n - 1)
        def _():
            hat, _ = norm_rows(h_ref[...])
            n_ref[...] = (hat * g_ref[...].astype(F32) + b_ref[...].astype(F32)).astype(BF16)

    full = lambda d: (0, 0)
    return pl.pallas_call(
        body,
        grid=(n,),
        in_specs=[
            pl.BlockSpec((1, rows, cw), lambda d: (d, 0, 0)),
            pl.BlockSpec((1, dm, cw), lambda d: (d, 0, 3)),
            pl.BlockSpec((rows, dm), full),
            pl.BlockSpec((1, dm), full),
            pl.BlockSpec((1, dm), full),
            pl.BlockSpec((1, dm), full),
        ],
        out_specs=[pl.BlockSpec((rows, dm), full), pl.BlockSpec((rows, dm), full)],
        out_shape=[jax.ShapeDtypeStruct((rows, dm), F32), jax.ShapeDtypeStruct((rows, dm), BF16)],
        compiler_params=params("arbitrary"),
        cost_estimate=pl.CostEstimate(flops=2 * n * rows * cw * dm, bytes_accessed=2 * n * dm * cw, transcendentals=0),
    )(attn, packed, resid, b_out[None], gain[None], bias[None])


def ffn_call(core, n2, hidden, cot, w_up, w_down, b_up, b_down, halves):
    rows, dm = n2.shape
    n, _, ffw = w_up.shape
    tile = ffw // halves

    def body(core_ref, x_ref, h_ref, c_ref, wu_ref, wd_ref, bu_ref, bd_ref, o_ref, gn_ref, a_ref, gu_ref, gb_ref, acc):
        t = pl.program_id(0)
        u = dot_nn(x_ref[...], wu_ref[0]) + bu_ref[...].astype(F32)
        cdf = 0.5 * (1.0 + lax.erf(u * 0.7071067811865476))
        act = (u * cdf).astype(BF16)
        slope = cdf + u * jnp.exp(-0.5 * u * u) * 0.3989422804014327
        a_ref[...] = act
        grad = dot_nt(c_ref[...], wd_ref[0]) * slope
        gu = grad.astype(BF16)
        gu_ref[...] = gu
        gb_ref[...] = jnp.sum(gu.astype(F32), axis=0, keepdims=True)
        out = dot_nn(act, wd_ref[0])
        gn = dot_nt(gu, wu_ref[0])

        @pl.when(t == 0)
        def _():
            acc[...] = h_ref[...] + bd_ref[...].astype(F32) + out
            gn_ref[...] = gn

        @pl.when(t > 0)
        def _():
            acc[...] += out
            gn_ref[...] += gn

        @pl.when(t == n * halves - 1)
        def _():
            o_ref[...] = acc[...].astype(BF16)

    full = lambda t, c: (0, 0)

    def part(t, c):
        return lax.bitwise_xor(t // n, c[0]) if halves > 1 else 0

    return pl.pallas_call(
        body,
        grid_spec=pltpu.PrefetchScalarGridSpec(
            num_scalar_prefetch=1,
            grid=(n * halves,),
            in_specs=[
                pl.BlockSpec((rows, dm), full),
                pl.BlockSpec((rows, dm), full),
                pl.BlockSpec((rows, dm), full),
                pl.BlockSpec((1, dm, tile), lambda t, c: (t % n, 0, part(t, c))),
                pl.BlockSpec((1, tile, dm), lambda t, c: (t % n, part(t, c), 0)),
                pl.BlockSpec((1, tile), lambda t, c: (0, t)),
                pl.BlockSpec((1, dm), full),
            ],
            out_specs=[
                pl.BlockSpec((rows, dm), full),
                pl.BlockSpec((rows, dm), full),
                pl.BlockSpec((rows, tile), lambda t, c: (0, t)),
                pl.BlockSpec((rows, tile), lambda t, c: (0, t)),
                pl.BlockSpec((1, tile), lambda t, c: (0, t)),
            ],
            scratch_shapes=[pltpu.VMEM((rows, dm), F32)],
        ),
        out_shape=[
            jax.ShapeDtypeStruct((rows, dm), BF16),
            jax.ShapeDtypeStruct((rows, dm), F32),
            jax.ShapeDtypeStruct((rows, n * ffw), BF16),
            jax.ShapeDtypeStruct((rows, n * ffw), BF16),
            jax.ShapeDtypeStruct((1, n * ffw), F32),
        ],
        compiler_params=params("arbitrary"),
        cost_estimate=pl.CostEstimate(
            flops=8 * rows * dm * n * ffw, bytes_accessed=4 * n * dm * ffw, transcendentals=2 * rows * n * ffw
        ),
    )(core, n2, hidden, cot, w_up, w_down, b_up[None], b_down[None])


def norm1_back_call(dq, dk, dv, packed, info, own):
    halves, rows, _ = dq.shape
    n, dm, four = packed.shape
    cw = four // 4
    win = dk.shape[1]
    width = cw // halves

    def body(info_ref, dq_ref, dk_ref, dv_ref, w_ref, o_ref, h_ref, t_ref, acc):
        step = pl.program_id(0)

        def weight(which, j):
            at = lax.bitwise_xor(j, info_ref[1]) if halves > 1 else 0
            return w_ref[0, :, pl.ds(pl.multiple_of(which * cw + at * width, width), width)]

        left = jnp.concatenate([r[j] for r in (dk_ref, dv_ref) for j in range(halves)], axis=1)
        right = jnp.concatenate([weight(m, j) for m in (1, 2) for j in range(halves)], axis=1)
        part = dot_nt(left, right)
        left = jnp.concatenate([dq_ref[j] for j in range(halves)], axis=1)
        right = jnp.concatenate([weight(0, j) for j in range(halves)], axis=1)
        mine = dot_nt(left, right)

        @pl.when(step == 0)
        def _():
            acc[...] = part

        @pl.when(step > 0)
        def _():
            acc[...] += part

        acc[own : own + rows, :] += mine

        @pl.when(step == n - 1)
        def _():
            o_ref[...] = acc[own : own + rows, :]
            h_ref[...] = acc[0:own, :].astype(BF16)
            t_ref[...] = acc[own + rows : own + rows + HALO, :].astype(BF16)

    full = lambda s, info: (0, 0)
    return pl.pallas_call(
        body,
        grid_spec=pltpu.PrefetchScalarGridSpec(
            num_scalar_prefetch=1,
            grid=(n,),
            in_specs=[
                pl.BlockSpec((halves, rows, width), lambda s, info: (0, 0, s)),
                pl.BlockSpec((halves, win, width), lambda s, info: (0, 0, s)),
                pl.BlockSpec((halves, win, width), lambda s, info: (0, 0, s)),
                pl.BlockSpec((1, dm, four), lambda s, info: (s, 0, 0)),
            ],
            out_specs=[
                pl.BlockSpec((rows, dm), full),
                pl.BlockSpec((own, dm), full),
                pl.BlockSpec((HALO, dm), full),
            ],
            scratch_shapes=[pltpu.VMEM((win, dm), F32)],
        ),
        out_shape=[
            jax.ShapeDtypeStruct((rows, dm), F32),
            jax.ShapeDtypeStruct((own, dm), BF16),
            jax.ShapeDtypeStruct((HALO, dm), BF16),
        ],
        compiler_params=params("arbitrary"),
        cost_estimate=pl.CostEstimate(
            flops=2 * n * cw * dm * (rows + 2 * win), bytes_accessed=2 * n * cw * (3 * dm + rows + 2 * win), transcendentals=0
        ),
    )(info, dq, dk, dv, packed)


MESH = pl.DeviceIdType.MESH


class Place:
    def __init__(self):
        self.me = lax.axis_index("dp")
        self.z = lax.axis_index("mp")
        self.k = lax.rem(self.me, 2)
        self.x = lax.rem(self.me // 2, 2)
        self.y = self.me // 4
        self.me_k = self.me + 1 - 2 * self.k
        self.me_x = self.me + 2 - 4 * self.x
        self.me_y = self.me + 4 - 8 * self.y
        self.me_xy = self.me_x + 4 - 8 * self.y
        self.core = {"dp": self.me_k, "mp": self.z}
        self.by_x = {"dp": self.me_x, "mp": self.z}
        self.by_y = {"dp": self.me_y, "mp": self.z}

    def along(self, d):
        return {"dp": self.me, "mp": lax.rem(self.z + d, 4)}

    def meet(self):
        sem = pltpu.get_barrier_semaphore()
        for dev in (self.core, self.by_x, self.by_y, self.along(1), self.along(2), self.along(3)):
            pl.semaphore_signal(sem, inc=1, device_id=dev, device_id_type=MESH)
        pl.semaphore_wait(sem, 6)


class Wire:
    def __init__(self, send, recv, dev):
        self.send, self.recv, self.dev = send, recv, dev

    def start(self, slot, src, dst, dev):
        copy = pltpu.make_async_remote_copy(
            src_ref=src, dst_ref=dst, send_sem=self.send.at[slot], recv_sem=self.recv.at[slot],
            device_id=dev, device_id_type=MESH,
        )
        copy.start()

    def sent(self, slot, ref):
        pltpu.make_async_remote_copy(
            src_ref=ref, dst_ref=ref, send_sem=self.send.at[slot], recv_sem=self.recv.at[slot],
            device_id=dict(self.dev), device_id_type=MESH,
        ).wait_send()

    def landed(self, slot, ref, dev):
        pltpu.make_async_remote_copy(
            src_ref=ref, dst_ref=ref, send_sem=self.send.at[slot], recv_sem=self.recv.at[slot],
            device_id=dev, device_id_type=MESH,
        ).wait_recv()


def gather_steps(place, wire, base, shard, whole):
    step = shard.shape[0] // 8
    half = step // 2

    def rows(who, at=0, size=step):
        return pl.ds(pl.multiple_of(who * step + at, half), size)

    def slot(d, kind):
        return base + (d - 1) * 9 + kind

    def begin():
        for d in (1, 2, 3):
            wire.start(slot(d, 0), shard.at[rows(place.me)], whole.at[d, rows(place.me)], place.along(4 - d))

    def first(d):
        mine = whole.at[d, rows(place.me)]
        wire.landed(slot(d, 0), mine, place.along(d))
        wire.start(slot(d, 2), mine, mine, place.by_x)
        wire.start(slot(d, 3), mine, mine, place.by_y)
        wire.start(slot(d, 1), mine, mine, place.core)

    def second(d):
        got = whole.at[d, rows(place.me_x)]
        wire.landed(slot(d, 2), got, place.by_x)
        part = whole.at[d, rows(place.me_x, 0, half)]
        wire.start(slot(d, 4), part, part, place.by_y)
        wire.start(slot(d, 6), got, got, place.core)
        got = whole.at[d, rows(place.me_y)]
        wire.landed(slot(d, 3), got, place.by_y)
        part = whole.at[d, rows(place.me_y, half, half)]
        wire.start(slot(d, 5), part, part, place.by_x)
        wire.start(slot(d, 7), got, got, place.core)

    def third(d):
        wire.landed(slot(d, 4), whole.at[d, rows(place.me_xy, 0, half)], place.by_y)
        wire.landed(slot(d, 5), whole.at[d, rows(place.me_xy, half, half)], place.by_x)
        got = whole.at[d, rows(place.me_xy)]
        wire.start(slot(d, 8), got, got, place.core)

    def finish():
        flip = 1 - 2 * place.k
        for d in (1, 2, 3):
            for kind, who in ((1, place.me), (6, place.me_x), (7, place.me_y), (8, place.me_xy)):
                wire.landed(slot(d, kind), whole.at[d, rows(who + flip)], place.core)
            for kind in range(9):
                wire.sent(slot(d, kind), whole.at[d, pl.ds(0, half if kind in (4, 5) else step)])

    return begin, first, second, third, finish


def gather_call(shards):
    count = len(shards)

    def body(*refs):
        ins, outs = refs[:count], refs[count : 2 * count]
        send, recv, local_sem = refs[2 * count :]
        place = Place()
        wire = Wire(send, recv, place.core)
        copies = [pltpu.make_async_copy(ins[g], outs[g].at[0], local_sem.at[g]) for g in range(count)]
        place.meet()
        groups = [gather_steps(place, wire, g * 27, ins[g], outs[g]) for g in range(count)]
        for begin, *_ in groups:
            begin()
        for c in copies:
            c.start()
        order = [(g, d) for g in range(count) for d in (1, 3, 2)]
        for i in range(len(order) + 2):
            for lag in range(3):
                if 0 <= i - lag < len(order):
                    g, d = order[i - lag]
                    groups[g][1 + lag](d)
        for *_, finish in groups:
            finish()
        for c in copies:
            c.wait()

    return pl.pallas_call(
        body,
        in_specs=[pl.BlockSpec(memory_space=pltpu.VMEM)] * count,
        out_specs=[pl.BlockSpec(memory_space=pl.ANY)] * count,
        out_shape=[jax.ShapeDtypeStruct((4,) + s.shape, s.dtype) for s in shards],
        scratch_shapes=[
            pltpu.SemaphoreType.DMA((27 * count,)),
            pltpu.SemaphoreType.DMA((27 * count,)),
            pltpu.SemaphoreType.DMA((count,)),
        ],
        compiler_params=pltpu.CompilerParams(collective_id=0, has_side_effects=True, vmem_limit_bytes=VMEM),
    )(*shards)


class Reduce:
    SLOTS = 32

    @staticmethod
    def scratch(dm, w):
        q = dm // 4
        e = q // 2
        return [
            pltpu.VMEM((4, q, w), BF16),
            pltpu.VMEM((4, q, w), BF16),
            pltpu.VMEM((4, e, w), BF16),
            pltpu.VMEM((4, e, w), BF16),
            pltpu.VMEM((3, q, w), BF16),
            pltpu.SemaphoreType.DMA((Reduce.SLOTS,)),
            pltpu.SemaphoreType.DMA((Reduce.SLOTS,)),
        ]

    def __init__(self, place, grad, landing, scratch):
        self.place, self.g, self.f = place, grad, landing
        self.ra1, self.rb1, self.ra2, self.rb2, self.zb = scratch[:5]
        self.wire = Wire(scratch[5], scratch[6], place.core)
        self.q = grad.shape[0] // 4
        self.e = self.q // 2
        self.w = grad.shape[1] // 4

    def at(self, base, big, small=None):
        start = base * 2 * self.q + big * self.q + (0 if small is None else small * self.e)
        return pl.ds(pl.multiple_of(start, self.e), self.q if small is None else self.e)

    def eighth(self, small):
        return pl.ds(pl.multiple_of(small * self.e, self.e), self.e)

    def cols(self, d):
        return pl.ds(pl.multiple_of(d * self.w, self.w), self.w)

    def one(self, d):
        p, wire = self.place, self.wire
        wire.start(d, self.g.at[self.at(0, 1 - p.x), self.cols(d)], self.ra1.at[d], p.by_x)
        wire.start(4 + d, self.g.at[self.at(1, 1 - p.y), self.cols(d)], self.rb1.at[d], p.by_y)

    def two(self, d):
        p, wire, c = self.place, self.wire, self.cols(d)
        for slot, buf, to, at, mine, dev, nxt in (
            (0, self.ra1, self.ra2, self.at(0, p.x, 1 - p.y), self.eighth(1 - p.y), p.by_x, p.by_y),
            (4, self.rb1, self.rb2, self.at(1, p.y, 1 - p.x), self.eighth(1 - p.x), p.by_y, p.by_x),
        ):
            wire.landed(slot + d, buf.at[d], dev)
            self.g[at, c] = (self.g[at, c].astype(F32) + buf[d, mine, :].astype(F32)).astype(BF16)
            wire.start(8 + slot + d, self.g.at[at, c], to.at[d], nxt)

    def sums(self, d):
        p, wire, c = self.place, self.wire, self.cols(d)
        wire.landed(8 + d, self.ra2.at[d], p.by_y)
        wire.landed(12 + d, self.rb2.at[d], p.by_x)
        up = (
            self.g[self.at(0, p.x, p.y), c].astype(F32)
            + self.ra1[d, self.eighth(p.y), :].astype(F32)
            + self.ra2[d].astype(F32)
        )
        low = (
            self.g[self.at(1, p.y, p.x), c].astype(F32)
            + self.rb1[d, self.eighth(p.x), :].astype(F32)
            + self.rb2[d].astype(F32)
        )
        return up, low

    def three(self, d):
        p, wire, c, e = self.place, self.wire, self.cols(d), self.e
        up, low = self.sums(d)
        for part, (at, val) in enumerate(((self.at(0, p.x, p.y), up), (self.at(1, p.y, p.x), low))):
            self.g[at, c] = val.astype(BF16)
            wire.start(
                16 + 12 * part + d, self.g.at[at, c], self.zb.at[d - 1, part * e : (part + 1) * e], p.along(d)
            )

    def last(self):
        p, wire, e = self.place, self.wire, self.e
        up, low = self.sums(0)
        for s in (1, 2, 3):
            wire.landed(16 + s, self.zb.at[s - 1, 0:e], p.along(4 - s))
            wire.landed(28 + s, self.zb.at[s - 1, e : 2 * e], p.along(4 - s))
            up = up + self.zb[s - 1, 0:e].astype(F32)
            low = low + self.zb[s - 1, e : 2 * e].astype(F32)
        self.f[0, 0:e] = up.astype(BF16)
        self.f[0, e : 2 * e] = low.astype(BF16)
        wire.start(20, self.f.at[0], self.f.at[2], p.by_x)
        wire.start(21, self.f.at[0], self.f.at[4], p.by_y)
        wire.start(22, self.f.at[0], self.f.at[1], p.core)

    def four(self):
        p, wire, e = self.place, self.wire, self.e
        wire.landed(20, self.f.at[2], p.by_x)
        wire.start(23, self.f.at[2, 0:e], self.f.at[6, 0:e], p.by_y)
        wire.start(25, self.f.at[2], self.f.at[3], p.core)
        wire.landed(21, self.f.at[4], p.by_y)
        wire.start(24, self.f.at[4, e : 2 * e], self.f.at[6, e : 2 * e], p.by_x)
        wire.start(26, self.f.at[4], self.f.at[5], p.core)

    def five(self):
        p, wire, e = self.place, self.wire, self.e
        wire.landed(23, self.f.at[6, 0:e], p.by_y)
        wire.landed(24, self.f.at[6, e : 2 * e], p.by_x)
        wire.start(27, self.f.at[6], self.f.at[7], p.core)

    def six(self):
        for slot, to in ((22, 1), (25, 3), (26, 5), (27, 7)):
            self.wire.landed(slot, self.f.at[to], self.place.core)
        e, sent = self.e, self.wire.sent
        for d in range(4):
            sent(d, self.ra1.at[d])
            sent(4 + d, self.rb1.at[d])
            sent(8 + d, self.ra2.at[d])
            sent(12 + d, self.rb2.at[d])
        for d in range(1, 4):
            sent(16 + d, self.zb.at[d - 1, 0:e])
            sent(28 + d, self.zb.at[d - 1, 0:e])
        for slot in (20, 21, 22, 25, 26, 27):
            sent(slot, self.f.at[0])
        for slot in (23, 24):
            sent(slot, self.f.at[0, 0:e])

    def sweep(self):
        return [
            functools.partial(f, d)
            for f, d in (
                (self.two, 1), (self.two, 2), (self.three, 1), (self.two, 3), (self.three, 2), (self.two, 0), (self.three, 3)
            )
        ]

    def tail(self):
        return [self.last, self.four, self.five, self.six]


def reduce_call(grads, cid):
    count = len(grads)
    dm, cols = grads[0].shape
    w = cols // 4
    each = len(Reduce.scratch(dm, w))

    def body(*refs):
        ins, outs, scr = refs[:count], refs[count : 2 * count], refs[2 * count :]
        place = Place()
        place.meet()
        work = scr[each * count :]
        for i in range(count):
            work[i][...] = ins[i][...]
        todo = [Reduce(place, work[i], outs[i], scr[each * i : each * (i + 1)]) for i in range(count)]
        for r in todo:
            for d in (1, 2, 3, 0):
                r.one(d)
        for r in todo:
            for f in r.sweep() + r.tail():
                f()

    return pl.pallas_call(
        body,
        in_specs=[pl.BlockSpec(memory_space=pltpu.VMEM)] * count,
        out_specs=[pl.BlockSpec(memory_space=pltpu.VMEM)] * count,
        out_shape=[jax.ShapeDtypeStruct((8, dm // 4, w), BF16) for _ in grads],
        scratch_shapes=Reduce.scratch(dm, w) * count + [pltpu.VMEM((dm, cols), BF16)] * count,
        compiler_params=pltpu.CompilerParams(collective_id=cid, has_side_effects=True, vmem_limit_bytes=VMEM),
    )(*grads)


def back_call(cot, act, n2, gup, ghb, n1w, q, k, v, attn, gattn, lse, qseg, kseg, own, near):
    n, rows, cw = q.shape
    win = k.shape[1]
    dm = cot.shape[0]
    hw = act.shape[1] // 2
    half = n * cw // 2
    w = hw // 4
    pairs = cw // PAIR
    scale = HEAD_DIM**-0.5
    each = len(Reduce.scratch(dm, w))

    def body(
        cot_ref, act_ref, n2_ref, gup_ref, ghb_ref, n1_ref, q_ref, k_ref, v_ref, a_ref, g_ref, l_ref, qs_ref, ks_ref,
        fd, fu, gp_ref, dq, dk, dv,
        cot2, act2, n22, gup2, ghb2, n12, gd, gu, dq_o, dk_o, dv_o, at2, dkt, dvt, xs, xr, ls, *scr,
    ):
        place = Place()
        core = place.k
        big_z = place.z < near
        wire = Wire(xs, xr, place.core)
        whole = (
            (cot_ref, cot2, rows), (n2_ref, n22, rows), (ghb_ref, ghb2, rows), (n1_ref, n12, win)
        )
        mixed = ((act_ref, act2), (gup_ref, gup2))
        local = [pltpu.make_async_copy(src, dst.at[:, 0:wide], ls.at[i]) for i, (src, dst, wide) in enumerate(whole)]
        local += [pltpu.make_async_copy(src.at[:, 0:hw], dst.at[0:rows], ls.at[4 + i]) for i, (src, dst) in enumerate(mixed)]
        for i in (0, 4, 1, 5, 2, 3):
            local[i].start()
        place.meet()

        def give_whole(i):
            src, dst, wide = whole[i]
            wire.start(i, src, dst.at[:, wide : 2 * wide], place.core)

        def give_mixed(i):
            src, dst = mixed[i]
            wire.start(4 + i, src.at[:, hw : 2 * hw], dst.at[rows : 2 * rows], place.core)

        def take(*which):
            for i in which:
                local[i].wait()
                if i < 4:
                    dst, wide = whole[i][1:]
                    wire.landed(i, dst.at[:, wide : 2 * wide], place.core)
                else:
                    wire.landed(i, mixed[i - 4][1].at[rows : 2 * rows], place.core)

        give_whole(0)
        give_mixed(0)
        give_whole(1)
        give_mixed(1)
        give_whole(2)
        give_whole(3)
        for d in range(n):
            to = slice(d * PAIR, (d + 1) * PAIR)
            theirs = pl.ds(pl.multiple_of((1 - core) * PAIR, PAIR), PAIR)
            mine = pl.ds(pl.multiple_of(core * PAIR, PAIR), PAIR)
            wire.start(6 + d, a_ref.at[d, :, theirs], at2.at[rows : 2 * rows, to], place.core)
            at2[0:rows, to] = a_ref[d, :, mine]

        down = Reduce(place, gd, fd, scr[:each])
        up = Reduce(place, gu, fu, scr[each : 2 * each])

        def make(red, grad, left, right):
            def step(i, carry):
                d = lax.rem(i + 1, 4)
                c = pl.ds(pl.multiple_of(d * w, w), w)
                grad[:, c] = dot_nn(left[...], right[:, c]).astype(BF16)
                red.one(d)
                return carry

            lax.fori_loop(0, 4, step, 0)

        take(0, 4)
        make(down, gd, cot2, act2)
        take(1, 5)
        make(up, gu, n22, gup2)

        def work(big, d, p):
            at = pl.ds(pl.multiple_of(p * PAIR, PAIR), PAIR)
            to = pl.ds(pl.multiple_of(d * PAIR, PAIR), PAIR)
            rel = lax.rem(p + core, 2)
            if not big:
                dkt[...] = jnp.zeros_like(dkt)
                dvt[...] = jnp.zeros_like(dvt)
            for i, (qs, qn, ks, kn) in enumerate(blocks_of(rows, own, win, big)):
                mask = qs_ref[qs : qs + qn, :] == ks_ref[:, ks : ks + kn]
                qq, kk, vv = q_ref[d, qs : qs + qn, at], k_ref[d, ks : ks + kn, at], v_ref[d, ks : ks + kn, at]
                gg = g_ref[d, qs : qs + qn, at]
                prod = gg.astype(F32) * a_ref[d, qs : qs + qn, at].astype(F32)
                dqs = []
                for h in range(2):
                    lanes = slice(h * HEAD_DIM, (h + 1) * HEAD_DIM)
                    qh, kh, gh = qq[:, lanes] * BF16(scale), kk[:, lanes], gg[:, lanes]
                    s = jnp.where(mask, dot_nt(qh, kh) - l_ref[d * pairs + p, qs : qs + qn, h : h + 1], NEG)
                    pr = jnp.exp(s)
                    dp = dot_nt(gh, vv[:, lanes])
                    delta = jnp.sum(prod[:, lanes], axis=1, keepdims=True)
                    ds = (pr * (dp - delta)).astype(BF16)
                    dqs.append(dot_nn(ds, kh) * scale)
                    gk = dot_tn(qh, ds)
                    gv = dot_tn(gh, pr.astype(BF16))
                    if big and i == 0:
                        dkt[lanes, :] = gk
                        dvt[lanes, :] = gv
                    else:
                        dkt[lanes, ks : ks + kn] += gk
                        dvt[lanes, ks : ks + kn] += gv
                dq[rel, qs : qs + qn, to] = jnp.concatenate(dqs, axis=1).astype(BF16)
            dk[rel, :, to] = dkt[...].T.astype(BF16)
            dv[rel, :, to] = dvt[...].T.astype(BF16)

        todo = down.sweep() + up.sweep()
        turns = [todo[2 * i : 2 * i + 2] for i in range(n * pairs)]
        turns[-1] = todo[2 * (n * pairs - 1) :]

        def head_pair(i, carry):
            d, p = i // pairs, lax.rem(i, pairs)

            @pl.when(big_z)
            def _():
                work(True, d, p)

            @pl.when(jnp.logical_not(big_z))
            def _():
                work(False, d, p)

            for t, steps in enumerate(turns):
                if steps:

                    @pl.when(i == t)
                    def _():
                        for f in steps:
                            f()

            return carry

        lax.fori_loop(0, n * pairs, head_pair, 0)
        halves = ((dq, dq_o), (dk, dk_o), (dv, dv_o))
        for i, (src, dst) in enumerate(halves):
            wire.start(10 + i, src.at[1], dst, place.core)
        down.last()
        take(2, 3)
        for d in range(n):
            wire.landed(6 + d, at2.at[rows : 2 * rows, d * PAIR : (d + 1) * PAIR], place.core)

        def put(m, val):
            for d in range(n):
                at = d * w + m * PAIR
                act2[:, at : at + PAIR] = val[:, d * PAIR : (d + 1) * PAIR].astype(BF16)

        put(3, dot_nn(ghb2[...], at2[...]))
        up.last()
        down.four()
        wire.landed(10, dq_o, place.core)
        put(0, dot_nn(n12[:, own : own + rows], dq[0]) + dot_nn(n12[:, win + own : win + own + rows], dq_o[...]))
        down.five()
        up.four()
        wire.landed(11, dk_o, place.core)
        put(1, dot_nn(n12[:, 0:win], dk[0]) + dot_nn(n12[:, win : 2 * win], dk_o[...]))
        up.five()
        wire.landed(12, dv_o, place.core)
        put(2, dot_nn(n12[:, 0:win], dv[0]) + dot_nn(n12[:, win : 2 * win], dv_o[...]))
        out = pltpu.make_async_copy(act2, gp_ref, ls.at[6])
        out.start()
        down.six()
        up.six()
        for i in range(4):
            wire.sent(i, whole[i][0])
        for i in range(2):
            wire.sent(4 + i, act2.at[0:rows])
        for d in range(n):
            wire.sent(6 + d, at2.at[0:rows, 0:PAIR])
        for i in range(3):
            wire.sent(10 + i, halves[i][1])
        out.wait()

    hbm = pl.BlockSpec(memory_space=pl.ANY)
    vmem = pl.BlockSpec(memory_space=pltpu.VMEM)
    shaped = lambda *shape: jax.ShapeDtypeStruct(shape, BF16)
    buf = lambda *shape: pltpu.VMEM(shape, BF16)
    return pl.pallas_call(
        body,
        in_specs=[hbm] * 6 + [vmem] * 8,
        out_specs=[vmem, vmem, hbm, vmem, vmem, vmem],
        out_shape=[
            shaped(8, dm // 4, w), shaped(8, dm // 4, w), shaped(dm, hw), shaped(2, rows, half), shaped(2, win, half), shaped(2, win, half)
        ],
        scratch_shapes=[
            buf(dm, 2 * rows), buf(2 * rows, hw), buf(dm, 2 * rows), buf(2 * rows, hw), buf(dm, 2 * rows), buf(dm, 2 * win),
            buf(dm, hw), buf(dm, hw), buf(rows, half), buf(win, half), buf(win, half), buf(2 * rows, half),
            pltpu.VMEM((PAIR, win), F32), pltpu.VMEM((PAIR, win), F32),
            pltpu.SemaphoreType.DMA((13,)), pltpu.SemaphoreType.DMA((13,)), pltpu.SemaphoreType.DMA((7,)),
        ]
        + Reduce.scratch(dm, w) * 2,
        compiler_params=pltpu.CompilerParams(collective_id=1, has_side_effects=True, vmem_limit_bytes=VMEM_ALL),
    )(cot, act, n2, gup, ghb, n1w, q, k, v, attn, gattn, lse, qseg, kseg)


def place_grads(coords, done, mode):
    _, q, w = done.shape
    e = q // 2
    dm = 4 * q
    lanes = w // 4

    def body(c_ref, f_ref, *outs):
        for off in range(8):
            y = lax.bitwise_xor(c_ref[0], off >> 2)
            x = lax.bitwise_xor(c_ref[1], (off >> 1) & 1)
            k = lax.bitwise_xor(c_ref[2], off & 1)
            for part in range(2):
                val = f_ref[off, part * e : (part + 1) * e, :].astype(F32)
                block = x * 2 + y if part == 0 else 4 + y * 2 + x
                rows = pl.ds(pl.multiple_of(block * e, e), e)
                if mode == "up":
                    outs[0][rows, pl.ds(pl.multiple_of(k * w, w), w)] = val
                elif mode == "down":
                    outs[0][pl.ds(pl.multiple_of(k * w, w), w), rows] = val.T
                else:
                    at = pl.ds(pl.multiple_of(k * lanes, lanes), lanes)
                    for m in range(3):
                        outs[m][rows, at] = val[:, m * lanes : (m + 1) * lanes]
                    outs[3][at, rows] = val[:, 3 * lanes :].T

    if mode == "up":
        shapes = [(dm, 2 * w)]
    elif mode == "down":
        shapes = [(2 * w, dm)]
    else:
        shapes = [(dm, w // 2)] * 3 + [(w // 2, dm)]
    return pl.pallas_call(
        body,
        in_specs=[pl.BlockSpec(memory_space=pltpu.SMEM), pl.BlockSpec(memory_space=pltpu.VMEM)],
        out_specs=[pl.BlockSpec(memory_space=pltpu.VMEM)] * len(shapes),
        out_shape=[jax.ShapeDtypeStruct(s, F32) for s in shapes],
        compiler_params=pltpu.CompilerParams(vmem_limit_bytes=VMEM),
        cost_estimate=pl.CostEstimate(flops=0, bytes_accessed=12 * dm * w, transcendentals=0),
    )(coords, done)


def relative(stack, z):
    return jnp.roll(stack, -z, axis=0)


def core_first(v, core, axis):
    return jnp.where(core == 0, v, jnp.flip(v, axis))


def gather_any(shard, z):
    return relative(lax.all_gather(shard, "mp", axis=0, tiled=False), z)


def reduce_any(half, z, core):
    zero = jnp.zeros_like(half)
    v = jnp.stack([jnp.where(core == 0, half, zero), jnp.where(core == 1, half, zero)], axis=2)
    v = jnp.roll(jnp.moveaxis(v, 1, 0), z, axis=0)
    v = lax.psum_scatter(v, "mp", scatter_dimension=0, tiled=True)[0]
    return lax.psum(v, "dp").astype(F32).reshape(half.shape[0], -1)


def local(
    tokens,
    segments,
    ln1_gain,
    ln1_bias,
    w_query,
    b_query,
    w_key,
    w_value,
    b_value,
    w_out,
    b_out,
    ln2_gain,
    ln2_bias,
    w_up,
    b_up,
    w_down,
    b_down,
    cotangent,
):
    rows, dm = tokens.shape
    cw = w_query.shape[1]
    ffw = w_up.shape[1]
    mp = lax.axis_size("mp")
    dp = lax.axis_size("dp")
    fast = mp == 4 and dp == 8 and rows % 256 == 0 and cw == 2 * PAIR
    z = lax.axis_index("mp")
    me = lax.axis_index("dp")
    core = lax.rem(me, 2)
    x = lax.rem(me // 2, 2)
    y = me // 4
    f32 = lambda v: v.astype(F32)

    near = -(-LONGEST // rows)
    own = (near - 1) * rows
    win = own + rows + 2 * HALO
    halo = [
        lax.ppermute(tokens, "mp", [((i + j) % near, i) for i in range(near)]) for j in range(1, near)
    ]
    before = lax.ppermute(tokens[-HALO:], "mp", [(i - 1, i) for i in range(near, mp)])
    behind = lax.ppermute(tokens[:HALO], "mp", [(i + 1, i) for i in range(near - 1, mp - 1)])
    small_vec = jnp.concatenate([b_query, b_value, b_up])
    if fast:
        vecs = [small_vec] + [
            lax.ppermute(small_vec, "mp", [((i + d) % mp, i) for i in range(mp)]) for d in range(1, mp)
        ]
        vecs = jnp.stack(vecs)
    else:
        vecs = relative(lax.all_gather(small_vec, "mp", axis=0, tiled=False), z)
    bq_all, bv_all = vecs[:, :cw], vecs[:, cw : 2 * cw]
    bu_all = vecs[:, 2 * cw :].reshape(mp, 2, ffw // 2).transpose(1, 0, 2)
    bu_all = core_first(bu_all, core, 0).reshape(mp * ffw)

    is_near = z < near
    seg_parts = [
        jnp.where(is_near, lax.dynamic_slice_in_dim(segments, lax.rem(z + j, near) * rows, rows), -1)
        for j in range(1, near)
    ]
    seg_own = lax.dynamic_slice_in_dim(segments, z * rows, rows)
    seg_prev = lax.dynamic_slice_in_dim(segments, jnp.maximum(z * rows - HALO, 0), HALO)
    seg_next = lax.dynamic_slice_in_dim(segments, jnp.minimum((z + 1) * rows, segments.shape[0] - HALO), HALO)
    seg_far = jnp.concatenate(seg_parts)
    seg_far = jnp.concatenate([seg_far[:-HALO], jnp.where(is_near, seg_far[-HALO:], seg_prev)])
    has_next = jnp.logical_and(z >= near - 1, z < mp - 1)
    seg_win = jnp.concatenate(
        [seg_far, seg_own, jnp.where(has_next, seg_next, -1), jnp.full((HALO,), -1, segments.dtype)]
    )
    kseg, qseg = seg_win[None, :], seg_own[:, None]
    info = jnp.stack([is_near.astype(jnp.int32), core]).astype(jnp.int32)

    pack = jnp.concatenate([w_query, w_key, w_value, w_out.T], axis=1)
    if fast:
        packed, up_all, down_all = gather_call([pack, w_up, w_down])
    else:
        packed, up_all, down_all = (gather_any(w, z) for w in (pack, w_up, w_down))

    far = jnp.concatenate(halo, axis=0)
    far = jnp.concatenate([far[:-HALO], far[-HALO:] + before], axis=0)
    tok_win = jnp.concatenate([far, tokens, behind, jnp.zeros((HALO, dm), tokens.dtype)], axis=0)
    hat_win, inv_win = norm_rows(f32(tok_win))
    n1w = (hat_win * f32(ln1_gain) + f32(ln1_bias)).astype(BF16)
    q, k, v = qkv_call(n1w, packed, bq_all, bv_all, own, rows, cw)
    attn, lse = attn_fwd_call(info, q, k, v, qseg, kseg, own)
    hidden, n2 = out_call(attn, packed, tokens, b_out, ln2_gain, ln2_bias)
    output, g_n2, active, g_upper, g_b_up = ffn_call(
        info[1:], n2, hidden, cotangent, up_all, down_all, bu_all, b_down, 2
    )

    gout = f32(cotangent)
    hat2, inv2 = norm_rows(hidden)

    def norm_back(g, hat, inv, gain):
        gg = g * gain
        first = jnp.mean(gg, axis=1, keepdims=True)
        second = jnp.mean(gg * hat, axis=1, keepdims=True)
        return inv * (gg - first - hat * second), jnp.sum(g * hat, axis=0), jnp.sum(g, axis=0)

    g_hidden, g_gain2, g_bias2 = norm_back(g_n2, hat2, inv2, f32(ln2_gain))
    g_hidden = g_hidden + gout
    ghb = g_hidden.astype(BF16)

    g_attn = jnp.stack([dot_nn(ghb, packed[d, :, 3 * cw :]).astype(BF16) for d in range(mp)])
    if fast:
        done_d, done_u, gp, dq, dk, dv = back_call(
            cotangent.T, active, n2.T, g_upper, ghb.T, n1w.T, q, k, v, attn, g_attn, lse, qseg, kseg, own, near
        )
    else:
        dq, dk, dv = attn_bwd_call(info, q, k, v, attn, g_attn, lse, qseg, kseg, own)
    halves = dq.shape[0]
    g_own, g_far, g_next = norm1_back_call(dq, dk, dv, packed, info, own)
    back = g_own
    for j in range(1, near):
        part = g_far[(j - 1) * rows : j * rows]
        back = back + f32(lax.ppermute(part, "mp", [(i, (i + j) % near) for i in range(near)]))
    to_prev = f32(lax.ppermute(g_far[-HALO:], "mp", [(i, i - 1) for i in range(near, mp)]))
    to_next = f32(lax.ppermute(g_next, "mp", [(i, i + 1) for i in range(near - 1, mp - 1)]))
    back = jnp.concatenate([back[:HALO] + to_next, back[HALO:-HALO], back[-HALO:] + to_prev], axis=0)
    hat1 = hat_win[own : own + rows]
    inv1 = inv_win[own : own + rows]
    g_in, g_gain1, g_bias1 = norm_back(back, hat1, inv1, f32(ln1_gain))
    g_tokens = g_in + g_hidden

    n1 = n1w[own : own + rows]
    if fast:
        coords = jnp.stack([y, x, core]).astype(jnp.int32)
        (done_p,) = reduce_call([gp], 2)
        (g_w_down,) = place_grads(coords, done_d, "down")
        (g_w_up,) = place_grads(coords, done_u, "up")
        g_w_query, g_w_key, g_w_value, g_w_out = place_grads(coords, done_p, "pack")
    else:
        other = lambda v: lax.ppermute(v, "dp", [(i, i - i % 2 + (i + 1) % 2) for i in range(dp)])
        hw = mp * ffw // 2

        def pair_grad(left, right):
            return (dot_tn(left, right[:, :hw]) + dot_tn(other(left), other(right[:, hw:]))).astype(BF16)

        gd = pair_grad(cotangent, active)
        gu = pair_grad(n2, g_upper)
        g_w_up = reduce_any(gu.reshape(dm, mp, ffw // 2), z, core)
        g_w_down = reduce_any(gd.reshape(dm, mp, ffw // 2), z, core).T

        def whole_grad(left, right, name=None):
            v = dot_tn(left, right).astype(BF16).reshape(dm, mp, cw)
            v = jnp.roll(jnp.moveaxis(v, 1, 0), z, axis=0)
            v = lax.psum_scatter(v, "mp", scatter_dimension=0, tiled=True)[0]
            return lax.psum(v, "dp").astype(F32)

        def whole(v):
            if halves == 1:
                return v[0]
            v = v.reshape(2, v.shape[1], mp, cw // 2).transpose(1, 2, 0, 3)
            return core_first(v, core, 2).reshape(v.shape[0], mp * cw)

        g_w_query = whole_grad(n1, whole(dq))
        g_w_key = whole_grad(n1w, whole(dk))
        g_w_value = whole_grad(n1w, whole(dv))
        g_w_out = whole_grad(ghb, attn.transpose(1, 0, 2).reshape(rows, mp * cw)).T

    def shards(v, width):
        if v.shape[0] == 2:
            v = core_first(v.reshape(2, mp, width // 2), core, 0).transpose(1, 0, 2)
        return jnp.roll(v.reshape(mp, width), z, axis=0).reshape(mp * width)

    gbq = shards(jnp.sum(f32(dq), axis=1), cw)
    gbv = shards(jnp.sum(f32(dv), axis=1), cw)
    gbu = core_first(g_b_up.reshape(2, mp, ffw // 2), core, 0).transpose(1, 0, 2)
    gbu = jnp.roll(gbu.reshape(mp, ffw), z, axis=0).reshape(-1)
    vec = jnp.concatenate(
        [g_gain1, g_bias1, jnp.sum(g_hidden, axis=0), g_gain2, g_bias2, jnp.sum(gout, axis=0), gbq, gbv, gbu]
    )
    vec = lax.psum(vec, ("dp", "mp"))
    g_gain1, g_bias1, g_b_out, g_gain2, g_bias2, g_b_down = (vec[i * dm : (i + 1) * dm] for i in range(6))
    at = 6 * dm
    g_b_query = lax.dynamic_slice_in_dim(vec, at + z * cw, cw)
    g_b_value = lax.dynamic_slice_in_dim(vec, at + mp * cw + z * cw, cw)
    g_b_up = lax.dynamic_slice_in_dim(vec, at + 2 * mp * cw + z * ffw, ffw)
    return (
        output,
        g_tokens,
        g_gain1,
        g_bias1,
        g_w_query,
        g_b_query,
        g_w_key,
        g_w_value,
        g_b_value,
        g_w_out,
        g_b_out,
        g_gain2,
        g_bias2,
        g_w_up,
        g_b_up,
        g_w_down,
        g_b_down,
    )


def solution(mesh):
    in_specs = (
        P(("dp", "mp"), None),
        P("dp"),
        P(),
        P(),
        P(None, "mp"),
        P("mp"),
        P(None, "mp"),
        P(None, "mp"),
        P("mp"),
        P("mp", None),
        P(),
        P(),
        P(),
        P(None, "mp"),
        P("mp"),
        P("mp", None),
        P(),
        P(("dp", "mp"), None),
    )
    out_specs = (
        P(("dp", "mp"), None),
        P(("dp", "mp"), None),
        P(),
        P(),
        P(None, "mp"),
        P("mp"),
        P(None, "mp"),
        P(None, "mp"),
        P("mp"),
        P("mp", None),
        P(),
        P(),
        P(),
        P(None, "mp"),
        P("mp"),
        P("mp", None),
        P(),
    )
    return jax.shard_map(local, mesh=mesh, in_specs=in_specs, out_specs=out_specs, check_vma=False)
```

```python
import functools

import jax
import jax.numpy as jnp
from jax import lax
from jax.experimental import pallas as pl
from jax.experimental.pallas import tpu as pltpu
from jax.sharding import PartitionSpec as P

HEAD_DIM = 64
LONGEST = 900
HALO = 64
PAIR = 128
EPS = 1e-06
NEG = -1e30
VMEM = 60 * 1024 * 1024
VMEM_ALL = 67043328
F32 = jnp.float32
BF16 = jnp.bfloat16


def dot_nn(a, b):
    return lax.dot_general(a, b, (((1,), (0,)), ((), ())), preferred_element_type=F32)


def dot_nt(a, b):
    return lax.dot_general(a, b, (((1,), (1,)), ((), ())), preferred_element_type=F32)


def dot_tn(a, b):
    return lax.dot_general(a, b, (((0,), (0,)), ((), ())), preferred_element_type=F32)


def barrier(*xs):
    return lax.optimization_barrier(xs)


def params(*sem, **kw):
    return pltpu.CompilerParams(dimension_semantics=sem, vmem_limit_bytes=VMEM, **kw)


def norm_rows(x):
    mean = jnp.mean(x, axis=1, keepdims=True)
    cent = x - mean
    inv = lax.rsqrt(jnp.mean(cent * cent, axis=1, keepdims=True) + EPS)
    return cent * inv, inv


def qkv_call(n1w, packed, b_q, b_v, own, rows, cw):
    n, dm, _ = packed.shape
    win = n1w.shape[0]

    def body(x_ref, w_ref, bq_ref, bv_ref, q_ref, k_ref, v_ref):
        x = x_ref[...]
        q_ref[0] = (dot_nn(x[own : own + rows], w_ref[0, :, 0:cw]) + bq_ref[0].astype(F32)).astype(BF16)
        k_ref[0] = dot_nn(x, w_ref[0, :, cw : 2 * cw]).astype(BF16)
        v_ref[0] = (dot_nn(x, w_ref[0, :, 2 * cw : 3 * cw]) + bv_ref[0].astype(F32)).astype(BF16)

    return pl.pallas_call(
        body,
        grid=(n,),
        in_specs=[
            pl.BlockSpec((win, dm), lambda d: (0, 0)),
            pl.BlockSpec((1, dm, 4 * cw), lambda d: (d, 0, 0)),
            pl.BlockSpec((1, 1, cw), lambda d: (d, 0, 0)),
            pl.BlockSpec((1, 1, cw), lambda d: (d, 0, 0)),
        ],
        out_specs=[
            pl.BlockSpec((1, rows, cw), lambda d: (d, 0, 0)),
            pl.BlockSpec((1, win, cw), lambda d: (d, 0, 0)),
            pl.BlockSpec((1, win, cw), lambda d: (d, 0, 0)),
        ],
        out_shape=[
            jax.ShapeDtypeStruct((n, rows, cw), BF16),
            jax.ShapeDtypeStruct((n, win, cw), BF16),
            jax.ShapeDtypeStruct((n, win, cw), BF16),
        ],
        compiler_params=params("arbitrary"),
        cost_estimate=pl.CostEstimate(
            flops=2 * n * dm * cw * (rows + 2 * win), bytes_accessed=2 * (n * dm * 4 * cw + win * dm), transcendentals=0
        ),
    )(n1w, packed, b_q[:, None, :], b_v[:, None, :])


def blocks_of(rows, own, win, big):
    if big:
        step = min(256, rows)
        return [(s, step, 0, win) for s in range(0, rows, step)]
    return [(s, 128, own + s - 128, 384) for s in range(0, rows, 128)]


def attn_fwd_call(is_big, q, k, v, qseg, kseg, own):
    n, rows, cw = q.shape
    win = k.shape[1]
    pairs = cw // PAIR

    def work(big, q_ref, k_ref, v_ref, qs_ref, ks_ref, o_ref, l_ref):
        for qs, qn, ks, kn in blocks_of(rows, own, win, big):
            mask = qs_ref[qs : qs + qn, :] == ks_ref[:, ks : ks + kn]
            for h in range(2):
                lanes = slice(h * HEAD_DIM, (h + 1) * HEAD_DIM)
                qh = q_ref[0, qs : qs + qn, lanes] * BF16(HEAD_DIM**-0.5)
                s = jnp.where(mask, dot_nt(qh, k_ref[0, ks : ks + kn, lanes]), NEG)
                top = jnp.max(s, axis=1, keepdims=True)
                p = jnp.exp(s - top)
                total = jnp.sum(p, axis=1, keepdims=True)
                o = dot_nn(p.astype(BF16), v_ref[0, ks : ks + kn, lanes])
                o_ref[0, qs : qs + qn, lanes] = (o / total).astype(BF16)
                l_ref[0, qs : qs + qn, h : h + 1] = top + jnp.log(total)

    def body(big_ref, *refs):
        @pl.when(big_ref[0] == 1)
        def _():
            work(True, *refs)

        @pl.when(big_ref[0] == 0)
        def _():
            work(False, *refs)

    return pl.pallas_call(
        body,
        grid_spec=pltpu.PrefetchScalarGridSpec(
            num_scalar_prefetch=1,
            grid=(n, pairs),
            in_specs=[
                pl.BlockSpec((1, rows, PAIR), lambda d, p, *_: (d, 0, p)),
                pl.BlockSpec((1, win, PAIR), lambda d, p, *_: (d, 0, p)),
                pl.BlockSpec((1, win, PAIR), lambda d, p, *_: (d, 0, p)),
                pl.BlockSpec((rows, 1), lambda d, p, *_: (0, 0)),
                pl.BlockSpec((1, win), lambda d, p, *_: (0, 0)),
            ],
            out_specs=[
                pl.BlockSpec((1, rows, PAIR), lambda d, p, *_: (d, 0, p)),
                pl.BlockSpec((1, rows, 2), lambda d, p, *_: (d * pairs + p, 0, 0)),
            ],
        ),
        out_shape=[
            jax.ShapeDtypeStruct((n, rows, cw), BF16),
            jax.ShapeDtypeStruct((n * pairs, rows, 2), F32),
        ],
        compiler_params=params("arbitrary", "arbitrary"),
        cost_estimate=pl.CostEstimate(
            flops=16 * n * rows * win * cw, bytes_accessed=2 * n * cw * (2 * rows + 2 * win), transcendentals=n * rows * win * 4
        ),
    )(is_big, q, k, v, qseg, kseg)


def attn_bwd_call(info, q, k, v, attn, gattn, lse, qseg, kseg, own):
    n, rows, cw = q.shape
    win = k.shape[1]
    pairs = cw // PAIR
    scale = HEAD_DIM**-0.5

    def work(big, q_ref, k_ref, v_ref, a_ref, g_ref, l_ref, qs_ref, ks_ref, dq_ref, dk_ref, dv_ref, dkt, dvt):
        if not big:
            dkt[...] = jnp.zeros_like(dkt)
            dvt[...] = jnp.zeros_like(dvt)
        for i, (qs, qn, ks, kn) in enumerate(blocks_of(rows, own, win, big)):
            mask = qs_ref[qs : qs + qn, :] == ks_ref[:, ks : ks + kn]
            for h in range(2):
                lanes = slice(h * HEAD_DIM, (h + 1) * HEAD_DIM)
                qh = q_ref[0, qs : qs + qn, lanes] * BF16(scale)
                kh = k_ref[0, ks : ks + kn, lanes]
                gh = g_ref[0, qs : qs + qn, lanes]
                s = jnp.where(mask, dot_nt(qh, kh) - l_ref[0, qs : qs + qn, h : h + 1], NEG)
                p = jnp.exp(s)
                dp = dot_nt(gh, v_ref[0, ks : ks + kn, lanes])
                delta = jnp.sum(
                    gh.astype(F32) * a_ref[0, qs : qs + qn, lanes].astype(F32), axis=1, keepdims=True
                )
                ds = (p * (dp - delta)).astype(BF16)
                dq_ref[0, qs : qs + qn, lanes] = (dot_nn(ds, kh) * scale).astype(BF16)
                dk = dot_tn(qh, ds)
                dv = dot_tn(gh, p.astype(BF16))
                if big and i == 0:
                    dkt[lanes, :] = dk
                    dvt[lanes, :] = dv
                else:
                    dkt[lanes, ks : ks + kn] += dk
                    dvt[lanes, ks : ks + kn] += dv
        dk_ref[0] = dkt[...].T.astype(BF16)
        dv_ref[0] = dvt[...].T.astype(BF16)

    def body(info_ref, *refs):
        @pl.when(info_ref[0] == 1)
        def _():
            work(True, *refs)

        @pl.when(info_ref[0] == 0)
        def _():
            work(False, *refs)

    if pairs > 1:

        def put(d, p, info):
            rel = lax.bitwise_xor(p // (pairs // 2), info[1])
            return (rel, 0, d * (pairs // 2) + p % (pairs // 2))

        half_shape = (2, rows, n * cw // 2)
        half_win = (2, win, n * cw // 2)
    else:

        def put(d, p, info):
            return (0, 0, d)

        half_shape = (1, rows, n * cw)
        half_win = (1, win, n * cw)
    return pl.pallas_call(
        body,
        grid_spec=pltpu.PrefetchScalarGridSpec(
            num_scalar_prefetch=1,
            grid=(n, pairs),
            in_specs=[
                pl.BlockSpec((1, rows, PAIR), lambda d, p, *_: (d, 0, p)),
                pl.BlockSpec((1, win, PAIR), lambda d, p, *_: (d, 0, p)),
                pl.BlockSpec((1, win, PAIR), lambda d, p, *_: (d, 0, p)),
                pl.BlockSpec((1, rows, PAIR), lambda d, p, *_: (d, 0, p)),
                pl.BlockSpec((1, rows, PAIR), lambda d, p, *_: (d, 0, p)),
                pl.BlockSpec((1, rows, 2), lambda d, p, *_: (d * pairs + p, 0, 0)),
                pl.BlockSpec((rows, 1), lambda d, p, *_: (0, 0)),
                pl.BlockSpec((1, win), lambda d, p, *_: (0, 0)),
            ],
            out_specs=[
                pl.BlockSpec((1, rows, PAIR), put),
                pl.BlockSpec((1, win, PAIR), put),
                pl.BlockSpec((1, win, PAIR), put),
            ],
            scratch_shapes=[pltpu.VMEM((PAIR, win), F32), pltpu.VMEM((PAIR, win), F32)],
        ),
        out_shape=[
            jax.ShapeDtypeStruct(half_shape, BF16),
            jax.ShapeDtypeStruct(half_win, BF16),
            jax.ShapeDtypeStruct(half_win, BF16),
        ],
        compiler_params=params("arbitrary", "arbitrary"),
        cost_estimate=pl.CostEstimate(
            flops=40 * n * rows * win * cw, bytes_accessed=2 * n * cw * (4 * rows + 4 * win), transcendentals=n * rows * win * 4
        ),
    )(info, q, k, v, attn, gattn, lse, qseg, kseg)


def out_call(attn, packed, resid, b_out, gain, bias):
    n, rows, cw = attn.shape
    dm = packed.shape[1]

    def body(a_ref, w_ref, x_ref, bo_ref, g_ref, b_ref, h_ref, n_ref):
        d = pl.program_id(0)
        part = dot_nt(a_ref[0], w_ref[0])

        @pl.when(d == 0)
        def _():
            h_ref[...] = part + x_ref[...].astype(F32) + bo_ref[...].astype(F32)

        @pl.when(d > 0)
        def _():
            h_ref[...] += part

        @pl.when(d == n - 1)
        def _():
            hat, _ = norm_rows(h_ref[...])
            n_ref[...] = (hat * g_ref[...].astype(F32) + b_ref[...].astype(F32)).astype(BF16)

    full = lambda d: (0, 0)
    return pl.pallas_call(
        body,
        grid=(n,),
        in_specs=[
            pl.BlockSpec((1, rows, cw), lambda d: (d, 0, 0)),
            pl.BlockSpec((1, dm, cw), lambda d: (d, 0, 3)),
            pl.BlockSpec((rows, dm), full),
            pl.BlockSpec((1, dm), full),
            pl.BlockSpec((1, dm), full),
            pl.BlockSpec((1, dm), full),
        ],
        out_specs=[pl.BlockSpec((rows, dm), full), pl.BlockSpec((rows, dm), full)],
        out_shape=[jax.ShapeDtypeStruct((rows, dm), F32), jax.ShapeDtypeStruct((rows, dm), BF16)],
        compiler_params=params("arbitrary"),
        cost_estimate=pl.CostEstimate(flops=2 * n * rows * cw * dm, bytes_accessed=2 * n * dm * cw, transcendentals=0),
    )(attn, packed, resid, b_out[None], gain[None], bias[None])


def ffn_call(core, n2, hidden, cot, w_up, w_down, b_up, b_down, halves):
    rows, dm = n2.shape
    n, _, ffw = w_up.shape
    tile = ffw // halves

    def body(core_ref, x_ref, h_ref, c_ref, wu_ref, wd_ref, bu_ref, bd_ref, o_ref, gn_ref, a_ref, gu_ref, gb_ref, acc):
        t = pl.program_id(0)
        u = dot_nn(x_ref[...], wu_ref[0]) + bu_ref[...].astype(F32)
        cdf = 0.5 * (1.0 + lax.erf(u * 0.7071067811865476))
        act = (u * cdf).astype(BF16)
        slope = cdf + u * jnp.exp(-0.5 * u * u) * 0.3989422804014327
        a_ref[...] = act
        grad = dot_nt(c_ref[...], wd_ref[0]) * slope
        gu = grad.astype(BF16)
        gu_ref[...] = gu
        gb_ref[...] = jnp.sum(gu.astype(F32), axis=0, keepdims=True)
        out = dot_nn(act, wd_ref[0])
        gn = dot_nt(gu, wu_ref[0])

        @pl.when(t == 0)
        def _():
            acc[...] = h_ref[...] + bd_ref[...].astype(F32) + out
            gn_ref[...] = gn

        @pl.when(t > 0)
        def _():
            acc[...] += out
            gn_ref[...] += gn

        @pl.when(t == n * halves - 1)
        def _():
            o_ref[...] = acc[...].astype(BF16)

    full = lambda t, c: (0, 0)

    def part(t, c):
        return lax.bitwise_xor(t // n, c[0]) if halves > 1 else 0

    return pl.pallas_call(
        body,
        grid_spec=pltpu.PrefetchScalarGridSpec(
            num_scalar_prefetch=1,
            grid=(n * halves,),
            in_specs=[
                pl.BlockSpec((rows, dm), full),
                pl.BlockSpec((rows, dm), full),
                pl.BlockSpec((rows, dm), full),
                pl.BlockSpec((1, dm, tile), lambda t, c: (t % n, 0, part(t, c))),
                pl.BlockSpec((1, tile, dm), lambda t, c: (t % n, part(t, c), 0)),
                pl.BlockSpec((1, tile), lambda t, c: (0, t)),
                pl.BlockSpec((1, dm), full),
            ],
            out_specs=[
                pl.BlockSpec((rows, dm), full),
                pl.BlockSpec((rows, dm), full),
                pl.BlockSpec((rows, tile), lambda t, c: (0, t)),
                pl.BlockSpec((rows, tile), lambda t, c: (0, t)),
                pl.BlockSpec((1, tile), lambda t, c: (0, t)),
            ],
            scratch_shapes=[pltpu.VMEM((rows, dm), F32)],
        ),
        out_shape=[
            jax.ShapeDtypeStruct((rows, dm), BF16),
            jax.ShapeDtypeStruct((rows, dm), F32),
            jax.ShapeDtypeStruct((rows, n * ffw), BF16),
            jax.ShapeDtypeStruct((rows, n * ffw), BF16),
            jax.ShapeDtypeStruct((1, n * ffw), F32),
        ],
        compiler_params=params("arbitrary"),
        cost_estimate=pl.CostEstimate(
            flops=8 * rows * dm * n * ffw, bytes_accessed=4 * n * dm * ffw, transcendentals=2 * rows * n * ffw
        ),
    )(core, n2, hidden, cot, w_up, w_down, b_up[None], b_down[None])


def norm1_back_call(dq, dk, dv, packed, info, own):
    halves, rows, _ = dq.shape
    n, dm, four = packed.shape
    cw = four // 4
    win = dk.shape[1]
    width = cw // halves

    def body(info_ref, dq_ref, dk_ref, dv_ref, w_ref, o_ref, h_ref, t_ref, acc):
        step = pl.program_id(0)

        def weight(which, j):
            at = lax.bitwise_xor(j, info_ref[1]) if halves > 1 else 0
            return w_ref[0, :, pl.ds(pl.multiple_of(which * cw + at * width, width), width)]

        left = jnp.concatenate([r[j] for r in (dk_ref, dv_ref) for j in range(halves)], axis=1)
        right = jnp.concatenate([weight(m, j) for m in (1, 2) for j in range(halves)], axis=1)
        part = dot_nt(left, right)
        left = jnp.concatenate([dq_ref[j] for j in range(halves)], axis=1)
        right = jnp.concatenate([weight(0, j) for j in range(halves)], axis=1)
        mine = dot_nt(left, right)

        @pl.when(step == 0)
        def _():
            acc[...] = part

        @pl.when(step > 0)
        def _():
            acc[...] += part

        acc[own : own + rows, :] += mine

        @pl.when(step == n - 1)
        def _():
            o_ref[...] = acc[own : own + rows, :]
            h_ref[...] = acc[0:own, :].astype(BF16)
            t_ref[...] = acc[own + rows : own + rows + HALO, :].astype(BF16)

    full = lambda s, info: (0, 0)
    return pl.pallas_call(
        body,
        grid_spec=pltpu.PrefetchScalarGridSpec(
            num_scalar_prefetch=1,
            grid=(n,),
            in_specs=[
                pl.BlockSpec((halves, rows, width), lambda s, info: (0, 0, s)),
                pl.BlockSpec((halves, win, width), lambda s, info: (0, 0, s)),
                pl.BlockSpec((halves, win, width), lambda s, info: (0, 0, s)),
                pl.BlockSpec((1, dm, four), lambda s, info: (s, 0, 0)),
            ],
            out_specs=[
                pl.BlockSpec((rows, dm), full),
                pl.BlockSpec((own, dm), full),
                pl.BlockSpec((HALO, dm), full),
            ],
            scratch_shapes=[pltpu.VMEM((win, dm), F32)],
        ),
        out_shape=[
            jax.ShapeDtypeStruct((rows, dm), F32),
            jax.ShapeDtypeStruct((own, dm), BF16),
            jax.ShapeDtypeStruct((HALO, dm), BF16),
        ],
        compiler_params=params("arbitrary"),
        cost_estimate=pl.CostEstimate(
            flops=2 * n * cw * dm * (rows + 2 * win), bytes_accessed=2 * n * cw * (3 * dm + rows + 2 * win), transcendentals=0
        ),
    )(info, dq, dk, dv, packed)


MESH = pl.DeviceIdType.MESH


class Place:
    def __init__(self):
        self.me = lax.axis_index("dp")
        self.z = lax.axis_index("mp")
        self.k = lax.rem(self.me, 2)
        self.x = lax.rem(self.me // 2, 2)
        self.y = self.me // 4
        self.me_k = self.me + 1 - 2 * self.k
        self.me_x = self.me + 2 - 4 * self.x
        self.me_y = self.me + 4 - 8 * self.y
        self.me_xy = self.me_x + 4 - 8 * self.y
        self.core = {"dp": self.me_k, "mp": self.z}
        self.by_x = {"dp": self.me_x, "mp": self.z}
        self.by_y = {"dp": self.me_y, "mp": self.z}

    def along(self, d):
        return {"dp": self.me, "mp": lax.rem(self.z + d, 4)}

    def meet(self):
        sem = pltpu.get_barrier_semaphore()
        for dev in (self.core, self.by_x, self.by_y, self.along(1), self.along(2), self.along(3)):
            pl.semaphore_signal(sem, inc=1, device_id=dev, device_id_type=MESH)
        pl.semaphore_wait(sem, 6)


class Wire:
    def __init__(self, send, recv, dev):
        self.send, self.recv, self.dev = send, recv, dev

    def start(self, slot, src, dst, dev):
        copy = pltpu.make_async_remote_copy(
            src_ref=src, dst_ref=dst, send_sem=self.send.at[slot], recv_sem=self.recv.at[slot],
            device_id=dev, device_id_type=MESH,
        )
        copy.start()

    def sent(self, slot, ref):
        pltpu.make_async_remote_copy(
            src_ref=ref, dst_ref=ref, send_sem=self.send.at[slot], recv_sem=self.recv.at[slot],
            device_id=dict(self.dev), device_id_type=MESH,
        ).wait_send()

    def landed(self, slot, ref, dev):
        pltpu.make_async_remote_copy(
            src_ref=ref, dst_ref=ref, send_sem=self.send.at[slot], recv_sem=self.recv.at[slot],
            device_id=dev, device_id_type=MESH,
        ).wait_recv()


def gather_steps(place, wire, base, shard, whole):
    step = shard.shape[0] // 8
    half = step // 2

    def rows(who, at=0, size=step):
        return pl.ds(pl.multiple_of(who * step + at, half), size)

    def slot(d, kind):
        return base + (d - 1) * 9 + kind

    def begin():
        for d in (1, 2, 3):
            wire.start(slot(d, 0), shard.at[rows(place.me)], whole.at[d, rows(place.me)], place.along(4 - d))

    def first(d):
        mine = whole.at[d, rows(place.me)]
        wire.landed(slot(d, 0), mine, place.along(d))
        wire.start(slot(d, 2), mine, mine, place.by_x)
        wire.start(slot(d, 3), mine, mine, place.by_y)
        wire.start(slot(d, 1), mine, mine, place.core)

    def second(d):
        got = whole.at[d, rows(place.me_x)]
        wire.landed(slot(d, 2), got, place.by_x)
        part = whole.at[d, rows(place.me_x, 0, half)]
        wire.start(slot(d, 4), part, part, place.by_y)
        wire.start(slot(d, 6), got, got, place.core)
        got = whole.at[d, rows(place.me_y)]
        wire.landed(slot(d, 3), got, place.by_y)
        part = whole.at[d, rows(place.me_y, half, half)]
        wire.start(slot(d, 5), part, part, place.by_x)
        wire.start(slot(d, 7), got, got, place.core)

    def third(d):
        wire.landed(slot(d, 4), whole.at[d, rows(place.me_xy, 0, half)], place.by_y)
        wire.landed(slot(d, 5), whole.at[d, rows(place.me_xy, half, half)], place.by_x)
        got = whole.at[d, rows(place.me_xy)]
        wire.start(slot(d, 8), got, got, place.core)

    def finish():
        flip = 1 - 2 * place.k
        for d in (1, 2, 3):
            for kind, who in ((1, place.me), (6, place.me_x), (7, place.me_y), (8, place.me_xy)):
                wire.landed(slot(d, kind), whole.at[d, rows(who + flip)], place.core)
            for kind in range(9):
                wire.sent(slot(d, kind), whole.at[d, pl.ds(0, half if kind in (4, 5) else step)])

    return begin, first, second, third, finish


def gather_call(shards):
    count = len(shards)

    def body(*refs):
        ins, outs = refs[:count], refs[count : 2 * count]
        send, recv, local_sem = refs[2 * count :]
        place = Place()
        wire = Wire(send, recv, place.core)
        copies = [pltpu.make_async_copy(ins[g], outs[g].at[0], local_sem.at[g]) for g in range(count)]
        place.meet()
        groups = [gather_steps(place, wire, g * 27, ins[g], outs[g]) for g in range(count)]
        for begin, *_ in groups:
            begin()
        for c in copies:
            c.start()
        order = [(g, d) for g in range(count) for d in (1, 3, 2)]
        for i in range(len(order) + 2):
            for lag in range(3):
                if 0 <= i - lag < len(order):
                    g, d = order[i - lag]
                    groups[g][1 + lag](d)
        for *_, finish in groups:
            finish()
        for c in copies:
            c.wait()

    return pl.pallas_call(
        body,
        in_specs=[pl.BlockSpec(memory_space=pltpu.VMEM)] * count,
        out_specs=[pl.BlockSpec(memory_space=pl.ANY)] * count,
        out_shape=[jax.ShapeDtypeStruct((4,) + s.shape, s.dtype) for s in shards],
        scratch_shapes=[
            pltpu.SemaphoreType.DMA((27 * count,)),
            pltpu.SemaphoreType.DMA((27 * count,)),
            pltpu.SemaphoreType.DMA((count,)),
        ],
        compiler_params=pltpu.CompilerParams(collective_id=0, has_side_effects=True, vmem_limit_bytes=VMEM),
    )(*shards)


class Reduce:
    SLOTS = 32

    @staticmethod
    def scratch(dm, w):
        q = dm // 4
        e = q // 2
        return [
            pltpu.VMEM((4, q, w), BF16),
            pltpu.VMEM((4, q, w), BF16),
            pltpu.VMEM((4, e, w), BF16),
            pltpu.VMEM((4, e, w), BF16),
            pltpu.VMEM((3, q, w), BF16),
            pltpu.SemaphoreType.DMA((Reduce.SLOTS,)),
            pltpu.SemaphoreType.DMA((Reduce.SLOTS,)),
        ]

    def __init__(self, place, grad, landing, scratch):
        self.place, self.g, self.f = place, grad, landing
        self.ra1, self.rb1, self.ra2, self.rb2, self.zb = scratch[:5]
        self.wire = Wire(scratch[5], scratch[6], place.core)
        self.q = grad.shape[0] // 4
        self.e = self.q // 2
        self.w = grad.shape[1] // 4

    def at(self, base, big, small=None):
        start = base * 2 * self.q + big * self.q + (0 if small is None else small * self.e)
        return pl.ds(pl.multiple_of(start, self.e), self.q if small is None else self.e)

    def eighth(self, small):
        return pl.ds(pl.multiple_of(small * self.e, self.e), self.e)

    def cols(self, d):
        return pl.ds(pl.multiple_of(d * self.w, self.w), self.w)

    def one(self, d):
        p, wire = self.place, self.wire
        wire.start(d, self.g.at[self.at(0, 1 - p.x), self.cols(d)], self.ra1.at[d], p.by_x)
        wire.start(4 + d, self.g.at[self.at(1, 1 - p.y), self.cols(d)], self.rb1.at[d], p.by_y)

    def two(self, d):
        p, wire, c = self.place, self.wire, self.cols(d)
        for slot, buf, to, at, mine, dev, nxt in (
            (0, self.ra1, self.ra2, self.at(0, p.x, 1 - p.y), self.eighth(1 - p.y), p.by_x, p.by_y),
            (4, self.rb1, self.rb2, self.at(1, p.y, 1 - p.x), self.eighth(1 - p.x), p.by_y, p.by_x),
        ):
            wire.landed(slot + d, buf.at[d], dev)
            self.g[at, c] = (self.g[at, c].astype(F32) + buf[d, mine, :].astype(F32)).astype(BF16)
            wire.start(8 + slot + d, self.g.at[at, c], to.at[d], nxt)

    def sums(self, d):
        p, wire, c = self.place, self.wire, self.cols(d)
        wire.landed(8 + d, self.ra2.at[d], p.by_y)
        wire.landed(12 + d, self.rb2.at[d], p.by_x)
        up = (
            self.g[self.at(0, p.x, p.y), c].astype(F32)
            + self.ra1[d, self.eighth(p.y), :].astype(F32)
            + self.ra2[d].astype(F32)
        )
        low = (
            self.g[self.at(1, p.y, p.x), c].astype(F32)
            + self.rb1[d, self.eighth(p.x), :].astype(F32)
            + self.rb2[d].astype(F32)
        )
        return up, low

    def three(self, d):
        p, wire, c, e = self.place, self.wire, self.cols(d), self.e
        up, low = self.sums(d)
        for part, (at, val) in enumerate(((self.at(0, p.x, p.y), up), (self.at(1, p.y, p.x), low))):
            self.g[at, c] = val.astype(BF16)
            wire.start(
                16 + 12 * part + d, self.g.at[at, c], self.zb.at[d - 1, part * e : (part + 1) * e], p.along(d)
            )

    def last(self):
        p, wire, e = self.place, self.wire, self.e
        up, low = self.sums(0)
        for s in (1, 2, 3):
            wire.landed(16 + s, self.zb.at[s - 1, 0:e], p.along(4 - s))
            wire.landed(28 + s, self.zb.at[s - 1, e : 2 * e], p.along(4 - s))
            up = up + self.zb[s - 1, 0:e].astype(F32)
            low = low + self.zb[s - 1, e : 2 * e].astype(F32)
        self.f[0, 0:e] = up.astype(BF16)
        self.f[0, e : 2 * e] = low.astype(BF16)
        wire.start(20, self.f.at[0], self.f.at[2], p.by_x)
        wire.start(21, self.f.at[0], self.f.at[4], p.by_y)
        wire.start(22, self.f.at[0], self.f.at[1], p.core)

    def four(self):
        p, wire, e = self.place, self.wire, self.e
        wire.landed(20, self.f.at[2], p.by_x)
        wire.start(23, self.f.at[2, 0:e], self.f.at[6, 0:e], p.by_y)
        wire.start(25, self.f.at[2], self.f.at[3], p.core)
        wire.landed(21, self.f.at[4], p.by_y)
        wire.start(24, self.f.at[4, e : 2 * e], self.f.at[6, e : 2 * e], p.by_x)
        wire.start(26, self.f.at[4], self.f.at[5], p.core)

    def five(self):
        p, wire, e = self.place, self.wire, self.e
        wire.landed(23, self.f.at[6, 0:e], p.by_y)
        wire.landed(24, self.f.at[6, e : 2 * e], p.by_x)
        wire.start(27, self.f.at[6], self.f.at[7], p.core)

    def six(self):
        for slot, to in ((22, 1), (25, 3), (26, 5), (27, 7)):
            self.wire.landed(slot, self.f.at[to], self.place.core)
        e, sent = self.e, self.wire.sent
        for d in range(4):
            sent(d, self.ra1.at[d])
            sent(4 + d, self.rb1.at[d])
            sent(8 + d, self.ra2.at[d])
            sent(12 + d, self.rb2.at[d])
        for d in range(1, 4):
            sent(16 + d, self.zb.at[d - 1, 0:e])
            sent(28 + d, self.zb.at[d - 1, 0:e])
        for slot in (20, 21, 22, 25, 26, 27):
            sent(slot, self.f.at[0])
        for slot in (23, 24):
            sent(slot, self.f.at[0, 0:e])

    def sweep(self):
        return [
            functools.partial(f, d)
            for f, d in (
                (self.two, 1), (self.two, 2), (self.three, 1), (self.two, 3), (self.three, 2), (self.two, 0), (self.three, 3)
            )
        ]

    def tail(self):
        return [self.last, self.four, self.five, self.six]


def back_call(cot, act, n2, gup, ghb, n1w, q, k, v, attn, gattn, lse, qseg, kseg, own, near):
    n, rows, cw = q.shape
    win = k.shape[1]
    dm = cot.shape[0]
    hw = act.shape[1] // 2
    half = n * cw // 2
    w = hw // 4
    pairs = cw // PAIR
    scale = HEAD_DIM**-0.5
    each = len(Reduce.scratch(dm, w))

    def body(
        cot_ref, act_ref, n2_ref, gup_ref, ghb_ref, n1_ref, q_ref, k_ref, v_ref, a_ref, g_ref, l_ref, qs_ref, ks_ref,
        fd, fu, gp_ref, dq, dk, dv,
        cot2, act2, n22, gup2, ghb2, n12, gd, gu, dq_o, dk_o, dv_o, at2, dkt, dvt, xs, xr, ls, *scr,
    ):
        place = Place()
        core = place.k
        big_z = place.z < near
        wire = Wire(xs, xr, place.core)
        whole = (
            (cot_ref, cot2, rows), (n2_ref, n22, rows), (ghb_ref, ghb2, rows), (n1_ref, n12, win)
        )
        mixed = ((act_ref, act2), (gup_ref, gup2))
        local = [pltpu.make_async_copy(src, dst.at[:, 0:wide], ls.at[i]) for i, (src, dst, wide) in enumerate(whole)]
        local += [pltpu.make_async_copy(src.at[:, 0:hw], dst.at[0:rows], ls.at[4 + i]) for i, (src, dst) in enumerate(mixed)]
        for i in (0, 4, 1, 5, 2, 3):
            local[i].start()
        place.meet()

        def give_whole(i):
            src, dst, wide = whole[i]
            wire.start(i, src, dst.at[:, wide : 2 * wide], place.core)

        def give_mixed(i):
            src, dst = mixed[i]
            wire.start(4 + i, src.at[:, hw : 2 * hw], dst.at[rows : 2 * rows], place.core)

        def take(*which):
            for i in which:
                local[i].wait()
                if i < 4:
                    dst, wide = whole[i][1:]
                    wire.landed(i, dst.at[:, wide : 2 * wide], place.core)
                else:
                    wire.landed(i, mixed[i - 4][1].at[rows : 2 * rows], place.core)

        give_whole(0)
        give_mixed(0)
        give_whole(1)
        give_mixed(1)
        give_whole(2)
        give_whole(3)
        for d in range(n):
            to = slice(d * PAIR, (d + 1) * PAIR)
            theirs = pl.ds(pl.multiple_of((1 - core) * PAIR, PAIR), PAIR)
            mine = pl.ds(pl.multiple_of(core * PAIR, PAIR), PAIR)
            wire.start(6 + d, a_ref.at[d, :, theirs], at2.at[rows : 2 * rows, to], place.core)
            at2[0:rows, to] = a_ref[d, :, mine]

        down = Reduce(place, gd, fd, scr[:each])
        up = Reduce(place, gu, fu, scr[each : 2 * each])

        def make(red, grad, left, right):
            def step(i, carry):
                d = lax.rem(i + 1, 4)
                c = pl.ds(pl.multiple_of(d * w, w), w)
                grad[:, c] = dot_nn(left[...], right[:, c]).astype(BF16)
                red.one(d)
                return carry

            lax.fori_loop(0, 4, step, 0)

        take(0, 4)
        make(down, gd, cot2, act2)
        take(1, 5)
        make(up, gu, n22, gup2)

        def work(big, d, p):
            at = pl.ds(pl.multiple_of(p * PAIR, PAIR), PAIR)
            to = pl.ds(pl.multiple_of(d * PAIR, PAIR), PAIR)
            rel = lax.rem(p + core, 2)
            if not big:
                dkt[...] = jnp.zeros_like(dkt)
                dvt[...] = jnp.zeros_like(dvt)
            for i, (qs, qn, ks, kn) in enumerate(blocks_of(rows, own, win, big)):
                mask = qs_ref[qs : qs + qn, :] == ks_ref[:, ks : ks + kn]
                qq, kk, vv = q_ref[d, qs : qs + qn, at], k_ref[d, ks : ks + kn, at], v_ref[d, ks : ks + kn, at]
                gg = g_ref[d, qs : qs + qn, at]
                prod = gg.astype(F32) * a_ref[d, qs : qs + qn, at].astype(F32)
                dqs = []
                for h in range(2):
                    lanes = slice(h * HEAD_DIM, (h + 1) * HEAD_DIM)
                    qh, kh, gh = qq[:, lanes] * BF16(scale), kk[:, lanes], gg[:, lanes]
                    s = jnp.where(mask, dot_nt(qh, kh) - l_ref[d * pairs + p, qs : qs + qn, h : h + 1], NEG)
                    pr = jnp.exp(s)
                    dp = dot_nt(gh, vv[:, lanes])
                    delta = jnp.sum(prod[:, lanes], axis=1, keepdims=True)
                    ds = (pr * (dp - delta)).astype(BF16)
                    dqs.append(dot_nn(ds, kh) * scale)
                    gk = dot_tn(qh, ds)
                    gv = dot_tn(gh, pr.astype(BF16))
                    if big and i == 0:
                        dkt[lanes, :] = gk
                        dvt[lanes, :] = gv
                    else:
                        dkt[lanes, ks : ks + kn] += gk
                        dvt[lanes, ks : ks + kn] += gv
                dq[rel, qs : qs + qn, to] = jnp.concatenate(dqs, axis=1).astype(BF16)
            dk[rel, :, to] = dkt[...].T.astype(BF16)
            dv[rel, :, to] = dvt[...].T.astype(BF16)

        todo = down.sweep() + up.sweep()
        turns = [todo[2 * i : 2 * i + 2] for i in range(n * pairs)]
        turns[-1] = todo[2 * (n * pairs - 1) :]

        def head_pair(i, carry):
            d, p = i // pairs, lax.rem(i, pairs)

            @pl.when(big_z)
            def _():
                work(True, d, p)

            @pl.when(jnp.logical_not(big_z))
            def _():
                work(False, d, p)

            for t, steps in enumerate(turns):
                if steps:

                    @pl.when(i == t)
                    def _():
                        for f in steps:
                            f()

            return carry

        lax.fori_loop(0, n * pairs, head_pair, 0)
        halves = ((dq, dq_o), (dk, dk_o), (dv, dv_o))
        for i, (src, dst) in enumerate(halves):
            wire.start(10 + i, src.at[1], dst, place.core)
        down.last()
        take(2, 3)
        for d in range(n):
            wire.landed(6 + d, at2.at[rows : 2 * rows, d * PAIR : (d + 1) * PAIR], place.core)

        def put(m, val):
            for d in range(n):
                at = d * w + m * PAIR
                act2[:, at : at + PAIR] = val[:, d * PAIR : (d + 1) * PAIR].astype(BF16)

        put(3, dot_nn(ghb2[...], at2[...]))
        up.last()
        down.four()
        wire.landed(10, dq_o, place.core)
        put(0, dot_nn(n12[:, own : own + rows], dq[0]) + dot_nn(n12[:, win + own : win + own + rows], dq_o[...]))
        down.five()
        up.four()
        wire.landed(11, dk_o, place.core)
        put(1, dot_nn(n12[:, 0:win], dk[0]) + dot_nn(n12[:, win : 2 * win], dk_o[...]))
        up.five()
        wire.landed(12, dv_o, place.core)
        put(2, dot_nn(n12[:, 0:win], dv[0]) + dot_nn(n12[:, win : 2 * win], dv_o[...]))
        out = pltpu.make_async_copy(act2, gp_ref, ls.at[6])
        out.start()
        down.six()
        up.six()
        for i in range(4):
            wire.sent(i, whole[i][0])
        for i in range(2):
            wire.sent(4 + i, act2.at[0:rows])
        for d in range(n):
            wire.sent(6 + d, at2.at[0:rows, 0:PAIR])
        for i in range(3):
            wire.sent(10 + i, halves[i][1])
        out.wait()

    hbm = pl.BlockSpec(memory_space=pl.ANY)
    vmem = pl.BlockSpec(memory_space=pltpu.VMEM)
    shaped = lambda *shape: jax.ShapeDtypeStruct(shape, BF16)
    buf = lambda *shape: pltpu.VMEM(shape, BF16)
    return pl.pallas_call(
        body,
        in_specs=[hbm] * 6 + [vmem] * 8,
        out_specs=[vmem, vmem, hbm, vmem, vmem, vmem],
        out_shape=[
            shaped(8, dm // 4, w), shaped(8, dm // 4, w), shaped(dm, hw), shaped(2, rows, half), shaped(2, win, half), shaped(2, win, half)
        ],
        scratch_shapes=[
            buf(dm, 2 * rows), buf(2 * rows, hw), buf(dm, 2 * rows), buf(2 * rows, hw), buf(dm, 2 * rows), buf(dm, 2 * win),
            buf(dm, hw), buf(dm, hw), buf(rows, half), buf(win, half), buf(win, half), buf(2 * rows, half),
            pltpu.VMEM((PAIR, win), F32), pltpu.VMEM((PAIR, win), F32),
            pltpu.SemaphoreType.DMA((13,)), pltpu.SemaphoreType.DMA((13,)), pltpu.SemaphoreType.DMA((7,)),
        ]
        + Reduce.scratch(dm, w) * 2,
        compiler_params=pltpu.CompilerParams(collective_id=1, has_side_effects=True, vmem_limit_bytes=VMEM_ALL),
    )(cot, act, n2, gup, ghb, n1w, q, k, v, attn, gattn, lse, qseg, kseg)


def finish_call(gp, dq, dk, dv, packed, tokens, gain, vec, own):
    n, dm, four = packed.shape
    cw = four // 4
    rows = tokens.shape[0]
    win = dk.shape[1]
    cols = gp.shape[1]
    w = cols // 4
    length = vec.shape[1]
    each = len(Reduce.scratch(dm, w))
    strip = 128

    def body(
        gp_ref, dq_ref, dk_ref, dv_ref, w_ref, x_ref, gain_ref, vec_ref,
        fp, gi_ref, sum_ref,
        g, acc, far_out, next_out, far_in, prev_in, next_in, va, vr, vz, xs, xr, ls, *scr,
    ):
        place = Place()
        core, z = place.k, place.z
        load = pltpu.make_async_copy(gp_ref, g, ls)
        load.start()
        place.meet()
        wire = Wire(xs, xr, place.core)
        red = Reduce(place, g, fp, scr)
        load.wait()
        for d in (1, 2, 3, 0):
            red.one(d)

        def dots(d, carry):
            def weight(which, j):
                at = which * cw + lax.rem(j + core, 2) * PAIR
                return w_ref[d, :, pl.ds(pl.multiple_of(at, PAIR), PAIR)]

            to = pl.ds(pl.multiple_of(d * PAIR, PAIR), PAIR)
            left = jnp.concatenate([r[j, :, to] for r in (dk_ref, dv_ref) for j in range(2)], axis=1)
            right = jnp.concatenate([weight(m, j) for m in (1, 2) for j in range(2)], axis=1)
            part = dot_nt(left, right)
            left = jnp.concatenate([dq_ref[j, :, to] for j in range(2)], axis=1)
            right = jnp.concatenate([weight(0, j) for j in range(2)], axis=1)
            mine = dot_nt(left, right)

            @pl.when(d == 0)
            def _():
                acc[...] = part

            @pl.when(d > 0)
            def _():
                acc[...] += part

            acc[own : own + rows, :] += mine
            for t, f in ((2, red.sweep()[0]), (3, red.sweep()[1])):

                @pl.when(d == t)
                def _():
                    f()

            return carry

        lax.fori_loop(0, n, dots, 0)

        long, gives_prev, gives_next = z < 2, z >= 2, jnp.logical_and(z >= 1, z < 3)
        swap = {"dp": place.me, "mp": lax.rem(z + 1, 2)}
        left_dev = {"dp": place.me, "mp": lax.rem(z + 3, 4)}
        right_dev = {"dp": place.me, "mp": lax.rem(z + 1, 4)}
        far_out[...] = acc[0:own, :].astype(BF16)
        next_out[...] = acc[own + rows : own + rows + HALO, :].astype(BF16)

        @pl.when(long)
        def _():
            wire.start(0, far_out, far_in, swap)

        @pl.when(gives_prev)
        def _():
            wire.start(1, far_out.at[own - HALO : own], prev_in, left_dev)

        @pl.when(gives_next)
        def _():
            wire.start(2, next_out, next_in, right_dev)

        for f in red.sweep()[2:]:
            f()

        @pl.when(long)
        def _():
            wire.landed(0, far_in, swap)
            acc[own : own + rows, :] += far_in[...].astype(F32)

        @pl.when(gives_next)
        def _():
            wire.landed(1, prev_in, right_dev)
            acc[own + rows - HALO : own + rows, :] += prev_in[...].astype(F32)

        @pl.when(gives_prev)
        def _():
            wire.landed(2, next_in, left_dev)
            acc[own : own + HALO, :] += next_in[...].astype(F32)

        va[0] = vec_ref[...]
        va[0, :, 0 : 2 * dm] = jnp.zeros((1, 2 * dm), F32)
        gains = gain_ref[...].astype(F32)

        def norm(i, carry):
            at = pl.ds(pl.multiple_of(i * strip, strip), strip)
            hat, inv = norm_rows(x_ref[at, :].astype(F32))
            back = acc[pl.ds(pl.multiple_of(own + i * strip, strip), strip), :]
            gg = back * gains
            first = jnp.mean(gg, axis=1, keepdims=True)
            second = jnp.mean(gg * hat, axis=1, keepdims=True)
            gi_ref[at, :] = inv * (gg - first - hat * second)
            va[0, :, 0:dm] += jnp.sum(back * hat, axis=0, keepdims=True)
            va[0, :, dm : 2 * dm] += jnp.sum(back, axis=0, keepdims=True)
            return carry

        lax.fori_loop(0, rows // strip, norm, 0)

        hops = (place.core, place.by_x, place.by_y)
        between = (red.last, red.four, red.five)
        for i, dev in enumerate(hops):
            wire.start(3 + i, va.at[i], vr.at[i], dev)
            if i == 0:
                between[0]()
            wire.landed(3 + i, vr.at[i], dev)
            if i < 2:
                va[i + 1] = va[i] + vr[i]
            else:
                vz[0] = va[i] + vr[i]
        for d in (1, 2, 3):
            wire.start(5 + d, vz.at[0], vz.at[d], place.along(d))
        between[1]()
        between[2]()
        for d in (1, 2, 3):
            wire.landed(5 + d, vz.at[d], place.along(4 - d))
        terms = [vz[lax.rem(z - a + 4, 4)] for a in range(4)]
        sum_ref[...] = (terms[0] + terms[1]) + (terms[2] + terms[3])
        red.six()

        @pl.when(long)
        def _():
            wire.sent(0, far_out)

        @pl.when(gives_prev)
        def _():
            wire.sent(1, prev_in)

        @pl.when(gives_next)
        def _():
            wire.sent(2, next_out)

        for i in range(3):
            wire.sent(3 + i, va.at[i])
        for d in (1, 2, 3):
            wire.sent(5 + d, vz.at[0])

    hbm = pl.BlockSpec(memory_space=pl.ANY)
    vmem = pl.BlockSpec(memory_space=pltpu.VMEM)
    buf = lambda *shape: pltpu.VMEM(shape, BF16)
    return pl.pallas_call(
        body,
        in_specs=[hbm] + [vmem] * 7,
        out_specs=[vmem] * 3,
        out_shape=[
            jax.ShapeDtypeStruct((8, dm // 4, w), BF16),
            jax.ShapeDtypeStruct((rows, dm), F32),
            jax.ShapeDtypeStruct((1, length), F32),
        ],
        scratch_shapes=[
            buf(dm, cols), pltpu.VMEM((win, dm), F32),
            buf(own, dm), buf(HALO, dm), buf(own, dm), buf(HALO, dm), buf(HALO, dm),
            pltpu.VMEM((3, 1, length), F32), pltpu.VMEM((3, 1, length), F32), pltpu.VMEM((4, 1, length), F32),
            pltpu.SemaphoreType.DMA((9,)), pltpu.SemaphoreType.DMA((9,)), pltpu.SemaphoreType.DMA(()),
        ]
        + Reduce.scratch(dm, w),
        compiler_params=pltpu.CompilerParams(collective_id=2, has_side_effects=True, vmem_limit_bytes=VMEM),
    )(gp, dq, dk, dv, packed, tokens, gain[None], vec)


def place_grads(coords, done, mode):
    _, q, w = done.shape
    e = q // 2
    dm = 4 * q
    lanes = w // 4

    def body(c_ref, f_ref, *outs):
        for off in range(8):
            y = lax.bitwise_xor(c_ref[0], off >> 2)
            x = lax.bitwise_xor(c_ref[1], (off >> 1) & 1)
            k = lax.bitwise_xor(c_ref[2], off & 1)
            for part in range(2):
                val = f_ref[off, part * e : (part + 1) * e, :].astype(F32)
                block = x * 2 + y if part == 0 else 4 + y * 2 + x
                rows = pl.ds(pl.multiple_of(block * e, e), e)
                if mode == "up":
                    outs[0][rows, pl.ds(pl.multiple_of(k * w, w), w)] = val
                elif mode == "down":
                    outs[0][pl.ds(pl.multiple_of(k * w, w), w), rows] = val.T
                else:
                    at = pl.ds(pl.multiple_of(k * lanes, lanes), lanes)
                    for m in range(3):
                        outs[m][rows, at] = val[:, m * lanes : (m + 1) * lanes]
                    outs[3][at, rows] = val[:, 3 * lanes :].T

    if mode == "up":
        shapes = [(dm, 2 * w)]
    elif mode == "down":
        shapes = [(2 * w, dm)]
    else:
        shapes = [(dm, w // 2)] * 3 + [(w // 2, dm)]
    return pl.pallas_call(
        body,
        in_specs=[pl.BlockSpec(memory_space=pltpu.SMEM), pl.BlockSpec(memory_space=pltpu.VMEM)],
        out_specs=[pl.BlockSpec(memory_space=pltpu.VMEM)] * len(shapes),
        out_shape=[jax.ShapeDtypeStruct(s, F32) for s in shapes],
        compiler_params=pltpu.CompilerParams(vmem_limit_bytes=VMEM),
        cost_estimate=pl.CostEstimate(flops=0, bytes_accessed=12 * dm * w, transcendentals=0),
    )(coords, done)


def relative(stack, z):
    return jnp.roll(stack, -z, axis=0)


def core_first(v, core, axis):
    return jnp.where(core == 0, v, jnp.flip(v, axis))


def gather_any(shard, z):
    return relative(lax.all_gather(shard, "mp", axis=0, tiled=False), z)


def reduce_any(half, z, core):
    zero = jnp.zeros_like(half)
    v = jnp.stack([jnp.where(core == 0, half, zero), jnp.where(core == 1, half, zero)], axis=2)
    v = jnp.roll(jnp.moveaxis(v, 1, 0), z, axis=0)
    v = lax.psum_scatter(v, "mp", scatter_dimension=0, tiled=True)[0]
    return lax.psum(v, "dp").astype(F32).reshape(half.shape[0], -1)


def local(
    tokens,
    segments,
    ln1_gain,
    ln1_bias,
    w_query,
    b_query,
    w_key,
    w_value,
    b_value,
    w_out,
    b_out,
    ln2_gain,
    ln2_bias,
    w_up,
    b_up,
    w_down,
    b_down,
    cotangent,
):
    rows, dm = tokens.shape
    cw = w_query.shape[1]
    ffw = w_up.shape[1]
    mp = lax.axis_size("mp")
    dp = lax.axis_size("dp")
    fast = mp == 4 and dp == 8 and rows % 256 == 0 and cw == 2 * PAIR and rows < LONGEST <= 2 * rows
    z = lax.axis_index("mp")
    me = lax.axis_index("dp")
    core = lax.rem(me, 2)
    x = lax.rem(me // 2, 2)
    y = me // 4
    f32 = lambda v: v.astype(F32)

    near = -(-LONGEST // rows)
    own = (near - 1) * rows
    win = own + rows + 2 * HALO
    halo = [
        lax.ppermute(tokens, "mp", [((i + j) % near, i) for i in range(near)]) for j in range(1, near)
    ]
    before = lax.ppermute(tokens[-HALO:], "mp", [(i - 1, i) for i in range(near, mp)])
    behind = lax.ppermute(tokens[:HALO], "mp", [(i + 1, i) for i in range(near - 1, mp - 1)])
    small_vec = jnp.concatenate([b_query, b_value, b_up])
    if fast:
        vecs = [small_vec] + [
            lax.ppermute(small_vec, "mp", [((i + d) % mp, i) for i in range(mp)]) for d in range(1, mp)
        ]
        vecs = jnp.stack(vecs)
    else:
        vecs = relative(lax.all_gather(small_vec, "mp", axis=0, tiled=False), z)
    bq_all, bv_all = vecs[:, :cw], vecs[:, cw : 2 * cw]
    bu_all = vecs[:, 2 * cw :].reshape(mp, 2, ffw // 2).transpose(1, 0, 2)
    bu_all = core_first(bu_all, core, 0).reshape(mp * ffw)

    is_near = z < near
    seg_parts = [
        jnp.where(is_near, lax.dynamic_slice_in_dim(segments, lax.rem(z + j, near) * rows, rows), -1)
        for j in range(1, near)
    ]
    seg_own = lax.dynamic_slice_in_dim(segments, z * rows, rows)
    seg_prev = lax.dynamic_slice_in_dim(segments, jnp.maximum(z * rows - HALO, 0), HALO)
    seg_next = lax.dynamic_slice_in_dim(segments, jnp.minimum((z + 1) * rows, segments.shape[0] - HALO), HALO)
    seg_far = jnp.concatenate(seg_parts)
    seg_far = jnp.concatenate([seg_far[:-HALO], jnp.where(is_near, seg_far[-HALO:], seg_prev)])
    has_next = jnp.logical_and(z >= near - 1, z < mp - 1)
    seg_win = jnp.concatenate(
        [seg_far, seg_own, jnp.where(has_next, seg_next, -1), jnp.full((HALO,), -1, segments.dtype)]
    )
    kseg, qseg = seg_win[None, :], seg_own[:, None]
    info = jnp.stack([is_near.astype(jnp.int32), core]).astype(jnp.int32)

    pack = jnp.concatenate([w_query, w_key, w_value, w_out.T], axis=1)
    if fast:
        packed, up_all, down_all = gather_call([pack, w_up, w_down])
    else:
        packed, up_all, down_all = (gather_any(w, z) for w in (pack, w_up, w_down))

    far = jnp.concatenate(halo, axis=0)
    far = jnp.concatenate([far[:-HALO], far[-HALO:] + before], axis=0)
    tok_win = jnp.concatenate([far, tokens, behind, jnp.zeros((HALO, dm), tokens.dtype)], axis=0)
    hat_win, inv_win = norm_rows(f32(tok_win))
    n1w = (hat_win * f32(ln1_gain) + f32(ln1_bias)).astype(BF16)
    q, k, v = qkv_call(n1w, packed, bq_all, bv_all, own, rows, cw)
    attn, lse = attn_fwd_call(info, q, k, v, qseg, kseg, own)
    hidden, n2 = out_call(attn, packed, tokens, b_out, ln2_gain, ln2_bias)
    output, g_n2, active, g_upper, g_b_up = ffn_call(
        info[1:], n2, hidden, cotangent, up_all, down_all, bu_all, b_down, 2
    )

    gout = f32(cotangent)
    hat2, inv2 = norm_rows(hidden)

    def norm_back(g, hat, inv, gain):
        gg = g * gain
        first = jnp.mean(gg, axis=1, keepdims=True)
        second = jnp.mean(gg * hat, axis=1, keepdims=True)
        return inv * (gg - first - hat * second), jnp.sum(g * hat, axis=0), jnp.sum(g, axis=0)

    g_hidden, g_gain2, g_bias2 = norm_back(g_n2, hat2, inv2, f32(ln2_gain))
    g_hidden = g_hidden + gout
    ghb = g_hidden.astype(BF16)

    g_attn = jnp.stack([dot_nn(ghb, packed[d, :, 3 * cw :]).astype(BF16) for d in range(mp)])
    if fast:
        done_d, done_u, gp, dq, dk, dv = back_call(
            cotangent.T, active, n2.T, g_upper, ghb.T, n1w.T, q, k, v, attn, g_attn, lse, qseg, kseg, own, near
        )
    else:
        dq, dk, dv = attn_bwd_call(info, q, k, v, attn, g_attn, lse, qseg, kseg, own)
    halves = dq.shape[0]
    def shards(v, width):
        if v.shape[0] == 2:
            v = core_first(v.reshape(2, mp, width // 2), core, 0).transpose(1, 0, 2)
        return jnp.roll(v.reshape(mp, width), z, axis=0).reshape(mp * width)

    gbq = shards(jnp.sum(f32(dq), axis=1), cw)
    gbv = shards(jnp.sum(f32(dv), axis=1), cw)
    gbu = core_first(g_b_up.reshape(2, mp, ffw // 2), core, 0).transpose(1, 0, 2)
    gbu = jnp.roll(gbu.reshape(mp, ffw), z, axis=0).reshape(-1)
    sums = [jnp.sum(g_hidden, axis=0), g_gain2, g_bias2, jnp.sum(gout, axis=0), gbq, gbv, gbu]
    n1 = n1w[own : own + rows]
    if fast:
        vec = jnp.concatenate([jnp.zeros((2 * dm,), F32)] + sums)[None]
        done_p, g_in, vec = finish_call(gp, dq, dk, dv, packed, tokens, ln1_gain, vec, own)
        vec = vec[0]
        g_tokens = g_in + g_hidden
        coords = jnp.stack([y, x, core]).astype(jnp.int32)
        (g_w_down,) = place_grads(coords, done_d, "down")
        (g_w_up,) = place_grads(coords, done_u, "up")
        g_w_query, g_w_key, g_w_value, g_w_out = place_grads(coords, done_p, "pack")
    else:
        g_own, g_far, g_next = norm1_back_call(dq, dk, dv, packed, info, own)
        back = g_own
        for j in range(1, near):
            part = g_far[(j - 1) * rows : j * rows]
            back = back + f32(lax.ppermute(part, "mp", [(i, (i + j) % near) for i in range(near)]))
        to_prev = f32(lax.ppermute(g_far[-HALO:], "mp", [(i, i - 1) for i in range(near, mp)]))
        to_next = f32(lax.ppermute(g_next, "mp", [(i, i + 1) for i in range(near - 1, mp - 1)]))
        back = jnp.concatenate([back[:HALO] + to_next, back[HALO:-HALO], back[-HALO:] + to_prev], axis=0)
        hat1 = hat_win[own : own + rows]
        inv1 = inv_win[own : own + rows]
        g_in, g_gain1, g_bias1 = norm_back(back, hat1, inv1, f32(ln1_gain))
        g_tokens = g_in + g_hidden

        other = lambda v: lax.ppermute(v, "dp", [(i, i - i % 2 + (i + 1) % 2) for i in range(dp)])
        hw = mp * ffw // 2

        def pair_grad(left, right):
            return (dot_tn(left, right[:, :hw]) + dot_tn(other(left), other(right[:, hw:]))).astype(BF16)

        gd = pair_grad(cotangent, active)
        gu = pair_grad(n2, g_upper)
        g_w_up = reduce_any(gu.reshape(dm, mp, ffw // 2), z, core)
        g_w_down = reduce_any(gd.reshape(dm, mp, ffw // 2), z, core).T

        def whole_grad(left, right, name=None):
            v = dot_tn(left, right).astype(BF16).reshape(dm, mp, cw)
            v = jnp.roll(jnp.moveaxis(v, 1, 0), z, axis=0)
            v = lax.psum_scatter(v, "mp", scatter_dimension=0, tiled=True)[0]
            return lax.psum(v, "dp").astype(F32)

        def whole(v):
            if halves == 1:
                return v[0]
            v = v.reshape(2, v.shape[1], mp, cw // 2).transpose(1, 2, 0, 3)
            return core_first(v, core, 2).reshape(v.shape[0], mp * cw)

        g_w_query = whole_grad(n1, whole(dq))
        g_w_key = whole_grad(n1w, whole(dk))
        g_w_value = whole_grad(n1w, whole(dv))
        g_w_out = whole_grad(ghb, attn.transpose(1, 0, 2).reshape(rows, mp * cw)).T

        vec = lax.psum(jnp.concatenate([g_gain1, g_bias1] + sums), ("dp", "mp"))
    g_gain1, g_bias1, g_b_out, g_gain2, g_bias2, g_b_down = (vec[i * dm : (i + 1) * dm] for i in range(6))
    at = 6 * dm
    g_b_query = lax.dynamic_slice_in_dim(vec, at + z * cw, cw)
    g_b_value = lax.dynamic_slice_in_dim(vec, at + mp * cw + z * cw, cw)
    g_b_up = lax.dynamic_slice_in_dim(vec, at + 2 * mp * cw + z * ffw, ffw)
    return (
        output,
        g_tokens,
        g_gain1,
        g_bias1,
        g_w_query,
        g_b_query,
        g_w_key,
        g_w_value,
        g_b_value,
        g_w_out,
        g_b_out,
        g_gain2,
        g_bias2,
        g_w_up,
        g_b_up,
        g_w_down,
        g_b_down,
    )


def solution(mesh):
    in_specs = (
        P(("dp", "mp"), None),
        P("dp"),
        P(),
        P(),
        P(None, "mp"),
        P("mp"),
        P(None, "mp"),
        P(None, "mp"),
        P("mp"),
        P("mp", None),
        P(),
        P(),
        P(),
        P(None, "mp"),
        P("mp"),
        P("mp", None),
        P(),
        P(("dp", "mp"), None),
    )
    out_specs = (
        P(("dp", "mp"), None),
        P(("dp", "mp"), None),
        P(),
        P(),
        P(None, "mp"),
        P("mp"),
        P(None, "mp"),
        P(None, "mp"),
        P("mp"),
        P("mp", None),
        P(),
        P(),
        P(),
        P(None, "mp"),
        P("mp"),
        P("mp", None),
        P(),
    )
    return jax.shard_map(local, mesh=mesh, in_specs=in_specs, out_specs=out_specs, check_vma=False)
```

```python
import functools

import jax
import jax.numpy as jnp
from jax import lax
from jax.experimental import pallas as pl
from jax.experimental.pallas import tpu as pltpu
from jax.sharding import PartitionSpec as P

HEAD_DIM = 64
LONGEST = 900
HALO = 64
PAIR = 128
EPS = 1e-06
NEG = -1e30
VMEM = 60 * 1024 * 1024
VMEM_ALL = 67043328
F32 = jnp.float32
BF16 = jnp.bfloat16


def dot_nn(a, b):
    return lax.dot_general(a, b, (((1,), (0,)), ((), ())), preferred_element_type=F32)


def dot_nt(a, b):
    return lax.dot_general(a, b, (((1,), (1,)), ((), ())), preferred_element_type=F32)


def dot_tn(a, b):
    return lax.dot_general(a, b, (((0,), (0,)), ((), ())), preferred_element_type=F32)


def barrier(*xs):
    return lax.optimization_barrier(xs)


def params(*sem, **kw):
    return pltpu.CompilerParams(dimension_semantics=sem, vmem_limit_bytes=VMEM, **kw)


def norm_rows(x):
    mean = jnp.mean(x, axis=1, keepdims=True)
    cent = x - mean
    inv = lax.rsqrt(jnp.mean(cent * cent, axis=1, keepdims=True) + EPS)
    return cent * inv, inv


def qkv_call(n1w, packed, b_q, b_v, own, rows, cw):
    n, dm, _ = packed.shape
    win = n1w.shape[0]

    def body(x_ref, w_ref, bq_ref, bv_ref, q_ref, k_ref, v_ref):
        x = x_ref[...]
        q_ref[0] = (dot_nn(x[own : own + rows], w_ref[0, :, 0:cw]) + bq_ref[0].astype(F32)).astype(BF16)
        k_ref[0] = dot_nn(x, w_ref[0, :, cw : 2 * cw]).astype(BF16)
        v_ref[0] = (dot_nn(x, w_ref[0, :, 2 * cw : 3 * cw]) + bv_ref[0].astype(F32)).astype(BF16)

    return pl.pallas_call(
        body,
        grid=(n,),
        in_specs=[
            pl.BlockSpec((win, dm), lambda d: (0, 0)),
            pl.BlockSpec((1, dm, 4 * cw), lambda d: (d, 0, 0)),
            pl.BlockSpec((1, 1, cw), lambda d: (d, 0, 0)),
            pl.BlockSpec((1, 1, cw), lambda d: (d, 0, 0)),
        ],
        out_specs=[
            pl.BlockSpec((1, rows, cw), lambda d: (d, 0, 0)),
            pl.BlockSpec((1, win, cw), lambda d: (d, 0, 0)),
            pl.BlockSpec((1, win, cw), lambda d: (d, 0, 0)),
        ],
        out_shape=[
            jax.ShapeDtypeStruct((n, rows, cw), BF16),
            jax.ShapeDtypeStruct((n, win, cw), BF16),
            jax.ShapeDtypeStruct((n, win, cw), BF16),
        ],
        compiler_params=params("arbitrary"),
        cost_estimate=pl.CostEstimate(
            flops=2 * n * dm * cw * (rows + 2 * win), bytes_accessed=2 * (n * dm * 4 * cw + win * dm), transcendentals=0
        ),
    )(n1w, packed, b_q[:, None, :], b_v[:, None, :])


def blocks_of(rows, own, win, big):
    if big:
        step = min(256, rows)
        return [(s, step, 0, win) for s in range(0, rows, step)]
    return [(s, 128, own + s - 128, 384) for s in range(0, rows, 128)]


def attn_fwd_call(is_big, q, k, v, qseg, kseg, own):
    n, rows, cw = q.shape
    win = k.shape[1]
    pairs = cw // PAIR

    def work(big, q_ref, k_ref, v_ref, qs_ref, ks_ref, o_ref, l_ref):
        for qs, qn, ks, kn in blocks_of(rows, own, win, big):
            mask = qs_ref[qs : qs + qn, :] == ks_ref[:, ks : ks + kn]
            for h in range(2):
                lanes = slice(h * HEAD_DIM, (h + 1) * HEAD_DIM)
                qh = q_ref[0, qs : qs + qn, lanes] * BF16(HEAD_DIM**-0.5)
                s = jnp.where(mask, dot_nt(qh, k_ref[0, ks : ks + kn, lanes]), NEG)
                top = jnp.max(s, axis=1, keepdims=True)
                p = jnp.exp(s - top)
                total = jnp.sum(p, axis=1, keepdims=True)
                o = dot_nn(p.astype(BF16), v_ref[0, ks : ks + kn, lanes])
                o_ref[0, qs : qs + qn, lanes] = (o / total).astype(BF16)
                l_ref[0, qs : qs + qn, h : h + 1] = top + jnp.log(total)

    def body(big_ref, *refs):
        @pl.when(big_ref[0] == 1)
        def _():
            work(True, *refs)

        @pl.when(big_ref[0] == 0)
        def _():
            work(False, *refs)

    return pl.pallas_call(
        body,
        grid_spec=pltpu.PrefetchScalarGridSpec(
            num_scalar_prefetch=1,
            grid=(n, pairs),
            in_specs=[
                pl.BlockSpec((1, rows, PAIR), lambda d, p, *_: (d, 0, p)),
                pl.BlockSpec((1, win, PAIR), lambda d, p, *_: (d, 0, p)),
                pl.BlockSpec((1, win, PAIR), lambda d, p, *_: (d, 0, p)),
                pl.BlockSpec((rows, 1), lambda d, p, *_: (0, 0)),
                pl.BlockSpec((1, win), lambda d, p, *_: (0, 0)),
            ],
            out_specs=[
                pl.BlockSpec((1, rows, PAIR), lambda d, p, *_: (d, 0, p)),
                pl.BlockSpec((1, rows, 2), lambda d, p, *_: (d * pairs + p, 0, 0)),
            ],
        ),
        out_shape=[
            jax.ShapeDtypeStruct((n, rows, cw), BF16),
            jax.ShapeDtypeStruct((n * pairs, rows, 2), F32),
        ],
        compiler_params=params("arbitrary", "arbitrary"),
        cost_estimate=pl.CostEstimate(
            flops=16 * n * rows * win * cw, bytes_accessed=2 * n * cw * (2 * rows + 2 * win), transcendentals=n * rows * win * 4
        ),
    )(is_big, q, k, v, qseg, kseg)


def attn_bwd_call(info, q, k, v, attn, gattn, lse, qseg, kseg, own):
    n, rows, cw = q.shape
    win = k.shape[1]
    pairs = cw // PAIR
    scale = HEAD_DIM**-0.5

    def work(big, q_ref, k_ref, v_ref, a_ref, g_ref, l_ref, qs_ref, ks_ref, dq_ref, dk_ref, dv_ref, dkt, dvt):
        if not big:
            dkt[...] = jnp.zeros_like(dkt)
            dvt[...] = jnp.zeros_like(dvt)
        for i, (qs, qn, ks, kn) in enumerate(blocks_of(rows, own, win, big)):
            mask = qs_ref[qs : qs + qn, :] == ks_ref[:, ks : ks + kn]
            for h in range(2):
                lanes = slice(h * HEAD_DIM, (h + 1) * HEAD_DIM)
                qh = q_ref[0, qs : qs + qn, lanes] * BF16(scale)
                kh = k_ref[0, ks : ks + kn, lanes]
                gh = g_ref[0, qs : qs + qn, lanes]
                s = jnp.where(mask, dot_nt(qh, kh) - l_ref[0, qs : qs + qn, h : h + 1], NEG)
                p = jnp.exp(s)
                dp = dot_nt(gh, v_ref[0, ks : ks + kn, lanes])
                delta = jnp.sum(
                    gh.astype(F32) * a_ref[0, qs : qs + qn, lanes].astype(F32), axis=1, keepdims=True
                )
                ds = (p * (dp - delta)).astype(BF16)
                dq_ref[0, qs : qs + qn, lanes] = (dot_nn(ds, kh) * scale).astype(BF16)
                dk = dot_tn(qh, ds)
                dv = dot_tn(gh, p.astype(BF16))
                if big and i == 0:
                    dkt[lanes, :] = dk
                    dvt[lanes, :] = dv
                else:
                    dkt[lanes, ks : ks + kn] += dk
                    dvt[lanes, ks : ks + kn] += dv
        dk_ref[0] = dkt[...].T.astype(BF16)
        dv_ref[0] = dvt[...].T.astype(BF16)

    def body(info_ref, *refs):
        @pl.when(info_ref[0] == 1)
        def _():
            work(True, *refs)

        @pl.when(info_ref[0] == 0)
        def _():
            work(False, *refs)

    if pairs > 1:

        def put(d, p, info):
            rel = lax.bitwise_xor(p // (pairs // 2), info[1])
            return (rel, 0, d * (pairs // 2) + p % (pairs // 2))

        half_shape = (2, rows, n * cw // 2)
        half_win = (2, win, n * cw // 2)
    else:

        def put(d, p, info):
            return (0, 0, d)

        half_shape = (1, rows, n * cw)
        half_win = (1, win, n * cw)
    return pl.pallas_call(
        body,
        grid_spec=pltpu.PrefetchScalarGridSpec(
            num_scalar_prefetch=1,
            grid=(n, pairs),
            in_specs=[
                pl.BlockSpec((1, rows, PAIR), lambda d, p, *_: (d, 0, p)),
                pl.BlockSpec((1, win, PAIR), lambda d, p, *_: (d, 0, p)),
                pl.BlockSpec((1, win, PAIR), lambda d, p, *_: (d, 0, p)),
                pl.BlockSpec((1, rows, PAIR), lambda d, p, *_: (d, 0, p)),
                pl.BlockSpec((1, rows, PAIR), lambda d, p, *_: (d, 0, p)),
                pl.BlockSpec((1, rows, 2), lambda d, p, *_: (d * pairs + p, 0, 0)),
                pl.BlockSpec((rows, 1), lambda d, p, *_: (0, 0)),
                pl.BlockSpec((1, win), lambda d, p, *_: (0, 0)),
            ],
            out_specs=[
                pl.BlockSpec((1, rows, PAIR), put),
                pl.BlockSpec((1, win, PAIR), put),
                pl.BlockSpec((1, win, PAIR), put),
            ],
            scratch_shapes=[pltpu.VMEM((PAIR, win), F32), pltpu.VMEM((PAIR, win), F32)],
        ),
        out_shape=[
            jax.ShapeDtypeStruct(half_shape, BF16),
            jax.ShapeDtypeStruct(half_win, BF16),
            jax.ShapeDtypeStruct(half_win, BF16),
        ],
        compiler_params=params("arbitrary", "arbitrary"),
        cost_estimate=pl.CostEstimate(
            flops=40 * n * rows * win * cw, bytes_accessed=2 * n * cw * (4 * rows + 4 * win), transcendentals=n * rows * win * 4
        ),
    )(info, q, k, v, attn, gattn, lse, qseg, kseg)


def out_call(attn, packed, resid, b_out, gain, bias):
    n, rows, cw = attn.shape
    dm = packed.shape[1]

    def body(a_ref, w_ref, x_ref, bo_ref, g_ref, b_ref, h_ref, n_ref):
        d = pl.program_id(0)
        part = dot_nt(a_ref[0], w_ref[0])

        @pl.when(d == 0)
        def _():
            h_ref[...] = part + x_ref[...].astype(F32) + bo_ref[...].astype(F32)

        @pl.when(d > 0)
        def _():
            h_ref[...] += part

        @pl.when(d == n - 1)
        def _():
            hat, _ = norm_rows(h_ref[...])
            n_ref[...] = (hat * g_ref[...].astype(F32) + b_ref[...].astype(F32)).astype(BF16)

    full = lambda d: (0, 0)
    return pl.pallas_call(
        body,
        grid=(n,),
        in_specs=[
            pl.BlockSpec((1, rows, cw), lambda d: (d, 0, 0)),
            pl.BlockSpec((1, dm, cw), lambda d: (d, 0, 3)),
            pl.BlockSpec((rows, dm), full),
            pl.BlockSpec((1, dm), full),
            pl.BlockSpec((1, dm), full),
            pl.BlockSpec((1, dm), full),
        ],
        out_specs=[pl.BlockSpec((rows, dm), full), pl.BlockSpec((rows, dm), full)],
        out_shape=[jax.ShapeDtypeStruct((rows, dm), F32), jax.ShapeDtypeStruct((rows, dm), BF16)],
        compiler_params=params("arbitrary"),
        cost_estimate=pl.CostEstimate(flops=2 * n * rows * cw * dm, bytes_accessed=2 * n * dm * cw, transcendentals=0),
    )(attn, packed, resid, b_out[None], gain[None], bias[None])


def ffn_call(core, n2, hidden, cot, w_up, w_down, b_up, b_down, halves):
    rows, dm = n2.shape
    n, _, ffw = w_up.shape
    tile = ffw // halves

    def body(core_ref, x_ref, h_ref, c_ref, wu_ref, wd_ref, bu_ref, bd_ref, o_ref, gn_ref, a_ref, gu_ref, gb_ref, acc):
        t = pl.program_id(0)
        u = dot_nn(x_ref[...], wu_ref[0]) + bu_ref[...].astype(F32)
        cdf = 0.5 * (1.0 + lax.erf(u * 0.7071067811865476))
        act = (u * cdf).astype(BF16)
        slope = cdf + u * jnp.exp(-0.5 * u * u) * 0.3989422804014327
        a_ref[...] = act
        grad = dot_nt(c_ref[...], wd_ref[0]) * slope
        gu = grad.astype(BF16)
        gu_ref[...] = gu
        gb_ref[...] = jnp.sum(gu.astype(F32), axis=0, keepdims=True)
        out = dot_nn(act, wd_ref[0])
        gn = dot_nt(gu, wu_ref[0])

        @pl.when(t == 0)
        def _():
            acc[...] = h_ref[...] + bd_ref[...].astype(F32) + out
            gn_ref[...] = gn

        @pl.when(t > 0)
        def _():
            acc[...] += out
            gn_ref[...] += gn

        @pl.when(t == n * halves - 1)
        def _():
            o_ref[...] = acc[...].astype(BF16)

    full = lambda t, c: (0, 0)

    def part(t, c):
        return lax.bitwise_xor(t // n, c[0]) if halves > 1 else 0

    return pl.pallas_call(
        body,
        grid_spec=pltpu.PrefetchScalarGridSpec(
            num_scalar_prefetch=1,
            grid=(n * halves,),
            in_specs=[
                pl.BlockSpec((rows, dm), full),
                pl.BlockSpec((rows, dm), full),
                pl.BlockSpec((rows, dm), full),
                pl.BlockSpec((1, dm, tile), lambda t, c: (t % n, 0, part(t, c))),
                pl.BlockSpec((1, tile, dm), lambda t, c: (t % n, part(t, c), 0)),
                pl.BlockSpec((1, tile), lambda t, c: (0, t)),
                pl.BlockSpec((1, dm), full),
            ],
            out_specs=[
                pl.BlockSpec((rows, dm), full),
                pl.BlockSpec((rows, dm), full),
                pl.BlockSpec((rows, tile), lambda t, c: (0, t)),
                pl.BlockSpec((rows, tile), lambda t, c: (0, t)),
                pl.BlockSpec((1, tile), lambda t, c: (0, t)),
            ],
            scratch_shapes=[pltpu.VMEM((rows, dm), F32)],
        ),
        out_shape=[
            jax.ShapeDtypeStruct((rows, dm), BF16),
            jax.ShapeDtypeStruct((rows, dm), F32),
            jax.ShapeDtypeStruct((rows, n * ffw), BF16),
            jax.ShapeDtypeStruct((rows, n * ffw), BF16),
            jax.ShapeDtypeStruct((1, n * ffw), F32),
        ],
        compiler_params=params("arbitrary"),
        cost_estimate=pl.CostEstimate(
            flops=8 * rows * dm * n * ffw, bytes_accessed=4 * n * dm * ffw, transcendentals=2 * rows * n * ffw
        ),
    )(core, n2, hidden, cot, w_up, w_down, b_up[None], b_down[None])


def norm1_back_call(dq, dk, dv, packed, info, own):
    halves, rows, _ = dq.shape
    n, dm, four = packed.shape
    cw = four // 4
    win = dk.shape[1]
    width = cw // halves

    def body(info_ref, dq_ref, dk_ref, dv_ref, w_ref, o_ref, h_ref, t_ref, acc):
        step = pl.program_id(0)

        def weight(which, j):
            at = lax.bitwise_xor(j, info_ref[1]) if halves > 1 else 0
            return w_ref[0, :, pl.ds(pl.multiple_of(which * cw + at * width, width), width)]

        left = jnp.concatenate([r[j] for r in (dk_ref, dv_ref) for j in range(halves)], axis=1)
        right = jnp.concatenate([weight(m, j) for m in (1, 2) for j in range(halves)], axis=1)
        part = dot_nt(left, right)
        left = jnp.concatenate([dq_ref[j] for j in range(halves)], axis=1)
        right = jnp.concatenate([weight(0, j) for j in range(halves)], axis=1)
        mine = dot_nt(left, right)

        @pl.when(step == 0)
        def _():
            acc[...] = part

        @pl.when(step > 0)
        def _():
            acc[...] += part

        acc[own : own + rows, :] += mine

        @pl.when(step == n - 1)
        def _():
            o_ref[...] = acc[own : own + rows, :]
            h_ref[...] = acc[0:own, :].astype(BF16)
            t_ref[...] = acc[own + rows : own + rows + HALO, :].astype(BF16)

    full = lambda s, info: (0, 0)
    return pl.pallas_call(
        body,
        grid_spec=pltpu.PrefetchScalarGridSpec(
            num_scalar_prefetch=1,
            grid=(n,),
            in_specs=[
                pl.BlockSpec((halves, rows, width), lambda s, info: (0, 0, s)),
                pl.BlockSpec((halves, win, width), lambda s, info: (0, 0, s)),
                pl.BlockSpec((halves, win, width), lambda s, info: (0, 0, s)),
                pl.BlockSpec((1, dm, four), lambda s, info: (s, 0, 0)),
            ],
            out_specs=[
                pl.BlockSpec((rows, dm), full),
                pl.BlockSpec((own, dm), full),
                pl.BlockSpec((HALO, dm), full),
            ],
            scratch_shapes=[pltpu.VMEM((win, dm), F32)],
        ),
        out_shape=[
            jax.ShapeDtypeStruct((rows, dm), F32),
            jax.ShapeDtypeStruct((own, dm), BF16),
            jax.ShapeDtypeStruct((HALO, dm), BF16),
        ],
        compiler_params=params("arbitrary"),
        cost_estimate=pl.CostEstimate(
            flops=2 * n * cw * dm * (rows + 2 * win), bytes_accessed=2 * n * cw * (3 * dm + rows + 2 * win), transcendentals=0
        ),
    )(info, dq, dk, dv, packed)


MESH = pl.DeviceIdType.MESH


class Place:
    def __init__(self):
        self.me = lax.axis_index("dp")
        self.z = lax.axis_index("mp")
        self.k = lax.rem(self.me, 2)
        self.x = lax.rem(self.me // 2, 2)
        self.y = self.me // 4
        self.me_k = self.me + 1 - 2 * self.k
        self.me_x = self.me + 2 - 4 * self.x
        self.me_y = self.me + 4 - 8 * self.y
        self.me_xy = self.me_x + 4 - 8 * self.y
        self.core = {"dp": self.me_k, "mp": self.z}
        self.by_x = {"dp": self.me_x, "mp": self.z}
        self.by_y = {"dp": self.me_y, "mp": self.z}

    def along(self, d):
        return {"dp": self.me, "mp": lax.rem(self.z + d, 4)}

    def meet(self):
        sem = pltpu.get_barrier_semaphore()
        for dev in (self.core, self.by_x, self.by_y, self.along(1), self.along(2), self.along(3)):
            pl.semaphore_signal(sem, inc=1, device_id=dev, device_id_type=MESH)
        pl.semaphore_wait(sem, 6)


class Wire:
    def __init__(self, send, recv, dev):
        self.send, self.recv, self.dev = send, recv, dev

    def start(self, slot, src, dst, dev):
        copy = pltpu.make_async_remote_copy(
            src_ref=src, dst_ref=dst, send_sem=self.send.at[slot], recv_sem=self.recv.at[slot],
            device_id=dev, device_id_type=MESH,
        )
        copy.start()

    def sent(self, slot, ref):
        pltpu.make_async_remote_copy(
            src_ref=ref, dst_ref=ref, send_sem=self.send.at[slot], recv_sem=self.recv.at[slot],
            device_id=dict(self.dev), device_id_type=MESH,
        ).wait_send()

    def landed(self, slot, ref, dev):
        pltpu.make_async_remote_copy(
            src_ref=ref, dst_ref=ref, send_sem=self.send.at[slot], recv_sem=self.recv.at[slot],
            device_id=dev, device_id_type=MESH,
        ).wait_recv()


def gather_steps(place, wire, base, shard, whole):
    step = shard.shape[0] // 8
    half = step // 2

    def rows(who, at=0, size=step):
        return pl.ds(pl.multiple_of(who * step + at, half), size)

    def slot(d, kind):
        return base + (d - 1) * 9 + kind

    def begin(d):
        wire.start(slot(d, 0), shard.at[rows(place.me)], whole.at[d, rows(place.me)], place.along(4 - d))

    def first(d):
        mine = whole.at[d, rows(place.me)]
        wire.landed(slot(d, 0), mine, place.along(d))
        wire.start(slot(d, 2), mine, mine, place.by_x)
        wire.start(slot(d, 3), mine, mine, place.by_y)
        wire.start(slot(d, 1), mine, mine, place.core)

    def second(d):
        got = whole.at[d, rows(place.me_x)]
        wire.landed(slot(d, 2), got, place.by_x)
        part = whole.at[d, rows(place.me_x, 0, half)]
        wire.start(slot(d, 4), part, part, place.by_y)
        wire.start(slot(d, 6), got, got, place.core)
        got = whole.at[d, rows(place.me_y)]
        wire.landed(slot(d, 3), got, place.by_y)
        part = whole.at[d, rows(place.me_y, half, half)]
        wire.start(slot(d, 5), part, part, place.by_x)
        wire.start(slot(d, 7), got, got, place.core)

    def third(d):
        wire.landed(slot(d, 4), whole.at[d, rows(place.me_xy, 0, half)], place.by_y)
        wire.landed(slot(d, 5), whole.at[d, rows(place.me_xy, half, half)], place.by_x)
        got = whole.at[d, rows(place.me_xy)]
        wire.start(slot(d, 8), got, got, place.core)

    def done(d):
        flip = 1 - 2 * place.k
        for kind, who in ((1, place.me), (6, place.me_x), (7, place.me_y), (8, place.me_xy)):
            wire.landed(slot(d, kind), whole.at[d, rows(who + flip)], place.core)

    def drain():
        for d in (1, 2, 3):
            for kind in range(9):
                wire.sent(slot(d, kind), whole.at[d, pl.ds(0, half if kind in (4, 5) else step)])

    return begin, first, second, third, done, drain


def front_call(tokens, cot, pack, w_up, w_down, bias, small, qseg, kseg, own):
    rows, dm = tokens.shape
    cw = pack.shape[1] // 4
    ffw = w_up.shape[1]
    n = 4
    tile = ffw // 2
    hw = n * tile
    win = own + rows + 2 * HALO
    pairs = cw // PAIR
    strip = 128
    per = rows // strip
    scale = HEAD_DIM**-0.5
    length = bias.shape[1]
    base = 6

    def body(
        tok_ref, cot_ref, pack_ref, up_ref, down_ref, small_ref, bias_ref, qs_ref, ks_ref,
        packed, n1t, n2t, cott, ghbt, q_ref, k_ref, v_ref, a_ref, l_ref, ga_ref, act_ref, gup_ref, gbu_ref, gh_ref, o_ref, sum_ref,
        up, down, n1, hid, n2, acc, act, gup, biases, xs, xr, ls, fs,
    ):
        place = Place()
        core, z = place.k, place.z
        long, takes_prev, takes_next = z < 2, z >= 2, jnp.logical_and(z >= 1, z < 3)
        swap = {"dp": place.me, "mp": lax.rem(z + 1, 2)}
        left_dev = {"dp": place.me, "mp": lax.rem(z + 3, 4)}
        right_dev = {"dp": place.me, "mp": lax.rem(z + 1, 4)}
        wire = Wire(xs, xr, place.core)
        local = [
            pltpu.make_async_copy(src, dst, ls.at[i])
            for i, (src, dst) in enumerate(
                ((tok_ref, n1.at[own : own + rows]), (pack_ref, packed.at[0]), (up_ref, up.at[0]), (down_ref, down.at[0]))
            )
        ]
        for c in local:
            c.start()
        place.meet()
        for d in (1, 2, 3):
            wire.start(d - 1, bias_ref, biases.at[d], place.along(4 - d))

        @pl.when(long)
        def _():
            wire.start(3, tok_ref, n1.at[0:own], swap)

        @pl.when(takes_next)
        def _():
            wire.start(4, tok_ref.at[rows - HALO : rows], n1.at[own - HALO : own], right_dev)

        @pl.when(takes_prev)
        def _():
            wire.start(5, tok_ref.at[0:HALO], n1.at[own + rows : own + rows + HALO], left_dev)

        groups = [
            gather_steps(place, wire, base + 27 * g, src, dst)
            for g, (src, dst) in enumerate(((pack_ref, packed), (up_ref, up), (down_ref, down)))
        ]
        items = [(0, 1), (0, 3), (0, 2), (1, 1), (2, 1), (1, 3), (2, 3), (1, 2), (2, 2)]
        for g, d in items:
            groups[g][0](d)

        def relay(i):
            for lag in range(3):
                if 0 <= i - lag < len(items):
                    g, d = items[i - lag]
                    groups[g][1 + lag](d)

        def arrived(d, *which):
            for g in which:
                groups[g][4](d)

        def turns(i, table):
            for t, f in table.items():

                @pl.when(i == t)
                def _():
                    f()

        def shard_at(k):
            return k + (k // 2) * (5 - 2 * k)

        def strip_at(i, start=0):
            return pl.ds(pl.multiple_of(start + i * strip, strip), strip)

        row = lambda i: small_ref[i : i + 1, :]

        @pl.when(takes_prev)
        def _():
            n1[0 : own - HALO, :] = jnp.zeros((own - HALO, dm), BF16)

        @pl.when(jnp.logical_not(takes_next))
        def _():
            n1[own + rows : own + rows + HALO, :] = jnp.zeros((HALO, dm), BF16)

        n1[own + rows + HALO :, :] = jnp.zeros((HALO, dm), BF16)
        biases[0] = bias_ref[...]

        def turn_cot(i, carry):
            cott[:, strip_at(i)] = cot_ref[strip_at(i), :].astype(F32).T.astype(BF16)
            return carry

        lax.fori_loop(0, per, turn_cot, 0)

        def norm1(i):
            at = strip_at(i)
            x = n1[at, :].astype(F32)
            hat, _ = norm_rows(x)
            val = hat * row(0) + row(1)
            n1[at, :] = val.astype(BF16)
            n1t[:, at] = val.T.astype(BF16)
            return x

        def norm_own(i, carry):
            hid[strip_at(i), :] = norm1(own // strip + i) + row(4)
            return carry

        def norm_far(i, carry):
            norm1(i)
            return carry

        local[0].wait()
        lax.fori_loop(0, per, norm_own, 0)

        @pl.when(long)
        def _():
            wire.landed(3, n1.at[0:own], swap)

        @pl.when(takes_prev)
        def _():
            wire.landed(4, n1.at[own - HALO : own], left_dev)

        @pl.when(takes_next)
        def _():
            wire.landed(5, n1.at[own + rows : own + rows + HALO], right_dev)

        lax.fori_loop(0, own // strip, norm_far, 0)
        norm1((own + rows) // strip)
        for d in (1, 2, 3):
            wire.landed(d - 1, biases.at[d], place.along(d))
        for c in local[1:]:
            c.wait()

        def attend(big, d, p):
            at = pl.ds(pl.multiple_of(p * PAIR, PAIR), PAIR)
            for qs, qn, ks, kn in blocks_of(rows, own, win, big):
                mask = qs_ref[qs : qs + qn, :] == ks_ref[:, ks : ks + kn]
                qq, kk, vv = q_ref[d, qs : qs + qn, at], k_ref[d, ks : ks + kn, at], v_ref[d, ks : ks + kn, at]
                outs = []
                for h in range(2):
                    lanes = slice(h * HEAD_DIM, (h + 1) * HEAD_DIM)
                    s = jnp.where(mask, dot_nt(qq[:, lanes] * BF16(scale), kk[:, lanes]), NEG)
                    top = jnp.max(s, axis=1, keepdims=True)
                    pr = jnp.exp(s - top)
                    total = jnp.sum(pr, axis=1, keepdims=True)
                    outs.append(dot_nn(pr.astype(BF16), vv[:, lanes]) / total)
                    l_ref[d * pairs + p, qs : qs + qn, h : h + 1] = top + jnp.log(total)
                a_ref[d, qs : qs + qn, at] = jnp.concatenate(outs, axis=1).astype(BF16)

        def heads(kk, carry):
            turns(
                kk,
                {
                    0: lambda: relay(0),
                    1: lambda: (relay(1), relay(2), relay(3), arrived(1, 0)),
                    2: lambda: (relay(4), arrived(3, 0)),
                    3: lambda: (relay(5), arrived(2, 0)),
                },
            )
            d = shard_at(kk)
            q_ref[d] = (dot_nn(n1[own : own + rows, :], packed[d, :, 0:cw]) + biases[d, :, 0:cw]).astype(BF16)
            k_ref[d] = dot_nn(n1[...], packed[d, :, cw : 2 * cw]).astype(BF16)
            v_ref[d] = (dot_nn(n1[...], packed[d, :, 2 * cw : 3 * cw]) + biases[d, :, cw : 2 * cw]).astype(BF16)

            def one(p, inner):
                @pl.when(long)
                def _():
                    attend(True, d, p)

                @pl.when(jnp.logical_not(long))
                def _():
                    attend(False, d, p)

                return inner

            lax.fori_loop(0, pairs, one, 0)
            hid[...] += dot_nt(a_ref[d], packed[d, :, 3 * cw : 4 * cw])
            return carry

        lax.fori_loop(0, n, heads, 0)
        relay(6)

        def norm2(i, carry):
            at = strip_at(i)
            hidden = hid[at, :]
            hat, _ = norm_rows(hidden)
            val = hat * row(2) + row(3)
            n2[at, :] = val.astype(BF16)
            n2t[:, at] = val.T.astype(BF16)
            acc[at, :] = hidden + row(5)
            return carry

        lax.fori_loop(0, per, norm2, 0)

        def out_copies(i, col):
            at = pl.ds(pl.multiple_of(col, tile), tile)
            return (
                pltpu.make_async_copy(act.at[:, at], act_ref.at[:, at], fs.at[i]),
                pltpu.make_async_copy(gup.at[:, at], gup_ref.at[:, at], fs.at[2 * n + i]),
            )

        def column(i):
            return lax.rem(i, 2) * hw + shard_at(i // 2) * tile

        def feed(i, carry):
            turns(
                i,
                {
                    1: lambda: relay(7),
                    2: lambda: (relay(8), arrived(1, 1, 2)),
                    3: lambda: relay(9),
                    4: lambda: (relay(10), arrived(3, 1, 2)),
                    6: lambda: arrived(2, 1, 2),
                },
            )
            d = shard_at(i // 2)
            part = lax.rem(lax.rem(i, 2) + core, 2) * tile
            at = pl.ds(pl.multiple_of(part, tile), tile)
            to = pl.ds(pl.multiple_of(column(i), tile), tile)
            u = dot_nn(n2[...], up[d, :, at]) + biases[d, :, pl.ds(pl.multiple_of(2 * cw + part, PAIR), tile)]
            cdf = 0.5 * (1.0 + lax.erf(u * 0.7071067811865476))
            val = (u * cdf).astype(BF16)
            slope = cdf + u * jnp.exp(-0.5 * u * u) * 0.3989422804014327
            act[:, to] = val
            gu = (dot_nt(cot_ref[...], down[d, at, :]) * slope).astype(BF16)
            gup[:, to] = gu
            gbu_ref[:, to] = jnp.sum(gu.astype(F32), axis=0, keepdims=True)
            for c in out_copies(i, column(i)):
                c.start()
            acc[...] += dot_nn(val, down[d, at, :])
            gn = dot_nt(gu, up[d, :, at])

            @pl.when(i == 0)
            def _():
                gh_ref[...] = gn

            @pl.when(i > 0)
            def _():
                gh_ref[...] += gn

            return carry

        lax.fori_loop(0, 2 * n, feed, 0)
        sum_ref[...] = jnp.zeros_like(sum_ref)

        def back2(i, carry):
            at = strip_at(i)
            o_ref[at, :] = acc[at, :].astype(BF16)
            hat, inv = norm_rows(hid[at, :])
            g = gh_ref[at, :]
            gout = cot_ref[at, :].astype(F32)
            gg = g * row(2)
            first = jnp.mean(gg, axis=1, keepdims=True)
            second = jnp.mean(gg * hat, axis=1, keepdims=True)
            val = inv * (gg - first - hat * second) + gout
            gh_ref[at, :] = val
            n2[at, :] = val.astype(BF16)
            ghbt[:, at] = val.T.astype(BF16)
            for j, v in enumerate((val, g * hat, g, gout)):
                sum_ref[:, j * dm : (j + 1) * dm] += jnp.sum(v, axis=0, keepdims=True)
            return carry

        lax.fori_loop(0, per, back2, 0)

        def back_attn(d, carry):
            ga_ref[d] = dot_nn(n2[...], packed[d, :, 3 * cw : 4 * cw]).astype(BF16)
            return carry

        lax.fori_loop(0, n, back_attn, 0)
        for i in range(2 * n):
            for c in out_copies(i, 0):
                c.wait()
        for group in groups:
            group[5]()
        for d in (1, 2, 3):
            wire.sent(d - 1, biases.at[d])

        @pl.when(long)
        def _():
            wire.sent(3, n1.at[0:own])

        @pl.when(takes_next)
        def _():
            wire.sent(4, n1.at[0:HALO])

        @pl.when(takes_prev)
        def _():
            wire.sent(5, n1.at[0:HALO])

    hbm = pl.BlockSpec(memory_space=pl.ANY)
    vmem = pl.BlockSpec(memory_space=pltpu.VMEM)
    half = lambda *shape: jax.ShapeDtypeStruct(shape, BF16)
    full = lambda *shape: jax.ShapeDtypeStruct(shape, F32)
    b16 = lambda *shape: pltpu.VMEM(shape, BF16)
    b32 = lambda *shape: pltpu.VMEM(shape, F32)
    slots = base + 27 * 3
    return pl.pallas_call(
        body,
        in_specs=[hbm, vmem, hbm, hbm, hbm, vmem, vmem, vmem, vmem],
        out_specs=[vmem] * 11 + [hbm] * 2 + [vmem] * 4,
        out_shape=[
            half(n, dm, 4 * cw), half(dm, win), half(dm, rows), half(dm, rows), half(dm, rows),
            half(n, rows, cw), half(n, win, cw), half(n, win, cw), half(n, rows, cw), full(n * pairs, rows, 2), half(n, rows, cw),
            half(rows, 2 * hw), half(rows, 2 * hw), full(1, 2 * hw), full(rows, dm), half(rows, dm), full(1, 4 * dm),
        ],
        scratch_shapes=[
            b16(n, dm, ffw), b16(n, ffw, dm), b16(win, dm), b32(rows, dm), b16(rows, dm), b32(rows, dm),
            b16(rows, 2 * hw), b16(rows, 2 * hw), b32(n, 1, length),
            pltpu.SemaphoreType.DMA((slots,)), pltpu.SemaphoreType.DMA((slots,)), pltpu.SemaphoreType.DMA((4,)),
            pltpu.SemaphoreType.DMA((4 * n,)),
        ],
        compiler_params=pltpu.CompilerParams(collective_id=0, has_side_effects=True, vmem_limit_bytes=VMEM_ALL),
    )(tokens, cot, pack, w_up, w_down, small, bias, qseg, kseg)


class Reduce:
    SLOTS = 32

    @staticmethod
    def scratch(dm, w):
        q = dm // 4
        e = q // 2
        return [
            pltpu.VMEM((4, q, w), BF16),
            pltpu.VMEM((4, q, w), BF16),
            pltpu.VMEM((4, e, w), BF16),
            pltpu.VMEM((4, e, w), BF16),
            pltpu.VMEM((3, q, w), BF16),
            pltpu.SemaphoreType.DMA((Reduce.SLOTS,)),
            pltpu.SemaphoreType.DMA((Reduce.SLOTS,)),
        ]

    def __init__(self, place, grad, landing, scratch):
        self.place, self.g, self.f = place, grad, landing
        self.ra1, self.rb1, self.ra2, self.rb2, self.zb = scratch[:5]
        self.wire = Wire(scratch[5], scratch[6], place.core)
        self.q = grad.shape[0] // 4
        self.e = self.q // 2
        self.w = grad.shape[1] // 4

    def at(self, base, big, small=None):
        start = base * 2 * self.q + big * self.q + (0 if small is None else small * self.e)
        return pl.ds(pl.multiple_of(start, self.e), self.q if small is None else self.e)

    def eighth(self, small):
        return pl.ds(pl.multiple_of(small * self.e, self.e), self.e)

    def cols(self, d):
        return pl.ds(pl.multiple_of(d * self.w, self.w), self.w)

    def one(self, d):
        p, wire = self.place, self.wire
        wire.start(d, self.g.at[self.at(0, 1 - p.x), self.cols(d)], self.ra1.at[d], p.by_x)
        wire.start(4 + d, self.g.at[self.at(1, 1 - p.y), self.cols(d)], self.rb1.at[d], p.by_y)

    def two(self, d):
        p, wire, c = self.place, self.wire, self.cols(d)
        for slot, buf, to, at, mine, dev, nxt in (
            (0, self.ra1, self.ra2, self.at(0, p.x, 1 - p.y), self.eighth(1 - p.y), p.by_x, p.by_y),
            (4, self.rb1, self.rb2, self.at(1, p.y, 1 - p.x), self.eighth(1 - p.x), p.by_y, p.by_x),
        ):
            wire.landed(slot + d, buf.at[d], dev)
            self.g[at, c] = (self.g[at, c].astype(F32) + buf[d, mine, :].astype(F32)).astype(BF16)
            wire.start(8 + slot + d, self.g.at[at, c], to.at[d], nxt)

    def sums(self, d):
        p, wire, c = self.place, self.wire, self.cols(d)
        wire.landed(8 + d, self.ra2.at[d], p.by_y)
        wire.landed(12 + d, self.rb2.at[d], p.by_x)
        up = (
            self.g[self.at(0, p.x, p.y), c].astype(F32)
            + self.ra1[d, self.eighth(p.y), :].astype(F32)
            + self.ra2[d].astype(F32)
        )
        low = (
            self.g[self.at(1, p.y, p.x), c].astype(F32)
            + self.rb1[d, self.eighth(p.x), :].astype(F32)
            + self.rb2[d].astype(F32)
        )
        return up, low

    def three(self, d):
        p, wire, c, e = self.place, self.wire, self.cols(d), self.e
        up, low = self.sums(d)
        for part, (at, val) in enumerate(((self.at(0, p.x, p.y), up), (self.at(1, p.y, p.x), low))):
            self.g[at, c] = val.astype(BF16)
            wire.start(
                16 + 12 * part + d, self.g.at[at, c], self.zb.at[d - 1, part * e : (part + 1) * e], p.along(d)
            )

    def last(self):
        p, wire, e = self.place, self.wire, self.e
        up, low = self.sums(0)
        for s in (1, 2, 3):
            wire.landed(16 + s, self.zb.at[s - 1, 0:e], p.along(4 - s))
            wire.landed(28 + s, self.zb.at[s - 1, e : 2 * e], p.along(4 - s))
            up = up + self.zb[s - 1, 0:e].astype(F32)
            low = low + self.zb[s - 1, e : 2 * e].astype(F32)
        self.f[0, 0:e] = up.astype(BF16)
        self.f[0, e : 2 * e] = low.astype(BF16)
        wire.start(20, self.f.at[0], self.f.at[2], p.by_x)
        wire.start(21, self.f.at[0], self.f.at[4], p.by_y)
        wire.start(22, self.f.at[0], self.f.at[1], p.core)

    def four(self):
        p, wire, e = self.place, self.wire, self.e
        wire.landed(20, self.f.at[2], p.by_x)
        wire.start(23, self.f.at[2, 0:e], self.f.at[6, 0:e], p.by_y)
        wire.start(25, self.f.at[2], self.f.at[3], p.core)
        wire.landed(21, self.f.at[4], p.by_y)
        wire.start(24, self.f.at[4, e : 2 * e], self.f.at[6, e : 2 * e], p.by_x)
        wire.start(26, self.f.at[4], self.f.at[5], p.core)

    def five(self):
        p, wire, e = self.place, self.wire, self.e
        wire.landed(23, self.f.at[6, 0:e], p.by_y)
        wire.landed(24, self.f.at[6, e : 2 * e], p.by_x)
        wire.start(27, self.f.at[6], self.f.at[7], p.core)

    def six(self):
        for slot, to in ((22, 1), (25, 3), (26, 5), (27, 7)):
            self.wire.landed(slot, self.f.at[to], self.place.core)
        e, sent = self.e, self.wire.sent
        for d in range(4):
            sent(d, self.ra1.at[d])
            sent(4 + d, self.rb1.at[d])
            sent(8 + d, self.ra2.at[d])
            sent(12 + d, self.rb2.at[d])
        for d in range(1, 4):
            sent(16 + d, self.zb.at[d - 1, 0:e])
            sent(28 + d, self.zb.at[d - 1, 0:e])
        for slot in (20, 21, 22, 25, 26, 27):
            sent(slot, self.f.at[0])
        for slot in (23, 24):
            sent(slot, self.f.at[0, 0:e])

    def sweep(self):
        return [
            functools.partial(f, d)
            for f, d in (
                (self.two, 1), (self.two, 2), (self.three, 1), (self.two, 3), (self.three, 2), (self.two, 0), (self.three, 3)
            )
        ]

    def tail(self):
        return [self.last, self.four, self.five, self.six]


def back_call(cot, act, n2, gup, ghb, n1w, q, k, v, attn, gattn, lse, qseg, kseg, own, near):
    n, rows, cw = q.shape
    win = k.shape[1]
    dm = cot.shape[0]
    hw = act.shape[1] // 2
    half = n * cw // 2
    w = hw // 4
    pairs = cw // PAIR
    scale = HEAD_DIM**-0.5
    each = len(Reduce.scratch(dm, w))

    def body(
        cot_ref, act_ref, n2_ref, gup_ref, ghb_ref, n1_ref, q_ref, k_ref, v_ref, a_ref, g_ref, l_ref, qs_ref, ks_ref,
        fd, fu, gp_ref, dq, dk, dv,
        cot2, act2, n22, gup2, ghb2, n12, gd, gu, dq_o, dk_o, dv_o, at2, dkt, dvt, xs, xr, ls, *scr,
    ):
        place = Place()
        core = place.k
        big_z = place.z < near
        wire = Wire(xs, xr, place.core)
        whole = (
            (cot_ref, cot2, rows), (n2_ref, n22, rows), (ghb_ref, ghb2, rows), (n1_ref, n12, win)
        )
        mixed = ((act_ref, act2), (gup_ref, gup2))
        local = [pltpu.make_async_copy(src, dst.at[:, 0:wide], ls.at[i]) for i, (src, dst, wide) in enumerate(whole)]
        local += [pltpu.make_async_copy(src.at[:, 0:hw], dst.at[0:rows], ls.at[4 + i]) for i, (src, dst) in enumerate(mixed)]
        for i in (0, 4, 1, 5, 2, 3):
            local[i].start()
        place.meet()

        def give_whole(i):
            src, dst, wide = whole[i]
            wire.start(i, src, dst.at[:, wide : 2 * wide], place.core)

        def give_mixed(i):
            src, dst = mixed[i]
            wire.start(4 + i, src.at[:, hw : 2 * hw], dst.at[rows : 2 * rows], place.core)

        def take(*which):
            for i in which:
                local[i].wait()
                if i < 4:
                    dst, wide = whole[i][1:]
                    wire.landed(i, dst.at[:, wide : 2 * wide], place.core)
                else:
                    wire.landed(i, mixed[i - 4][1].at[rows : 2 * rows], place.core)

        give_whole(0)
        give_mixed(0)
        give_whole(1)
        give_mixed(1)
        give_whole(2)
        give_whole(3)
        for d in range(n):
            to = slice(d * PAIR, (d + 1) * PAIR)
            theirs = pl.ds(pl.multiple_of((1 - core) * PAIR, PAIR), PAIR)
            mine = pl.ds(pl.multiple_of(core * PAIR, PAIR), PAIR)
            wire.start(6 + d, a_ref.at[d, :, theirs], at2.at[rows : 2 * rows, to], place.core)
            at2[0:rows, to] = a_ref[d, :, mine]

        down = Reduce(place, gd, fd, scr[:each])
        up = Reduce(place, gu, fu, scr[each : 2 * each])

        def make(red, grad, left, right):
            def step(i, carry):
                d = lax.rem(i + 1, 4)
                c = pl.ds(pl.multiple_of(d * w, w), w)
                grad[:, c] = dot_nn(left[...], right[:, c]).astype(BF16)
                red.one(d)
                return carry

            lax.fori_loop(0, 4, step, 0)

        take(0, 4)
        make(down, gd, cot2, act2)
        take(1, 5)
        make(up, gu, n22, gup2)

        def work(big, d, p):
            at = pl.ds(pl.multiple_of(p * PAIR, PAIR), PAIR)
            to = pl.ds(pl.multiple_of(d * PAIR, PAIR), PAIR)
            rel = lax.rem(p + core, 2)
            if not big:
                dkt[...] = jnp.zeros_like(dkt)
                dvt[...] = jnp.zeros_like(dvt)
            for i, (qs, qn, ks, kn) in enumerate(blocks_of(rows, own, win, big)):
                mask = qs_ref[qs : qs + qn, :] == ks_ref[:, ks : ks + kn]
                qq, kk, vv = q_ref[d, qs : qs + qn, at], k_ref[d, ks : ks + kn, at], v_ref[d, ks : ks + kn, at]
                gg = g_ref[d, qs : qs + qn, at]
                prod = gg.astype(F32) * a_ref[d, qs : qs + qn, at].astype(F32)
                dqs = []
                for h in range(2):
                    lanes = slice(h * HEAD_DIM, (h + 1) * HEAD_DIM)
                    qh, kh, gh = qq[:, lanes] * BF16(scale), kk[:, lanes], gg[:, lanes]
                    s = jnp.where(mask, dot_nt(qh, kh) - l_ref[d * pairs + p, qs : qs + qn, h : h + 1], NEG)
                    pr = jnp.exp(s)
                    dp = dot_nt(gh, vv[:, lanes])
                    delta = jnp.sum(prod[:, lanes], axis=1, keepdims=True)
                    ds = (pr * (dp - delta)).astype(BF16)
                    dqs.append(dot_nn(ds, kh) * scale)
                    gk = dot_tn(qh, ds)
                    gv = dot_tn(gh, pr.astype(BF16))
                    if big and i == 0:
                        dkt[lanes, :] = gk
                        dvt[lanes, :] = gv
                    else:
                        dkt[lanes, ks : ks + kn] += gk
                        dvt[lanes, ks : ks + kn] += gv
                dq[rel, qs : qs + qn, to] = jnp.concatenate(dqs, axis=1).astype(BF16)
            dk[rel, :, to] = dkt[...].T.astype(BF16)
            dv[rel, :, to] = dvt[...].T.astype(BF16)

        todo = down.sweep() + up.sweep()
        turns = [todo[2 * i : 2 * i + 2] for i in range(n * pairs)]
        turns[-1] = todo[2 * (n * pairs - 1) :]

        def head_pair(i, carry):
            d, p = i // pairs, lax.rem(i, pairs)

            @pl.when(big_z)
            def _():
                work(True, d, p)

            @pl.when(jnp.logical_not(big_z))
            def _():
                work(False, d, p)

            for t, steps in enumerate(turns):
                if steps:

                    @pl.when(i == t)
                    def _():
                        for f in steps:
                            f()

            return carry

        lax.fori_loop(0, n * pairs, head_pair, 0)
        halves = ((dq, dq_o), (dk, dk_o), (dv, dv_o))
        for i, (src, dst) in enumerate(halves):
            wire.start(10 + i, src.at[1], dst, place.core)
        down.last()
        take(2, 3)
        for d in range(n):
            wire.landed(6 + d, at2.at[rows : 2 * rows, d * PAIR : (d + 1) * PAIR], place.core)

        def put(m, val):
            for d in range(n):
                at = d * w + m * PAIR
                act2[:, at : at + PAIR] = val[:, d * PAIR : (d + 1) * PAIR].astype(BF16)

        put(3, dot_nn(ghb2[...], at2[...]))
        up.last()
        down.four()
        wire.landed(10, dq_o, place.core)
        put(0, dot_nn(n12[:, own : own + rows], dq[0]) + dot_nn(n12[:, win + own : win + own + rows], dq_o[...]))
        down.five()
        up.four()
        wire.landed(11, dk_o, place.core)
        put(1, dot_nn(n12[:, 0:win], dk[0]) + dot_nn(n12[:, win : 2 * win], dk_o[...]))
        up.five()
        wire.landed(12, dv_o, place.core)
        put(2, dot_nn(n12[:, 0:win], dv[0]) + dot_nn(n12[:, win : 2 * win], dv_o[...]))
        out = pltpu.make_async_copy(act2, gp_ref, ls.at[6])
        out.start()
        down.six()
        up.six()
        for i in range(4):
            wire.sent(i, whole[i][0])
        for i in range(2):
            wire.sent(4 + i, act2.at[0:rows])
        for d in range(n):
            wire.sent(6 + d, at2.at[0:rows, 0:PAIR])
        for i in range(3):
            wire.sent(10 + i, halves[i][1])
        out.wait()

    hbm = pl.BlockSpec(memory_space=pl.ANY)
    vmem = pl.BlockSpec(memory_space=pltpu.VMEM)
    shaped = lambda *shape: jax.ShapeDtypeStruct(shape, BF16)
    buf = lambda *shape: pltpu.VMEM(shape, BF16)
    return pl.pallas_call(
        body,
        in_specs=[hbm] * 6 + [vmem] * 8,
        out_specs=[vmem, vmem, hbm, vmem, vmem, vmem],
        out_shape=[
            shaped(8, dm // 4, w), shaped(8, dm // 4, w), shaped(dm, hw), shaped(2, rows, half), shaped(2, win, half), shaped(2, win, half)
        ],
        scratch_shapes=[
            buf(dm, 2 * rows), buf(2 * rows, hw), buf(dm, 2 * rows), buf(2 * rows, hw), buf(dm, 2 * rows), buf(dm, 2 * win),
            buf(dm, hw), buf(dm, hw), buf(rows, half), buf(win, half), buf(win, half), buf(2 * rows, half),
            pltpu.VMEM((PAIR, win), F32), pltpu.VMEM((PAIR, win), F32),
            pltpu.SemaphoreType.DMA((13,)), pltpu.SemaphoreType.DMA((13,)), pltpu.SemaphoreType.DMA((7,)),
        ]
        + Reduce.scratch(dm, w) * 2,
        compiler_params=pltpu.CompilerParams(collective_id=1, has_side_effects=True, vmem_limit_bytes=VMEM_ALL),
    )(cot, act, n2, gup, ghb, n1w, q, k, v, attn, gattn, lse, qseg, kseg)


def finish_call(gp, dq, dk, dv, packed, tokens, gain, vec, own):
    n, dm, four = packed.shape
    cw = four // 4
    rows = tokens.shape[0]
    win = dk.shape[1]
    cols = gp.shape[1]
    w = cols // 4
    length = vec.shape[1]
    each = len(Reduce.scratch(dm, w))
    strip = 128

    def body(
        gp_ref, dq_ref, dk_ref, dv_ref, w_ref, x_ref, gain_ref, vec_ref,
        fp, gi_ref, sum_ref,
        g, acc, far_out, next_out, far_in, prev_in, next_in, va, vr, vz, xs, xr, ls, *scr,
    ):
        place = Place()
        core, z = place.k, place.z
        load = pltpu.make_async_copy(gp_ref, g, ls)
        load.start()
        place.meet()
        wire = Wire(xs, xr, place.core)
        red = Reduce(place, g, fp, scr)
        load.wait()
        for d in (1, 2, 3, 0):
            red.one(d)

        def dots(d, carry):
            def weight(which, j):
                at = which * cw + lax.rem(j + core, 2) * PAIR
                return w_ref[d, :, pl.ds(pl.multiple_of(at, PAIR), PAIR)]

            to = pl.ds(pl.multiple_of(d * PAIR, PAIR), PAIR)
            left = jnp.concatenate([r[j, :, to] for r in (dk_ref, dv_ref) for j in range(2)], axis=1)
            right = jnp.concatenate([weight(m, j) for m in (1, 2) for j in range(2)], axis=1)
            part = dot_nt(left, right)
            left = jnp.concatenate([dq_ref[j, :, to] for j in range(2)], axis=1)
            right = jnp.concatenate([weight(0, j) for j in range(2)], axis=1)
            mine = dot_nt(left, right)

            @pl.when(d == 0)
            def _():
                acc[...] = part

            @pl.when(d > 0)
            def _():
                acc[...] += part

            acc[own : own + rows, :] += mine
            for t, f in ((2, red.sweep()[0]), (3, red.sweep()[1])):

                @pl.when(d == t)
                def _():
                    f()

            return carry

        lax.fori_loop(0, n, dots, 0)

        long, gives_prev, gives_next = z < 2, z >= 2, jnp.logical_and(z >= 1, z < 3)
        swap = {"dp": place.me, "mp": lax.rem(z + 1, 2)}
        left_dev = {"dp": place.me, "mp": lax.rem(z + 3, 4)}
        right_dev = {"dp": place.me, "mp": lax.rem(z + 1, 4)}
        far_out[...] = acc[0:own, :].astype(BF16)
        next_out[...] = acc[own + rows : own + rows + HALO, :].astype(BF16)

        @pl.when(long)
        def _():
            wire.start(0, far_out, far_in, swap)

        @pl.when(gives_prev)
        def _():
            wire.start(1, far_out.at[own - HALO : own], prev_in, left_dev)

        @pl.when(gives_next)
        def _():
            wire.start(2, next_out, next_in, right_dev)

        for f in red.sweep()[2:]:
            f()

        @pl.when(long)
        def _():
            wire.landed(0, far_in, swap)
            acc[own : own + rows, :] += far_in[...].astype(F32)

        @pl.when(gives_next)
        def _():
            wire.landed(1, prev_in, right_dev)
            acc[own + rows - HALO : own + rows, :] += prev_in[...].astype(F32)

        @pl.when(gives_prev)
        def _():
            wire.landed(2, next_in, left_dev)
            acc[own : own + HALO, :] += next_in[...].astype(F32)

        va[0] = vec_ref[...]
        va[0, :, 0 : 2 * dm] = jnp.zeros((1, 2 * dm), F32)
        gains = gain_ref[...].astype(F32)

        def norm(i, carry):
            at = pl.ds(pl.multiple_of(i * strip, strip), strip)
            hat, inv = norm_rows(x_ref[at, :].astype(F32))
            back = acc[pl.ds(pl.multiple_of(own + i * strip, strip), strip), :]
            gg = back * gains
            first = jnp.mean(gg, axis=1, keepdims=True)
            second = jnp.mean(gg * hat, axis=1, keepdims=True)
            gi_ref[at, :] = inv * (gg - first - hat * second)
            va[0, :, 0:dm] += jnp.sum(back * hat, axis=0, keepdims=True)
            va[0, :, dm : 2 * dm] += jnp.sum(back, axis=0, keepdims=True)
            return carry

        lax.fori_loop(0, rows // strip, norm, 0)

        hops = (place.core, place.by_x, place.by_y)
        between = (red.last, red.four, red.five)
        for i, dev in enumerate(hops):
            wire.start(3 + i, va.at[i], vr.at[i], dev)
            if i == 0:
                between[0]()
            wire.landed(3 + i, vr.at[i], dev)
            if i < 2:
                va[i + 1] = va[i] + vr[i]
            else:
                vz[0] = va[i] + vr[i]
        for d in (1, 2, 3):
            wire.start(5 + d, vz.at[0], vz.at[d], place.along(d))
        between[1]()
        between[2]()
        for d in (1, 2, 3):
            wire.landed(5 + d, vz.at[d], place.along(4 - d))
        terms = [vz[lax.rem(z - a + 4, 4)] for a in range(4)]
        sum_ref[...] = (terms[0] + terms[1]) + (terms[2] + terms[3])
        red.six()

        @pl.when(long)
        def _():
            wire.sent(0, far_out)

        @pl.when(gives_prev)
        def _():
            wire.sent(1, prev_in)

        @pl.when(gives_next)
        def _():
            wire.sent(2, next_out)

        for i in range(3):
            wire.sent(3 + i, va.at[i])
        for d in (1, 2, 3):
            wire.sent(5 + d, vz.at[0])

    hbm = pl.BlockSpec(memory_space=pl.ANY)
    vmem = pl.BlockSpec(memory_space=pltpu.VMEM)
    buf = lambda *shape: pltpu.VMEM(shape, BF16)
    return pl.pallas_call(
        body,
        in_specs=[hbm] + [vmem] * 7,
        out_specs=[vmem] * 3,
        out_shape=[
            jax.ShapeDtypeStruct((8, dm // 4, w), BF16),
            jax.ShapeDtypeStruct((rows, dm), F32),
            jax.ShapeDtypeStruct((1, length), F32),
        ],
        scratch_shapes=[
            buf(dm, cols), pltpu.VMEM((win, dm), F32),
            buf(own, dm), buf(HALO, dm), buf(own, dm), buf(HALO, dm), buf(HALO, dm),
            pltpu.VMEM((3, 1, length), F32), pltpu.VMEM((3, 1, length), F32), pltpu.VMEM((4, 1, length), F32),
            pltpu.SemaphoreType.DMA((9,)), pltpu.SemaphoreType.DMA((9,)), pltpu.SemaphoreType.DMA(()),
        ]
        + Reduce.scratch(dm, w),
        compiler_params=pltpu.CompilerParams(collective_id=2, has_side_effects=True, vmem_limit_bytes=VMEM),
    )(gp, dq, dk, dv, packed, tokens, gain[None], vec)


def place_grads(coords, done, mode):
    _, q, w = done.shape
    e = q // 2
    dm = 4 * q
    lanes = w // 4

    def body(c_ref, f_ref, *outs):
        for off in range(8):
            y = lax.bitwise_xor(c_ref[0], off >> 2)
            x = lax.bitwise_xor(c_ref[1], (off >> 1) & 1)
            k = lax.bitwise_xor(c_ref[2], off & 1)
            for part in range(2):
                val = f_ref[off, part * e : (part + 1) * e, :].astype(F32)
                block = x * 2 + y if part == 0 else 4 + y * 2 + x
                rows = pl.ds(pl.multiple_of(block * e, e), e)
                if mode == "up":
                    outs[0][rows, pl.ds(pl.multiple_of(k * w, w), w)] = val
                elif mode == "down":
                    outs[0][pl.ds(pl.multiple_of(k * w, w), w), rows] = val.T
                else:
                    at = pl.ds(pl.multiple_of(k * lanes, lanes), lanes)
                    for m in range(3):
                        outs[m][rows, at] = val[:, m * lanes : (m + 1) * lanes]
                    outs[3][at, rows] = val[:, 3 * lanes :].T

    if mode == "up":
        shapes = [(dm, 2 * w)]
    elif mode == "down":
        shapes = [(2 * w, dm)]
    else:
        shapes = [(dm, w // 2)] * 3 + [(w // 2, dm)]
    return pl.pallas_call(
        body,
        in_specs=[pl.BlockSpec(memory_space=pltpu.SMEM), pl.BlockSpec(memory_space=pltpu.VMEM)],
        out_specs=[pl.BlockSpec(memory_space=pltpu.VMEM)] * len(shapes),
        out_shape=[jax.ShapeDtypeStruct(s, F32) for s in shapes],
        compiler_params=pltpu.CompilerParams(vmem_limit_bytes=VMEM),
        cost_estimate=pl.CostEstimate(flops=0, bytes_accessed=12 * dm * w, transcendentals=0),
    )(coords, done)


def relative(stack, z):
    return jnp.roll(stack, -z, axis=0)


def core_first(v, core, axis):
    return jnp.where(core == 0, v, jnp.flip(v, axis))


def gather_any(shard, z):
    return relative(lax.all_gather(shard, "mp", axis=0, tiled=False), z)


def reduce_any(half, z, core):
    zero = jnp.zeros_like(half)
    v = jnp.stack([jnp.where(core == 0, half, zero), jnp.where(core == 1, half, zero)], axis=2)
    v = jnp.roll(jnp.moveaxis(v, 1, 0), z, axis=0)
    v = lax.psum_scatter(v, "mp", scatter_dimension=0, tiled=True)[0]
    return lax.psum(v, "dp").astype(F32).reshape(half.shape[0], -1)


def local(
    tokens,
    segments,
    ln1_gain,
    ln1_bias,
    w_query,
    b_query,
    w_key,
    w_value,
    b_value,
    w_out,
    b_out,
    ln2_gain,
    ln2_bias,
    w_up,
    b_up,
    w_down,
    b_down,
    cotangent,
):
    rows, dm = tokens.shape
    cw = w_query.shape[1]
    ffw = w_up.shape[1]
    mp = lax.axis_size("mp")
    dp = lax.axis_size("dp")
    fast = mp == 4 and dp == 8 and rows % 256 == 0 and cw == 2 * PAIR and rows < LONGEST <= 2 * rows
    z = lax.axis_index("mp")
    me = lax.axis_index("dp")
    core = lax.rem(me, 2)
    x = lax.rem(me // 2, 2)
    y = me // 4
    f32 = lambda v: v.astype(F32)

    near = -(-LONGEST // rows)
    own = (near - 1) * rows
    win = own + rows + 2 * HALO
    is_near = z < near
    seg_parts = [
        jnp.where(is_near, lax.dynamic_slice_in_dim(segments, lax.rem(z + j, near) * rows, rows), -1)
        for j in range(1, near)
    ]
    seg_own = lax.dynamic_slice_in_dim(segments, z * rows, rows)
    seg_prev = lax.dynamic_slice_in_dim(segments, jnp.maximum(z * rows - HALO, 0), HALO)
    seg_next = lax.dynamic_slice_in_dim(segments, jnp.minimum((z + 1) * rows, segments.shape[0] - HALO), HALO)
    seg_far = jnp.concatenate(seg_parts)
    seg_far = jnp.concatenate([seg_far[:-HALO], jnp.where(is_near, seg_far[-HALO:], seg_prev)])
    has_next = jnp.logical_and(z >= near - 1, z < mp - 1)
    seg_win = jnp.concatenate(
        [seg_far, seg_own, jnp.where(has_next, seg_next, -1), jnp.full((HALO,), -1, segments.dtype)]
    )
    kseg, qseg = seg_win[None, :], seg_own[:, None]
    info = jnp.stack([is_near.astype(jnp.int32), core]).astype(jnp.int32)

    pack = jnp.concatenate([w_query, w_key, w_value, w_out.T], axis=1)
    hw = mp * ffw // 2
    if fast:
        small = jnp.stack([f32(v) for v in (ln1_gain, ln1_bias, ln2_gain, ln2_bias, b_out, b_down)])
        bias = f32(jnp.concatenate([b_query, b_value, b_up]))[None]
        (
            packed, n1_t, n2_t, cot_t, ghb_t, q, k, v, attn, lse, g_attn, active, g_upper, g_b_up, g_hidden, output, done
        ) = front_call(tokens, cotangent, pack, w_up, w_down, bias, small, qseg, kseg, own)
        done_d, done_u, gp, dq, dk, dv = back_call(
            cot_t, active, n2_t, g_upper, ghb_t, n1_t, q, k, v, attn, g_attn, lse, qseg, kseg, own, near
        )
        sums = [done[0]]
    else:
        halo = [
            lax.ppermute(tokens, "mp", [((i + j) % near, i) for i in range(near)]) for j in range(1, near)
        ]
        before = lax.ppermute(tokens[-HALO:], "mp", [(i - 1, i) for i in range(near, mp)])
        behind = lax.ppermute(tokens[:HALO], "mp", [(i + 1, i) for i in range(near - 1, mp - 1)])
        small_vec = jnp.concatenate([b_query, b_value, b_up])
        vecs = relative(lax.all_gather(small_vec, "mp", axis=0, tiled=False), z)
        bq_all, bv_all = vecs[:, :cw], vecs[:, cw : 2 * cw]
        bu_all = vecs[:, 2 * cw :].reshape(mp, 2, ffw // 2).transpose(1, 0, 2)
        bu_all = core_first(bu_all, core, 0).reshape(mp * ffw)

        packed, up_all, down_all = (gather_any(w, z) for w in (pack, w_up, w_down))

        far = jnp.concatenate(halo, axis=0)
        far = jnp.concatenate([far[:-HALO], far[-HALO:] + before], axis=0)
        tok_win = jnp.concatenate([far, tokens, behind, jnp.zeros((HALO, dm), tokens.dtype)], axis=0)
        hat_win, inv_win = norm_rows(f32(tok_win))
        n1w = (hat_win * f32(ln1_gain) + f32(ln1_bias)).astype(BF16)
        q, k, v = qkv_call(n1w, packed, bq_all, bv_all, own, rows, cw)
        attn, lse = attn_fwd_call(info, q, k, v, qseg, kseg, own)
        hidden, n2 = out_call(attn, packed, tokens, b_out, ln2_gain, ln2_bias)
        output, g_n2, active, g_upper, g_b_up = ffn_call(
            info[1:], n2, hidden, cotangent, up_all, down_all, bu_all, b_down, 2
        )

        gout = f32(cotangent)
        hat2, inv2 = norm_rows(hidden)

        def norm_back(g, hat, inv, gain):
            gg = g * gain
            first = jnp.mean(gg, axis=1, keepdims=True)
            second = jnp.mean(gg * hat, axis=1, keepdims=True)
            return inv * (gg - first - hat * second), jnp.sum(g * hat, axis=0), jnp.sum(g, axis=0)

        g_hidden, g_gain2, g_bias2 = norm_back(g_n2, hat2, inv2, f32(ln2_gain))
        g_hidden = g_hidden + gout
        ghb = g_hidden.astype(BF16)

        g_attn = jnp.stack([dot_nn(ghb, packed[d, :, 3 * cw :]).astype(BF16) for d in range(mp)])
        dq, dk, dv = attn_bwd_call(info, q, k, v, attn, g_attn, lse, qseg, kseg, own)
        n1 = n1w[own : own + rows]
        sums = [jnp.sum(g_hidden, axis=0), g_gain2, g_bias2, jnp.sum(gout, axis=0)]
    halves = dq.shape[0]

    def shards(v, width):
        if v.shape[0] == 2:
            v = core_first(v.reshape(2, mp, width // 2), core, 0).transpose(1, 0, 2)
        return jnp.roll(v.reshape(mp, width), z, axis=0).reshape(mp * width)

    gbq = shards(jnp.sum(f32(dq), axis=1), cw)
    gbv = shards(jnp.sum(f32(dv), axis=1), cw)
    gbu = core_first(g_b_up.reshape(2, mp, ffw // 2), core, 0).transpose(1, 0, 2)
    gbu = jnp.roll(gbu.reshape(mp, ffw), z, axis=0).reshape(-1)
    sums = sums + [gbq, gbv, gbu]
    if fast:
        vec = jnp.concatenate([jnp.zeros((2 * dm,), F32)] + sums)[None]
        done_p, g_in, vec = finish_call(gp, dq, dk, dv, packed, tokens, ln1_gain, vec, own)
        vec = vec[0]
        g_tokens = g_in + g_hidden
        coords = jnp.stack([y, x, core]).astype(jnp.int32)
        (g_w_down,) = place_grads(coords, done_d, "down")
        (g_w_up,) = place_grads(coords, done_u, "up")
        g_w_query, g_w_key, g_w_value, g_w_out = place_grads(coords, done_p, "pack")
    else:
        g_own, g_far, g_next = norm1_back_call(dq, dk, dv, packed, info, own)
        back = g_own
        for j in range(1, near):
            part = g_far[(j - 1) * rows : j * rows]
            back = back + f32(lax.ppermute(part, "mp", [(i, (i + j) % near) for i in range(near)]))
        to_prev = f32(lax.ppermute(g_far[-HALO:], "mp", [(i, i - 1) for i in range(near, mp)]))
        to_next = f32(lax.ppermute(g_next, "mp", [(i, i + 1) for i in range(near - 1, mp - 1)]))
        back = jnp.concatenate([back[:HALO] + to_next, back[HALO:-HALO], back[-HALO:] + to_prev], axis=0)
        hat1 = hat_win[own : own + rows]
        inv1 = inv_win[own : own + rows]
        g_in, g_gain1, g_bias1 = norm_back(back, hat1, inv1, f32(ln1_gain))
        g_tokens = g_in + g_hidden

        other = lambda v: lax.ppermute(v, "dp", [(i, i - i % 2 + (i + 1) % 2) for i in range(dp)])
        hw = mp * ffw // 2

        def pair_grad(left, right):
            return (dot_tn(left, right[:, :hw]) + dot_tn(other(left), other(right[:, hw:]))).astype(BF16)

        gd = pair_grad(cotangent, active)
        gu = pair_grad(n2, g_upper)
        g_w_up = reduce_any(gu.reshape(dm, mp, ffw // 2), z, core)
        g_w_down = reduce_any(gd.reshape(dm, mp, ffw // 2), z, core).T

        def whole_grad(left, right, name=None):
            v = dot_tn(left, right).astype(BF16).reshape(dm, mp, cw)
            v = jnp.roll(jnp.moveaxis(v, 1, 0), z, axis=0)
            v = lax.psum_scatter(v, "mp", scatter_dimension=0, tiled=True)[0]
            return lax.psum(v, "dp").astype(F32)

        def whole(v):
            if halves == 1:
                return v[0]
            v = v.reshape(2, v.shape[1], mp, cw // 2).transpose(1, 2, 0, 3)
            return core_first(v, core, 2).reshape(v.shape[0], mp * cw)

        g_w_query = whole_grad(n1, whole(dq))
        g_w_key = whole_grad(n1w, whole(dk))
        g_w_value = whole_grad(n1w, whole(dv))
        g_w_out = whole_grad(ghb, attn.transpose(1, 0, 2).reshape(rows, mp * cw)).T

        vec = lax.psum(jnp.concatenate([g_gain1, g_bias1] + sums), ("dp", "mp"))
    g_gain1, g_bias1, g_b_out, g_gain2, g_bias2, g_b_down = (vec[i * dm : (i + 1) * dm] for i in range(6))
    at = 6 * dm
    g_b_query = lax.dynamic_slice_in_dim(vec, at + z * cw, cw)
    g_b_value = lax.dynamic_slice_in_dim(vec, at + mp * cw + z * cw, cw)
    g_b_up = lax.dynamic_slice_in_dim(vec, at + 2 * mp * cw + z * ffw, ffw)
    return (
        output,
        g_tokens,
        g_gain1,
        g_bias1,
        g_w_query,
        g_b_query,
        g_w_key,
        g_w_value,
        g_b_value,
        g_w_out,
        g_b_out,
        g_gain2,
        g_bias2,
        g_w_up,
        g_b_up,
        g_w_down,
        g_b_down,
    )


def solution(mesh):
    in_specs = (
        P(("dp", "mp"), None),
        P("dp"),
        P(),
        P(),
        P(None, "mp"),
        P("mp"),
        P(None, "mp"),
        P(None, "mp"),
        P("mp"),
        P("mp", None),
        P(),
        P(),
        P(),
        P(None, "mp"),
        P("mp"),
        P("mp", None),
        P(),
        P(("dp", "mp"), None),
    )
    out_specs = (
        P(("dp", "mp"), None),
        P(("dp", "mp"), None),
        P(),
        P(),
        P(None, "mp"),
        P("mp"),
        P(None, "mp"),
        P(None, "mp"),
        P("mp"),
        P("mp", None),
        P(),
        P(),
        P(),
        P(None, "mp"),
        P("mp"),
        P("mp", None),
        P(),
    )
    return jax.shard_map(local, mesh=mesh, in_specs=in_specs, out_specs=out_specs, check_vma=False)
```

```python
import functools

import jax
import jax.numpy as jnp
from jax import lax
from jax.experimental import pallas as pl
from jax.experimental.pallas import tpu as pltpu
from jax.sharding import PartitionSpec as P

HEAD_DIM = 64
LONGEST = 900
HALO = 64
PAIR = 128
SPAN = 400
EPS = 1e-06
NEG = -1e30
VMEM = 60 * 1024 * 1024
VMEM_ALL = 67043328
F32 = jnp.float32
BF16 = jnp.bfloat16


def dot_nn(a, b):
    return lax.dot_general(a, b, (((1,), (0,)), ((), ())), preferred_element_type=F32)


def dot_nt(a, b):
    return lax.dot_general(a, b, (((1,), (1,)), ((), ())), preferred_element_type=F32)


def dot_tn(a, b):
    return lax.dot_general(a, b, (((0,), (0,)), ((), ())), preferred_element_type=F32)


def barrier(*xs):
    return lax.optimization_barrier(xs)


def params(*sem, **kw):
    return pltpu.CompilerParams(dimension_semantics=sem, vmem_limit_bytes=VMEM, **kw)


def norm_rows(x):
    mean = jnp.mean(x, axis=1, keepdims=True)
    cent = x - mean
    inv = lax.rsqrt(jnp.mean(cent * cent, axis=1, keepdims=True) + EPS)
    return cent * inv, inv


def qkv_call(n1w, packed, b_q, b_v, own, rows, cw):
    n, dm, _ = packed.shape
    win = n1w.shape[0]

    def body(x_ref, w_ref, bq_ref, bv_ref, q_ref, k_ref, v_ref):
        x = x_ref[...]
        q_ref[0] = (dot_nn(x[own : own + rows], w_ref[0, :, 0:cw]) + bq_ref[0].astype(F32)).astype(BF16)
        k_ref[0] = dot_nn(x, w_ref[0, :, cw : 2 * cw]).astype(BF16)
        v_ref[0] = (dot_nn(x, w_ref[0, :, 2 * cw : 3 * cw]) + bv_ref[0].astype(F32)).astype(BF16)

    return pl.pallas_call(
        body,
        grid=(n,),
        in_specs=[
            pl.BlockSpec((win, dm), lambda d: (0, 0)),
            pl.BlockSpec((1, dm, 4 * cw), lambda d: (d, 0, 0)),
            pl.BlockSpec((1, 1, cw), lambda d: (d, 0, 0)),
            pl.BlockSpec((1, 1, cw), lambda d: (d, 0, 0)),
        ],
        out_specs=[
            pl.BlockSpec((1, rows, cw), lambda d: (d, 0, 0)),
            pl.BlockSpec((1, win, cw), lambda d: (d, 0, 0)),
            pl.BlockSpec((1, win, cw), lambda d: (d, 0, 0)),
        ],
        out_shape=[
            jax.ShapeDtypeStruct((n, rows, cw), BF16),
            jax.ShapeDtypeStruct((n, win, cw), BF16),
            jax.ShapeDtypeStruct((n, win, cw), BF16),
        ],
        compiler_params=params("arbitrary"),
        cost_estimate=pl.CostEstimate(
            flops=2 * n * dm * cw * (rows + 2 * win), bytes_accessed=2 * (n * dm * 4 * cw + win * dm), transcendentals=0
        ),
    )(n1w, packed, b_q[:, None, :], b_v[:, None, :])


def blocks_of(rows, own, win, big):
    if big:
        step = min(256, rows)
        return [(s, step, 0, win) for s in range(0, rows, step)]
    return [(s, 128, own + s - 128, 384) for s in range(0, rows, 128)]


def attn_fwd_call(is_big, q, k, v, qseg, kseg, own):
    n, rows, cw = q.shape
    win = k.shape[1]
    pairs = cw // PAIR

    def work(big, q_ref, k_ref, v_ref, qs_ref, ks_ref, o_ref, l_ref):
        for qs, qn, ks, kn in blocks_of(rows, own, win, big):
            mask = qs_ref[qs : qs + qn, :] == ks_ref[:, ks : ks + kn]
            for h in range(2):
                lanes = slice(h * HEAD_DIM, (h + 1) * HEAD_DIM)
                qh = q_ref[0, qs : qs + qn, lanes] * BF16(HEAD_DIM**-0.5)
                s = jnp.where(mask, dot_nt(qh, k_ref[0, ks : ks + kn, lanes]), NEG)
                top = jnp.max(s, axis=1, keepdims=True)
                p = jnp.exp(s - top)
                total = jnp.sum(p, axis=1, keepdims=True)
                o = dot_nn(p.astype(BF16), v_ref[0, ks : ks + kn, lanes])
                o_ref[0, qs : qs + qn, lanes] = (o / total).astype(BF16)
                l_ref[0, qs : qs + qn, h : h + 1] = top + jnp.log(total)

    def body(big_ref, *refs):
        @pl.when(big_ref[0] == 1)
        def _():
            work(True, *refs)

        @pl.when(big_ref[0] == 0)
        def _():
            work(False, *refs)

    return pl.pallas_call(
        body,
        grid_spec=pltpu.PrefetchScalarGridSpec(
            num_scalar_prefetch=1,
            grid=(n, pairs),
            in_specs=[
                pl.BlockSpec((1, rows, PAIR), lambda d, p, *_: (d, 0, p)),
                pl.BlockSpec((1, win, PAIR), lambda d, p, *_: (d, 0, p)),
                pl.BlockSpec((1, win, PAIR), lambda d, p, *_: (d, 0, p)),
                pl.BlockSpec((rows, 1), lambda d, p, *_: (0, 0)),
                pl.BlockSpec((1, win), lambda d, p, *_: (0, 0)),
            ],
            out_specs=[
                pl.BlockSpec((1, rows, PAIR), lambda d, p, *_: (d, 0, p)),
                pl.BlockSpec((1, rows, 2), lambda d, p, *_: (d * pairs + p, 0, 0)),
            ],
        ),
        out_shape=[
            jax.ShapeDtypeStruct((n, rows, cw), BF16),
            jax.ShapeDtypeStruct((n * pairs, rows, 2), F32),
        ],
        compiler_params=params("arbitrary", "arbitrary"),
        cost_estimate=pl.CostEstimate(
            flops=16 * n * rows * win * cw, bytes_accessed=2 * n * cw * (2 * rows + 2 * win), transcendentals=n * rows * win * 4
        ),
    )(is_big, q, k, v, qseg, kseg)


def attn_bwd_call(info, q, k, v, attn, gattn, lse, qseg, kseg, own):
    n, rows, cw = q.shape
    win = k.shape[1]
    pairs = cw // PAIR
    scale = HEAD_DIM**-0.5

    def work(big, q_ref, k_ref, v_ref, a_ref, g_ref, l_ref, qs_ref, ks_ref, dq_ref, dk_ref, dv_ref, dkt, dvt):
        if not big:
            dkt[...] = jnp.zeros_like(dkt)
            dvt[...] = jnp.zeros_like(dvt)
        for i, (qs, qn, ks, kn) in enumerate(blocks_of(rows, own, win, big)):
            mask = qs_ref[qs : qs + qn, :] == ks_ref[:, ks : ks + kn]
            for h in range(2):
                lanes = slice(h * HEAD_DIM, (h + 1) * HEAD_DIM)
                qh = q_ref[0, qs : qs + qn, lanes] * BF16(scale)
                kh = k_ref[0, ks : ks + kn, lanes]
                gh = g_ref[0, qs : qs + qn, lanes]
                s = jnp.where(mask, dot_nt(qh, kh) - l_ref[0, qs : qs + qn, h : h + 1], NEG)
                p = jnp.exp(s)
                dp = dot_nt(gh, v_ref[0, ks : ks + kn, lanes])
                delta = jnp.sum(
                    gh.astype(F32) * a_ref[0, qs : qs + qn, lanes].astype(F32), axis=1, keepdims=True
                )
                ds = (p * (dp - delta)).astype(BF16)
                dq_ref[0, qs : qs + qn, lanes] = (dot_nn(ds, kh) * scale).astype(BF16)
                dk = dot_tn(qh, ds)
                dv = dot_tn(gh, p.astype(BF16))
                if big and i == 0:
                    dkt[lanes, :] = dk
                    dvt[lanes, :] = dv
                else:
                    dkt[lanes, ks : ks + kn] += dk
                    dvt[lanes, ks : ks + kn] += dv
        dk_ref[0] = dkt[...].T.astype(BF16)
        dv_ref[0] = dvt[...].T.astype(BF16)

    def body(info_ref, *refs):
        @pl.when(info_ref[0] == 1)
        def _():
            work(True, *refs)

        @pl.when(info_ref[0] == 0)
        def _():
            work(False, *refs)

    if pairs > 1:

        def put(d, p, info):
            rel = lax.bitwise_xor(p // (pairs // 2), info[1])
            return (rel, 0, d * (pairs // 2) + p % (pairs // 2))

        half_shape = (2, rows, n * cw // 2)
        half_win = (2, win, n * cw // 2)
    else:

        def put(d, p, info):
            return (0, 0, d)

        half_shape = (1, rows, n * cw)
        half_win = (1, win, n * cw)
    return pl.pallas_call(
        body,
        grid_spec=pltpu.PrefetchScalarGridSpec(
            num_scalar_prefetch=1,
            grid=(n, pairs),
            in_specs=[
                pl.BlockSpec((1, rows, PAIR), lambda d, p, *_: (d, 0, p)),
                pl.BlockSpec((1, win, PAIR), lambda d, p, *_: (d, 0, p)),
                pl.BlockSpec((1, win, PAIR), lambda d, p, *_: (d, 0, p)),
                pl.BlockSpec((1, rows, PAIR), lambda d, p, *_: (d, 0, p)),
                pl.BlockSpec((1, rows, PAIR), lambda d, p, *_: (d, 0, p)),
                pl.BlockSpec((1, rows, 2), lambda d, p, *_: (d * pairs + p, 0, 0)),
                pl.BlockSpec((rows, 1), lambda d, p, *_: (0, 0)),
                pl.BlockSpec((1, win), lambda d, p, *_: (0, 0)),
            ],
            out_specs=[
                pl.BlockSpec((1, rows, PAIR), put),
                pl.BlockSpec((1, win, PAIR), put),
                pl.BlockSpec((1, win, PAIR), put),
            ],
            scratch_shapes=[pltpu.VMEM((PAIR, win), F32), pltpu.VMEM((PAIR, win), F32)],
        ),
        out_shape=[
            jax.ShapeDtypeStruct(half_shape, BF16),
            jax.ShapeDtypeStruct(half_win, BF16),
            jax.ShapeDtypeStruct(half_win, BF16),
        ],
        compiler_params=params("arbitrary", "arbitrary"),
        cost_estimate=pl.CostEstimate(
            flops=40 * n * rows * win * cw, bytes_accessed=2 * n * cw * (4 * rows + 4 * win), transcendentals=n * rows * win * 4
        ),
    )(info, q, k, v, attn, gattn, lse, qseg, kseg)


def out_call(attn, packed, resid, b_out, gain, bias):
    n, rows, cw = attn.shape
    dm = packed.shape[1]

    def body(a_ref, w_ref, x_ref, bo_ref, g_ref, b_ref, h_ref, n_ref):
        d = pl.program_id(0)
        part = dot_nt(a_ref[0], w_ref[0])

        @pl.when(d == 0)
        def _():
            h_ref[...] = part + x_ref[...].astype(F32) + bo_ref[...].astype(F32)

        @pl.when(d > 0)
        def _():
            h_ref[...] += part

        @pl.when(d == n - 1)
        def _():
            hat, _ = norm_rows(h_ref[...])
            n_ref[...] = (hat * g_ref[...].astype(F32) + b_ref[...].astype(F32)).astype(BF16)

    full = lambda d: (0, 0)
    return pl.pallas_call(
        body,
        grid=(n,),
        in_specs=[
            pl.BlockSpec((1, rows, cw), lambda d: (d, 0, 0)),
            pl.BlockSpec((1, dm, cw), lambda d: (d, 0, 3)),
            pl.BlockSpec((rows, dm), full),
            pl.BlockSpec((1, dm), full),
            pl.BlockSpec((1, dm), full),
            pl.BlockSpec((1, dm), full),
        ],
        out_specs=[pl.BlockSpec((rows, dm), full), pl.BlockSpec((rows, dm), full)],
        out_shape=[jax.ShapeDtypeStruct((rows, dm), F32), jax.ShapeDtypeStruct((rows, dm), BF16)],
        compiler_params=params("arbitrary"),
        cost_estimate=pl.CostEstimate(flops=2 * n * rows * cw * dm, bytes_accessed=2 * n * dm * cw, transcendentals=0),
    )(attn, packed, resid, b_out[None], gain[None], bias[None])


def ffn_call(core, n2, hidden, cot, w_up, w_down, b_up, b_down, halves):
    rows, dm = n2.shape
    n, _, ffw = w_up.shape
    tile = ffw // halves

    def body(core_ref, x_ref, h_ref, c_ref, wu_ref, wd_ref, bu_ref, bd_ref, o_ref, gn_ref, a_ref, gu_ref, gb_ref, acc):
        t = pl.program_id(0)
        u = dot_nn(x_ref[...], wu_ref[0]) + bu_ref[...].astype(F32)
        cdf = 0.5 * (1.0 + lax.erf(u * 0.7071067811865476))
        act = (u * cdf).astype(BF16)
        slope = cdf + u * jnp.exp(-0.5 * u * u) * 0.3989422804014327
        a_ref[...] = act
        grad = dot_nt(c_ref[...], wd_ref[0]) * slope
        gu = grad.astype(BF16)
        gu_ref[...] = gu
        gb_ref[...] = jnp.sum(gu.astype(F32), axis=0, keepdims=True)
        out = dot_nn(act, wd_ref[0])
        gn = dot_nt(gu, wu_ref[0])

        @pl.when(t == 0)
        def _():
            acc[...] = h_ref[...] + bd_ref[...].astype(F32) + out
            gn_ref[...] = gn

        @pl.when(t > 0)
        def _():
            acc[...] += out
            gn_ref[...] += gn

        @pl.when(t == n * halves - 1)
        def _():
            o_ref[...] = acc[...].astype(BF16)

    full = lambda t, c: (0, 0)

    def part(t, c):
        return lax.bitwise_xor(t // n, c[0]) if halves > 1 else 0

    return pl.pallas_call(
        body,
        grid_spec=pltpu.PrefetchScalarGridSpec(
            num_scalar_prefetch=1,
            grid=(n * halves,),
            in_specs=[
                pl.BlockSpec((rows, dm), full),
                pl.BlockSpec((rows, dm), full),
                pl.BlockSpec((rows, dm), full),
                pl.BlockSpec((1, dm, tile), lambda t, c: (t % n, 0, part(t, c))),
                pl.BlockSpec((1, tile, dm), lambda t, c: (t % n, part(t, c), 0)),
                pl.BlockSpec((1, tile), lambda t, c: (0, t)),
                pl.BlockSpec((1, dm), full),
            ],
            out_specs=[
                pl.BlockSpec((rows, dm), full),
                pl.BlockSpec((rows, dm), full),
                pl.BlockSpec((rows, tile), lambda t, c: (0, t)),
                pl.BlockSpec((rows, tile), lambda t, c: (0, t)),
                pl.BlockSpec((1, tile), lambda t, c: (0, t)),
            ],
            scratch_shapes=[pltpu.VMEM((rows, dm), F32)],
        ),
        out_shape=[
            jax.ShapeDtypeStruct((rows, dm), BF16),
            jax.ShapeDtypeStruct((rows, dm), F32),
            jax.ShapeDtypeStruct((rows, n * ffw), BF16),
            jax.ShapeDtypeStruct((rows, n * ffw), BF16),
            jax.ShapeDtypeStruct((1, n * ffw), F32),
        ],
        compiler_params=params("arbitrary"),
        cost_estimate=pl.CostEstimate(
            flops=8 * rows * dm * n * ffw, bytes_accessed=4 * n * dm * ffw, transcendentals=2 * rows * n * ffw
        ),
    )(core, n2, hidden, cot, w_up, w_down, b_up[None], b_down[None])


def norm1_back_call(dq, dk, dv, packed, info, own):
    halves, rows, _ = dq.shape
    n, dm, four = packed.shape
    cw = four // 4
    win = dk.shape[1]
    width = cw // halves

    def body(info_ref, dq_ref, dk_ref, dv_ref, w_ref, o_ref, h_ref, t_ref, acc):
        step = pl.program_id(0)

        def weight(which, j):
            at = lax.bitwise_xor(j, info_ref[1]) if halves > 1 else 0
            return w_ref[0, :, pl.ds(pl.multiple_of(which * cw + at * width, width), width)]

        left = jnp.concatenate([r[j] for r in (dk_ref, dv_ref) for j in range(halves)], axis=1)
        right = jnp.concatenate([weight(m, j) for m in (1, 2) for j in range(halves)], axis=1)
        part = dot_nt(left, right)
        left = jnp.concatenate([dq_ref[j] for j in range(halves)], axis=1)
        right = jnp.concatenate([weight(0, j) for j in range(halves)], axis=1)
        mine = dot_nt(left, right)

        @pl.when(step == 0)
        def _():
            acc[...] = part

        @pl.when(step > 0)
        def _():
            acc[...] += part

        acc[own : own + rows, :] += mine

        @pl.when(step == n - 1)
        def _():
            o_ref[...] = acc[own : own + rows, :]
            h_ref[...] = acc[0:own, :].astype(BF16)
            t_ref[...] = acc[own + rows : own + rows + HALO, :].astype(BF16)

    full = lambda s, info: (0, 0)
    return pl.pallas_call(
        body,
        grid_spec=pltpu.PrefetchScalarGridSpec(
            num_scalar_prefetch=1,
            grid=(n,),
            in_specs=[
                pl.BlockSpec((halves, rows, width), lambda s, info: (0, 0, s)),
                pl.BlockSpec((halves, win, width), lambda s, info: (0, 0, s)),
                pl.BlockSpec((halves, win, width), lambda s, info: (0, 0, s)),
                pl.BlockSpec((1, dm, four), lambda s, info: (s, 0, 0)),
            ],
            out_specs=[
                pl.BlockSpec((rows, dm), full),
                pl.BlockSpec((own, dm), full),
                pl.BlockSpec((HALO, dm), full),
            ],
            scratch_shapes=[pltpu.VMEM((win, dm), F32)],
        ),
        out_shape=[
            jax.ShapeDtypeStruct((rows, dm), F32),
            jax.ShapeDtypeStruct((own, dm), BF16),
            jax.ShapeDtypeStruct((HALO, dm), BF16),
        ],
        compiler_params=params("arbitrary"),
        cost_estimate=pl.CostEstimate(
            flops=2 * n * cw * dm * (rows + 2 * win), bytes_accessed=2 * n * cw * (3 * dm + rows + 2 * win), transcendentals=0
        ),
    )(info, dq, dk, dv, packed)


MESH = pl.DeviceIdType.MESH


class Place:
    def __init__(self):
        self.me = lax.axis_index("dp")
        self.z = lax.axis_index("mp")
        self.k = lax.rem(self.me, 2)
        self.x = lax.rem(self.me // 2, 2)
        self.y = self.me // 4
        self.me_k = self.me + 1 - 2 * self.k
        self.me_x = self.me + 2 - 4 * self.x
        self.me_y = self.me + 4 - 8 * self.y
        self.me_xy = self.me_x + 4 - 8 * self.y
        self.core = {"dp": self.me_k, "mp": self.z}
        self.by_x = {"dp": self.me_x, "mp": self.z}
        self.by_y = {"dp": self.me_y, "mp": self.z}

    def along(self, d):
        return {"dp": self.me, "mp": lax.rem(self.z + d, 4)}

    def meet(self):
        sem = pltpu.get_barrier_semaphore()
        for dev in (self.core, self.by_x, self.by_y, self.along(1), self.along(2), self.along(3)):
            pl.semaphore_signal(sem, inc=1, device_id=dev, device_id_type=MESH)
        pl.semaphore_wait(sem, 6)


class Wire:
    def __init__(self, send, recv, dev):
        self.send, self.recv, self.dev = send, recv, dev

    def start(self, slot, src, dst, dev):
        copy = pltpu.make_async_remote_copy(
            src_ref=src, dst_ref=dst, send_sem=self.send.at[slot], recv_sem=self.recv.at[slot],
            device_id=dev, device_id_type=MESH,
        )
        copy.start()

    def sent(self, slot, ref):
        pltpu.make_async_remote_copy(
            src_ref=ref, dst_ref=ref, send_sem=self.send.at[slot], recv_sem=self.recv.at[slot],
            device_id=dict(self.dev), device_id_type=MESH,
        ).wait_send()

    def landed(self, slot, ref, dev):
        pltpu.make_async_remote_copy(
            src_ref=ref, dst_ref=ref, send_sem=self.send.at[slot], recv_sem=self.recv.at[slot],
            device_id=dev, device_id_type=MESH,
        ).wait_recv()


def gather_steps(place, wire, base, shard, whole):
    step = shard.shape[0] // 8
    half = step // 2

    def rows(who, at=0, size=step):
        return pl.ds(pl.multiple_of(who * step + at, half), size)

    def slot(d, kind):
        return base + (d - 1) * 9 + kind

    def begin(d):
        wire.start(slot(d, 0), shard.at[rows(place.me)], whole.at[d, rows(place.me)], place.along(4 - d))

    def first(d):
        mine = whole.at[d, rows(place.me)]
        wire.landed(slot(d, 0), mine, place.along(d))
        wire.start(slot(d, 2), mine, mine, place.by_x)
        wire.start(slot(d, 3), mine, mine, place.by_y)
        wire.start(slot(d, 1), mine, mine, place.core)

    def second(d):
        got = whole.at[d, rows(place.me_x)]
        wire.landed(slot(d, 2), got, place.by_x)
        part = whole.at[d, rows(place.me_x, 0, half)]
        wire.start(slot(d, 4), part, part, place.by_y)
        wire.start(slot(d, 6), got, got, place.core)
        got = whole.at[d, rows(place.me_y)]
        wire.landed(slot(d, 3), got, place.by_y)
        part = whole.at[d, rows(place.me_y, half, half)]
        wire.start(slot(d, 5), part, part, place.by_x)
        wire.start(slot(d, 7), got, got, place.core)

    def third(d):
        wire.landed(slot(d, 4), whole.at[d, rows(place.me_xy, 0, half)], place.by_y)
        wire.landed(slot(d, 5), whole.at[d, rows(place.me_xy, half, half)], place.by_x)
        got = whole.at[d, rows(place.me_xy)]
        wire.start(slot(d, 8), got, got, place.core)

    def done(d):
        flip = 1 - 2 * place.k
        for kind, who in ((1, place.me), (6, place.me_x), (7, place.me_y), (8, place.me_xy)):
            wire.landed(slot(d, kind), whole.at[d, rows(who + flip)], place.core)

    def drain():
        for d in (1, 2, 3):
            for kind in range(9):
                wire.sent(slot(d, kind), whole.at[d, pl.ds(0, half if kind in (4, 5) else step)])

    return begin, first, second, third, done, drain


def front_call(tokens, cot, pack, w_up, w_down, small, qseg, kseg, own):
    rows, dm = tokens.shape
    cw = pack.shape[1] // 4
    ffw = w_up.shape[1]
    n = 4
    tile = ffw // 2
    hw = n * tile
    win = own + rows + 2 * HALO
    pairs = cw // PAIR
    strip = 128
    per = rows // strip
    scale = HEAD_DIM**-0.5
    length = small.shape[1] - 6 * dm
    base = 6

    def body(
        tok_ref, cot_ref, pack_ref, up_ref, down_ref, small_ref, qs_ref, ks_ref,
        packed, n1t, n2t, cott, ghbt, q_ref, k_ref, v_ref, a_ref, l_ref, ga_ref, act_ref, gup_ref, gbu_ref, gh_ref, o_ref, sum_ref,
        up, down, n1, hid, n2, acc, act, gup, biases, xs, xr, ls, fs,
    ):
        place = Place()
        core, z = place.k, place.z
        long, takes_prev, takes_next = z < 2, z >= 2, jnp.logical_and(z >= 1, z < 3)
        swap = {"dp": place.me, "mp": lax.rem(z + 1, 2)}
        left_dev = {"dp": place.me, "mp": lax.rem(z + 3, 4)}
        right_dev = {"dp": place.me, "mp": lax.rem(z + 1, 4)}
        wire = Wire(xs, xr, place.core)
        local = [
            pltpu.make_async_copy(src, dst, ls.at[i])
            for i, (src, dst) in enumerate(
                ((tok_ref, n1.at[own : own + rows]), (pack_ref, packed.at[0]), (up_ref, up.at[0]), (down_ref, down.at[0]))
            )
        ]
        for c in local:
            c.start()
        place.meet()
        bias_ref = small_ref.at[:, 6 * dm : 6 * dm + length]
        for d in (1, 2, 3):
            wire.start(d - 1, bias_ref, biases.at[d], place.along(4 - d))

        @pl.when(z == 0)
        def _():
            wire.start(3, tok_ref, n1.at[0:own], swap)

        @pl.when(z == 1)
        def _():
            wire.start(3, tok_ref.at[0:SPAN], n1.at[0:SPAN], swap)

        @pl.when(takes_next)
        def _():
            wire.start(4, tok_ref.at[rows - HALO : rows], n1.at[own - HALO : own], right_dev)

        @pl.when(takes_prev)
        def _():
            wire.start(5, tok_ref.at[0:HALO], n1.at[own + rows : own + rows + HALO], left_dev)

        groups = [
            gather_steps(place, wire, base + 27 * g, src, dst)
            for g, (src, dst) in enumerate(((pack_ref, packed), (up_ref, up), (down_ref, down)))
        ]
        for g in range(3):
            for d in (1, 2, 3):
                groups[g][0](d)

        def near_shard(i):
            return lax.rem(4 - z + i, 3) + 1

        items = [(0, 0), (0, 1), (0, 2), (1, 0), (2, 0), (1, 1), (2, 1), (1, 2), (2, 2)]

        def relay(i):
            for lag in range(3):
                if 0 <= i - lag < len(items):
                    g, j = items[i - lag]
                    groups[g][1 + lag](near_shard(j))

        def arrived(j, *which):
            for g in which:
                groups[g][4](near_shard(j))

        def turns(i, table):
            for t, f in table.items():

                @pl.when(i == t)
                def _():
                    f()

        def shard_at(k):
            return near_shard(k + 2) * ((k + 3) // 4)

        def strip_at(i, start=0):
            return pl.ds(pl.multiple_of(start + i * strip, strip), strip)

        row = lambda i: small_ref[:, i * dm : (i + 1) * dm]

        @pl.when(z == 0)
        def _():
            n1[SPAN:own, :] = jnp.zeros((own - SPAN, dm), BF16)

        @pl.when(takes_prev)
        def _():
            n1[0 : own - HALO, :] = jnp.zeros((own - HALO, dm), BF16)

        @pl.when(jnp.logical_not(takes_next))
        def _():
            n1[own + rows : own + rows + HALO, :] = jnp.zeros((HALO, dm), BF16)

        n1[own + rows + HALO :, :] = jnp.zeros((HALO, dm), BF16)
        biases[0] = bias_ref[...]

        def turn_cot(i, carry):
            cott[:, strip_at(i)] = cot_ref[strip_at(i), :].astype(F32).T.astype(BF16)
            return carry

        lax.fori_loop(0, per, turn_cot, 0)

        def norm1(i):
            at = strip_at(i)
            x = n1[at, :].astype(F32)
            hat, _ = norm_rows(x)
            val = hat * row(0) + row(1)
            n1[at, :] = val.astype(BF16)
            n1t[:, at] = val.T.astype(BF16)
            return x

        def norm_own(i, carry):
            hid[strip_at(i), :] = norm1(own // strip + i) + row(4)
            return carry

        def norm_far(i, carry):
            norm1(i)
            return carry

        local[0].wait()
        lax.fori_loop(0, per, norm_own, 0)
        for c in local[1:]:
            c.wait()
        relay(0)

        @pl.when(z == 0)
        def _():
            wire.landed(3, n1.at[0:SPAN], swap)

        @pl.when(z == 1)
        def _():
            wire.landed(3, n1.at[0:own], swap)

        @pl.when(takes_prev)
        def _():
            wire.landed(4, n1.at[own - HALO : own], left_dev)

        @pl.when(takes_next)
        def _():
            wire.landed(5, n1.at[own + rows : own + rows + HALO], right_dev)

        lax.fori_loop(0, own // strip, norm_far, 0)
        norm1((own + rows) // strip)
        for d in (1, 2, 3):
            wire.landed(d - 1, biases.at[d], place.along(d))
        relay(1)

        def attend(big, d, p):
            at = pl.ds(pl.multiple_of(p * PAIR, PAIR), PAIR)
            for qs, qn, ks, kn in blocks_of(rows, own, win, big):
                mask = qs_ref[qs : qs + qn, :] == ks_ref[:, ks : ks + kn]
                qq, kk, vv = q_ref[d, qs : qs + qn, at], k_ref[d, ks : ks + kn, at], v_ref[d, ks : ks + kn, at]
                outs = []
                for h in range(2):
                    lanes = slice(h * HEAD_DIM, (h + 1) * HEAD_DIM)
                    s = jnp.where(mask, dot_nt(qq[:, lanes] * BF16(scale), kk[:, lanes]), NEG)
                    top = jnp.max(s, axis=1, keepdims=True)
                    pr = jnp.exp(s - top)
                    total = jnp.sum(pr, axis=1, keepdims=True)
                    outs.append(dot_nn(pr.astype(BF16), vv[:, lanes]) / total)
                    l_ref[d * pairs + p, qs : qs + qn, h : h + 1] = top + jnp.log(total)
                a_ref[d, qs : qs + qn, at] = jnp.concatenate(outs, axis=1).astype(BF16)

        def heads(kk, carry):
            turns(kk, {j + 1: functools.partial(arrived, j, 0) for j in range(3)})
            d = shard_at(kk)
            q_ref[d] = (dot_nn(n1[own : own + rows, :], packed[d, :, 0:cw]) + biases[d, :, 0:cw]).astype(BF16)
            k_ref[d] = dot_nn(n1[...], packed[d, :, cw : 2 * cw]).astype(BF16)
            v_ref[d] = (dot_nn(n1[...], packed[d, :, 2 * cw : 3 * cw]) + biases[d, :, cw : 2 * cw]).astype(BF16)

            def one(p, inner):
                @pl.when(long)
                def _():
                    attend(True, d, p)

                @pl.when(jnp.logical_not(long))
                def _():
                    attend(False, d, p)

                turns(kk * pairs + p, {pairs * j: functools.partial(relay, 2 + j) for j in range(4)})
                return inner

            lax.fori_loop(0, pairs, one, 0)
            hid[...] += dot_nt(a_ref[d], packed[d, :, 3 * cw : 4 * cw])
            return carry

        lax.fori_loop(0, n, heads, 0)
        relay(6)

        def norm2(i, carry):
            at = strip_at(i)
            hidden = hid[at, :]
            hat, _ = norm_rows(hidden)
            val = hat * row(2) + row(3)
            n2[at, :] = val.astype(BF16)
            n2t[:, at] = val.T.astype(BF16)
            acc[at, :] = hidden + row(5)
            return carry

        lax.fori_loop(0, per, norm2, 0)

        def out_copies(i, col):
            at = pl.ds(pl.multiple_of(col, tile), tile)
            return (
                pltpu.make_async_copy(act.at[:, at], act_ref.at[:, at], fs.at[i]),
                pltpu.make_async_copy(gup.at[:, at], gup_ref.at[:, at], fs.at[2 * n + i]),
            )

        def column(i):
            return lax.rem(i, 2) * hw + shard_at(i // 2) * tile

        def feed(i, carry):
            turns(
                i,
                {
                    1: lambda: relay(7),
                    2: lambda: arrived(0, 1, 2),
                    3: lambda: relay(8),
                    4: lambda: (arrived(1, 1, 2), relay(9)),
                    5: lambda: relay(10),
                    6: lambda: arrived(2, 1, 2),
                },
            )
            d = shard_at(i // 2)
            part = lax.rem(lax.rem(i, 2) + core, 2) * tile
            at = pl.ds(pl.multiple_of(part, tile), tile)
            to = pl.ds(pl.multiple_of(column(i), tile), tile)
            u = dot_nn(n2[...], up[d, :, at]) + biases[d, :, pl.ds(pl.multiple_of(2 * cw + part, PAIR), tile)]
            cdf = 0.5 * (1.0 + lax.erf(u * 0.7071067811865476))
            val = (u * cdf).astype(BF16)
            slope = cdf + u * jnp.exp(-0.5 * u * u) * 0.3989422804014327
            act[:, to] = val
            gu = (dot_nt(cot_ref[...], down[d, at, :]) * slope).astype(BF16)
            gup[:, to] = gu
            gbu_ref[:, to] = jnp.sum(gu.astype(F32), axis=0, keepdims=True)
            for c in out_copies(i, column(i)):
                c.start()
            acc[...] += dot_nn(val, down[d, at, :])
            gn = dot_nt(gu, up[d, :, at])

            @pl.when(i == 0)
            def _():
                gh_ref[...] = gn

            @pl.when(i > 0)
            def _():
                gh_ref[...] += gn

            return carry

        lax.fori_loop(0, 2 * n, feed, 0)
        sum_ref[...] = jnp.zeros_like(sum_ref)

        def back2(i, carry):
            at = strip_at(i)
            o_ref[at, :] = acc[at, :].astype(BF16)
            hat, inv = norm_rows(hid[at, :])
            g = gh_ref[at, :]
            gout = cot_ref[at, :].astype(F32)
            gg = g * row(2)
            first = jnp.mean(gg, axis=1, keepdims=True)
            second = jnp.mean(gg * hat, axis=1, keepdims=True)
            val = inv * (gg - first - hat * second) + gout
            gh_ref[at, :] = val
            n2[at, :] = val.astype(BF16)
            ghbt[:, at] = val.T.astype(BF16)
            for j, v in enumerate((val, g * hat, g, gout)):
                sum_ref[:, j * dm : (j + 1) * dm] += jnp.sum(v, axis=0, keepdims=True)
            return carry

        lax.fori_loop(0, per, back2, 0)

        def back_attn(d, carry):
            ga_ref[d] = dot_nn(n2[...], packed[d, :, 3 * cw : 4 * cw]).astype(BF16)
            return carry

        lax.fori_loop(0, n, back_attn, 0)
        for i in range(2 * n):
            for c in out_copies(i, 0):
                c.wait()
        for group in groups:
            group[5]()
        for d in (1, 2, 3):
            wire.sent(d - 1, biases.at[d])

        @pl.when(z == 0)
        def _():
            wire.sent(3, n1.at[0:own])

        @pl.when(z == 1)
        def _():
            wire.sent(3, n1.at[0:SPAN])

        @pl.when(takes_next)
        def _():
            wire.sent(4, n1.at[0:HALO])

        @pl.when(takes_prev)
        def _():
            wire.sent(5, n1.at[0:HALO])

    hbm = pl.BlockSpec(memory_space=pl.ANY)
    vmem = pl.BlockSpec(memory_space=pltpu.VMEM)
    half = lambda *shape: jax.ShapeDtypeStruct(shape, BF16)
    full = lambda *shape: jax.ShapeDtypeStruct(shape, F32)
    b16 = lambda *shape: pltpu.VMEM(shape, BF16)
    b32 = lambda *shape: pltpu.VMEM(shape, F32)
    slots = base + 27 * 3
    return pl.pallas_call(
        body,
        in_specs=[hbm, vmem, hbm, hbm, hbm, vmem, vmem, vmem],
        out_specs=[vmem] * 11 + [hbm] * 2 + [vmem] * 4,
        out_shape=[
            half(n, dm, 4 * cw), half(dm, win), half(dm, rows), half(dm, rows), half(dm, rows),
            half(n, rows, cw), half(n, win, cw), half(n, win, cw), half(n, rows, cw), full(n * pairs, rows, 2), half(n, rows, cw),
            half(rows, 2 * hw), half(rows, 2 * hw), full(1, 2 * hw), full(rows, dm), half(rows, dm), full(1, 4 * dm),
        ],
        scratch_shapes=[
            b16(n, dm, ffw), b16(n, ffw, dm), b16(win, dm), b32(rows, dm), b16(rows, dm), b32(rows, dm),
            b16(rows, 2 * hw), b16(rows, 2 * hw), b32(n, 1, length),
            pltpu.SemaphoreType.DMA((slots,)), pltpu.SemaphoreType.DMA((slots,)), pltpu.SemaphoreType.DMA((4,)),
            pltpu.SemaphoreType.DMA((4 * n,)),
        ],
        compiler_params=pltpu.CompilerParams(collective_id=0, has_side_effects=True, vmem_limit_bytes=VMEM_ALL),
    )(tokens, cot, pack, w_up, w_down, small, qseg, kseg)


class Reduce:
    SLOTS = 32

    @staticmethod
    def scratch(dm, w):
        q = dm // 4
        e = q // 2
        return [
            pltpu.VMEM((4, q, w), BF16),
            pltpu.VMEM((4, q, w), BF16),
            pltpu.VMEM((4, e, w), BF16),
            pltpu.VMEM((4, e, w), BF16),
            pltpu.VMEM((3, q, w), BF16),
            pltpu.SemaphoreType.DMA((Reduce.SLOTS,)),
            pltpu.SemaphoreType.DMA((Reduce.SLOTS,)),
        ]

    def __init__(self, place, grad, landing, scratch):
        self.place, self.g, self.f = place, grad, landing
        self.ra1, self.rb1, self.ra2, self.rb2, self.zb = scratch[:5]
        self.wire = Wire(scratch[5], scratch[6], place.core)
        self.q = grad.shape[0] // 4
        self.e = self.q // 2
        self.w = grad.shape[1] // 4

    def at(self, base, big, small=None):
        start = base * 2 * self.q + big * self.q + (0 if small is None else small * self.e)
        return pl.ds(pl.multiple_of(start, self.e), self.q if small is None else self.e)

    def eighth(self, small):
        return pl.ds(pl.multiple_of(small * self.e, self.e), self.e)

    def cols(self, d):
        return pl.ds(pl.multiple_of(d * self.w, self.w), self.w)

    def one(self, d):
        p, wire = self.place, self.wire
        wire.start(d, self.g.at[self.at(0, 1 - p.x), self.cols(d)], self.ra1.at[d], p.by_x)
        wire.start(4 + d, self.g.at[self.at(1, 1 - p.y), self.cols(d)], self.rb1.at[d], p.by_y)

    def two(self, d):
        p, wire, c = self.place, self.wire, self.cols(d)
        for slot, buf, to, at, mine, dev, nxt in (
            (0, self.ra1, self.ra2, self.at(0, p.x, 1 - p.y), self.eighth(1 - p.y), p.by_x, p.by_y),
            (4, self.rb1, self.rb2, self.at(1, p.y, 1 - p.x), self.eighth(1 - p.x), p.by_y, p.by_x),
        ):
            wire.landed(slot + d, buf.at[d], dev)
            self.g[at, c] = (self.g[at, c].astype(F32) + buf[d, mine, :].astype(F32)).astype(BF16)
            wire.start(8 + slot + d, self.g.at[at, c], to.at[d], nxt)

    def sums(self, d):
        p, wire, c = self.place, self.wire, self.cols(d)
        wire.landed(8 + d, self.ra2.at[d], p.by_y)
        wire.landed(12 + d, self.rb2.at[d], p.by_x)
        up = (
            self.g[self.at(0, p.x, p.y), c].astype(F32)
            + self.ra1[d, self.eighth(p.y), :].astype(F32)
            + self.ra2[d].astype(F32)
        )
        low = (
            self.g[self.at(1, p.y, p.x), c].astype(F32)
            + self.rb1[d, self.eighth(p.x), :].astype(F32)
            + self.rb2[d].astype(F32)
        )
        return up, low

    def three(self, d):
        p, wire, c, e = self.place, self.wire, self.cols(d), self.e
        up, low = self.sums(d)
        for part, (at, val) in enumerate(((self.at(0, p.x, p.y), up), (self.at(1, p.y, p.x), low))):
            self.g[at, c] = val.astype(BF16)
            wire.start(
                16 + 12 * part + d, self.g.at[at, c], self.zb.at[d - 1, part * e : (part + 1) * e], p.along(d)
            )

    def last(self):
        p, wire, e = self.place, self.wire, self.e
        up, low = self.sums(0)
        for s in (1, 2, 3):
            wire.landed(16 + s, self.zb.at[s - 1, 0:e], p.along(4 - s))
            wire.landed(28 + s, self.zb.at[s - 1, e : 2 * e], p.along(4 - s))
            up = up + self.zb[s - 1, 0:e].astype(F32)
            low = low + self.zb[s - 1, e : 2 * e].astype(F32)
        self.f[0, 0:e] = up.astype(BF16)
        self.f[0, e : 2 * e] = low.astype(BF16)
        wire.start(20, self.f.at[0], self.f.at[2], p.by_x)
        wire.start(21, self.f.at[0], self.f.at[4], p.by_y)
        wire.start(22, self.f.at[0], self.f.at[1], p.core)

    def four(self):
        p, wire, e = self.place, self.wire, self.e
        wire.landed(20, self.f.at[2], p.by_x)
        wire.start(23, self.f.at[2, 0:e], self.f.at[6, 0:e], p.by_y)
        wire.start(25, self.f.at[2], self.f.at[3], p.core)
        wire.landed(21, self.f.at[4], p.by_y)
        wire.start(24, self.f.at[4, e : 2 * e], self.f.at[6, e : 2 * e], p.by_x)
        wire.start(26, self.f.at[4], self.f.at[5], p.core)

    def five(self):
        p, wire, e = self.place, self.wire, self.e
        wire.landed(23, self.f.at[6, 0:e], p.by_y)
        wire.landed(24, self.f.at[6, e : 2 * e], p.by_x)
        wire.start(27, self.f.at[6], self.f.at[7], p.core)

    def six(self):
        for slot, to in ((22, 1), (25, 3), (26, 5), (27, 7)):
            self.wire.landed(slot, self.f.at[to], self.place.core)
        e, sent = self.e, self.wire.sent
        for d in range(4):
            sent(d, self.ra1.at[d])
            sent(4 + d, self.rb1.at[d])
            sent(8 + d, self.ra2.at[d])
            sent(12 + d, self.rb2.at[d])
        for d in range(1, 4):
            sent(16 + d, self.zb.at[d - 1, 0:e])
            sent(28 + d, self.zb.at[d - 1, 0:e])
        for slot in (20, 21, 22, 25, 26, 27):
            sent(slot, self.f.at[0])
        for slot in (23, 24):
            sent(slot, self.f.at[0, 0:e])

    def sweep(self):
        return [
            functools.partial(f, d)
            for f, d in (
                (self.two, 1), (self.two, 2), (self.three, 1), (self.two, 3), (self.three, 2), (self.two, 0), (self.three, 3)
            )
        ]

    def tail(self):
        return [self.last, self.four, self.five, self.six]


def back_call(cot, act, n2, gup, ghb, n1w, q, k, v, attn, gattn, lse, qseg, kseg, own, near):
    n, rows, cw = q.shape
    win = k.shape[1]
    dm = cot.shape[0]
    hw = act.shape[1] // 2
    half = n * cw // 2
    w = hw // 4
    pairs = cw // PAIR
    scale = HEAD_DIM**-0.5
    each = len(Reduce.scratch(dm, w))

    def body(
        cot_ref, act_ref, n2_ref, gup_ref, ghb_ref, n1_ref, q_ref, k_ref, v_ref, a_ref, g_ref, l_ref, qs_ref, ks_ref,
        fd, fu, gp_ref, dq, dk, dv,
        cot2, act2, n22, gup2, ghb2, n12, gd, gu, dq_o, dk_o, dv_o, at2, dkt, dvt, xs, xr, ls, *scr,
    ):
        place = Place()
        core = place.k
        big_z = place.z < near
        wire = Wire(xs, xr, place.core)
        whole = (
            (cot_ref, cot2, rows), (n2_ref, n22, rows), (ghb_ref, ghb2, rows), (n1_ref, n12, win)
        )
        mixed = ((act_ref, act2), (gup_ref, gup2))
        local = [pltpu.make_async_copy(src, dst.at[:, 0:wide], ls.at[i]) for i, (src, dst, wide) in enumerate(whole)]
        local += [pltpu.make_async_copy(src.at[:, 0:hw], dst.at[0:rows], ls.at[4 + i]) for i, (src, dst) in enumerate(mixed)]
        for i in (0, 4, 1, 5, 2, 3):
            local[i].start()
        place.meet()

        def give_whole(i):
            src, dst, wide = whole[i]
            wire.start(i, src, dst.at[:, wide : 2 * wide], place.core)

        def give_mixed(i):
            src, dst = mixed[i]
            wire.start(4 + i, src.at[:, hw : 2 * hw], dst.at[rows : 2 * rows], place.core)

        def take(*which):
            for i in which:
                local[i].wait()
                if i < 4:
                    dst, wide = whole[i][1:]
                    wire.landed(i, dst.at[:, wide : 2 * wide], place.core)
                else:
                    wire.landed(i, mixed[i - 4][1].at[rows : 2 * rows], place.core)

        give_whole(0)
        give_mixed(0)
        give_whole(1)
        give_mixed(1)
        give_whole(2)
        give_whole(3)
        for d in range(n):
            to = slice(d * PAIR, (d + 1) * PAIR)
            theirs = pl.ds(pl.multiple_of((1 - core) * PAIR, PAIR), PAIR)
            mine = pl.ds(pl.multiple_of(core * PAIR, PAIR), PAIR)
            wire.start(6 + d, a_ref.at[d, :, theirs], at2.at[rows : 2 * rows, to], place.core)
            at2[0:rows, to] = a_ref[d, :, mine]

        down = Reduce(place, gd, fd, scr[:each])
        up = Reduce(place, gu, fu, scr[each : 2 * each])

        def make(red, grad, left, right):
            def step(i, carry):
                d = lax.rem(i + 1, 4)
                c = pl.ds(pl.multiple_of(d * w, w), w)
                grad[:, c] = dot_nn(left[...], right[:, c]).astype(BF16)
                red.one(d)
                return carry

            lax.fori_loop(0, 4, step, 0)

        take(0, 4)
        make(down, gd, cot2, act2)
        take(1, 5)
        make(up, gu, n22, gup2)

        def work(big, d, p):
            at = pl.ds(pl.multiple_of(p * PAIR, PAIR), PAIR)
            to = pl.ds(pl.multiple_of(d * PAIR, PAIR), PAIR)
            rel = lax.rem(p + core, 2)
            if not big:
                dkt[...] = jnp.zeros_like(dkt)
                dvt[...] = jnp.zeros_like(dvt)
            for i, (qs, qn, ks, kn) in enumerate(blocks_of(rows, own, win, big)):
                mask = qs_ref[qs : qs + qn, :] == ks_ref[:, ks : ks + kn]
                qq, kk, vv = q_ref[d, qs : qs + qn, at], k_ref[d, ks : ks + kn, at], v_ref[d, ks : ks + kn, at]
                gg = g_ref[d, qs : qs + qn, at]
                prod = gg.astype(F32) * a_ref[d, qs : qs + qn, at].astype(F32)
                dqs = []
                for h in range(2):
                    lanes = slice(h * HEAD_DIM, (h + 1) * HEAD_DIM)
                    qh, kh, gh = qq[:, lanes] * BF16(scale), kk[:, lanes], gg[:, lanes]
                    s = jnp.where(mask, dot_nt(qh, kh) - l_ref[d * pairs + p, qs : qs + qn, h : h + 1], NEG)
                    pr = jnp.exp(s)
                    dp = dot_nt(gh, vv[:, lanes])
                    delta = jnp.sum(prod[:, lanes], axis=1, keepdims=True)
                    ds = (pr * (dp - delta)).astype(BF16)
                    dqs.append(dot_nn(ds, kh) * scale)
                    gk = dot_tn(qh, ds)
                    gv = dot_tn(gh, pr.astype(BF16))
                    if big and i == 0:
                        dkt[lanes, :] = gk
                        dvt[lanes, :] = gv
                    else:
                        dkt[lanes, ks : ks + kn] += gk
                        dvt[lanes, ks : ks + kn] += gv
                dq[rel, qs : qs + qn, to] = jnp.concatenate(dqs, axis=1).astype(BF16)
            dk[rel, :, to] = dkt[...].T.astype(BF16)
            dv[rel, :, to] = dvt[...].T.astype(BF16)

        todo = down.sweep() + up.sweep()
        turns = [todo[2 * i : 2 * i + 2] for i in range(n * pairs)]
        turns[-1] = todo[2 * (n * pairs - 1) :]

        def head_pair(i, carry):
            d, p = i // pairs, lax.rem(i, pairs)

            @pl.when(big_z)
            def _():
                work(True, d, p)

            @pl.when(jnp.logical_not(big_z))
            def _():
                work(False, d, p)

            for t, steps in enumerate(turns):
                if steps:

                    @pl.when(i == t)
                    def _():
                        for f in steps:
                            f()

            return carry

        lax.fori_loop(0, n * pairs, head_pair, 0)
        halves = ((dq, dq_o), (dk, dk_o), (dv, dv_o))
        for i, (src, dst) in enumerate(halves):
            wire.start(10 + i, src.at[1], dst, place.core)
        down.last()
        take(2, 3)
        for d in range(n):
            wire.landed(6 + d, at2.at[rows : 2 * rows, d * PAIR : (d + 1) * PAIR], place.core)

        def put(m, val):
            for d in range(n):
                at = d * w + m * PAIR
                act2[:, at : at + PAIR] = val[:, d * PAIR : (d + 1) * PAIR].astype(BF16)

        put(3, dot_nn(ghb2[...], at2[...]))
        up.last()
        down.four()
        wire.landed(10, dq_o, place.core)
        put(0, dot_nn(n12[:, own : own + rows], dq[0]) + dot_nn(n12[:, win + own : win + own + rows], dq_o[...]))
        down.five()
        up.four()
        wire.landed(11, dk_o, place.core)
        put(1, dot_nn(n12[:, 0:win], dk[0]) + dot_nn(n12[:, win : 2 * win], dk_o[...]))
        up.five()
        wire.landed(12, dv_o, place.core)
        put(2, dot_nn(n12[:, 0:win], dv[0]) + dot_nn(n12[:, win : 2 * win], dv_o[...]))
        out = pltpu.make_async_copy(act2, gp_ref, ls.at[6])
        out.start()
        down.six()
        up.six()
        for i in range(4):
            wire.sent(i, whole[i][0])
        for i in range(2):
            wire.sent(4 + i, act2.at[0:rows])
        for d in range(n):
            wire.sent(6 + d, at2.at[0:rows, 0:PAIR])
        for i in range(3):
            wire.sent(10 + i, halves[i][1])
        out.wait()

    hbm = pl.BlockSpec(memory_space=pl.ANY)
    vmem = pl.BlockSpec(memory_space=pltpu.VMEM)
    shaped = lambda *shape: jax.ShapeDtypeStruct(shape, BF16)
    buf = lambda *shape: pltpu.VMEM(shape, BF16)
    return pl.pallas_call(
        body,
        in_specs=[hbm] * 6 + [vmem] * 8,
        out_specs=[vmem, vmem, hbm, vmem, vmem, vmem],
        out_shape=[
            shaped(8, dm // 4, w), shaped(8, dm // 4, w), shaped(dm, hw), shaped(2, rows, half), shaped(2, win, half), shaped(2, win, half)
        ],
        scratch_shapes=[
            buf(dm, 2 * rows), buf(2 * rows, hw), buf(dm, 2 * rows), buf(2 * rows, hw), buf(dm, 2 * rows), buf(dm, 2 * win),
            buf(dm, hw), buf(dm, hw), buf(rows, half), buf(win, half), buf(win, half), buf(2 * rows, half),
            pltpu.VMEM((PAIR, win), F32), pltpu.VMEM((PAIR, win), F32),
            pltpu.SemaphoreType.DMA((13,)), pltpu.SemaphoreType.DMA((13,)), pltpu.SemaphoreType.DMA((7,)),
        ]
        + Reduce.scratch(dm, w) * 2,
        compiler_params=pltpu.CompilerParams(collective_id=1, has_side_effects=True, vmem_limit_bytes=VMEM_ALL),
    )(cot, act, n2, gup, ghb, n1w, q, k, v, attn, gattn, lse, qseg, kseg)


def finish_call(gp, dq, dk, dv, packed, tokens, gain, vec, own):
    n, dm, four = packed.shape
    cw = four // 4
    rows = tokens.shape[0]
    win = dk.shape[1]
    cols = gp.shape[1]
    w = cols // 4
    length = vec.shape[1]
    each = len(Reduce.scratch(dm, w))
    strip = 128

    def body(
        gp_ref, dq_ref, dk_ref, dv_ref, w_ref, x_ref, gain_ref, vec_ref,
        fp, gi_ref, sum_ref,
        g, acc, far_out, next_out, far_in, prev_in, next_in, va, vr, vz, xs, xr, ls, *scr,
    ):
        place = Place()
        core, z = place.k, place.z
        load = pltpu.make_async_copy(gp_ref, g, ls)
        load.start()
        place.meet()
        wire = Wire(xs, xr, place.core)
        red = Reduce(place, g, fp, scr)
        load.wait()
        for d in (1, 2, 3, 0):
            red.one(d)

        def dots(d, carry):
            def weight(which, j):
                at = which * cw + lax.rem(j + core, 2) * PAIR
                return w_ref[d, :, pl.ds(pl.multiple_of(at, PAIR), PAIR)]

            to = pl.ds(pl.multiple_of(d * PAIR, PAIR), PAIR)
            left = jnp.concatenate([r[j, :, to] for r in (dk_ref, dv_ref) for j in range(2)], axis=1)
            right = jnp.concatenate([weight(m, j) for m in (1, 2) for j in range(2)], axis=1)
            part = dot_nt(left, right)
            left = jnp.concatenate([dq_ref[j, :, to] for j in range(2)], axis=1)
            right = jnp.concatenate([weight(0, j) for j in range(2)], axis=1)
            mine = dot_nt(left, right)

            @pl.when(d == 0)
            def _():
                acc[...] = part

            @pl.when(d > 0)
            def _():
                acc[...] += part

            acc[own : own + rows, :] += mine
            for t, f in ((2, red.sweep()[0]), (3, red.sweep()[1])):

                @pl.when(d == t)
                def _():
                    f()

            return carry

        lax.fori_loop(0, n, dots, 0)

        long, gives_prev, gives_next = z < 2, z >= 2, jnp.logical_and(z >= 1, z < 3)
        swap = {"dp": place.me, "mp": lax.rem(z + 1, 2)}
        left_dev = {"dp": place.me, "mp": lax.rem(z + 3, 4)}
        right_dev = {"dp": place.me, "mp": lax.rem(z + 1, 4)}
        far_out[...] = acc[0:own, :].astype(BF16)
        next_out[...] = acc[own + rows : own + rows + HALO, :].astype(BF16)

        @pl.when(long)
        def _():
            wire.start(0, far_out, far_in, swap)

        @pl.when(gives_prev)
        def _():
            wire.start(1, far_out.at[own - HALO : own], prev_in, left_dev)

        @pl.when(gives_next)
        def _():
            wire.start(2, next_out, next_in, right_dev)

        for f in red.sweep()[2:]:
            f()

        @pl.when(long)
        def _():
            wire.landed(0, far_in, swap)
            acc[own : own + rows, :] += far_in[...].astype(F32)

        @pl.when(gives_next)
        def _():
            wire.landed(1, prev_in, right_dev)
            acc[own + rows - HALO : own + rows, :] += prev_in[...].astype(F32)

        @pl.when(gives_prev)
        def _():
            wire.landed(2, next_in, left_dev)
            acc[own : own + HALO, :] += next_in[...].astype(F32)

        va[0] = vec_ref[...]
        va[0, :, 0 : 2 * dm] = jnp.zeros((1, 2 * dm), F32)
        gains = gain_ref[...].astype(F32)

        def norm(i, carry):
            at = pl.ds(pl.multiple_of(i * strip, strip), strip)
            hat, inv = norm_rows(x_ref[at, :].astype(F32))
            back = acc[pl.ds(pl.multiple_of(own + i * strip, strip), strip), :]
            gg = back * gains
            first = jnp.mean(gg, axis=1, keepdims=True)
            second = jnp.mean(gg * hat, axis=1, keepdims=True)
            gi_ref[at, :] = inv * (gg - first - hat * second)
            va[0, :, 0:dm] += jnp.sum(back * hat, axis=0, keepdims=True)
            va[0, :, dm : 2 * dm] += jnp.sum(back, axis=0, keepdims=True)
            return carry

        lax.fori_loop(0, rows // strip, norm, 0)

        hops = (place.core, place.by_x, place.by_y)
        between = (red.last, red.four, red.five)
        for i, dev in enumerate(hops):
            wire.start(3 + i, va.at[i], vr.at[i], dev)
            if i == 0:
                between[0]()
            wire.landed(3 + i, vr.at[i], dev)
            if i < 2:
                va[i + 1] = va[i] + vr[i]
            else:
                vz[0] = va[i] + vr[i]
        for d in (1, 2, 3):
            wire.start(5 + d, vz.at[0], vz.at[d], place.along(d))
        between[1]()
        between[2]()
        for d in (1, 2, 3):
            wire.landed(5 + d, vz.at[d], place.along(4 - d))
        terms = [vz[lax.rem(z - a + 4, 4)] for a in range(4)]
        sum_ref[...] = (terms[0] + terms[1]) + (terms[2] + terms[3])
        red.six()

        @pl.when(long)
        def _():
            wire.sent(0, far_out)

        @pl.when(gives_prev)
        def _():
            wire.sent(1, prev_in)

        @pl.when(gives_next)
        def _():
            wire.sent(2, next_out)

        for i in range(3):
            wire.sent(3 + i, va.at[i])
        for d in (1, 2, 3):
            wire.sent(5 + d, vz.at[0])

    hbm = pl.BlockSpec(memory_space=pl.ANY)
    vmem = pl.BlockSpec(memory_space=pltpu.VMEM)
    buf = lambda *shape: pltpu.VMEM(shape, BF16)
    return pl.pallas_call(
        body,
        in_specs=[hbm] + [vmem] * 7,
        out_specs=[vmem] * 3,
        out_shape=[
            jax.ShapeDtypeStruct((8, dm // 4, w), BF16),
            jax.ShapeDtypeStruct((rows, dm), F32),
            jax.ShapeDtypeStruct((1, length), F32),
        ],
        scratch_shapes=[
            buf(dm, cols), pltpu.VMEM((win, dm), F32),
            buf(own, dm), buf(HALO, dm), buf(own, dm), buf(HALO, dm), buf(HALO, dm),
            pltpu.VMEM((3, 1, length), F32), pltpu.VMEM((3, 1, length), F32), pltpu.VMEM((4, 1, length), F32),
            pltpu.SemaphoreType.DMA((9,)), pltpu.SemaphoreType.DMA((9,)), pltpu.SemaphoreType.DMA(()),
        ]
        + Reduce.scratch(dm, w),
        compiler_params=pltpu.CompilerParams(collective_id=2, has_side_effects=True, vmem_limit_bytes=VMEM),
    )(gp, dq, dk, dv, packed, tokens, gain[None], vec)


def place_grads(coords, down, up, pack):
    _, q, w = up.shape
    e = q // 2
    dm = 4 * q
    lanes = w // 4

    def spot(off, part, c):
        y = lax.bitwise_xor(c[0], off // 4)
        x = lax.bitwise_xor(c[1], lax.rem(off // 2, 2))
        k = lax.bitwise_xor(c[2], lax.rem(off, 2))
        return (1 - part) * (2 * x + y) + part * (4 + 2 * y + x), k

    def across(off, part, c):
        return spot(off, part, c)

    def flipped(off, part, c):
        block, k = spot(off, part, c)
        return k, block

    def body(c_ref, d_ref, u_ref, p_ref, gd_ref, gu_ref, gq_ref, gk_ref, gv_ref, go_ref):
        gd_ref[...] = d_ref[0].astype(F32).T
        gu_ref[...] = u_ref[0].astype(F32)
        val = p_ref[0].astype(F32)
        for m, ref in enumerate((gq_ref, gk_ref, gv_ref)):
            ref[...] = val[:, m * lanes : (m + 1) * lanes]
        go_ref[...] = val[:, 3 * lanes :].T

    piece = pl.BlockSpec((1, e, w), lambda off, part, c: (off, part, 0))
    return pl.pallas_call(
        body,
        grid_spec=pltpu.PrefetchScalarGridSpec(
            num_scalar_prefetch=1,
            grid=(8, 2),
            in_specs=[piece] * 3,
            out_specs=[
                pl.BlockSpec((w, e), flipped),
                pl.BlockSpec((e, w), across),
                pl.BlockSpec((e, lanes), across),
                pl.BlockSpec((e, lanes), across),
                pl.BlockSpec((e, lanes), across),
                pl.BlockSpec((lanes, e), flipped),
            ],
        ),
        out_shape=[
            jax.ShapeDtypeStruct(shape, F32)
            for shape in ((2 * w, dm), (dm, 2 * w), (dm, w // 2), (dm, w // 2), (dm, w // 2), (w // 2, dm))
        ],
        compiler_params=params("arbitrary", "arbitrary"),
        cost_estimate=pl.CostEstimate(flops=0, bytes_accessed=36 * dm * w, transcendentals=0),
    )(coords, down, up, pack)


def relative(stack, z):
    return jnp.roll(stack, -z, axis=0)


def core_first(v, core, axis):
    return jnp.where(core == 0, v, jnp.flip(v, axis))


def gather_any(shard, z):
    return relative(lax.all_gather(shard, "mp", axis=0, tiled=False), z)


def reduce_any(half, z, core):
    zero = jnp.zeros_like(half)
    v = jnp.stack([jnp.where(core == 0, half, zero), jnp.where(core == 1, half, zero)], axis=2)
    v = jnp.roll(jnp.moveaxis(v, 1, 0), z, axis=0)
    v = lax.psum_scatter(v, "mp", scatter_dimension=0, tiled=True)[0]
    return lax.psum(v, "dp").astype(F32).reshape(half.shape[0], -1)


def local(
    tokens,
    segments,
    ln1_gain,
    ln1_bias,
    w_query,
    b_query,
    w_key,
    w_value,
    b_value,
    w_out,
    b_out,
    ln2_gain,
    ln2_bias,
    w_up,
    b_up,
    w_down,
    b_down,
    cotangent,
):
    rows, dm = tokens.shape
    cw = w_query.shape[1]
    ffw = w_up.shape[1]
    mp = lax.axis_size("mp")
    dp = lax.axis_size("dp")
    fast = mp == 4 and dp == 8 and rows % 256 == 0 and cw == 2 * PAIR and rows < LONGEST <= rows + SPAN <= 2 * rows
    z = lax.axis_index("mp")
    me = lax.axis_index("dp")
    core = lax.rem(me, 2)
    x = lax.rem(me // 2, 2)
    y = me // 4
    f32 = lambda v: v.astype(F32)

    near = -(-LONGEST // rows)
    own = (near - 1) * rows
    win = own + rows + 2 * HALO
    is_near = z < near
    seg_parts = [
        jnp.where(is_near, lax.dynamic_slice_in_dim(segments, lax.rem(z + j, near) * rows, rows), -1)
        for j in range(1, near)
    ]
    seg_own = lax.dynamic_slice_in_dim(segments, z * rows, rows)
    seg_prev = lax.dynamic_slice_in_dim(segments, jnp.maximum(z * rows - HALO, 0), HALO)
    seg_next = lax.dynamic_slice_in_dim(segments, jnp.minimum((z + 1) * rows, segments.shape[0] - HALO), HALO)
    seg_far = jnp.concatenate(seg_parts)
    seg_far = jnp.concatenate([seg_far[:-HALO], jnp.where(is_near, seg_far[-HALO:], seg_prev)])
    has_next = jnp.logical_and(z >= near - 1, z < mp - 1)
    seg_win = jnp.concatenate(
        [seg_far, seg_own, jnp.where(has_next, seg_next, -1), jnp.full((HALO,), -1, segments.dtype)]
    )
    kseg, qseg = seg_win[None, :], seg_own[:, None]
    info = jnp.stack([is_near.astype(jnp.int32), core]).astype(jnp.int32)

    pack = jnp.concatenate([w_query, w_key, w_value, w_out.T], axis=1)
    hw = mp * ffw // 2
    if fast:
        small = jnp.concatenate([ln1_gain, ln1_bias, ln2_gain, ln2_bias, b_out, b_down, b_query, b_value, b_up])
        small = f32(small)[None]
        (
            packed, n1_t, n2_t, cot_t, ghb_t, q, k, v, attn, lse, g_attn, active, g_upper, g_b_up, g_hidden, output, done
        ) = front_call(tokens, cotangent, pack, w_up, w_down, small, qseg, kseg, own)
        done_d, done_u, gp, dq, dk, dv = back_call(
            cot_t, active, n2_t, g_upper, ghb_t, n1_t, q, k, v, attn, g_attn, lse, qseg, kseg, own, near
        )
        sums = [done[0]]
    else:
        halo = [
            lax.ppermute(tokens, "mp", [((i + j) % near, i) for i in range(near)]) for j in range(1, near)
        ]
        before = lax.ppermute(tokens[-HALO:], "mp", [(i - 1, i) for i in range(near, mp)])
        behind = lax.ppermute(tokens[:HALO], "mp", [(i + 1, i) for i in range(near - 1, mp - 1)])
        small_vec = jnp.concatenate([b_query, b_value, b_up])
        vecs = relative(lax.all_gather(small_vec, "mp", axis=0, tiled=False), z)
        bq_all, bv_all = vecs[:, :cw], vecs[:, cw : 2 * cw]
        bu_all = vecs[:, 2 * cw :].reshape(mp, 2, ffw // 2).transpose(1, 0, 2)
        bu_all = core_first(bu_all, core, 0).reshape(mp * ffw)

        packed, up_all, down_all = (gather_any(w, z) for w in (pack, w_up, w_down))

        far = jnp.concatenate(halo, axis=0)
        far = jnp.concatenate([far[:-HALO], far[-HALO:] + before], axis=0)
        tok_win = jnp.concatenate([far, tokens, behind, jnp.zeros((HALO, dm), tokens.dtype)], axis=0)
        hat_win, inv_win = norm_rows(f32(tok_win))
        n1w = (hat_win * f32(ln1_gain) + f32(ln1_bias)).astype(BF16)
        q, k, v = qkv_call(n1w, packed, bq_all, bv_all, own, rows, cw)
        attn, lse = attn_fwd_call(info, q, k, v, qseg, kseg, own)
        hidden, n2 = out_call(attn, packed, tokens, b_out, ln2_gain, ln2_bias)
        output, g_n2, active, g_upper, g_b_up = ffn_call(
            info[1:], n2, hidden, cotangent, up_all, down_all, bu_all, b_down, 2
        )

        gout = f32(cotangent)
        hat2, inv2 = norm_rows(hidden)

        def norm_back(g, hat, inv, gain):
            gg = g * gain
            first = jnp.mean(gg, axis=1, keepdims=True)
            second = jnp.mean(gg * hat, axis=1, keepdims=True)
            return inv * (gg - first - hat * second), jnp.sum(g * hat, axis=0), jnp.sum(g, axis=0)

        g_hidden, g_gain2, g_bias2 = norm_back(g_n2, hat2, inv2, f32(ln2_gain))
        g_hidden = g_hidden + gout
        ghb = g_hidden.astype(BF16)

        g_attn = jnp.stack([dot_nn(ghb, packed[d, :, 3 * cw :]).astype(BF16) for d in range(mp)])
        dq, dk, dv = attn_bwd_call(info, q, k, v, attn, g_attn, lse, qseg, kseg, own)
        n1 = n1w[own : own + rows]
        sums = [jnp.sum(g_hidden, axis=0), g_gain2, g_bias2, jnp.sum(gout, axis=0)]
    halves = dq.shape[0]

    def shards(v, width):
        if v.shape[0] == 2:
            v = core_first(v.reshape(2, mp, width // 2), core, 0).transpose(1, 0, 2)
        return jnp.roll(v.reshape(mp, width), z, axis=0).reshape(mp * width)

    gbq = shards(jnp.sum(f32(dq), axis=1), cw)
    gbv = shards(jnp.sum(f32(dv), axis=1), cw)
    gbu = core_first(g_b_up.reshape(2, mp, ffw // 2), core, 0).transpose(1, 0, 2)
    gbu = jnp.roll(gbu.reshape(mp, ffw), z, axis=0).reshape(-1)
    sums = sums + [gbq, gbv, gbu]
    if fast:
        vec = jnp.concatenate([jnp.zeros((2 * dm,), F32)] + sums)[None]
        done_p, g_in, vec = finish_call(gp, dq, dk, dv, packed, tokens, ln1_gain, vec, own)
        vec = vec[0]
        g_tokens = g_in + g_hidden
        coords = jnp.stack([y, x, core]).astype(jnp.int32)
        g_w_down, g_w_up, g_w_query, g_w_key, g_w_value, g_w_out = place_grads(coords, done_d, done_u, done_p)
    else:
        g_own, g_far, g_next = norm1_back_call(dq, dk, dv, packed, info, own)
        back = g_own
        for j in range(1, near):
            part = g_far[(j - 1) * rows : j * rows]
            back = back + f32(lax.ppermute(part, "mp", [(i, (i + j) % near) for i in range(near)]))
        to_prev = f32(lax.ppermute(g_far[-HALO:], "mp", [(i, i - 1) for i in range(near, mp)]))
        to_next = f32(lax.ppermute(g_next, "mp", [(i, i + 1) for i in range(near - 1, mp - 1)]))
        back = jnp.concatenate([back[:HALO] + to_next, back[HALO:-HALO], back[-HALO:] + to_prev], axis=0)
        hat1 = hat_win[own : own + rows]
        inv1 = inv_win[own : own + rows]
        g_in, g_gain1, g_bias1 = norm_back(back, hat1, inv1, f32(ln1_gain))
        g_tokens = g_in + g_hidden

        other = lambda v: lax.ppermute(v, "dp", [(i, i - i % 2 + (i + 1) % 2) for i in range(dp)])
        hw = mp * ffw // 2

        def pair_grad(left, right):
            return (dot_tn(left, right[:, :hw]) + dot_tn(other(left), other(right[:, hw:]))).astype(BF16)

        gd = pair_grad(cotangent, active)
        gu = pair_grad(n2, g_upper)
        g_w_up = reduce_any(gu.reshape(dm, mp, ffw // 2), z, core)
        g_w_down = reduce_any(gd.reshape(dm, mp, ffw // 2), z, core).T

        def whole_grad(left, right, name=None):
            v = dot_tn(left, right).astype(BF16).reshape(dm, mp, cw)
            v = jnp.roll(jnp.moveaxis(v, 1, 0), z, axis=0)
            v = lax.psum_scatter(v, "mp", scatter_dimension=0, tiled=True)[0]
            return lax.psum(v, "dp").astype(F32)

        def whole(v):
            if halves == 1:
                return v[0]
            v = v.reshape(2, v.shape[1], mp, cw // 2).transpose(1, 2, 0, 3)
            return core_first(v, core, 2).reshape(v.shape[0], mp * cw)

        g_w_query = whole_grad(n1, whole(dq))
        g_w_key = whole_grad(n1w, whole(dk))
        g_w_value = whole_grad(n1w, whole(dv))
        g_w_out = whole_grad(ghb, attn.transpose(1, 0, 2).reshape(rows, mp * cw)).T

        vec = lax.psum(jnp.concatenate([g_gain1, g_bias1] + sums), ("dp", "mp"))
    g_gain1, g_bias1, g_b_out, g_gain2, g_bias2, g_b_down = (vec[i * dm : (i + 1) * dm] for i in range(6))
    at = 6 * dm
    g_b_query = lax.dynamic_slice_in_dim(vec, at + z * cw, cw)
    g_b_value = lax.dynamic_slice_in_dim(vec, at + mp * cw + z * cw, cw)
    g_b_up = lax.dynamic_slice_in_dim(vec, at + 2 * mp * cw + z * ffw, ffw)
    return (
        output,
        g_tokens,
        g_gain1,
        g_bias1,
        g_w_query,
        g_b_query,
        g_w_key,
        g_w_value,
        g_b_value,
        g_w_out,
        g_b_out,
        g_gain2,
        g_bias2,
        g_w_up,
        g_b_up,
        g_w_down,
        g_b_down,
    )


def solution(mesh):
    in_specs = (
        P(("dp", "mp"), None),
        P("dp"),
        P(),
        P(),
        P(None, "mp"),
        P("mp"),
        P(None, "mp"),
        P(None, "mp"),
        P("mp"),
        P("mp", None),
        P(),
        P(),
        P(),
        P(None, "mp"),
        P("mp"),
        P("mp", None),
        P(),
        P(("dp", "mp"), None),
    )
    out_specs = (
        P(("dp", "mp"), None),
        P(("dp", "mp"), None),
        P(),
        P(),
        P(None, "mp"),
        P("mp"),
        P(None, "mp"),
        P(None, "mp"),
        P("mp"),
        P("mp", None),
        P(),
        P(),
        P(),
        P(None, "mp"),
        P("mp"),
        P("mp", None),
        P(),
    )
    return jax.shard_map(local, mesh=mesh, in_specs=in_specs, out_specs=out_specs, check_vma=False)
```

```python
import functools

import jax
import jax.numpy as jnp
from jax import lax
from jax.experimental import pallas as pl
from jax.experimental.pallas import tpu as pltpu
from jax.sharding import PartitionSpec as P

HEAD_DIM = 64
LONGEST = 900
HALO = 64
PAIR = 128
SPAN = 400
EPS = 1e-06
NEG = -1e30
VMEM = 60 * 1024 * 1024
VMEM_ALL = 67043328
F32 = jnp.float32
BF16 = jnp.bfloat16


def dot_nn(a, b):
    return lax.dot_general(a, b, (((1,), (0,)), ((), ())), preferred_element_type=F32)


def dot_nt(a, b):
    return lax.dot_general(a, b, (((1,), (1,)), ((), ())), preferred_element_type=F32)


def dot_tn(a, b):
    return lax.dot_general(a, b, (((0,), (0,)), ((), ())), preferred_element_type=F32)


def barrier(*xs):
    return lax.optimization_barrier(xs)


def params(*sem, **kw):
    return pltpu.CompilerParams(dimension_semantics=sem, vmem_limit_bytes=VMEM, **kw)


def norm_rows(x):
    mean = jnp.mean(x, axis=1, keepdims=True)
    cent = x - mean
    inv = lax.rsqrt(jnp.mean(cent * cent, axis=1, keepdims=True) + EPS)
    return cent * inv, inv


def qkv_call(n1w, packed, b_q, b_v, own, rows, cw):
    n, dm, _ = packed.shape
    win = n1w.shape[0]

    def body(x_ref, w_ref, bq_ref, bv_ref, q_ref, k_ref, v_ref):
        x = x_ref[...]
        q_ref[0] = (dot_nn(x[own : own + rows], w_ref[0, :, 0:cw]) + bq_ref[0].astype(F32)).astype(BF16)
        k_ref[0] = dot_nn(x, w_ref[0, :, cw : 2 * cw]).astype(BF16)
        v_ref[0] = (dot_nn(x, w_ref[0, :, 2 * cw : 3 * cw]) + bv_ref[0].astype(F32)).astype(BF16)

    return pl.pallas_call(
        body,
        grid=(n,),
        in_specs=[
            pl.BlockSpec((win, dm), lambda d: (0, 0)),
            pl.BlockSpec((1, dm, 4 * cw), lambda d: (d, 0, 0)),
            pl.BlockSpec((1, 1, cw), lambda d: (d, 0, 0)),
            pl.BlockSpec((1, 1, cw), lambda d: (d, 0, 0)),
        ],
        out_specs=[
            pl.BlockSpec((1, rows, cw), lambda d: (d, 0, 0)),
            pl.BlockSpec((1, win, cw), lambda d: (d, 0, 0)),
            pl.BlockSpec((1, win, cw), lambda d: (d, 0, 0)),
        ],
        out_shape=[
            jax.ShapeDtypeStruct((n, rows, cw), BF16),
            jax.ShapeDtypeStruct((n, win, cw), BF16),
            jax.ShapeDtypeStruct((n, win, cw), BF16),
        ],
        compiler_params=params("arbitrary"),
        cost_estimate=pl.CostEstimate(
            flops=2 * n * dm * cw * (rows + 2 * win), bytes_accessed=2 * (n * dm * 4 * cw + win * dm), transcendentals=0
        ),
    )(n1w, packed, b_q[:, None, :], b_v[:, None, :])


def blocks_of(rows, own, win, big):
    if big:
        step = min(256, rows)
        return [(s, step, 0, win) for s in range(0, rows, step)]
    return [(s, 128, own + s - 128, 384) for s in range(0, rows, 128)]


def attn_fwd_call(is_big, q, k, v, qseg, kseg, own):
    n, rows, cw = q.shape
    win = k.shape[1]
    pairs = cw // PAIR

    def work(big, q_ref, k_ref, v_ref, qs_ref, ks_ref, o_ref, l_ref):
        for qs, qn, ks, kn in blocks_of(rows, own, win, big):
            mask = qs_ref[qs : qs + qn, :] == ks_ref[:, ks : ks + kn]
            for h in range(2):
                lanes = slice(h * HEAD_DIM, (h + 1) * HEAD_DIM)
                qh = q_ref[0, qs : qs + qn, lanes] * BF16(HEAD_DIM**-0.5)
                s = jnp.where(mask, dot_nt(qh, k_ref[0, ks : ks + kn, lanes]), NEG)
                top = jnp.max(s, axis=1, keepdims=True)
                p = jnp.exp(s - top)
                total = jnp.sum(p, axis=1, keepdims=True)
                o = dot_nn(p.astype(BF16), v_ref[0, ks : ks + kn, lanes])
                o_ref[0, qs : qs + qn, lanes] = (o / total).astype(BF16)
                l_ref[0, qs : qs + qn, h : h + 1] = top + jnp.log(total)

    def body(big_ref, *refs):
        @pl.when(big_ref[0] == 1)
        def _():
            work(True, *refs)

        @pl.when(big_ref[0] == 0)
        def _():
            work(False, *refs)

    return pl.pallas_call(
        body,
        grid_spec=pltpu.PrefetchScalarGridSpec(
            num_scalar_prefetch=1,
            grid=(n, pairs),
            in_specs=[
                pl.BlockSpec((1, rows, PAIR), lambda d, p, *_: (d, 0, p)),
                pl.BlockSpec((1, win, PAIR), lambda d, p, *_: (d, 0, p)),
                pl.BlockSpec((1, win, PAIR), lambda d, p, *_: (d, 0, p)),
                pl.BlockSpec((rows, 1), lambda d, p, *_: (0, 0)),
                pl.BlockSpec((1, win), lambda d, p, *_: (0, 0)),
            ],
            out_specs=[
                pl.BlockSpec((1, rows, PAIR), lambda d, p, *_: (d, 0, p)),
                pl.BlockSpec((1, rows, 2), lambda d, p, *_: (d * pairs + p, 0, 0)),
            ],
        ),
        out_shape=[
            jax.ShapeDtypeStruct((n, rows, cw), BF16),
            jax.ShapeDtypeStruct((n * pairs, rows, 2), F32),
        ],
        compiler_params=params("arbitrary", "arbitrary"),
        cost_estimate=pl.CostEstimate(
            flops=16 * n * rows * win * cw, bytes_accessed=2 * n * cw * (2 * rows + 2 * win), transcendentals=n * rows * win * 4
        ),
    )(is_big, q, k, v, qseg, kseg)


def attn_bwd_call(info, q, k, v, attn, gattn, lse, qseg, kseg, own):
    n, rows, cw = q.shape
    win = k.shape[1]
    pairs = cw // PAIR
    scale = HEAD_DIM**-0.5

    def work(big, q_ref, k_ref, v_ref, a_ref, g_ref, l_ref, qs_ref, ks_ref, dq_ref, dk_ref, dv_ref, dkt, dvt):
        if not big:
            dkt[...] = jnp.zeros_like(dkt)
            dvt[...] = jnp.zeros_like(dvt)
        for i, (qs, qn, ks, kn) in enumerate(blocks_of(rows, own, win, big)):
            mask = qs_ref[qs : qs + qn, :] == ks_ref[:, ks : ks + kn]
            for h in range(2):
                lanes = slice(h * HEAD_DIM, (h + 1) * HEAD_DIM)
                qh = q_ref[0, qs : qs + qn, lanes] * BF16(scale)
                kh = k_ref[0, ks : ks + kn, lanes]
                gh = g_ref[0, qs : qs + qn, lanes]
                s = jnp.where(mask, dot_nt(qh, kh) - l_ref[0, qs : qs + qn, h : h + 1], NEG)
                p = jnp.exp(s)
                dp = dot_nt(gh, v_ref[0, ks : ks + kn, lanes])
                delta = jnp.sum(
                    gh.astype(F32) * a_ref[0, qs : qs + qn, lanes].astype(F32), axis=1, keepdims=True
                )
                ds = (p * (dp - delta)).astype(BF16)
                dq_ref[0, qs : qs + qn, lanes] = (dot_nn(ds, kh) * scale).astype(BF16)
                dk = dot_tn(qh, ds)
                dv = dot_tn(gh, p.astype(BF16))
                if big and i == 0:
                    dkt[lanes, :] = dk
                    dvt[lanes, :] = dv
                else:
                    dkt[lanes, ks : ks + kn] += dk
                    dvt[lanes, ks : ks + kn] += dv
        dk_ref[0] = dkt[...].T.astype(BF16)
        dv_ref[0] = dvt[...].T.astype(BF16)

    def body(info_ref, *refs):
        @pl.when(info_ref[0] == 1)
        def _():
            work(True, *refs)

        @pl.when(info_ref[0] == 0)
        def _():
            work(False, *refs)

    if pairs > 1:

        def put(d, p, info):
            rel = lax.bitwise_xor(p // (pairs // 2), info[1])
            return (rel, 0, d * (pairs // 2) + p % (pairs // 2))

        half_shape = (2, rows, n * cw // 2)
        half_win = (2, win, n * cw // 2)
    else:

        def put(d, p, info):
            return (0, 0, d)

        half_shape = (1, rows, n * cw)
        half_win = (1, win, n * cw)
    return pl.pallas_call(
        body,
        grid_spec=pltpu.PrefetchScalarGridSpec(
            num_scalar_prefetch=1,
            grid=(n, pairs),
            in_specs=[
                pl.BlockSpec((1, rows, PAIR), lambda d, p, *_: (d, 0, p)),
                pl.BlockSpec((1, win, PAIR), lambda d, p, *_: (d, 0, p)),
                pl.BlockSpec((1, win, PAIR), lambda d, p, *_: (d, 0, p)),
                pl.BlockSpec((1, rows, PAIR), lambda d, p, *_: (d, 0, p)),
                pl.BlockSpec((1, rows, PAIR), lambda d, p, *_: (d, 0, p)),
                pl.BlockSpec((1, rows, 2), lambda d, p, *_: (d * pairs + p, 0, 0)),
                pl.BlockSpec((rows, 1), lambda d, p, *_: (0, 0)),
                pl.BlockSpec((1, win), lambda d, p, *_: (0, 0)),
            ],
            out_specs=[
                pl.BlockSpec((1, rows, PAIR), put),
                pl.BlockSpec((1, win, PAIR), put),
                pl.BlockSpec((1, win, PAIR), put),
            ],
            scratch_shapes=[pltpu.VMEM((PAIR, win), F32), pltpu.VMEM((PAIR, win), F32)],
        ),
        out_shape=[
            jax.ShapeDtypeStruct(half_shape, BF16),
            jax.ShapeDtypeStruct(half_win, BF16),
            jax.ShapeDtypeStruct(half_win, BF16),
        ],
        compiler_params=params("arbitrary", "arbitrary"),
        cost_estimate=pl.CostEstimate(
            flops=40 * n * rows * win * cw, bytes_accessed=2 * n * cw * (4 * rows + 4 * win), transcendentals=n * rows * win * 4
        ),
    )(info, q, k, v, attn, gattn, lse, qseg, kseg)


def out_call(attn, packed, resid, b_out, gain, bias):
    n, rows, cw = attn.shape
    dm = packed.shape[1]

    def body(a_ref, w_ref, x_ref, bo_ref, g_ref, b_ref, h_ref, n_ref):
        d = pl.program_id(0)
        part = dot_nt(a_ref[0], w_ref[0])

        @pl.when(d == 0)
        def _():
            h_ref[...] = part + x_ref[...].astype(F32) + bo_ref[...].astype(F32)

        @pl.when(d > 0)
        def _():
            h_ref[...] += part

        @pl.when(d == n - 1)
        def _():
            hat, _ = norm_rows(h_ref[...])
            n_ref[...] = (hat * g_ref[...].astype(F32) + b_ref[...].astype(F32)).astype(BF16)

    full = lambda d: (0, 0)
    return pl.pallas_call(
        body,
        grid=(n,),
        in_specs=[
            pl.BlockSpec((1, rows, cw), lambda d: (d, 0, 0)),
            pl.BlockSpec((1, dm, cw), lambda d: (d, 0, 3)),
            pl.BlockSpec((rows, dm), full),
            pl.BlockSpec((1, dm), full),
            pl.BlockSpec((1, dm), full),
            pl.BlockSpec((1, dm), full),
        ],
        out_specs=[pl.BlockSpec((rows, dm), full), pl.BlockSpec((rows, dm), full)],
        out_shape=[jax.ShapeDtypeStruct((rows, dm), F32), jax.ShapeDtypeStruct((rows, dm), BF16)],
        compiler_params=params("arbitrary"),
        cost_estimate=pl.CostEstimate(flops=2 * n * rows * cw * dm, bytes_accessed=2 * n * dm * cw, transcendentals=0),
    )(attn, packed, resid, b_out[None], gain[None], bias[None])


def ffn_call(core, n2, hidden, cot, w_up, w_down, b_up, b_down, halves):
    rows, dm = n2.shape
    n, _, ffw = w_up.shape
    tile = ffw // halves

    def body(core_ref, x_ref, h_ref, c_ref, wu_ref, wd_ref, bu_ref, bd_ref, o_ref, gn_ref, a_ref, gu_ref, gb_ref, acc):
        t = pl.program_id(0)
        u = dot_nn(x_ref[...], wu_ref[0]) + bu_ref[...].astype(F32)
        cdf = 0.5 * (1.0 + lax.erf(u * 0.7071067811865476))
        act = (u * cdf).astype(BF16)
        slope = cdf + u * jnp.exp(-0.5 * u * u) * 0.3989422804014327
        a_ref[...] = act
        grad = dot_nt(c_ref[...], wd_ref[0]) * slope
        gu = grad.astype(BF16)
        gu_ref[...] = gu
        gb_ref[...] = jnp.sum(gu.astype(F32), axis=0, keepdims=True)
        out = dot_nn(act, wd_ref[0])
        gn = dot_nt(gu, wu_ref[0])

        @pl.when(t == 0)
        def _():
            acc[...] = h_ref[...] + bd_ref[...].astype(F32) + out
            gn_ref[...] = gn

        @pl.when(t > 0)
        def _():
            acc[...] += out
            gn_ref[...] += gn

        @pl.when(t == n * halves - 1)
        def _():
            o_ref[...] = acc[...].astype(BF16)

    full = lambda t, c: (0, 0)

    def part(t, c):
        return lax.bitwise_xor(t // n, c[0]) if halves > 1 else 0

    return pl.pallas_call(
        body,
        grid_spec=pltpu.PrefetchScalarGridSpec(
            num_scalar_prefetch=1,
            grid=(n * halves,),
            in_specs=[
                pl.BlockSpec((rows, dm), full),
                pl.BlockSpec((rows, dm), full),
                pl.BlockSpec((rows, dm), full),
                pl.BlockSpec((1, dm, tile), lambda t, c: (t % n, 0, part(t, c))),
                pl.BlockSpec((1, tile, dm), lambda t, c: (t % n, part(t, c), 0)),
                pl.BlockSpec((1, tile), lambda t, c: (0, t)),
                pl.BlockSpec((1, dm), full),
            ],
            out_specs=[
                pl.BlockSpec((rows, dm), full),
                pl.BlockSpec((rows, dm), full),
                pl.BlockSpec((rows, tile), lambda t, c: (0, t)),
                pl.BlockSpec((rows, tile), lambda t, c: (0, t)),
                pl.BlockSpec((1, tile), lambda t, c: (0, t)),
            ],
            scratch_shapes=[pltpu.VMEM((rows, dm), F32)],
        ),
        out_shape=[
            jax.ShapeDtypeStruct((rows, dm), BF16),
            jax.ShapeDtypeStruct((rows, dm), F32),
            jax.ShapeDtypeStruct((rows, n * ffw), BF16),
            jax.ShapeDtypeStruct((rows, n * ffw), BF16),
            jax.ShapeDtypeStruct((1, n * ffw), F32),
        ],
        compiler_params=params("arbitrary"),
        cost_estimate=pl.CostEstimate(
            flops=8 * rows * dm * n * ffw, bytes_accessed=4 * n * dm * ffw, transcendentals=2 * rows * n * ffw
        ),
    )(core, n2, hidden, cot, w_up, w_down, b_up[None], b_down[None])


def norm1_back_call(dq, dk, dv, packed, info, own):
    halves, rows, _ = dq.shape
    n, dm, four = packed.shape
    cw = four // 4
    win = dk.shape[1]
    width = cw // halves

    def body(info_ref, dq_ref, dk_ref, dv_ref, w_ref, o_ref, h_ref, t_ref, acc):
        step = pl.program_id(0)

        def weight(which, j):
            at = lax.bitwise_xor(j, info_ref[1]) if halves > 1 else 0
            return w_ref[0, :, pl.ds(pl.multiple_of(which * cw + at * width, width), width)]

        left = jnp.concatenate([r[j] for r in (dk_ref, dv_ref) for j in range(halves)], axis=1)
        right = jnp.concatenate([weight(m, j) for m in (1, 2) for j in range(halves)], axis=1)
        part = dot_nt(left, right)
        left = jnp.concatenate([dq_ref[j] for j in range(halves)], axis=1)
        right = jnp.concatenate([weight(0, j) for j in range(halves)], axis=1)
        mine = dot_nt(left, right)

        @pl.when(step == 0)
        def _():
            acc[...] = part

        @pl.when(step > 0)
        def _():
            acc[...] += part

        acc[own : own + rows, :] += mine

        @pl.when(step == n - 1)
        def _():
            o_ref[...] = acc[own : own + rows, :]
            h_ref[...] = acc[0:own, :].astype(BF16)
            t_ref[...] = acc[own + rows : own + rows + HALO, :].astype(BF16)

    full = lambda s, info: (0, 0)
    return pl.pallas_call(
        body,
        grid_spec=pltpu.PrefetchScalarGridSpec(
            num_scalar_prefetch=1,
            grid=(n,),
            in_specs=[
                pl.BlockSpec((halves, rows, width), lambda s, info: (0, 0, s)),
                pl.BlockSpec((halves, win, width), lambda s, info: (0, 0, s)),
                pl.BlockSpec((halves, win, width), lambda s, info: (0, 0, s)),
                pl.BlockSpec((1, dm, four), lambda s, info: (s, 0, 0)),
            ],
            out_specs=[
                pl.BlockSpec((rows, dm), full),
                pl.BlockSpec((own, dm), full),
                pl.BlockSpec((HALO, dm), full),
            ],
            scratch_shapes=[pltpu.VMEM((win, dm), F32)],
        ),
        out_shape=[
            jax.ShapeDtypeStruct((rows, dm), F32),
            jax.ShapeDtypeStruct((own, dm), BF16),
            jax.ShapeDtypeStruct((HALO, dm), BF16),
        ],
        compiler_params=params("arbitrary"),
        cost_estimate=pl.CostEstimate(
            flops=2 * n * cw * dm * (rows + 2 * win), bytes_accessed=2 * n * cw * (3 * dm + rows + 2 * win), transcendentals=0
        ),
    )(info, dq, dk, dv, packed)


MESH = pl.DeviceIdType.MESH


class Place:
    def __init__(self):
        self.me = lax.axis_index("dp")
        self.z = lax.axis_index("mp")
        self.k = lax.rem(self.me, 2)
        self.x = lax.rem(self.me // 2, 2)
        self.y = self.me // 4
        self.me_k = self.me + 1 - 2 * self.k
        self.me_x = self.me + 2 - 4 * self.x
        self.me_y = self.me + 4 - 8 * self.y
        self.me_xy = self.me_x + 4 - 8 * self.y
        self.core = {"dp": self.me_k, "mp": self.z}
        self.by_x = {"dp": self.me_x, "mp": self.z}
        self.by_y = {"dp": self.me_y, "mp": self.z}

    def along(self, d):
        return {"dp": self.me, "mp": lax.rem(self.z + d, 4)}

    def meet(self):
        sem = pltpu.get_barrier_semaphore()
        for dev in (self.core, self.by_x, self.by_y, self.along(1), self.along(2), self.along(3)):
            pl.semaphore_signal(sem, inc=1, device_id=dev, device_id_type=MESH)
        pl.semaphore_wait(sem, 6)


class Wire:
    def __init__(self, send, recv, dev):
        self.send, self.recv, self.dev = send, recv, dev

    def start(self, slot, src, dst, dev):
        copy = pltpu.make_async_remote_copy(
            src_ref=src, dst_ref=dst, send_sem=self.send.at[slot], recv_sem=self.recv.at[slot],
            device_id=dev, device_id_type=MESH,
        )
        copy.start()

    def sent(self, slot, ref):
        pltpu.make_async_remote_copy(
            src_ref=ref, dst_ref=ref, send_sem=self.send.at[slot], recv_sem=self.recv.at[slot],
            device_id=dict(self.dev), device_id_type=MESH,
        ).wait_send()

    def landed(self, slot, ref, dev):
        pltpu.make_async_remote_copy(
            src_ref=ref, dst_ref=ref, send_sem=self.send.at[slot], recv_sem=self.recv.at[slot],
            device_id=dev, device_id_type=MESH,
        ).wait_recv()


def gather_steps(place, wire, base, shard, whole):
    step = shard.shape[0] // 8
    half = step // 2

    def rows(who, at=0, size=step):
        return pl.ds(pl.multiple_of(who * step + at, half), size)

    def slot(d, kind):
        return base + (d - 1) * 9 + kind

    def begin(d):
        wire.start(slot(d, 0), shard.at[rows(place.me)], whole.at[d, rows(place.me)], place.along(4 - d))

    def first(d):
        mine = whole.at[d, rows(place.me)]
        wire.landed(slot(d, 0), mine, place.along(d))
        wire.start(slot(d, 2), mine, mine, place.by_x)
        wire.start(slot(d, 3), mine, mine, place.by_y)
        wire.start(slot(d, 1), mine, mine, place.core)

    def second(d):
        got = whole.at[d, rows(place.me_x)]
        wire.landed(slot(d, 2), got, place.by_x)
        part = whole.at[d, rows(place.me_x, 0, half)]
        wire.start(slot(d, 4), part, part, place.by_y)
        wire.start(slot(d, 6), got, got, place.core)
        got = whole.at[d, rows(place.me_y)]
        wire.landed(slot(d, 3), got, place.by_y)
        part = whole.at[d, rows(place.me_y, half, half)]
        wire.start(slot(d, 5), part, part, place.by_x)
        wire.start(slot(d, 7), got, got, place.core)

    def third(d):
        wire.landed(slot(d, 4), whole.at[d, rows(place.me_xy, 0, half)], place.by_y)
        wire.landed(slot(d, 5), whole.at[d, rows(place.me_xy, half, half)], place.by_x)
        got = whole.at[d, rows(place.me_xy)]
        wire.start(slot(d, 8), got, got, place.core)

    def done(d):
        flip = 1 - 2 * place.k
        for kind, who in ((1, place.me), (6, place.me_x), (7, place.me_y), (8, place.me_xy)):
            wire.landed(slot(d, kind), whole.at[d, rows(who + flip)], place.core)

    def drain():
        for d in (1, 2, 3):
            for kind in range(9):
                wire.sent(slot(d, kind), whole.at[d, pl.ds(0, half if kind in (4, 5) else step)])

    return begin, first, second, third, done, drain


def front_call(tokens, cot, pack, w_up, w_down, small, qseg, kseg, own):
    rows, dm = tokens.shape
    cw = pack.shape[1] // 4
    ffw = w_up.shape[1]
    n = 4
    tile = ffw // 2
    hw = n * tile
    win = own + rows + 2 * HALO
    pairs = cw // PAIR
    strip = 128
    per = rows // strip
    scale = HEAD_DIM**-0.5
    length = small.shape[1] - 6 * dm
    base = 6

    def body(
        tok_ref, cot_ref, pack_ref, up_ref, down_ref, small_ref, qs_ref, ks_ref,
        packed, n1t, n2t, cott, ghbt, q_ref, k_ref, v_ref, a_ref, l_ref, ga_ref, act_ref, gup_ref, gh_ref, o_ref, vec_ref,
        up, down, n1, hid, n2, acc, act, gup, biases, xs, xr, ls, fs,
    ):
        place = Place()
        core, z = place.k, place.z
        long, takes_prev, takes_next = z < 2, z >= 2, jnp.logical_and(z >= 1, z < 3)
        swap = {"dp": place.me, "mp": lax.rem(z + 1, 2)}
        left_dev = {"dp": place.me, "mp": lax.rem(z + 3, 4)}
        right_dev = {"dp": place.me, "mp": lax.rem(z + 1, 4)}
        wire = Wire(xs, xr, place.core)
        local = [
            pltpu.make_async_copy(src, dst, ls.at[i])
            for i, (src, dst) in enumerate(
                ((tok_ref, n1.at[own : own + rows]), (pack_ref, packed.at[0]), (up_ref, up.at[0]), (down_ref, down.at[0]))
            )
        ]
        for c in local:
            c.start()
        place.meet()
        bias_ref = small_ref.at[:, 6 * dm : 6 * dm + length]
        for d in (1, 2, 3):
            wire.start(d - 1, bias_ref, biases.at[d], place.along(4 - d))

        @pl.when(z == 0)
        def _():
            wire.start(3, tok_ref, n1.at[0:own], swap)

        @pl.when(z == 1)
        def _():
            wire.start(3, tok_ref.at[0:SPAN], n1.at[0:SPAN], swap)

        @pl.when(takes_next)
        def _():
            wire.start(4, tok_ref.at[rows - HALO : rows], n1.at[own - HALO : own], right_dev)

        @pl.when(takes_prev)
        def _():
            wire.start(5, tok_ref.at[0:HALO], n1.at[own + rows : own + rows + HALO], left_dev)

        groups = [
            gather_steps(place, wire, base + 27 * g, src, dst)
            for g, (src, dst) in enumerate(((pack_ref, packed), (up_ref, up), (down_ref, down)))
        ]
        for g in range(3):
            for d in (1, 2, 3):
                groups[g][0](d)

        def near_shard(i):
            return lax.rem(4 - z + i, 3) + 1

        items = [(0, 0), (0, 1), (0, 2), (1, 0), (2, 0), (1, 1), (2, 1), (1, 2), (2, 2)]

        def relay(i):
            for lag in range(3):
                if 0 <= i - lag < len(items):
                    g, j = items[i - lag]
                    groups[g][1 + lag](near_shard(j))

        def arrived(j, *which):
            for g in which:
                groups[g][4](near_shard(j))

        def turns(i, table):
            for t, f in table.items():

                @pl.when(i == t)
                def _():
                    f()

        def shard_at(k):
            return near_shard(k + 2) * ((k + 3) // 4)

        def strip_at(i, start=0):
            return pl.ds(pl.multiple_of(start + i * strip, strip), strip)

        row = lambda i: small_ref[:, i * dm : (i + 1) * dm]

        @pl.when(z == 0)
        def _():
            n1[SPAN:own, :] = jnp.zeros((own - SPAN, dm), BF16)

        @pl.when(takes_prev)
        def _():
            n1[0 : own - HALO, :] = jnp.zeros((own - HALO, dm), BF16)

        @pl.when(jnp.logical_not(takes_next))
        def _():
            n1[own + rows : own + rows + HALO, :] = jnp.zeros((HALO, dm), BF16)

        n1[own + rows + HALO :, :] = jnp.zeros((HALO, dm), BF16)
        biases[0] = bias_ref[...]
        l_ref[...] = jnp.zeros_like(l_ref)
        vec_ref[...] = jnp.zeros_like(vec_ref)

        def turn_cot(i, carry):
            cott[:, strip_at(i)] = cot_ref[strip_at(i), :].astype(F32).T.astype(BF16)
            return carry

        lax.fori_loop(0, per, turn_cot, 0)

        def norm1(i):
            at = strip_at(i)
            x = n1[at, :].astype(F32)
            hat, _ = norm_rows(x)
            val = hat * row(0) + row(1)
            n1[at, :] = val.astype(BF16)
            n1t[:, at] = val.T.astype(BF16)
            return x

        def norm_own(i, carry):
            hid[strip_at(i), :] = norm1(own // strip + i) + row(4)
            return carry

        def norm_far(i, carry):
            norm1(i)
            return carry

        local[0].wait()
        lax.fori_loop(0, per, norm_own, 0)
        for c in local[1:]:
            c.wait()
        relay(0)

        @pl.when(z == 0)
        def _():
            wire.landed(3, n1.at[0:SPAN], swap)

        @pl.when(z == 1)
        def _():
            wire.landed(3, n1.at[0:own], swap)

        @pl.when(takes_prev)
        def _():
            wire.landed(4, n1.at[own - HALO : own], left_dev)

        @pl.when(takes_next)
        def _():
            wire.landed(5, n1.at[own + rows : own + rows + HALO], right_dev)

        lax.fori_loop(0, own // strip, norm_far, 0)
        norm1((own + rows) // strip)
        for d in (1, 2, 3):
            wire.landed(d - 1, biases.at[d], place.along(d))
        relay(1)

        def attend(big, d, p):
            at = pl.ds(pl.multiple_of(p * PAIR, PAIR), PAIR)
            for qs, qn, ks, kn in blocks_of(rows, own, win, big):
                mask = qs_ref[qs : qs + qn, :] == ks_ref[:, ks : ks + kn]
                qq, kk, vv = q_ref[d, qs : qs + qn, at], k_ref[d, ks : ks + kn, at], v_ref[d, ks : ks + kn, at]
                outs = []
                for h in range(2):
                    lanes = slice(h * HEAD_DIM, (h + 1) * HEAD_DIM)
                    s = jnp.where(mask, dot_nt(qq[:, lanes] * BF16(scale), kk[:, lanes]), NEG)
                    top = jnp.max(s, axis=1, keepdims=True)
                    pr = jnp.exp(s - top)
                    total = jnp.sum(pr, axis=1, keepdims=True)
                    outs.append(dot_nn(pr.astype(BF16), vv[:, lanes]) / total)
                    lane = lax.broadcasted_iota(jnp.int32, (qn, 2 * n * pairs), 1)
                    seen = l_ref[qs : qs + qn, :]
                    l_ref[qs : qs + qn, :] = jnp.where(lane == (d * pairs + p) * 2 + h, top + jnp.log(total), seen)
                a_ref[d, qs : qs + qn, at] = jnp.concatenate(outs, axis=1).astype(BF16)

        def heads(kk, carry):
            turns(kk, {j + 1: functools.partial(arrived, j, 0) for j in range(3)})
            d = shard_at(kk)
            q_ref[d] = (dot_nn(n1[own : own + rows, :], packed[d, :, 0:cw]) + biases[d, :, 0:cw]).astype(BF16)
            k_ref[d] = dot_nn(n1[...], packed[d, :, cw : 2 * cw]).astype(BF16)
            v_ref[d] = (dot_nn(n1[...], packed[d, :, 2 * cw : 3 * cw]) + biases[d, :, cw : 2 * cw]).astype(BF16)

            def one(p, inner):
                @pl.when(long)
                def _():
                    attend(True, d, p)

                @pl.when(jnp.logical_not(long))
                def _():
                    attend(False, d, p)

                turns(kk * pairs + p, {pairs * j: functools.partial(relay, 2 + j) for j in range(4)})
                return inner

            lax.fori_loop(0, pairs, one, 0)
            hid[...] += dot_nt(a_ref[d], packed[d, :, 3 * cw : 4 * cw])
            return carry

        lax.fori_loop(0, n, heads, 0)
        relay(6)

        def norm2(i, carry):
            at = strip_at(i)
            hidden = hid[at, :]
            hat, _ = norm_rows(hidden)
            val = hat * row(2) + row(3)
            n2[at, :] = val.astype(BF16)
            n2t[:, at] = val.T.astype(BF16)
            acc[at, :] = hidden + row(5)
            return carry

        lax.fori_loop(0, per, norm2, 0)

        def out_copies(i, col):
            at = pl.ds(pl.multiple_of(col, tile), tile)
            return (
                pltpu.make_async_copy(act.at[:, at], act_ref.at[:, at], fs.at[i]),
                pltpu.make_async_copy(gup.at[:, at], gup_ref.at[:, at], fs.at[2 * n + i]),
            )

        def column(i):
            return lax.rem(i, 2) * hw + shard_at(i // 2) * tile

        def feed(i, carry):
            turns(
                i,
                {
                    1: lambda: relay(7),
                    2: lambda: arrived(0, 1, 2),
                    3: lambda: relay(8),
                    4: lambda: (arrived(1, 1, 2), relay(9)),
                    5: lambda: relay(10),
                    6: lambda: arrived(2, 1, 2),
                },
            )
            d = shard_at(i // 2)
            part = lax.rem(lax.rem(i, 2) + core, 2) * tile
            at = pl.ds(pl.multiple_of(part, tile), tile)
            to = pl.ds(pl.multiple_of(column(i), tile), tile)
            u = dot_nn(n2[...], up[d, :, at]) + biases[d, :, pl.ds(pl.multiple_of(2 * cw + part, PAIR), tile)]
            cdf = 0.5 * (1.0 + lax.erf(u * 0.7071067811865476))
            val = (u * cdf).astype(BF16)
            slope = cdf + u * jnp.exp(-0.5 * u * u) * 0.3989422804014327
            act[:, to] = val
            gu = (dot_nt(cot_ref[...], down[d, at, :]) * slope).astype(BF16)
            gup[:, to] = gu
            unit = 8 * dm + lax.rem(z + d, n) * ffw + part
            vec_ref[:, pl.ds(pl.multiple_of(unit, tile), tile)] = jnp.sum(gu.astype(F32), axis=0, keepdims=True)
            for c in out_copies(i, column(i)):
                c.start()
            acc[...] += dot_nn(val, down[d, at, :])
            gn = dot_nt(gu, up[d, :, at])

            @pl.when(i == 0)
            def _():
                gh_ref[...] = gn

            @pl.when(i > 0)
            def _():
                gh_ref[...] += gn

            return carry

        lax.fori_loop(0, 2 * n, feed, 0)

        def back2(i, carry):
            at = strip_at(i)
            o_ref[at, :] = acc[at, :].astype(BF16)
            hat, inv = norm_rows(hid[at, :])
            g = gh_ref[at, :]
            gout = cot_ref[at, :].astype(F32)
            gg = g * row(2)
            first = jnp.mean(gg, axis=1, keepdims=True)
            second = jnp.mean(gg * hat, axis=1, keepdims=True)
            val = inv * (gg - first - hat * second) + gout
            gh_ref[at, :] = val
            n2[at, :] = val.astype(BF16)
            ghbt[:, at] = val.T.astype(BF16)
            for j, v in enumerate((val, g * hat, g, gout)):
                vec_ref[:, (2 + j) * dm : (3 + j) * dm] += jnp.sum(v, axis=0, keepdims=True)
            return carry

        lax.fori_loop(0, per, back2, 0)

        def back_attn(d, carry):
            ga_ref[d] = dot_nn(n2[...], packed[d, :, 3 * cw : 4 * cw]).astype(BF16)
            return carry

        lax.fori_loop(0, n, back_attn, 0)
        for i in range(2 * n):
            for c in out_copies(i, 0):
                c.wait()
        for group in groups:
            group[5]()
        for d in (1, 2, 3):
            wire.sent(d - 1, biases.at[d])

        @pl.when(z == 0)
        def _():
            wire.sent(3, n1.at[0:own])

        @pl.when(z == 1)
        def _():
            wire.sent(3, n1.at[0:SPAN])

        @pl.when(takes_next)
        def _():
            wire.sent(4, n1.at[0:HALO])

        @pl.when(takes_prev)
        def _():
            wire.sent(5, n1.at[0:HALO])

    hbm = pl.BlockSpec(memory_space=pl.ANY)
    vmem = pl.BlockSpec(memory_space=pltpu.VMEM)
    half = lambda *shape: jax.ShapeDtypeStruct(shape, BF16)
    full = lambda *shape: jax.ShapeDtypeStruct(shape, F32)
    b16 = lambda *shape: pltpu.VMEM(shape, BF16)
    b32 = lambda *shape: pltpu.VMEM(shape, F32)
    slots = base + 27 * 3
    return pl.pallas_call(
        body,
        in_specs=[hbm, vmem, hbm, hbm, hbm, vmem, vmem, vmem],
        out_specs=[vmem] * 11 + [hbm] * 2 + [vmem] * 3,
        out_shape=[
            half(n, dm, 4 * cw), half(dm, win), half(dm, rows), half(dm, rows), half(dm, rows),
            half(n, rows, cw), half(n, win, cw), half(n, win, cw), half(n, rows, cw), full(rows, 2 * n * pairs), half(n, rows, cw),
            half(rows, 2 * hw), half(rows, 2 * hw), full(rows, dm), half(rows, dm), full(1, 8 * dm + 2 * hw),
        ],
        scratch_shapes=[
            b16(n, dm, ffw), b16(n, ffw, dm), b16(win, dm), b32(rows, dm), b16(rows, dm), b32(rows, dm),
            b16(rows, 2 * hw), b16(rows, 2 * hw), b32(n, 1, length),
            pltpu.SemaphoreType.DMA((slots,)), pltpu.SemaphoreType.DMA((slots,)), pltpu.SemaphoreType.DMA((4,)),
            pltpu.SemaphoreType.DMA((4 * n,)),
        ],
        compiler_params=pltpu.CompilerParams(collective_id=0, has_side_effects=True, vmem_limit_bytes=VMEM_ALL),
    )(tokens, cot, pack, w_up, w_down, small, qseg, kseg)


class Reduce:
    SLOTS = 32

    @staticmethod
    def scratch(dm, w):
        q = dm // 4
        e = q // 2
        return [
            pltpu.VMEM((4, q, w), BF16),
            pltpu.VMEM((4, q, w), BF16),
            pltpu.VMEM((4, e, w), BF16),
            pltpu.VMEM((4, e, w), BF16),
            pltpu.VMEM((3, q, w), BF16),
            pltpu.SemaphoreType.DMA((Reduce.SLOTS,)),
            pltpu.SemaphoreType.DMA((Reduce.SLOTS,)),
        ]

    def __init__(self, place, grad, landing, views, zb, send, recv):
        self.place, self.g, self.f = place, grad, landing
        self.ra1, self.rb1, self.ra2, self.rb2 = views
        self.zb = zb
        self.wire = Wire(send, recv, place.core)
        self.q = grad.shape[0] // 4
        self.e = self.q // 2
        self.w = grad.shape[1] // 4

    @staticmethod
    def of(place, grad, landing, scratch):
        views = [lambda d, ref=ref: ref.at[d] for ref in scratch[:4]]
        return Reduce(place, grad, landing, views, *scratch[4:])

    @staticmethod
    def within(place, grad, landing, spare, zb, send, recv):
        q, w = grad.shape[0] // 4, grad.shape[1] // 4
        bounds = (0, q, 2 * q, 2 * q + q // 2, 3 * q)
        views = [
            lambda d, a=a, b=b: spare.at[a:b, pl.ds(pl.multiple_of(d * w, w), w)] for a, b in zip(bounds[:-1], bounds[1:])
        ]
        return Reduce(place, grad, landing, views, zb, send, recv)

    def at(self, base, big, small=None):
        start = base * 2 * self.q + big * self.q + (0 if small is None else small * self.e)
        return pl.ds(pl.multiple_of(start, self.e), self.q if small is None else self.e)

    def eighth(self, small):
        return pl.ds(pl.multiple_of(small * self.e, self.e), self.e)

    def cols(self, d):
        return pl.ds(pl.multiple_of(d * self.w, self.w), self.w)

    def one(self, d):
        p, wire = self.place, self.wire
        wire.start(d, self.g.at[self.at(0, 1 - p.x), self.cols(d)], self.ra1(d), p.by_x)
        wire.start(4 + d, self.g.at[self.at(1, 1 - p.y), self.cols(d)], self.rb1(d), p.by_y)

    def two(self, d):
        p, wire, c = self.place, self.wire, self.cols(d)
        for slot, buf, to, at, mine, dev, nxt in (
            (0, self.ra1, self.ra2, self.at(0, p.x, 1 - p.y), self.eighth(1 - p.y), p.by_x, p.by_y),
            (4, self.rb1, self.rb2, self.at(1, p.y, 1 - p.x), self.eighth(1 - p.x), p.by_y, p.by_x),
        ):
            wire.landed(slot + d, buf(d), dev)
            self.g[at, c] = (self.g[at, c].astype(F32) + buf(d)[mine, :].astype(F32)).astype(BF16)
            wire.start(8 + slot + d, self.g.at[at, c], to(d), nxt)

    def sums(self, d):
        p, wire, c = self.place, self.wire, self.cols(d)
        wire.landed(8 + d, self.ra2(d), p.by_y)
        wire.landed(12 + d, self.rb2(d), p.by_x)
        up = (
            self.g[self.at(0, p.x, p.y), c].astype(F32)
            + self.ra1(d)[self.eighth(p.y), :].astype(F32)
            + self.ra2(d)[...].astype(F32)
        )
        low = (
            self.g[self.at(1, p.y, p.x), c].astype(F32)
            + self.rb1(d)[self.eighth(p.x), :].astype(F32)
            + self.rb2(d)[...].astype(F32)
        )
        return up, low

    def three(self, d):
        p, wire, c, e = self.place, self.wire, self.cols(d), self.e
        up, low = self.sums(d)
        for part, (at, val) in enumerate(((self.at(0, p.x, p.y), up), (self.at(1, p.y, p.x), low))):
            self.g[at, c] = val.astype(BF16)
            wire.start(
                16 + 12 * part + d, self.g.at[at, c], self.zb.at[d - 1, part * e : (part + 1) * e], p.along(d)
            )

    def last(self):
        p, wire, e = self.place, self.wire, self.e
        up, low = self.sums(0)
        for s in (1, 2, 3):
            wire.landed(16 + s, self.zb.at[s - 1, 0:e], p.along(4 - s))
            wire.landed(28 + s, self.zb.at[s - 1, e : 2 * e], p.along(4 - s))
            up = up + self.zb[s - 1, 0:e].astype(F32)
            low = low + self.zb[s - 1, e : 2 * e].astype(F32)
        ready = self.ra1(0)
        ready[0:e, :] = up.astype(BF16)
        ready[e : 2 * e, :] = low.astype(BF16)
        wire.start(20, ready, self.f.at[2], p.by_x)
        wire.start(21, ready, self.f.at[4], p.by_y)
        wire.start(22, ready, self.f.at[1], p.core)
        self.keep().start()

    def keep(self):
        return pltpu.make_async_copy(self.ra1(0), self.f.at[0], self.wire.send.at[16])

    def four(self):
        p, wire, e = self.place, self.wire, self.e
        wire.landed(20, self.f.at[2], p.by_x)
        wire.start(23, self.f.at[2, 0:e], self.f.at[6, 0:e], p.by_y)
        wire.start(25, self.f.at[2], self.f.at[3], p.core)
        wire.landed(21, self.f.at[4], p.by_y)
        wire.start(24, self.f.at[4, e : 2 * e], self.f.at[6, e : 2 * e], p.by_x)
        wire.start(26, self.f.at[4], self.f.at[5], p.core)

    def five(self):
        p, wire, e = self.place, self.wire, self.e
        wire.landed(23, self.f.at[6, 0:e], p.by_y)
        wire.landed(24, self.f.at[6, e : 2 * e], p.by_x)
        wire.start(27, self.f.at[6], self.f.at[7], p.core)

    def six(self):
        for slot, to in ((22, 1), (25, 3), (26, 5), (27, 7)):
            self.wire.landed(slot, self.f.at[to], self.place.core)
        e, sent = self.e, self.wire.sent
        for d in range(4):
            sent(d, self.ra1(d))
            sent(4 + d, self.rb1(d))
            sent(8 + d, self.ra2(d))
            sent(12 + d, self.rb2(d))
        for d in range(1, 4):
            sent(16 + d, self.zb.at[d - 1, 0:e])
            sent(28 + d, self.zb.at[d - 1, 0:e])
        for slot in (20, 21, 22, 25, 26, 27):
            sent(slot, self.f.at[0])
        for slot in (23, 24):
            sent(slot, self.f.at[0, 0:e])
        self.keep().wait()


def back_call(cot, act, n2, gup, ghb, n1w, packed, tokens, q, k, v, attn, gattn, lse, qseg, kseg, gain, vec, own):
    n, rows, cw = q.shape
    win = k.shape[1]
    dm = cot.shape[0]
    hw = act.shape[1] // 2
    half = n * cw // 2
    w = hw // 4
    pairs = cw // PAIR
    scale = HEAD_DIM**-0.5
    each = len(Reduce.scratch(dm, w))
    length = vec.shape[1]
    strip = 128

    def body(
        cot_ref, act_ref, n2_ref, gup_ref, ghb_ref, n1_ref, w_ref, x_ref,
        q_ref, k_ref, v_ref, a_ref, g_ref, l_ref, qs_ref, ks_ref, gain_ref, vec_ref,
        fd, fu, fp, gi_ref, sum_ref,
        wbuf, act2, gup2, n12, gd, gu, dq_o, dk_o, dv_o, at2, dq, dk, dv, dkt, dvt,
        far_in, prev_in, next_in, nxt, va, vr, vz, zb, ps, pr_sem, xs, xr, ls, ws, *scr,
    ):
        place = Place()
        core, z = place.k, place.z
        long, gives_prev, gives_next = z < 2, z >= 2, jnp.logical_and(z >= 1, z < 3)
        swap = {"dp": place.me, "mp": lax.rem(z + 1, 2)}
        left_dev = {"dp": place.me, "mp": lax.rem(z + 3, 4)}
        right_dev = {"dp": place.me, "mp": lax.rem(z + 1, 4)}
        wire = Wire(xs, xr, place.core)
        cot2, n22, ghb2 = wbuf.at[0], wbuf.at[1], wbuf.at[2]
        whole = (
            (cot_ref, cot2, rows), (n2_ref, n22, rows), (ghb_ref, ghb2, rows), (n1_ref, n12, win)
        )
        mixed = ((act_ref, act2), (gup_ref, gup2))
        local = [pltpu.make_async_copy(src, dst.at[:, 0:wide], ls.at[i]) for i, (src, dst, wide) in enumerate(whole)]
        local += [pltpu.make_async_copy(src.at[:, 0:hw], dst.at[0:rows], ls.at[4 + i]) for i, (src, dst) in enumerate(mixed)]
        for i in (0, 4, 1, 5, 2, 3):
            local[i].start()
        place.meet()

        def give_whole(i):
            src, dst, wide = whole[i]
            wire.start(i, src, dst.at[:, wide : 2 * wide], place.core)

        def give_mixed(i):
            src, dst = mixed[i]
            wire.start(4 + i, src.at[:, hw : 2 * hw], dst.at[rows : 2 * rows], place.core)

        def take(*which):
            for i in which:
                local[i].wait()
                if i < 4:
                    dst, wide = whole[i][1:]
                    wire.landed(i, dst.at[:, wide : 2 * wide], place.core)
                else:
                    wire.landed(i, mixed[i - 4][1].at[rows : 2 * rows], place.core)

        give_whole(0)
        give_mixed(0)
        give_whole(1)
        give_mixed(1)
        give_whole(2)
        give_whole(3)
        for d in range(n):
            to = slice(d * PAIR, (d + 1) * PAIR)
            theirs = pl.ds(pl.multiple_of((1 - core) * PAIR, PAIR), PAIR)
            mine = pl.ds(pl.multiple_of(core * PAIR, PAIR), PAIR)
            wire.start(6 + d, a_ref.at[d, :, theirs], at2.at[rows : 2 * rows, to], place.core)
            at2[0:rows, to] = a_ref[d, :, mine]

        down = Reduce.of(place, gd, fd, scr[:each])
        up = Reduce.of(place, gu, fu, scr[each : 2 * each])
        heads = Reduce.within(place, act2, fp, gup2, zb, ps, pr_sem)

        def make(red, grad, left, right):
            def step(i, carry):
                d = lax.rem(i + 1, 4)
                c = pl.ds(pl.multiple_of(d * w, w), w)
                grad[:, c] = dot_nn(left[...], right[:, c]).astype(BF16)
                red.one(d)
                return carry

            lax.fori_loop(0, 4, step, 0)

        take(0, 4)
        make(down, gd, cot2, act2)
        take(1, 5)
        make(up, gu, n22, gup2)

        def weights(t):
            at = lax.rem(t, 3)
            return pltpu.make_async_copy(w_ref.at[lax.rem(t, n)], wbuf.at[at], ws.at[at])

        weights(0).start()
        weights(1).start()

        def turns(i, table):
            for t, f in table.items():

                @pl.when(i == t)
                def _():
                    f()

        def work(big, d, p):
            at = pl.ds(pl.multiple_of(p * PAIR, PAIR), PAIR)
            to = pl.ds(pl.multiple_of(d * PAIR, PAIR), PAIR)
            rel = lax.rem(p + core, 2)
            if not big:
                dkt[...] = jnp.zeros_like(dkt)
                dvt[...] = jnp.zeros_like(dvt)
            for i, (qs, qn, ks, kn) in enumerate(blocks_of(rows, own, win, big)):
                mask = qs_ref[qs : qs + qn, :] == ks_ref[:, ks : ks + kn]
                qq, kk, vv = q_ref[d, qs : qs + qn, at], k_ref[d, ks : ks + kn, at], v_ref[d, ks : ks + kn, at]
                gg = g_ref[d, qs : qs + qn, at]
                prod = gg.astype(F32) * a_ref[d, qs : qs + qn, at].astype(F32)
                dqs = []
                for h in range(2):
                    lanes = slice(h * HEAD_DIM, (h + 1) * HEAD_DIM)
                    qh, kh, gh = qq[:, lanes] * BF16(scale), kk[:, lanes], gg[:, lanes]
                    lane = lax.broadcasted_iota(jnp.int32, (qn, 2 * n * pairs), 1)
                    picked = jnp.where(lane == (d * pairs + p) * 2 + h, l_ref[qs : qs + qn, :], 0.0)
                    s = jnp.where(mask, dot_nt(qh, kh) - jnp.sum(picked, axis=1, keepdims=True), NEG)
                    pr = jnp.exp(s)
                    dp = dot_nt(gh, vv[:, lanes])
                    delta = jnp.sum(prod[:, lanes], axis=1, keepdims=True)
                    ds = (pr * (dp - delta)).astype(BF16)
                    dqs.append(dot_nn(ds, kh) * scale)
                    gk = dot_tn(qh, ds)
                    gv = dot_tn(gh, pr.astype(BF16))
                    if big and i == 0:
                        dkt[lanes, :] = gk
                        dvt[lanes, :] = gv
                    else:
                        dkt[lanes, ks : ks + kn] += gk
                        dvt[lanes, ks : ks + kn] += gv
                dq[rel, qs : qs + qn, to] = jnp.concatenate(dqs, axis=1).astype(BF16)
            dk[rel, :, to] = dkt[...].T.astype(BF16)
            dv[rel, :, to] = dvt[...].T.astype(BF16)

        def head_pair(i, carry):
            d, p = i // pairs, lax.rem(i, pairs)

            @pl.when(long)
            def _():
                work(True, d, p)

            @pl.when(jnp.logical_not(long))
            def _():
                work(False, d, p)

            order = [(down, 1), (down, 2), (down, 3), (down, 0), (up, 1), (up, 2)]
            turns(i, {t + 2: functools.partial(red.two, shard) for t, (red, shard) in enumerate(order)})
            return carry

        lax.fori_loop(0, n * pairs, head_pair, 0)
        halves = ((dq, dq_o), (dk, dk_o), (dv, dv_o))
        for i, (src, dst) in enumerate(halves):
            wire.start(10 + i, src.at[1], dst, place.core)
        take(2, 3)
        for d in range(n):
            wire.landed(6 + d, at2.at[rows : 2 * rows, d * PAIR : (d + 1) * PAIR], place.core)

        def put(m, val):
            for d in range(n):
                at = d * w + m * PAIR
                act2[:, at : at + PAIR] = val[:, d * PAIR : (d + 1) * PAIR].astype(BF16)

        put(3, dot_nn(ghb2[...], at2[...]))
        weights(2).start()
        wire.landed(10, dq_o, place.core)
        put(0, dot_nn(n12[:, own : own + rows], dq[0]) + dot_nn(n12[:, win + own : win + own + rows], dq_o[...]))
        up.two(3)
        wire.landed(11, dk_o, place.core)
        put(1, dot_nn(n12[:, 0:win], dk[0]) + dot_nn(n12[:, win : 2 * win], dk_o[...]))
        up.two(0)
        wire.landed(12, dv_o, place.core)
        put(2, dot_nn(n12[:, 0:win], dv[0]) + dot_nn(n12[:, win : 2 * win], dv_o[...]))
        for d in (1, 2, 3, 0):
            heads.one(d)

        far_out, x_buf, next_out = n12.at[0:own, 0:dm], n12.at[0:rows, dm : 2 * dm], n12.at[own : own + HALO, 0:dm]
        tokens_in = pltpu.make_async_copy(x_ref, x_buf, ls.at[6])
        tokens_in.start()

        def dots(t, carry):
            weights(t).wait()
            slot = lax.rem(t, 3)
            to = pl.ds(pl.multiple_of(lax.rem(t, n) * PAIR, PAIR), PAIR)

            def weight(which, j):
                at = which * cw + lax.rem(j + core, 2) * PAIR
                return wbuf[slot, :, pl.ds(pl.multiple_of(at, PAIR), PAIR)]

            def add(ref, val, first):
                @pl.when(t == first)
                def _():
                    ref[...] = val

                @pl.when(t > first)
                def _():
                    ref[...] += val

            right = jnp.concatenate([weight(m, j) for m in (1, 2) for j in range(2)], axis=1)

            @pl.when(t < n)
            def _():
                left = jnp.concatenate([r[j, 0:own, to] for r in (dk, dv) for j in range(2)], axis=1)
                add(gi_ref, dot_nt(left, right), 0)

            @pl.when(t >= n)
            def _():
                left = jnp.concatenate([r[j, own : own + rows, to] for r in (dk, dv) for j in range(2)], axis=1)
                mine = jnp.concatenate([dq[j, :, to] for j in range(2)], axis=1)
                other = jnp.concatenate([weight(0, j) for j in range(2)], axis=1)
                add(gi_ref, dot_nt(left, right) + dot_nt(mine, other), n)
                left = jnp.concatenate(
                    [r[j, own + rows : own + rows + HALO, to] for r in (dk, dv) for j in range(2)], axis=1
                )
                add(nxt, dot_nt(left, right), n)

            @pl.when(t < 2 * n - 3)
            def _():
                weights(t + 3).start()

            @pl.when(t == n - 1)
            def _():
                far_out[...] = gi_ref[...].astype(BF16)

                @pl.when(z == 0)
                def _():
                    wire.start(13, far_out.at[0:SPAN], far_in.at[0:SPAN], swap)

                @pl.when(z == 1)
                def _():
                    wire.start(13, far_out, far_in, swap)

                @pl.when(gives_prev)
                def _():
                    wire.start(14, far_out.at[own - HALO : own], prev_in, left_dev)

            turns(t, {2 * i + 1: functools.partial(down.three, i + 1) for i in range(3)})
            return carry

        lax.fori_loop(0, 2 * n, dots, 0)
        next_out[...] = nxt[...].astype(BF16)

        @pl.when(gives_next)
        def _():
            wire.start(15, next_out, next_in, right_dev)

        up.three(1)
        up.three(2)
        up.three(3)
        heads.two(1)
        heads.two(2)
        down.last()
        heads.two(3)
        heads.two(0)
        heads.three(1)

        @pl.when(z == 0)
        def _():
            wire.landed(13, far_in, swap)
            gi_ref[...] += far_in[...].astype(F32)

        @pl.when(z == 1)
        def _():
            wire.landed(13, far_in.at[0:SPAN], swap)
            gi_ref[0:SPAN, :] += far_in[0:SPAN, :].astype(F32)

        @pl.when(gives_next)
        def _():
            wire.landed(14, prev_in, right_dev)
            gi_ref[rows - HALO : rows, :] += prev_in[...].astype(F32)

        @pl.when(gives_prev)
        def _():
            wire.landed(15, next_in, left_dev)
            gi_ref[0:HALO, :] += next_in[...].astype(F32)

        up.last()
        heads.three(2)
        heads.three(3)
        va[0] = vec_ref[...]
        for base, grad in ((6, dq), (7, dv)):
            for j in range(2):
                total = jnp.sum(grad[j].astype(F32), axis=0, keepdims=True)
                for d in range(n):
                    at = base * dm + lax.rem(z + d, n) * cw + lax.rem(j + core, 2) * PAIR
                    va[0, :, pl.ds(pl.multiple_of(at, PAIR), PAIR)] = total[:, d * PAIR : (d + 1) * PAIR]
        tokens_in.wait()
        gains = gain_ref[...].astype(F32)

        def norm(i, carry):
            at = pl.ds(pl.multiple_of(i * strip, strip), strip)
            hat, inv = norm_rows(x_buf[at, :].astype(F32))
            grad = gi_ref[at, :]
            gg = grad * gains
            first = jnp.mean(gg, axis=1, keepdims=True)
            second = jnp.mean(gg * hat, axis=1, keepdims=True)
            gi_ref[at, :] = inv * (gg - first - hat * second)
            va[0, :, 0:dm] += jnp.sum(grad * hat, axis=0, keepdims=True)
            va[0, :, dm : 2 * dm] += jnp.sum(grad, axis=0, keepdims=True)
            return carry

        lax.fori_loop(0, rows // strip, norm, 0)

        hops = (place.core, place.by_x, place.by_y)
        between = (down.four, up.four, down.five)
        for i, dev in enumerate(hops):
            wire.start(16 + i, va.at[i], vr.at[i], dev)
            between[i]()
            wire.landed(16 + i, vr.at[i], dev)
            if i < 2:
                va[i + 1] = va[i] + vr[i]
            else:
                vz[0] = va[i] + vr[i]
        for d in (1, 2, 3):
            wire.start(18 + d, vz.at[0], vz.at[d], place.along(d))
        up.five()
        heads.last()
        heads.four()
        for d in (1, 2, 3):
            wire.landed(18 + d, vz.at[d], place.along(4 - d))
        terms = [vz[lax.rem(z - a + 4, 4)] for a in range(4)]
        sum_ref[...] = (terms[0] + terms[1]) + (terms[2] + terms[3])
        heads.five()
        down.six()
        up.six()
        heads.six()
        for i in range(4):
            wire.sent(i, whole[i][0])
        for i in range(2):
            wire.sent(4 + i, act2.at[0:rows])
        for d in range(n):
            wire.sent(6 + d, at2.at[0:rows, 0:PAIR])
        for i in range(3):
            wire.sent(10 + i, halves[i][1])

        @pl.when(z == 0)
        def _():
            wire.sent(13, far_in.at[0:SPAN])

        @pl.when(z == 1)
        def _():
            wire.sent(13, far_in)

        @pl.when(gives_prev)
        def _():
            wire.sent(14, prev_in)

        @pl.when(gives_next)
        def _():
            wire.sent(15, next_in)

        for i in range(3):
            wire.sent(16 + i, va.at[i])
        for d in (1, 2, 3):
            wire.sent(18 + d, vz.at[0])

    hbm = pl.BlockSpec(memory_space=pl.ANY)
    vmem = pl.BlockSpec(memory_space=pltpu.VMEM)
    shaped = lambda *shape: jax.ShapeDtypeStruct(shape, BF16)
    buf = lambda *shape: pltpu.VMEM(shape, BF16)
    wide = lambda *shape: pltpu.VMEM(shape, F32)
    sem = lambda count: pltpu.SemaphoreType.DMA((count,))
    q4 = dm // 4
    return pl.pallas_call(
        body,
        in_specs=[hbm] * 8 + [vmem] * 10,
        out_specs=[hbm] * 3 + [vmem] * 2,
        out_shape=[shaped(8, q4, w)] * 3 + [jax.ShapeDtypeStruct((rows, dm), F32), jax.ShapeDtypeStruct((1, length), F32)],
        scratch_shapes=[
            buf(3, dm, 2 * rows), buf(2 * rows, hw), buf(2 * rows, hw), buf(dm, 2 * win), buf(dm, hw), buf(dm, hw),
            buf(rows, half), buf(win, half), buf(win, half), buf(2 * rows, half), buf(2, rows, half), buf(2, win, half), buf(2, win, half),
            wide(PAIR, win), wide(PAIR, win), buf(own, dm), buf(HALO, dm), buf(HALO, dm), wide(HALO, dm),
            wide(3, 1, length), wide(3, 1, length), wide(4, 1, length), buf(3, q4, w), sem(Reduce.SLOTS), sem(Reduce.SLOTS),
            sem(22), sem(22), sem(7), sem(3),
        ]
        + Reduce.scratch(dm, w) * 2,
        compiler_params=pltpu.CompilerParams(collective_id=1, has_side_effects=True, vmem_limit_bytes=VMEM_ALL),
    )(cot, act, n2, gup, ghb, n1w, packed, tokens, q, k, v, attn, gattn, lse, qseg, kseg, gain[None], vec)


def place_grads(coords, done, mode):
    _, q, w = done.shape
    e = q // 2
    dm = 4 * q
    lanes = w // 4

    def body(c_ref, f_ref, *outs):
        for off in range(8):
            y = lax.bitwise_xor(c_ref[0], off >> 2)
            x = lax.bitwise_xor(c_ref[1], (off >> 1) & 1)
            k = lax.bitwise_xor(c_ref[2], off & 1)
            for part in range(2):
                val = f_ref[off, part * e : (part + 1) * e, :].astype(F32)
                block = x * 2 + y if part == 0 else 4 + y * 2 + x
                rows = pl.ds(pl.multiple_of(block * e, e), e)
                if mode == "up":
                    outs[0][rows, pl.ds(pl.multiple_of(k * w, w), w)] = val
                elif mode == "down":
                    outs[0][pl.ds(pl.multiple_of(k * w, w), w), rows] = val.T
                else:
                    at = pl.ds(pl.multiple_of(k * lanes, lanes), lanes)
                    for m in range(3):
                        outs[m][rows, at] = val[:, m * lanes : (m + 1) * lanes]
                    outs[3][at, rows] = val[:, 3 * lanes :].T

    if mode == "up":
        shapes = [(dm, 2 * w)]
    elif mode == "down":
        shapes = [(2 * w, dm)]
    else:
        shapes = [(dm, w // 2)] * 3 + [(w // 2, dm)]
    return pl.pallas_call(
        body,
        in_specs=[pl.BlockSpec(memory_space=pltpu.SMEM), pl.BlockSpec(memory_space=pltpu.VMEM)],
        out_specs=[pl.BlockSpec(memory_space=pltpu.VMEM)] * len(shapes),
        out_shape=[jax.ShapeDtypeStruct(s, F32) for s in shapes],
        compiler_params=pltpu.CompilerParams(vmem_limit_bytes=VMEM),
        cost_estimate=pl.CostEstimate(flops=0, bytes_accessed=12 * dm * w, transcendentals=0),
    )(coords, done)


def relative(stack, z):
    return jnp.roll(stack, -z, axis=0)


def core_first(v, core, axis):
    return jnp.where(core == 0, v, jnp.flip(v, axis))


def gather_any(shard, z):
    return relative(lax.all_gather(shard, "mp", axis=0, tiled=False), z)


def reduce_any(half, z, core):
    zero = jnp.zeros_like(half)
    v = jnp.stack([jnp.where(core == 0, half, zero), jnp.where(core == 1, half, zero)], axis=2)
    v = jnp.roll(jnp.moveaxis(v, 1, 0), z, axis=0)
    v = lax.psum_scatter(v, "mp", scatter_dimension=0, tiled=True)[0]
    return lax.psum(v, "dp").astype(F32).reshape(half.shape[0], -1)


def local(
    tokens,
    segments,
    ln1_gain,
    ln1_bias,
    w_query,
    b_query,
    w_key,
    w_value,
    b_value,
    w_out,
    b_out,
    ln2_gain,
    ln2_bias,
    w_up,
    b_up,
    w_down,
    b_down,
    cotangent,
):
    rows, dm = tokens.shape
    cw = w_query.shape[1]
    ffw = w_up.shape[1]
    mp = lax.axis_size("mp")
    dp = lax.axis_size("dp")
    fast = mp == 4 and dp == 8 and rows % 256 == 0 and cw == 2 * PAIR and rows < LONGEST <= rows + SPAN <= 2 * rows
    z = lax.axis_index("mp")
    me = lax.axis_index("dp")
    core = lax.rem(me, 2)
    x = lax.rem(me // 2, 2)
    y = me // 4
    f32 = lambda v: v.astype(F32)

    near = -(-LONGEST // rows)
    own = (near - 1) * rows
    win = own + rows + 2 * HALO
    is_near = z < near
    seg_parts = [
        jnp.where(is_near, lax.dynamic_slice_in_dim(segments, lax.rem(z + j, near) * rows, rows), -1)
        for j in range(1, near)
    ]
    seg_own = lax.dynamic_slice_in_dim(segments, z * rows, rows)
    seg_prev = lax.dynamic_slice_in_dim(segments, jnp.maximum(z * rows - HALO, 0), HALO)
    seg_next = lax.dynamic_slice_in_dim(segments, jnp.minimum((z + 1) * rows, segments.shape[0] - HALO), HALO)
    seg_far = jnp.concatenate(seg_parts)
    seg_far = jnp.concatenate([seg_far[:-HALO], jnp.where(is_near, seg_far[-HALO:], seg_prev)])
    has_next = jnp.logical_and(z >= near - 1, z < mp - 1)
    seg_win = jnp.concatenate(
        [seg_far, seg_own, jnp.where(has_next, seg_next, -1), jnp.full((HALO,), -1, segments.dtype)]
    )
    kseg, qseg = seg_win[None, :], seg_own[:, None]
    info = jnp.stack([is_near.astype(jnp.int32), core]).astype(jnp.int32)

    pack = jnp.concatenate([w_query, w_key, w_value, w_out.T], axis=1)
    hw = mp * ffw // 2
    if fast:
        small = jnp.concatenate([ln1_gain, ln1_bias, ln2_gain, ln2_bias, b_out, b_down, b_query, b_value, b_up])
        small = f32(small)[None]
        (
            packed, n1_t, n2_t, cot_t, ghb_t, q, k, v, attn, lse, g_attn, active, g_upper, g_hidden, output, vec
        ) = front_call(tokens, cotangent, pack, w_up, w_down, small, qseg, kseg, own)
        done_d, done_u, done_p, g_in, vec = back_call(
            cot_t, active, n2_t, g_upper, ghb_t, n1_t, packed, tokens, q, k, v, attn, g_attn, lse, qseg, kseg, ln1_gain, vec, own
        )
        vec = vec[0]
        g_tokens = g_in + g_hidden
        coords = jnp.stack([y, x, core]).astype(jnp.int32)
        (g_w_down,) = place_grads(coords, done_d, "down")
        (g_w_up,) = place_grads(coords, done_u, "up")
        g_w_query, g_w_key, g_w_value, g_w_out = place_grads(coords, done_p, "pack")
    else:
        halo = [
            lax.ppermute(tokens, "mp", [((i + j) % near, i) for i in range(near)]) for j in range(1, near)
        ]
        before = lax.ppermute(tokens[-HALO:], "mp", [(i - 1, i) for i in range(near, mp)])
        behind = lax.ppermute(tokens[:HALO], "mp", [(i + 1, i) for i in range(near - 1, mp - 1)])
        small_vec = jnp.concatenate([b_query, b_value, b_up])
        vecs = relative(lax.all_gather(small_vec, "mp", axis=0, tiled=False), z)
        bq_all, bv_all = vecs[:, :cw], vecs[:, cw : 2 * cw]
        bu_all = vecs[:, 2 * cw :].reshape(mp, 2, ffw // 2).transpose(1, 0, 2)
        bu_all = core_first(bu_all, core, 0).reshape(mp * ffw)

        packed, up_all, down_all = (gather_any(w, z) for w in (pack, w_up, w_down))

        far = jnp.concatenate(halo, axis=0)
        far = jnp.concatenate([far[:-HALO], far[-HALO:] + before], axis=0)
        tok_win = jnp.concatenate([far, tokens, behind, jnp.zeros((HALO, dm), tokens.dtype)], axis=0)
        hat_win, inv_win = norm_rows(f32(tok_win))
        n1w = (hat_win * f32(ln1_gain) + f32(ln1_bias)).astype(BF16)
        q, k, v = qkv_call(n1w, packed, bq_all, bv_all, own, rows, cw)
        attn, lse = attn_fwd_call(info, q, k, v, qseg, kseg, own)
        hidden, n2 = out_call(attn, packed, tokens, b_out, ln2_gain, ln2_bias)
        output, g_n2, active, g_upper, g_b_up = ffn_call(
            info[1:], n2, hidden, cotangent, up_all, down_all, bu_all, b_down, 2
        )

        gout = f32(cotangent)
        hat2, inv2 = norm_rows(hidden)

        def norm_back(g, hat, inv, gain):
            gg = g * gain
            first = jnp.mean(gg, axis=1, keepdims=True)
            second = jnp.mean(gg * hat, axis=1, keepdims=True)
            return inv * (gg - first - hat * second), jnp.sum(g * hat, axis=0), jnp.sum(g, axis=0)

        g_hidden, g_gain2, g_bias2 = norm_back(g_n2, hat2, inv2, f32(ln2_gain))
        g_hidden = g_hidden + gout
        ghb = g_hidden.astype(BF16)

        g_attn = jnp.stack([dot_nn(ghb, packed[d, :, 3 * cw :]).astype(BF16) for d in range(mp)])
        dq, dk, dv = attn_bwd_call(info, q, k, v, attn, g_attn, lse, qseg, kseg, own)
        n1 = n1w[own : own + rows]
        sums = [jnp.sum(g_hidden, axis=0), g_gain2, g_bias2, jnp.sum(gout, axis=0)]
        halves = dq.shape[0]

        def shards(v, width):
            if v.shape[0] == 2:
                v = core_first(v.reshape(2, mp, width // 2), core, 0).transpose(1, 0, 2)
            return jnp.roll(v.reshape(mp, width), z, axis=0).reshape(mp * width)

        gbq = shards(jnp.sum(f32(dq), axis=1), cw)
        gbv = shards(jnp.sum(f32(dv), axis=1), cw)
        gbu = core_first(g_b_up.reshape(2, mp, ffw // 2), core, 0).transpose(1, 0, 2)
        gbu = jnp.roll(gbu.reshape(mp, ffw), z, axis=0).reshape(-1)
        sums = sums + [gbq, gbv, gbu]
        g_own, g_far, g_next = norm1_back_call(dq, dk, dv, packed, info, own)
        back = g_own
        for j in range(1, near):
            part = g_far[(j - 1) * rows : j * rows]
            back = back + f32(lax.ppermute(part, "mp", [(i, (i + j) % near) for i in range(near)]))
        to_prev = f32(lax.ppermute(g_far[-HALO:], "mp", [(i, i - 1) for i in range(near, mp)]))
        to_next = f32(lax.ppermute(g_next, "mp", [(i, i + 1) for i in range(near - 1, mp - 1)]))
        back = jnp.concatenate([back[:HALO] + to_next, back[HALO:-HALO], back[-HALO:] + to_prev], axis=0)
        hat1 = hat_win[own : own + rows]
        inv1 = inv_win[own : own + rows]
        g_in, g_gain1, g_bias1 = norm_back(back, hat1, inv1, f32(ln1_gain))
        g_tokens = g_in + g_hidden

        other = lambda v: lax.ppermute(v, "dp", [(i, i - i % 2 + (i + 1) % 2) for i in range(dp)])
        hw = mp * ffw // 2

        def pair_grad(left, right):
            return (dot_tn(left, right[:, :hw]) + dot_tn(other(left), other(right[:, hw:]))).astype(BF16)

        gd = pair_grad(cotangent, active)
        gu = pair_grad(n2, g_upper)
        g_w_up = reduce_any(gu.reshape(dm, mp, ffw // 2), z, core)
        g_w_down = reduce_any(gd.reshape(dm, mp, ffw // 2), z, core).T

        def whole_grad(left, right, name=None):
            v = dot_tn(left, right).astype(BF16).reshape(dm, mp, cw)
            v = jnp.roll(jnp.moveaxis(v, 1, 0), z, axis=0)
            v = lax.psum_scatter(v, "mp", scatter_dimension=0, tiled=True)[0]
            return lax.psum(v, "dp").astype(F32)

        def whole(v):
            if halves == 1:
                return v[0]
            v = v.reshape(2, v.shape[1], mp, cw // 2).transpose(1, 2, 0, 3)
            return core_first(v, core, 2).reshape(v.shape[0], mp * cw)

        g_w_query = whole_grad(n1, whole(dq))
        g_w_key = whole_grad(n1w, whole(dk))
        g_w_value = whole_grad(n1w, whole(dv))
        g_w_out = whole_grad(ghb, attn.transpose(1, 0, 2).reshape(rows, mp * cw)).T

        vec = lax.psum(jnp.concatenate([g_gain1, g_bias1] + sums), ("dp", "mp"))
    g_gain1, g_bias1, g_b_out, g_gain2, g_bias2, g_b_down = (vec[i * dm : (i + 1) * dm] for i in range(6))
    at = 6 * dm
    g_b_query = lax.dynamic_slice_in_dim(vec, at + z * cw, cw)
    g_b_value = lax.dynamic_slice_in_dim(vec, at + mp * cw + z * cw, cw)
    g_b_up = lax.dynamic_slice_in_dim(vec, at + 2 * mp * cw + z * ffw, ffw)
    return (
        output,
        g_tokens,
        g_gain1,
        g_bias1,
        g_w_query,
        g_b_query,
        g_w_key,
        g_w_value,
        g_b_value,
        g_w_out,
        g_b_out,
        g_gain2,
        g_bias2,
        g_w_up,
        g_b_up,
        g_w_down,
        g_b_down,
    )


def solution(mesh):
    in_specs = (
        P(("dp", "mp"), None),
        P("dp"),
        P(),
        P(),
        P(None, "mp"),
        P("mp"),
        P(None, "mp"),
        P(None, "mp"),
        P("mp"),
        P("mp", None),
        P(),
        P(),
        P(),
        P(None, "mp"),
        P("mp"),
        P("mp", None),
        P(),
        P(("dp", "mp"), None),
    )
    out_specs = (
        P(("dp", "mp"), None),
        P(("dp", "mp"), None),
        P(),
        P(),
        P(None, "mp"),
        P("mp"),
        P(None, "mp"),
        P(None, "mp"),
        P("mp"),
        P("mp", None),
        P(),
        P(),
        P(),
        P(None, "mp"),
        P("mp"),
        P("mp", None),
        P(),
    )
    return jax.shard_map(local, mesh=mesh, in_specs=in_specs, out_specs=out_specs, check_vma=False)
```

```python
import functools

import jax
import jax.numpy as jnp
from jax import lax
from jax.experimental import pallas as pl
from jax.experimental.pallas import tpu as pltpu
from jax.sharding import PartitionSpec as P

HEAD_DIM = 64
LONGEST = 900
HALO = 64
PAIR = 128
SPAN = 400
EPS = 1e-06
NEG = -1e30
VMEM = 60 * 1024 * 1024
VMEM_ALL = 67043328
F32 = jnp.float32
BF16 = jnp.bfloat16


def dot_nn(a, b):
    return lax.dot_general(a, b, (((1,), (0,)), ((), ())), preferred_element_type=F32)


def dot_nt(a, b):
    return lax.dot_general(a, b, (((1,), (1,)), ((), ())), preferred_element_type=F32)


def dot_tn(a, b):
    return lax.dot_general(a, b, (((0,), (0,)), ((), ())), preferred_element_type=F32)


def barrier(*xs):
    return lax.optimization_barrier(xs)


def params(*sem, **kw):
    return pltpu.CompilerParams(dimension_semantics=sem, vmem_limit_bytes=VMEM, **kw)


def norm_rows(x):
    mean = jnp.mean(x, axis=1, keepdims=True)
    cent = x - mean
    inv = lax.rsqrt(jnp.mean(cent * cent, axis=1, keepdims=True) + EPS)
    return cent * inv, inv


def qkv_call(n1w, packed, b_q, b_v, own, rows, cw):
    n, dm, _ = packed.shape
    win = n1w.shape[0]

    def body(x_ref, w_ref, bq_ref, bv_ref, q_ref, k_ref, v_ref):
        x = x_ref[...]
        q_ref[0] = (dot_nn(x[own : own + rows], w_ref[0, :, 0:cw]) + bq_ref[0].astype(F32)).astype(BF16)
        k_ref[0] = dot_nn(x, w_ref[0, :, cw : 2 * cw]).astype(BF16)
        v_ref[0] = (dot_nn(x, w_ref[0, :, 2 * cw : 3 * cw]) + bv_ref[0].astype(F32)).astype(BF16)

    return pl.pallas_call(
        body,
        grid=(n,),
        in_specs=[
            pl.BlockSpec((win, dm), lambda d: (0, 0)),
            pl.BlockSpec((1, dm, 4 * cw), lambda d: (d, 0, 0)),
            pl.BlockSpec((1, 1, cw), lambda d: (d, 0, 0)),
            pl.BlockSpec((1, 1, cw), lambda d: (d, 0, 0)),
        ],
        out_specs=[
            pl.BlockSpec((1, rows, cw), lambda d: (d, 0, 0)),
            pl.BlockSpec((1, win, cw), lambda d: (d, 0, 0)),
            pl.BlockSpec((1, win, cw), lambda d: (d, 0, 0)),
        ],
        out_shape=[
            jax.ShapeDtypeStruct((n, rows, cw), BF16),
            jax.ShapeDtypeStruct((n, win, cw), BF16),
            jax.ShapeDtypeStruct((n, win, cw), BF16),
        ],
        compiler_params=params("arbitrary"),
        cost_estimate=pl.CostEstimate(
            flops=2 * n * dm * cw * (rows + 2 * win), bytes_accessed=2 * (n * dm * 4 * cw + win * dm), transcendentals=0
        ),
    )(n1w, packed, b_q[:, None, :], b_v[:, None, :])


def blocks_of(rows, own, win, big):
    if big:
        step = min(256, rows)
        return [(s, step, 0, win) for s in range(0, rows, step)]
    return [(s, 128, own + s - 128, 384) for s in range(0, rows, 128)]


def attn_fwd_call(is_big, q, k, v, qseg, kseg, own):
    n, rows, cw = q.shape
    win = k.shape[1]
    pairs = cw // PAIR

    def work(big, q_ref, k_ref, v_ref, qs_ref, ks_ref, o_ref, l_ref):
        for qs, qn, ks, kn in blocks_of(rows, own, win, big):
            mask = qs_ref[qs : qs + qn, :] == ks_ref[:, ks : ks + kn]
            for h in range(2):
                lanes = slice(h * HEAD_DIM, (h + 1) * HEAD_DIM)
                qh = q_ref[0, qs : qs + qn, lanes] * BF16(HEAD_DIM**-0.5)
                s = jnp.where(mask, dot_nt(qh, k_ref[0, ks : ks + kn, lanes]), NEG)
                top = jnp.max(s, axis=1, keepdims=True)
                p = jnp.exp(s - top)
                total = jnp.sum(p, axis=1, keepdims=True)
                o = dot_nn(p.astype(BF16), v_ref[0, ks : ks + kn, lanes])
                o_ref[0, qs : qs + qn, lanes] = (o / total).astype(BF16)
                l_ref[0, qs : qs + qn, h : h + 1] = top + jnp.log(total)

    def body(big_ref, *refs):
        @pl.when(big_ref[0] == 1)
        def _():
            work(True, *refs)

        @pl.when(big_ref[0] == 0)
        def _():
            work(False, *refs)

    return pl.pallas_call(
        body,
        grid_spec=pltpu.PrefetchScalarGridSpec(
            num_scalar_prefetch=1,
            grid=(n, pairs),
            in_specs=[
                pl.BlockSpec((1, rows, PAIR), lambda d, p, *_: (d, 0, p)),
                pl.BlockSpec((1, win, PAIR), lambda d, p, *_: (d, 0, p)),
                pl.BlockSpec((1, win, PAIR), lambda d, p, *_: (d, 0, p)),
                pl.BlockSpec((rows, 1), lambda d, p, *_: (0, 0)),
                pl.BlockSpec((1, win), lambda d, p, *_: (0, 0)),
            ],
            out_specs=[
                pl.BlockSpec((1, rows, PAIR), lambda d, p, *_: (d, 0, p)),
                pl.BlockSpec((1, rows, 2), lambda d, p, *_: (d * pairs + p, 0, 0)),
            ],
        ),
        out_shape=[
            jax.ShapeDtypeStruct((n, rows, cw), BF16),
            jax.ShapeDtypeStruct((n * pairs, rows, 2), F32),
        ],
        compiler_params=params("arbitrary", "arbitrary"),
        cost_estimate=pl.CostEstimate(
            flops=16 * n * rows * win * cw, bytes_accessed=2 * n * cw * (2 * rows + 2 * win), transcendentals=n * rows * win * 4
        ),
    )(is_big, q, k, v, qseg, kseg)


def attn_bwd_call(info, q, k, v, attn, gattn, lse, qseg, kseg, own):
    n, rows, cw = q.shape
    win = k.shape[1]
    pairs = cw // PAIR
    scale = HEAD_DIM**-0.5

    def work(big, q_ref, k_ref, v_ref, a_ref, g_ref, l_ref, qs_ref, ks_ref, dq_ref, dk_ref, dv_ref, dkt, dvt):
        if not big:
            dkt[...] = jnp.zeros_like(dkt)
            dvt[...] = jnp.zeros_like(dvt)
        for i, (qs, qn, ks, kn) in enumerate(blocks_of(rows, own, win, big)):
            mask = qs_ref[qs : qs + qn, :] == ks_ref[:, ks : ks + kn]
            for h in range(2):
                lanes = slice(h * HEAD_DIM, (h + 1) * HEAD_DIM)
                qh = q_ref[0, qs : qs + qn, lanes] * BF16(scale)
                kh = k_ref[0, ks : ks + kn, lanes]
                gh = g_ref[0, qs : qs + qn, lanes]
                s = jnp.where(mask, dot_nt(qh, kh) - l_ref[0, qs : qs + qn, h : h + 1], NEG)
                p = jnp.exp(s)
                dp = dot_nt(gh, v_ref[0, ks : ks + kn, lanes])
                delta = jnp.sum(
                    gh.astype(F32) * a_ref[0, qs : qs + qn, lanes].astype(F32), axis=1, keepdims=True
                )
                ds = (p * (dp - delta)).astype(BF16)
                dq_ref[0, qs : qs + qn, lanes] = (dot_nn(ds, kh) * scale).astype(BF16)
                dk = dot_tn(qh, ds)
                dv = dot_tn(gh, p.astype(BF16))
                if big and i == 0:
                    dkt[lanes, :] = dk
                    dvt[lanes, :] = dv
                else:
                    dkt[lanes, ks : ks + kn] += dk
                    dvt[lanes, ks : ks + kn] += dv
        dk_ref[0] = dkt[...].T.astype(BF16)
        dv_ref[0] = dvt[...].T.astype(BF16)

    def body(info_ref, *refs):
        @pl.when(info_ref[0] == 1)
        def _():
            work(True, *refs)

        @pl.when(info_ref[0] == 0)
        def _():
            work(False, *refs)

    if pairs > 1:

        def put(d, p, info):
            rel = lax.bitwise_xor(p // (pairs // 2), info[1])
            return (rel, 0, d * (pairs // 2) + p % (pairs // 2))

        half_shape = (2, rows, n * cw // 2)
        half_win = (2, win, n * cw // 2)
    else:

        def put(d, p, info):
            return (0, 0, d)

        half_shape = (1, rows, n * cw)
        half_win = (1, win, n * cw)
    return pl.pallas_call(
        body,
        grid_spec=pltpu.PrefetchScalarGridSpec(
            num_scalar_prefetch=1,
            grid=(n, pairs),
            in_specs=[
                pl.BlockSpec((1, rows, PAIR), lambda d, p, *_: (d, 0, p)),
                pl.BlockSpec((1, win, PAIR), lambda d, p, *_: (d, 0, p)),
                pl.BlockSpec((1, win, PAIR), lambda d, p, *_: (d, 0, p)),
                pl.BlockSpec((1, rows, PAIR), lambda d, p, *_: (d, 0, p)),
                pl.BlockSpec((1, rows, PAIR), lambda d, p, *_: (d, 0, p)),
                pl.BlockSpec((1, rows, 2), lambda d, p, *_: (d * pairs + p, 0, 0)),
                pl.BlockSpec((rows, 1), lambda d, p, *_: (0, 0)),
                pl.BlockSpec((1, win), lambda d, p, *_: (0, 0)),
            ],
            out_specs=[
                pl.BlockSpec((1, rows, PAIR), put),
                pl.BlockSpec((1, win, PAIR), put),
                pl.BlockSpec((1, win, PAIR), put),
            ],
            scratch_shapes=[pltpu.VMEM((PAIR, win), F32), pltpu.VMEM((PAIR, win), F32)],
        ),
        out_shape=[
            jax.ShapeDtypeStruct(half_shape, BF16),
            jax.ShapeDtypeStruct(half_win, BF16),
            jax.ShapeDtypeStruct(half_win, BF16),
        ],
        compiler_params=params("arbitrary", "arbitrary"),
        cost_estimate=pl.CostEstimate(
            flops=40 * n * rows * win * cw, bytes_accessed=2 * n * cw * (4 * rows + 4 * win), transcendentals=n * rows * win * 4
        ),
    )(info, q, k, v, attn, gattn, lse, qseg, kseg)


def out_call(attn, packed, resid, b_out, gain, bias):
    n, rows, cw = attn.shape
    dm = packed.shape[1]

    def body(a_ref, w_ref, x_ref, bo_ref, g_ref, b_ref, h_ref, n_ref):
        d = pl.program_id(0)
        part = dot_nt(a_ref[0], w_ref[0])

        @pl.when(d == 0)
        def _():
            h_ref[...] = part + x_ref[...].astype(F32) + bo_ref[...].astype(F32)

        @pl.when(d > 0)
        def _():
            h_ref[...] += part

        @pl.when(d == n - 1)
        def _():
            hat, _ = norm_rows(h_ref[...])
            n_ref[...] = (hat * g_ref[...].astype(F32) + b_ref[...].astype(F32)).astype(BF16)

    full = lambda d: (0, 0)
    return pl.pallas_call(
        body,
        grid=(n,),
        in_specs=[
            pl.BlockSpec((1, rows, cw), lambda d: (d, 0, 0)),
            pl.BlockSpec((1, dm, cw), lambda d: (d, 0, 3)),
            pl.BlockSpec((rows, dm), full),
            pl.BlockSpec((1, dm), full),
            pl.BlockSpec((1, dm), full),
            pl.BlockSpec((1, dm), full),
        ],
        out_specs=[pl.BlockSpec((rows, dm), full), pl.BlockSpec((rows, dm), full)],
        out_shape=[jax.ShapeDtypeStruct((rows, dm), F32), jax.ShapeDtypeStruct((rows, dm), BF16)],
        compiler_params=params("arbitrary"),
        cost_estimate=pl.CostEstimate(flops=2 * n * rows * cw * dm, bytes_accessed=2 * n * dm * cw, transcendentals=0),
    )(attn, packed, resid, b_out[None], gain[None], bias[None])


def ffn_call(core, n2, hidden, cot, w_up, w_down, b_up, b_down, halves):
    rows, dm = n2.shape
    n, _, ffw = w_up.shape
    tile = ffw // halves

    def body(core_ref, x_ref, h_ref, c_ref, wu_ref, wd_ref, bu_ref, bd_ref, o_ref, gn_ref, a_ref, gu_ref, gb_ref, acc):
        t = pl.program_id(0)
        u = dot_nn(x_ref[...], wu_ref[0]) + bu_ref[...].astype(F32)
        cdf = 0.5 * (1.0 + lax.erf(u * 0.7071067811865476))
        act = (u * cdf).astype(BF16)
        slope = cdf + u * jnp.exp(-0.5 * u * u) * 0.3989422804014327
        a_ref[...] = act
        grad = dot_nt(c_ref[...], wd_ref[0]) * slope
        gu = grad.astype(BF16)
        gu_ref[...] = gu
        gb_ref[...] = jnp.sum(gu.astype(F32), axis=0, keepdims=True)
        out = dot_nn(act, wd_ref[0])
        gn = dot_nt(gu, wu_ref[0])

        @pl.when(t == 0)
        def _():
            acc[...] = h_ref[...] + bd_ref[...].astype(F32) + out
            gn_ref[...] = gn

        @pl.when(t > 0)
        def _():
            acc[...] += out
            gn_ref[...] += gn

        @pl.when(t == n * halves - 1)
        def _():
            o_ref[...] = acc[...].astype(BF16)

    full = lambda t, c: (0, 0)

    def part(t, c):
        return lax.bitwise_xor(t // n, c[0]) if halves > 1 else 0

    return pl.pallas_call(
        body,
        grid_spec=pltpu.PrefetchScalarGridSpec(
            num_scalar_prefetch=1,
            grid=(n * halves,),
            in_specs=[
                pl.BlockSpec((rows, dm), full),
                pl.BlockSpec((rows, dm), full),
                pl.BlockSpec((rows, dm), full),
                pl.BlockSpec((1, dm, tile), lambda t, c: (t % n, 0, part(t, c))),
                pl.BlockSpec((1, tile, dm), lambda t, c: (t % n, part(t, c), 0)),
                pl.BlockSpec((1, tile), lambda t, c: (0, t)),
                pl.BlockSpec((1, dm), full),
            ],
            out_specs=[
                pl.BlockSpec((rows, dm), full),
                pl.BlockSpec((rows, dm), full),
                pl.BlockSpec((rows, tile), lambda t, c: (0, t)),
                pl.BlockSpec((rows, tile), lambda t, c: (0, t)),
                pl.BlockSpec((1, tile), lambda t, c: (0, t)),
            ],
            scratch_shapes=[pltpu.VMEM((rows, dm), F32)],
        ),
        out_shape=[
            jax.ShapeDtypeStruct((rows, dm), BF16),
            jax.ShapeDtypeStruct((rows, dm), F32),
            jax.ShapeDtypeStruct((rows, n * ffw), BF16),
            jax.ShapeDtypeStruct((rows, n * ffw), BF16),
            jax.ShapeDtypeStruct((1, n * ffw), F32),
        ],
        compiler_params=params("arbitrary"),
        cost_estimate=pl.CostEstimate(
            flops=8 * rows * dm * n * ffw, bytes_accessed=4 * n * dm * ffw, transcendentals=2 * rows * n * ffw
        ),
    )(core, n2, hidden, cot, w_up, w_down, b_up[None], b_down[None])


def norm1_back_call(dq, dk, dv, packed, info, own):
    halves, rows, _ = dq.shape
    n, dm, four = packed.shape
    cw = four // 4
    win = dk.shape[1]
    width = cw // halves

    def body(info_ref, dq_ref, dk_ref, dv_ref, w_ref, o_ref, h_ref, t_ref, acc):
        step = pl.program_id(0)

        def weight(which, j):
            at = lax.bitwise_xor(j, info_ref[1]) if halves > 1 else 0
            return w_ref[0, :, pl.ds(pl.multiple_of(which * cw + at * width, width), width)]

        left = jnp.concatenate([r[j] for r in (dk_ref, dv_ref) for j in range(halves)], axis=1)
        right = jnp.concatenate([weight(m, j) for m in (1, 2) for j in range(halves)], axis=1)
        part = dot_nt(left, right)
        left = jnp.concatenate([dq_ref[j] for j in range(halves)], axis=1)
        right = jnp.concatenate([weight(0, j) for j in range(halves)], axis=1)
        mine = dot_nt(left, right)

        @pl.when(step == 0)
        def _():
            acc[...] = part

        @pl.when(step > 0)
        def _():
            acc[...] += part

        acc[own : own + rows, :] += mine

        @pl.when(step == n - 1)
        def _():
            o_ref[...] = acc[own : own + rows, :]
            h_ref[...] = acc[0:own, :].astype(BF16)
            t_ref[...] = acc[own + rows : own + rows + HALO, :].astype(BF16)

    full = lambda s, info: (0, 0)
    return pl.pallas_call(
        body,
        grid_spec=pltpu.PrefetchScalarGridSpec(
            num_scalar_prefetch=1,
            grid=(n,),
            in_specs=[
                pl.BlockSpec((halves, rows, width), lambda s, info: (0, 0, s)),
                pl.BlockSpec((halves, win, width), lambda s, info: (0, 0, s)),
                pl.BlockSpec((halves, win, width), lambda s, info: (0, 0, s)),
                pl.BlockSpec((1, dm, four), lambda s, info: (s, 0, 0)),
            ],
            out_specs=[
                pl.BlockSpec((rows, dm), full),
                pl.BlockSpec((own, dm), full),
                pl.BlockSpec((HALO, dm), full),
            ],
            scratch_shapes=[pltpu.VMEM((win, dm), F32)],
        ),
        out_shape=[
            jax.ShapeDtypeStruct((rows, dm), F32),
            jax.ShapeDtypeStruct((own, dm), BF16),
            jax.ShapeDtypeStruct((HALO, dm), BF16),
        ],
        compiler_params=params("arbitrary"),
        cost_estimate=pl.CostEstimate(
            flops=2 * n * cw * dm * (rows + 2 * win), bytes_accessed=2 * n * cw * (3 * dm + rows + 2 * win), transcendentals=0
        ),
    )(info, dq, dk, dv, packed)


MESH = pl.DeviceIdType.MESH


class Place:
    def __init__(self):
        self.me = lax.axis_index("dp")
        self.z = lax.axis_index("mp")
        self.k = lax.rem(self.me, 2)
        self.x = lax.rem(self.me // 2, 2)
        self.y = self.me // 4
        self.me_k = self.me + 1 - 2 * self.k
        self.me_x = self.me + 2 - 4 * self.x
        self.me_y = self.me + 4 - 8 * self.y
        self.me_xy = self.me_x + 4 - 8 * self.y
        self.core = {"dp": self.me_k, "mp": self.z}
        self.by_x = {"dp": self.me_x, "mp": self.z}
        self.by_y = {"dp": self.me_y, "mp": self.z}

    def along(self, d):
        return {"dp": self.me, "mp": lax.rem(self.z + d, 4)}

    def meet(self):
        sem = pltpu.get_barrier_semaphore()
        for dev in (self.core, self.by_x, self.by_y, self.along(1), self.along(2), self.along(3)):
            pl.semaphore_signal(sem, inc=1, device_id=dev, device_id_type=MESH)
        pl.semaphore_wait(sem, 6)


class Wire:
    def __init__(self, send, recv, dev):
        self.send, self.recv, self.dev = send, recv, dev

    def start(self, slot, src, dst, dev):
        copy = pltpu.make_async_remote_copy(
            src_ref=src, dst_ref=dst, send_sem=self.send.at[slot], recv_sem=self.recv.at[slot],
            device_id=dev, device_id_type=MESH,
        )
        copy.start()

    def sent(self, slot, ref):
        pltpu.make_async_remote_copy(
            src_ref=ref, dst_ref=ref, send_sem=self.send.at[slot], recv_sem=self.recv.at[slot],
            device_id=dict(self.dev), device_id_type=MESH,
        ).wait_send()

    def landed(self, slot, ref, dev):
        pltpu.make_async_remote_copy(
            src_ref=ref, dst_ref=ref, send_sem=self.send.at[slot], recv_sem=self.recv.at[slot],
            device_id=dev, device_id_type=MESH,
        ).wait_recv()


def gather_steps(place, wire, base, shard, whole):
    step = shard.shape[0] // 8
    half = step // 2

    def rows(who, at=0, size=step):
        return pl.ds(pl.multiple_of(who * step + at, half), size)

    def slot(d, kind):
        return base + (d - 1) * 9 + kind

    def begin(d):
        wire.start(slot(d, 0), shard.at[rows(place.me)], whole.at[d, rows(place.me)], place.along(4 - d))

    def first(d):
        mine = whole.at[d, rows(place.me)]
        wire.landed(slot(d, 0), mine, place.along(d))
        wire.start(slot(d, 2), mine, mine, place.by_x)
        wire.start(slot(d, 3), mine, mine, place.by_y)
        wire.start(slot(d, 1), mine, mine, place.core)

    def second(d):
        got = whole.at[d, rows(place.me_x)]
        wire.landed(slot(d, 2), got, place.by_x)
        part = whole.at[d, rows(place.me_x, 0, half)]
        wire.start(slot(d, 4), part, part, place.by_y)
        wire.start(slot(d, 6), got, got, place.core)
        got = whole.at[d, rows(place.me_y)]
        wire.landed(slot(d, 3), got, place.by_y)
        part = whole.at[d, rows(place.me_y, half, half)]
        wire.start(slot(d, 5), part, part, place.by_x)
        wire.start(slot(d, 7), got, got, place.core)

    def third(d):
        wire.landed(slot(d, 4), whole.at[d, rows(place.me_xy, 0, half)], place.by_y)
        wire.landed(slot(d, 5), whole.at[d, rows(place.me_xy, half, half)], place.by_x)
        got = whole.at[d, rows(place.me_xy)]
        wire.start(slot(d, 8), got, got, place.core)

    def done(d):
        flip = 1 - 2 * place.k
        for kind, who in ((1, place.me), (6, place.me_x), (7, place.me_y), (8, place.me_xy)):
            wire.landed(slot(d, kind), whole.at[d, rows(who + flip)], place.core)

    def drain():
        for d in (1, 2, 3):
            for kind in range(9):
                wire.sent(slot(d, kind), whole.at[d, pl.ds(0, half if kind in (4, 5) else step)])

    return begin, first, second, third, done, drain


def front_call(tokens, cot, pack, w_up, w_down, small, qseg, kseg, own):
    rows, dm = tokens.shape
    cw = pack.shape[1] // 4
    ffw = w_up.shape[1]
    n = 4
    tile = ffw // 2
    hw = n * tile
    win = own + rows + 2 * HALO
    pairs = cw // PAIR
    strip = 128
    per = rows // strip
    scale = HEAD_DIM**-0.5
    length = small.shape[1] - 6 * dm
    give = 6
    base = give + 3 + 3 * n

    def body(
        tok_ref, cot_ref, pack_ref, up_ref, down_ref, small_ref, qs_ref, ks_ref,
        packed_out, n1t_out, n2t_out, cott_out, ghbt_out, q_out, k_out, v_out, a_out, at_out, ga_out, act_out, gup_out, gh_out,
        l_ref, o_ref, vec_ref,
        up, down, n1, hid, n2, acc, act, gup, biases,
        packed, n1t, n2t, cott, ghbt, q_ref, k_ref, v_ref, a_ref, ga_ref, gh_ref, xs, xr, ls, fs, os,
    ):
        place = Place()
        core, z = place.k, place.z
        long, takes_prev, takes_next = z < 2, z >= 2, jnp.logical_and(z >= 1, z < 3)
        swap = {"dp": place.me, "mp": lax.rem(z + 1, 2)}
        left_dev = {"dp": place.me, "mp": lax.rem(z + 3, 4)}
        right_dev = {"dp": place.me, "mp": lax.rem(z + 1, 4)}
        wire = Wire(xs, xr, place.core)
        local = [
            pltpu.make_async_copy(src, dst, ls.at[i])
            for i, (src, dst) in enumerate(
                ((tok_ref, n1.at[own : own + rows]), (pack_ref, packed.at[0]), (up_ref, up.at[0]), (down_ref, down.at[0]))
            )
        ]
        for c in local:
            c.start()
        place.meet()
        bias_ref = small_ref.at[:, 6 * dm : 6 * dm + length]
        for d in (1, 2, 3):
            wire.start(d - 1, bias_ref, biases.at[d], place.along(4 - d))

        @pl.when(z == 0)
        def _():
            wire.start(3, tok_ref, n1.at[0:own], swap)

        @pl.when(z == 1)
        def _():
            wire.start(3, tok_ref.at[0:SPAN], n1.at[0:SPAN], swap)

        @pl.when(takes_next)
        def _():
            wire.start(4, tok_ref.at[rows - HALO : rows], n1.at[own - HALO : own], right_dev)

        @pl.when(takes_prev)
        def _():
            wire.start(5, tok_ref.at[0:HALO], n1.at[own + rows : own + rows + HALO], left_dev)

        groups = [
            gather_steps(place, wire, base + 27 * g, src, dst)
            for g, (src, dst) in enumerate(((pack_ref, packed), (up_ref, up), (down_ref, down)))
        ]
        for g in range(3):
            for d in (1, 2, 3):
                groups[g][0](d)

        def near_shard(i):
            return lax.rem(4 - z + i, 3) + 1

        items = [(0, 0), (0, 1), (0, 2), (1, 0), (2, 0), (1, 1), (2, 1), (1, 2), (2, 2)]

        def relay(i):
            for lag in range(3):
                if 0 <= i - lag < len(items):
                    g, j = items[i - lag]
                    groups[g][1 + lag](near_shard(j))

        def arrived(j, *which):
            for g in which:
                groups[g][4](near_shard(j))

        def turns(i, table):
            for t, f in table.items():

                @pl.when(i == t)
                def _():
                    f()

        def shard_at(k):
            return near_shard(k + 2) * ((k + 3) // 4)

        def strip_at(i, start=0):
            return pl.ds(pl.multiple_of(start + i * strip, strip), strip)

        row = lambda i: small_ref[:, i * dm : (i + 1) * dm]

        whole = [
            (n1t, n1t_out.at[:, 0:win]), (n2t, n2t_out.at[:, 0:rows]), (cott, cott_out.at[:, 0:rows]), (ghbt, ghbt_out),
            (q_ref, q_out), (k_ref, k_out), (v_ref, v_out), (a_ref, a_out), (ga_ref, ga_out), (gh_ref, gh_out), (packed, packed_out),
        ]
        leaving = [pltpu.make_async_copy(src, dst, os.at[i]) for i, (src, dst) in enumerate(whole)]
        shared = ((n1t, n1t_out.at[:, win : 2 * win]), (n2t, n2t_out.at[:, rows : 2 * rows]), (cott, cott_out.at[:, rows : 2 * rows]))

        def leave(i):
            leaving[i].start()
            if i < len(shared):
                wire.start(give + i, *shared[i], place.core)

        @pl.when(z == 0)
        def _():
            n1[SPAN:own, :] = jnp.zeros((own - SPAN, dm), BF16)

        @pl.when(takes_prev)
        def _():
            n1[0 : own - HALO, :] = jnp.zeros((own - HALO, dm), BF16)

        @pl.when(jnp.logical_not(takes_next))
        def _():
            n1[own + rows : own + rows + HALO, :] = jnp.zeros((HALO, dm), BF16)

        n1[own + rows + HALO :, :] = jnp.zeros((HALO, dm), BF16)
        biases[0] = bias_ref[...]
        l_ref[...] = jnp.zeros_like(l_ref)
        vec_ref[...] = jnp.zeros_like(vec_ref)

        def turn_cot(i, carry):
            cott[:, strip_at(i)] = cot_ref[strip_at(i), :].astype(F32).T.astype(BF16)
            return carry

        lax.fori_loop(0, per, turn_cot, 0)
        leave(2)

        def norm1(i):
            at = strip_at(i)
            x = n1[at, :].astype(F32)
            hat, _ = norm_rows(x)
            val = hat * row(0) + row(1)
            n1[at, :] = val.astype(BF16)
            n1t[:, at] = val.T.astype(BF16)
            return x

        def norm_own(i, carry):
            hid[strip_at(i), :] = norm1(own // strip + i) + row(4)
            return carry

        def norm_far(i, carry):
            norm1(i)
            return carry

        local[0].wait()
        lax.fori_loop(0, per, norm_own, 0)
        for c in local[1:]:
            c.wait()
        relay(0)

        @pl.when(z == 0)
        def _():
            wire.landed(3, n1.at[0:SPAN], swap)

        @pl.when(z == 1)
        def _():
            wire.landed(3, n1.at[0:own], swap)

        @pl.when(takes_prev)
        def _():
            wire.landed(4, n1.at[own - HALO : own], left_dev)

        @pl.when(takes_next)
        def _():
            wire.landed(5, n1.at[own + rows : own + rows + HALO], right_dev)

        lax.fori_loop(0, own // strip, norm_far, 0)
        norm1((own + rows) // strip)
        leave(0)
        for d in (1, 2, 3):
            wire.landed(d - 1, biases.at[d], place.along(d))
        relay(1)

        def attend(big, d, p):
            at = pl.ds(pl.multiple_of(p * PAIR, PAIR), PAIR)
            for qs, qn, ks, kn in blocks_of(rows, own, win, big):
                mask = qs_ref[qs : qs + qn, :] == ks_ref[:, ks : ks + kn]
                qq, kk, vv = q_ref[d, qs : qs + qn, at], k_ref[d, ks : ks + kn, at], v_ref[d, ks : ks + kn, at]
                outs = []
                for h in range(2):
                    lanes = slice(h * HEAD_DIM, (h + 1) * HEAD_DIM)
                    s = jnp.where(mask, dot_nt(qq[:, lanes] * BF16(scale), kk[:, lanes]), NEG)
                    top = jnp.max(s, axis=1, keepdims=True)
                    pr = jnp.exp(s - top)
                    total = jnp.sum(pr, axis=1, keepdims=True)
                    outs.append(dot_nn(pr.astype(BF16), vv[:, lanes]) / total)
                    lane = lax.broadcasted_iota(jnp.int32, (qn, 2 * n * pairs), 1)
                    seen = l_ref[qs : qs + qn, :]
                    l_ref[qs : qs + qn, :] = jnp.where(lane == (d * pairs + p) * 2 + h, top + jnp.log(total), seen)
                a_ref[d, qs : qs + qn, at] = jnp.concatenate(outs, axis=1).astype(BF16)

        def head_lanes(d):
            return pl.ds(pl.multiple_of(d * PAIR, PAIR), PAIR)

        def half_of_attn(d):
            mine = pl.ds(pl.multiple_of(core * PAIR, PAIR), PAIR)
            theirs = pl.ds(pl.multiple_of((1 - core) * PAIR, PAIR), PAIR)
            keep = pltpu.make_async_copy(a_ref.at[d, :, mine], at_out.at[0:rows, head_lanes(d)], fs.at[2 * n + d])
            return keep, a_ref.at[d, :, theirs]

        def heads(kk, carry):
            turns(kk, {j + 1: functools.partial(arrived, j, 0) for j in range(3)})
            d = shard_at(kk)
            q_ref[d] = (dot_nn(n1[own : own + rows, :], packed[d, :, 0:cw]) + biases[d, :, 0:cw]).astype(BF16)
            k_ref[d] = dot_nn(n1[...], packed[d, :, cw : 2 * cw]).astype(BF16)
            v_ref[d] = (dot_nn(n1[...], packed[d, :, 2 * cw : 3 * cw]) + biases[d, :, cw : 2 * cw]).astype(BF16)

            def one(p, inner):
                @pl.when(long)
                def _():
                    attend(True, d, p)

                @pl.when(jnp.logical_not(long))
                def _():
                    attend(False, d, p)

                turns(kk * pairs + p, {pairs * j: functools.partial(relay, 2 + j) for j in range(4)})
                return inner

            lax.fori_loop(0, pairs, one, 0)
            hid[...] += dot_nt(a_ref[d], packed[d, :, 3 * cw : 4 * cw])
            halves = half_of_attn(d)
            halves[0].start()
            wire.start(give + 3 + d, halves[1], at_out.at[rows : 2 * rows, head_lanes(d)], place.core)
            return carry

        lax.fori_loop(0, n, heads, 0)
        for i in (4, 5, 6, 7, 10):
            leave(i)
        relay(6)

        def norm2(i, carry):
            at = strip_at(i)
            hidden = hid[at, :]
            hat, _ = norm_rows(hidden)
            val = hat * row(2) + row(3)
            n2[at, :] = val.astype(BF16)
            n2t[:, at] = val.T.astype(BF16)
            acc[at, :] = hidden + row(5)
            return carry

        lax.fori_loop(0, per, norm2, 0)
        leave(1)

        def kept(d):
            at = pl.ds(pl.multiple_of(d * tile, tile), tile)
            return (
                pltpu.make_async_copy(act.at[:, at], act_out.at[0:rows, at], fs.at[d]),
                pltpu.make_async_copy(gup.at[:, at], gup_out.at[0:rows, at], fs.at[n + d]),
            )

        def feed(i, carry):
            turns(
                i,
                {
                    1: lambda: relay(7),
                    2: lambda: arrived(0, 1, 2),
                    3: lambda: relay(8),
                    4: lambda: (arrived(1, 1, 2), relay(9)),
                    5: lambda: relay(10),
                    6: lambda: arrived(2, 1, 2),
                },
            )
            d = shard_at(i // 2)
            rel = 1 - lax.rem(i, 2)
            part = lax.rem(rel + core, 2) * tile
            at = pl.ds(pl.multiple_of(part, tile), tile)
            to = pl.ds(pl.multiple_of(rel * hw + d * tile, tile), tile)
            u = dot_nn(n2[...], up[d, :, at]) + biases[d, :, pl.ds(pl.multiple_of(2 * cw + part, PAIR), tile)]
            cdf = 0.5 * (1.0 + lax.erf(u * 0.7071067811865476))
            val = (u * cdf).astype(BF16)
            slope = cdf + u * jnp.exp(-0.5 * u * u) * 0.3989422804014327
            act[:, to] = val
            gu = (dot_nt(cot_ref[...], down[d, at, :]) * slope).astype(BF16)
            gup[:, to] = gu
            unit = 8 * dm + lax.rem(z + d, n) * ffw + part
            vec_ref[:, pl.ds(pl.multiple_of(unit, tile), tile)] = jnp.sum(gu.astype(F32), axis=0, keepdims=True)

            @pl.when(rel == 0)
            def _():
                for c in kept(d):
                    c.start()

            @pl.when(rel == 1)
            def _():
                theirs = pl.ds(pl.multiple_of(d * tile, tile), tile)
                for j, (src, dst) in enumerate(((act, act_out), (gup, gup_out))):
                    wire.start(give + 3 + (j + 1) * n + d, src.at[:, to], dst.at[rows : 2 * rows, theirs], place.core)

            acc[...] += dot_nn(val, down[d, at, :])
            gn = dot_nt(gu, up[d, :, at])

            @pl.when(i == 0)
            def _():
                gh_ref[...] = gn

            @pl.when(i > 0)
            def _():
                gh_ref[...] += gn

            return carry

        lax.fori_loop(0, 2 * n, feed, 0)

        def back2(i, carry):
            at = strip_at(i)
            o_ref[at, :] = acc[at, :].astype(BF16)
            hat, inv = norm_rows(hid[at, :])
            g = gh_ref[at, :]
            gout = cot_ref[at, :].astype(F32)
            gg = g * row(2)
            first = jnp.mean(gg, axis=1, keepdims=True)
            second = jnp.mean(gg * hat, axis=1, keepdims=True)
            val = inv * (gg - first - hat * second) + gout
            gh_ref[at, :] = val
            n2[at, :] = val.astype(BF16)
            ghbt[:, at] = val.T.astype(BF16)
            for j, v in enumerate((val, g * hat, g, gout)):
                vec_ref[:, (2 + j) * dm : (3 + j) * dm] += jnp.sum(v, axis=0, keepdims=True)
            return carry

        lax.fori_loop(0, per, back2, 0)
        leave(9)
        leave(3)

        def back_attn(d, carry):
            ga_ref[d] = dot_nn(n2[...], packed[d, :, 3 * cw : 4 * cw]).astype(BF16)
            return carry

        lax.fori_loop(0, n, back_attn, 0)
        leave(8)
        for d in range(n):
            for c in (*kept(d), half_of_attn(d)[0]):
                c.wait()
        for i, (src, dst) in enumerate(shared):
            wire.landed(give + i, dst, place.core)
            wire.sent(give + i, src)
        for d in range(n):
            wire.landed(give + 3 + d, at_out.at[rows : 2 * rows, d * PAIR : (d + 1) * PAIR], place.core)
            wire.sent(give + 3 + d, at_out.at[0:rows, 0:PAIR])
            for j, dst in enumerate((act_out, gup_out)):
                wire.landed(give + 3 + (j + 1) * n + d, dst.at[rows : 2 * rows, d * tile : (d + 1) * tile], place.core)
                wire.sent(give + 3 + (j + 1) * n + d, dst.at[0:rows, 0:tile])
        for c in leaving:
            c.wait()
        for group in groups:
            group[5]()
        for d in (1, 2, 3):
            wire.sent(d - 1, biases.at[d])

        @pl.when(z == 0)
        def _():
            wire.sent(3, n1.at[0:own])

        @pl.when(z == 1)
        def _():
            wire.sent(3, n1.at[0:SPAN])

        @pl.when(takes_next)
        def _():
            wire.sent(4, n1.at[0:HALO])

        @pl.when(takes_prev)
        def _():
            wire.sent(5, n1.at[0:HALO])

    hbm = pl.BlockSpec(memory_space=pl.ANY)
    vmem = pl.BlockSpec(memory_space=pltpu.VMEM)
    half = lambda *shape: jax.ShapeDtypeStruct(shape, BF16)
    full = lambda *shape: jax.ShapeDtypeStruct(shape, F32)
    b16 = lambda *shape: pltpu.VMEM(shape, BF16)
    b32 = lambda *shape: pltpu.VMEM(shape, F32)
    slots = base + 27 * 3
    return pl.pallas_call(
        body,
        in_specs=[hbm, vmem, hbm, hbm, hbm, vmem, vmem, vmem],
        out_specs=[hbm] * 14 + [vmem] * 3,
        out_shape=[
            half(n, dm, 4 * cw), half(dm, 2 * win), half(dm, 2 * rows), half(dm, 2 * rows), half(dm, rows),
            half(n, rows, cw), half(n, win, cw), half(n, win, cw), half(n, rows, cw), half(2 * rows, n * PAIR), half(n, rows, cw),
            half(2 * rows, hw), half(2 * rows, hw), full(rows, dm),
            full(rows, 2 * n * pairs), half(rows, dm), full(1, 8 * dm + 2 * hw),
        ],
        scratch_shapes=[
            b16(n, dm, ffw), b16(n, ffw, dm), b16(win, dm), b32(rows, dm), b16(rows, dm), b32(rows, dm),
            b16(rows, 2 * hw), b16(rows, 2 * hw), b32(n, 1, length),
            b16(n, dm, 4 * cw), b16(dm, win), b16(dm, rows), b16(dm, rows), b16(dm, rows),
            b16(n, rows, cw), b16(n, win, cw), b16(n, win, cw), b16(n, rows, cw), b16(n, rows, cw), b32(rows, dm),
            pltpu.SemaphoreType.DMA((slots,)), pltpu.SemaphoreType.DMA((slots,)), pltpu.SemaphoreType.DMA((4,)),
            pltpu.SemaphoreType.DMA((3 * n,)), pltpu.SemaphoreType.DMA((11,)),
        ],
        compiler_params=pltpu.CompilerParams(collective_id=0, has_side_effects=True, vmem_limit_bytes=VMEM_ALL),
    )(tokens, cot, pack, w_up, w_down, small, qseg, kseg)


class Reduce:
    SLOTS = 32

    @staticmethod
    def scratch(dm, w):
        q = dm // 4
        e = q // 2
        return [
            pltpu.VMEM((4, q, w), BF16),
            pltpu.VMEM((4, q, w), BF16),
            pltpu.VMEM((4, e, w), BF16),
            pltpu.VMEM((4, e, w), BF16),
            pltpu.VMEM((3, q, w), BF16),
            pltpu.SemaphoreType.DMA((Reduce.SLOTS,)),
            pltpu.SemaphoreType.DMA((Reduce.SLOTS,)),
        ]

    def __init__(self, place, grad, landing, views, zb, send, recv):
        self.place, self.g, self.f = place, grad, landing
        self.ra1, self.rb1, self.ra2, self.rb2 = views
        self.zb = zb
        self.wire = Wire(send, recv, place.core)
        self.q = grad.shape[0] // 4
        self.e = self.q // 2
        self.w = grad.shape[1] // 4

    @staticmethod
    def of(place, grad, landing, scratch):
        views = [lambda d, ref=ref: ref.at[d] for ref in scratch[:4]]
        return Reduce(place, grad, landing, views, *scratch[4:])

    @staticmethod
    def within(place, grad, landing, spare, zb, send, recv):
        q, w = grad.shape[0] // 4, grad.shape[1] // 4
        bounds = (0, q, 2 * q, 2 * q + q // 2, 3 * q)
        views = [
            lambda d, a=a, b=b: spare.at[a:b, pl.ds(pl.multiple_of(d * w, w), w)] for a, b in zip(bounds[:-1], bounds[1:])
        ]
        return Reduce(place, grad, landing, views, zb, send, recv)

    def at(self, base, big, small=None):
        start = base * 2 * self.q + big * self.q + (0 if small is None else small * self.e)
        return pl.ds(pl.multiple_of(start, self.e), self.q if small is None else self.e)

    def eighth(self, small):
        return pl.ds(pl.multiple_of(small * self.e, self.e), self.e)

    def cols(self, d):
        return pl.ds(pl.multiple_of(d * self.w, self.w), self.w)

    def one(self, d):
        p, wire = self.place, self.wire
        wire.start(d, self.g.at[self.at(0, 1 - p.x), self.cols(d)], self.ra1(d), p.by_x)
        wire.start(4 + d, self.g.at[self.at(1, 1 - p.y), self.cols(d)], self.rb1(d), p.by_y)

    def two(self, d):
        p, wire, c = self.place, self.wire, self.cols(d)
        for slot, buf, to, at, mine, dev, nxt in (
            (0, self.ra1, self.ra2, self.at(0, p.x, 1 - p.y), self.eighth(1 - p.y), p.by_x, p.by_y),
            (4, self.rb1, self.rb2, self.at(1, p.y, 1 - p.x), self.eighth(1 - p.x), p.by_y, p.by_x),
        ):
            wire.landed(slot + d, buf(d), dev)
            self.g[at, c] = (self.g[at, c].astype(F32) + buf(d)[mine, :].astype(F32)).astype(BF16)
            wire.start(8 + slot + d, self.g.at[at, c], to(d), nxt)

    def sums(self, d):
        p, wire, c = self.place, self.wire, self.cols(d)
        wire.landed(8 + d, self.ra2(d), p.by_y)
        wire.landed(12 + d, self.rb2(d), p.by_x)
        up = (
            self.g[self.at(0, p.x, p.y), c].astype(F32)
            + self.ra1(d)[self.eighth(p.y), :].astype(F32)
            + self.ra2(d)[...].astype(F32)
        )
        low = (
            self.g[self.at(1, p.y, p.x), c].astype(F32)
            + self.rb1(d)[self.eighth(p.x), :].astype(F32)
            + self.rb2(d)[...].astype(F32)
        )
        return up, low

    def three(self, d):
        p, wire, c, e = self.place, self.wire, self.cols(d), self.e
        up, low = self.sums(d)
        for part, (at, val) in enumerate(((self.at(0, p.x, p.y), up), (self.at(1, p.y, p.x), low))):
            self.g[at, c] = val.astype(BF16)
            wire.start(
                16 + 12 * part + d, self.g.at[at, c], self.zb.at[d - 1, part * e : (part + 1) * e], p.along(d)
            )

    def last(self):
        p, wire, e = self.place, self.wire, self.e
        up, low = self.sums(0)
        for s in (1, 2, 3):
            wire.landed(16 + s, self.zb.at[s - 1, 0:e], p.along(4 - s))
            wire.landed(28 + s, self.zb.at[s - 1, e : 2 * e], p.along(4 - s))
            up = up + self.zb[s - 1, 0:e].astype(F32)
            low = low + self.zb[s - 1, e : 2 * e].astype(F32)
        ready = self.ra1(0)
        ready[0:e, :] = up.astype(BF16)
        ready[e : 2 * e, :] = low.astype(BF16)
        wire.start(20, ready, self.f.at[2], p.by_x)
        wire.start(21, ready, self.f.at[4], p.by_y)
        wire.start(22, ready, self.f.at[1], p.core)
        self.keep().start()

    def keep(self):
        return pltpu.make_async_copy(self.ra1(0), self.f.at[0], self.wire.send.at[16])

    def four(self):
        p, wire, e = self.place, self.wire, self.e
        wire.landed(20, self.f.at[2], p.by_x)
        wire.start(23, self.f.at[2, 0:e], self.f.at[6, 0:e], p.by_y)
        wire.start(25, self.f.at[2], self.f.at[3], p.core)
        wire.landed(21, self.f.at[4], p.by_y)
        wire.start(24, self.f.at[4, e : 2 * e], self.f.at[6, e : 2 * e], p.by_x)
        wire.start(26, self.f.at[4], self.f.at[5], p.core)

    def five(self):
        p, wire, e = self.place, self.wire, self.e
        wire.landed(23, self.f.at[6, 0:e], p.by_y)
        wire.landed(24, self.f.at[6, e : 2 * e], p.by_x)
        wire.start(27, self.f.at[6], self.f.at[7], p.core)

    def six(self):
        for slot, to in ((22, 1), (25, 3), (26, 5), (27, 7)):
            self.wire.landed(slot, self.f.at[to], self.place.core)
        e, sent = self.e, self.wire.sent
        for d in range(4):
            sent(d, self.ra1(d))
            sent(4 + d, self.rb1(d))
            sent(8 + d, self.ra2(d))
            sent(12 + d, self.rb2(d))
        for d in range(1, 4):
            sent(16 + d, self.zb.at[d - 1, 0:e])
            sent(28 + d, self.zb.at[d - 1, 0:e])
        for slot in (20, 21, 22, 25, 26, 27):
            sent(slot, self.f.at[0])
        for slot in (23, 24):
            sent(slot, self.f.at[0, 0:e])
        self.keep().wait()


def back_call(cot, act, n2, gup, ghb, n1w, attn2, packed, tokens, q, k, v, attn, gattn, lse, qseg, kseg, gain, vec, own):
    n, rows, cw = q.shape
    win = k.shape[1]
    dm = cot.shape[0]
    hw = act.shape[1]
    half = n * cw // 2
    w = hw // 4
    pairs = cw // PAIR
    scale = HEAD_DIM**-0.5
    each = len(Reduce.scratch(dm, w))
    length = vec.shape[1]
    strip = 128

    def body(
        cot_in, act_in, n2_in, gup_in, ghb_in, n1_in, at_in, w_ref, x_ref, q_in, k_in, v_in, a_in, g_in,
        l_ref, qs_ref, ks_ref, gain_ref, vec_ref,
        fd, fu, fp, gi_ref, sum_ref,
        wbuf, act2, gup2, n12, gd, gu, dq_o, dk_o, dv_o, at2, dq, dk, dv, dkt, dvt,
        far_in, prev_in, next_in, nxt, va, vr, vz, zb, q_ref, k_ref, v_ref, a_ref, g_ref, ps, pr_sem, xs, xr, ls, ws, *scr,
    ):
        place = Place()
        core, z = place.k, place.z
        long, gives_prev, gives_next = z < 2, z >= 2, jnp.logical_and(z >= 1, z < 3)
        swap = {"dp": place.me, "mp": lax.rem(z + 1, 2)}
        left_dev = {"dp": place.me, "mp": lax.rem(z + 3, 4)}
        right_dev = {"dp": place.me, "mp": lax.rem(z + 1, 4)}
        wire = Wire(xs, xr, place.core)
        cot2, n22, ghb2 = wbuf.at[0], wbuf.at[1], wbuf.at[2]
        loads = (
            (cot_in, cot2), (act_in, act2), (n2_in, n22), (gup_in, gup2), (q_in, q_ref), (k_in, k_ref), (v_in, v_ref),
            (a_in, a_ref), (g_in, g_ref), (ghb_in, ghb2.at[:, 0:rows]), (n1_in, n12), (at_in, at2),
        )
        local = [pltpu.make_async_copy(src, dst, ls.at[1 + i]) for i, (src, dst) in enumerate(loads)]
        for c in local:
            c.start()
        place.meet()
        wire.start(0, ghb_in, ghb2.at[:, rows : 2 * rows], place.core)

        def take(*which):
            for i in which:
                local[i].wait()

        down = Reduce.of(place, gd, fd, scr[:each])
        up = Reduce.of(place, gu, fu, scr[each : 2 * each])
        heads = Reduce.within(place, act2, fp, gup2, zb, ps, pr_sem)

        def make(red, grad, left, right):
            def step(i, carry):
                d = lax.rem(i + 1, 4)
                c = pl.ds(pl.multiple_of(d * w, w), w)
                grad[:, c] = dot_nn(left[...], right[:, c]).astype(BF16)
                red.one(d)
                return carry

            lax.fori_loop(0, 4, step, 0)

        take(0, 1)
        make(down, gd, cot2, act2)
        take(2, 3)
        make(up, gu, n22, gup2)

        def weights(t):
            at = lax.rem(t, 3)
            return pltpu.make_async_copy(w_ref.at[lax.rem(t, n)], wbuf.at[at], ws.at[at])

        weights(0).start()
        weights(1).start()

        def turns(i, table):
            for t, f in table.items():

                @pl.when(i == t)
                def _():
                    f()

        def work(big, d, p):
            at = pl.ds(pl.multiple_of(p * PAIR, PAIR), PAIR)
            to = pl.ds(pl.multiple_of(d * PAIR, PAIR), PAIR)
            rel = lax.rem(p + core, 2)
            if not big:
                dkt[...] = jnp.zeros_like(dkt)
                dvt[...] = jnp.zeros_like(dvt)
            for i, (qs, qn, ks, kn) in enumerate(blocks_of(rows, own, win, big)):
                mask = qs_ref[qs : qs + qn, :] == ks_ref[:, ks : ks + kn]
                qq, kk, vv = q_ref[d, qs : qs + qn, at], k_ref[d, ks : ks + kn, at], v_ref[d, ks : ks + kn, at]
                gg = g_ref[d, qs : qs + qn, at]
                prod = gg.astype(F32) * a_ref[d, qs : qs + qn, at].astype(F32)
                dqs = []
                for h in range(2):
                    lanes = slice(h * HEAD_DIM, (h + 1) * HEAD_DIM)
                    qh, kh, gh = qq[:, lanes] * BF16(scale), kk[:, lanes], gg[:, lanes]
                    lane = lax.broadcasted_iota(jnp.int32, (qn, 2 * n * pairs), 1)
                    picked = jnp.where(lane == (d * pairs + p) * 2 + h, l_ref[qs : qs + qn, :], 0.0)
                    s = jnp.where(mask, dot_nt(qh, kh) - jnp.sum(picked, axis=1, keepdims=True), NEG)
                    pr = jnp.exp(s)
                    dp = dot_nt(gh, vv[:, lanes])
                    delta = jnp.sum(prod[:, lanes], axis=1, keepdims=True)
                    ds = (pr * (dp - delta)).astype(BF16)
                    dqs.append(dot_nn(ds, kh) * scale)
                    gk = dot_tn(qh, ds)
                    gv = dot_tn(gh, pr.astype(BF16))
                    if big and i == 0:
                        dkt[lanes, :] = gk
                        dvt[lanes, :] = gv
                    else:
                        dkt[lanes, ks : ks + kn] += gk
                        dvt[lanes, ks : ks + kn] += gv
                dq[rel, qs : qs + qn, to] = jnp.concatenate(dqs, axis=1).astype(BF16)
            dk[rel, :, to] = dkt[...].T.astype(BF16)
            dv[rel, :, to] = dvt[...].T.astype(BF16)

        def head_pair(i, carry):
            d, p = i // pairs, lax.rem(i, pairs)

            @pl.when(long)
            def _():
                work(True, d, p)

            @pl.when(jnp.logical_not(long))
            def _():
                work(False, d, p)

            order = [(down, 1), (down, 2), (down, 3), (down, 0), (up, 1), (up, 2)]
            turns(i, {t + 2: functools.partial(red.two, shard) for t, (red, shard) in enumerate(order)})
            return carry

        take(4, 5, 6, 7, 8)
        lax.fori_loop(0, n * pairs, head_pair, 0)
        halves = ((dq, dq_o), (dk, dk_o), (dv, dv_o))
        for i, (src, dst) in enumerate(halves):
            wire.start(10 + i, src.at[1], dst, place.core)
        take(9, 10, 11)
        wire.landed(0, ghb2.at[:, rows : 2 * rows], place.core)

        def put(m, val):
            for d in range(n):
                at = d * w + m * PAIR
                act2[:, at : at + PAIR] = val[:, d * PAIR : (d + 1) * PAIR].astype(BF16)

        put(3, dot_nn(ghb2[...], at2[...]))
        weights(2).start()
        wire.landed(10, dq_o, place.core)
        put(0, dot_nn(n12[:, own : own + rows], dq[0]) + dot_nn(n12[:, win + own : win + own + rows], dq_o[...]))
        up.two(3)
        wire.landed(11, dk_o, place.core)
        put(1, dot_nn(n12[:, 0:win], dk[0]) + dot_nn(n12[:, win : 2 * win], dk_o[...]))
        up.two(0)
        wire.landed(12, dv_o, place.core)
        put(2, dot_nn(n12[:, 0:win], dv[0]) + dot_nn(n12[:, win : 2 * win], dv_o[...]))
        for d in (1, 2, 3, 0):
            heads.one(d)

        far_out, x_buf, next_out = n12.at[0:own, 0:dm], n12.at[0:rows, dm : 2 * dm], n12.at[own : own + HALO, 0:dm]
        tokens_in = pltpu.make_async_copy(x_ref, x_buf, ls.at[0])
        tokens_in.start()

        def dots(t, carry):
            weights(t).wait()
            slot = lax.rem(t, 3)
            to = pl.ds(pl.multiple_of(lax.rem(t, n) * PAIR, PAIR), PAIR)

            def weight(which, j):
                at = which * cw + lax.rem(j + core, 2) * PAIR
                return wbuf[slot, :, pl.ds(pl.multiple_of(at, PAIR), PAIR)]

            def add(ref, val, first):
                @pl.when(t == first)
                def _():
                    ref[...] = val

                @pl.when(t > first)
                def _():
                    ref[...] += val

            right = jnp.concatenate([weight(m, j) for m in (1, 2) for j in range(2)], axis=1)

            @pl.when(t < n)
            def _():
                left = jnp.concatenate([r[j, 0:own, to] for r in (dk, dv) for j in range(2)], axis=1)
                add(gi_ref, dot_nt(left, right), 0)

            @pl.when(t >= n)
            def _():
                left = jnp.concatenate([r[j, own : own + rows, to] for r in (dk, dv) for j in range(2)], axis=1)
                mine = jnp.concatenate([dq[j, :, to] for j in range(2)], axis=1)
                other = jnp.concatenate([weight(0, j) for j in range(2)], axis=1)
                add(gi_ref, dot_nt(left, right) + dot_nt(mine, other), n)
                left = jnp.concatenate(
                    [r[j, own + rows : own + rows + HALO, to] for r in (dk, dv) for j in range(2)], axis=1
                )
                add(nxt, dot_nt(left, right), n)

            @pl.when(t < 2 * n - 3)
            def _():
                weights(t + 3).start()

            @pl.when(t == n - 1)
            def _():
                far_out[...] = gi_ref[...].astype(BF16)

                @pl.when(z == 0)
                def _():
                    wire.start(13, far_out.at[0:SPAN], far_in.at[0:SPAN], swap)

                @pl.when(z == 1)
                def _():
                    wire.start(13, far_out, far_in, swap)

                @pl.when(gives_prev)
                def _():
                    wire.start(14, far_out.at[own - HALO : own], prev_in, left_dev)

            turns(t, {2 * i + 1: functools.partial(down.three, i + 1) for i in range(3)})
            return carry

        lax.fori_loop(0, 2 * n, dots, 0)
        next_out[...] = nxt[...].astype(BF16)

        @pl.when(gives_next)
        def _():
            wire.start(15, next_out, next_in, right_dev)

        up.three(1)
        up.three(2)
        up.three(3)
        heads.two(1)
        heads.two(2)
        down.last()
        heads.two(3)
        heads.two(0)
        heads.three(1)

        @pl.when(z == 0)
        def _():
            wire.landed(13, far_in, swap)
            gi_ref[...] += far_in[...].astype(F32)

        @pl.when(z == 1)
        def _():
            wire.landed(13, far_in.at[0:SPAN], swap)
            gi_ref[0:SPAN, :] += far_in[0:SPAN, :].astype(F32)

        @pl.when(gives_next)
        def _():
            wire.landed(14, prev_in, right_dev)
            gi_ref[rows - HALO : rows, :] += prev_in[...].astype(F32)

        @pl.when(gives_prev)
        def _():
            wire.landed(15, next_in, left_dev)
            gi_ref[0:HALO, :] += next_in[...].astype(F32)

        up.last()
        heads.three(2)
        heads.three(3)
        va[0] = vec_ref[...]
        for base, grad in ((6, dq), (7, dv)):
            for j in range(2):
                total = jnp.sum(grad[j].astype(F32), axis=0, keepdims=True)
                for d in range(n):
                    at = base * dm + lax.rem(z + d, n) * cw + lax.rem(j + core, 2) * PAIR
                    va[0, :, pl.ds(pl.multiple_of(at, PAIR), PAIR)] = total[:, d * PAIR : (d + 1) * PAIR]
        tokens_in.wait()
        gains = gain_ref[...].astype(F32)

        def norm(i, carry):
            at = pl.ds(pl.multiple_of(i * strip, strip), strip)
            hat, inv = norm_rows(x_buf[at, :].astype(F32))
            grad = gi_ref[at, :]
            gg = grad * gains
            first = jnp.mean(gg, axis=1, keepdims=True)
            second = jnp.mean(gg * hat, axis=1, keepdims=True)
            gi_ref[at, :] = inv * (gg - first - hat * second)
            va[0, :, 0:dm] += jnp.sum(grad * hat, axis=0, keepdims=True)
            va[0, :, dm : 2 * dm] += jnp.sum(grad, axis=0, keepdims=True)
            return carry

        lax.fori_loop(0, rows // strip, norm, 0)

        hops = (place.core, place.by_x, place.by_y)
        between = (down.four, up.four, down.five)
        for i, dev in enumerate(hops):
            wire.start(16 + i, va.at[i], vr.at[i], dev)
            between[i]()
            wire.landed(16 + i, vr.at[i], dev)
            if i < 2:
                va[i + 1] = va[i] + vr[i]
            else:
                vz[0] = va[i] + vr[i]
        for d in (1, 2, 3):
            wire.start(18 + d, vz.at[0], vz.at[d], place.along(d))
        up.five()
        heads.last()
        heads.four()
        for d in (1, 2, 3):
            wire.landed(18 + d, vz.at[d], place.along(4 - d))
        terms = [vz[lax.rem(z - a + 4, 4)] for a in range(4)]
        sum_ref[...] = (terms[0] + terms[1]) + (terms[2] + terms[3])
        heads.five()
        down.six()
        up.six()
        heads.six()
        wire.sent(0, ghb2.at[:, 0:rows])
        for i in range(3):
            wire.sent(10 + i, halves[i][1])

        @pl.when(z == 0)
        def _():
            wire.sent(13, far_in.at[0:SPAN])

        @pl.when(z == 1)
        def _():
            wire.sent(13, far_in)

        @pl.when(gives_prev)
        def _():
            wire.sent(14, prev_in)

        @pl.when(gives_next)
        def _():
            wire.sent(15, next_in)

        for i in range(3):
            wire.sent(16 + i, va.at[i])
        for d in (1, 2, 3):
            wire.sent(18 + d, vz.at[0])

    hbm = pl.BlockSpec(memory_space=pl.ANY)
    vmem = pl.BlockSpec(memory_space=pltpu.VMEM)
    shaped = lambda *shape: jax.ShapeDtypeStruct(shape, BF16)
    buf = lambda *shape: pltpu.VMEM(shape, BF16)
    wide = lambda *shape: pltpu.VMEM(shape, F32)
    sem = lambda count: pltpu.SemaphoreType.DMA((count,))
    q4 = dm // 4
    return pl.pallas_call(
        body,
        in_specs=[hbm] * 14 + [vmem] * 5,
        out_specs=[hbm] * 3 + [vmem] * 2,
        out_shape=[shaped(8, q4, w)] * 3 + [jax.ShapeDtypeStruct((rows, dm), F32), jax.ShapeDtypeStruct((1, length), F32)],
        scratch_shapes=[
            buf(3, dm, 2 * rows), buf(2 * rows, hw), buf(2 * rows, hw), buf(dm, 2 * win), buf(dm, hw), buf(dm, hw),
            buf(rows, half), buf(win, half), buf(win, half), buf(2 * rows, half), buf(2, rows, half), buf(2, win, half), buf(2, win, half),
            wide(PAIR, win), wide(PAIR, win), buf(own, dm), buf(HALO, dm), buf(HALO, dm), wide(HALO, dm),
            wide(3, 1, length), wide(3, 1, length), wide(4, 1, length), buf(3, q4, w),
            buf(n, rows, cw), buf(n, win, cw), buf(n, win, cw), buf(n, rows, cw), buf(n, rows, cw),
            sem(Reduce.SLOTS), sem(Reduce.SLOTS), sem(22), sem(22), sem(13), sem(3),
        ]
        + Reduce.scratch(dm, w) * 2,
        compiler_params=pltpu.CompilerParams(collective_id=1, has_side_effects=True, vmem_limit_bytes=VMEM_ALL),
    )(cot, act, n2, gup, ghb, n1w, attn2, packed, tokens, q, k, v, attn, gattn, lse, qseg, kseg, gain[None], vec)


def place_grads(coords, done, mode):
    _, q, w = done.shape
    e = q // 2
    dm = 4 * q
    lanes = w // 4

    def body(c_ref, f_ref, *outs):
        for off in range(8):
            y = lax.bitwise_xor(c_ref[0], off >> 2)
            x = lax.bitwise_xor(c_ref[1], (off >> 1) & 1)
            k = lax.bitwise_xor(c_ref[2], off & 1)
            for part in range(2):
                val = f_ref[off, part * e : (part + 1) * e, :].astype(F32)
                block = x * 2 + y if part == 0 else 4 + y * 2 + x
                rows = pl.ds(pl.multiple_of(block * e, e), e)
                if mode == "up":
                    outs[0][rows, pl.ds(pl.multiple_of(k * w, w), w)] = val
                elif mode == "down":
                    outs[0][pl.ds(pl.multiple_of(k * w, w), w), rows] = val.T
                else:
                    at = pl.ds(pl.multiple_of(k * lanes, lanes), lanes)
                    for m in range(3):
                        outs[m][rows, at] = val[:, m * lanes : (m + 1) * lanes]
                    outs[3][at, rows] = val[:, 3 * lanes :].T

    if mode == "up":
        shapes = [(dm, 2 * w)]
    elif mode == "down":
        shapes = [(2 * w, dm)]
    else:
        shapes = [(dm, w // 2)] * 3 + [(w // 2, dm)]
    return pl.pallas_call(
        body,
        in_specs=[pl.BlockSpec(memory_space=pltpu.SMEM), pl.BlockSpec(memory_space=pltpu.VMEM)],
        out_specs=[pl.BlockSpec(memory_space=pltpu.VMEM)] * len(shapes),
        out_shape=[jax.ShapeDtypeStruct(s, F32) for s in shapes],
        compiler_params=pltpu.CompilerParams(vmem_limit_bytes=VMEM),
        cost_estimate=pl.CostEstimate(flops=0, bytes_accessed=12 * dm * w, transcendentals=0),
    )(coords, done)


def relative(stack, z):
    return jnp.roll(stack, -z, axis=0)


def core_first(v, core, axis):
    return jnp.where(core == 0, v, jnp.flip(v, axis))


def gather_any(shard, z):
    return relative(lax.all_gather(shard, "mp", axis=0, tiled=False), z)


def reduce_any(half, z, core):
    zero = jnp.zeros_like(half)
    v = jnp.stack([jnp.where(core == 0, half, zero), jnp.where(core == 1, half, zero)], axis=2)
    v = jnp.roll(jnp.moveaxis(v, 1, 0), z, axis=0)
    v = lax.psum_scatter(v, "mp", scatter_dimension=0, tiled=True)[0]
    return lax.psum(v, "dp").astype(F32).reshape(half.shape[0], -1)


def local(
    tokens,
    segments,
    ln1_gain,
    ln1_bias,
    w_query,
    b_query,
    w_key,
    w_value,
    b_value,
    w_out,
    b_out,
    ln2_gain,
    ln2_bias,
    w_up,
    b_up,
    w_down,
    b_down,
    cotangent,
):
    rows, dm = tokens.shape
    cw = w_query.shape[1]
    ffw = w_up.shape[1]
    mp = lax.axis_size("mp")
    dp = lax.axis_size("dp")
    fast = mp == 4 and dp == 8 and rows % 256 == 0 and cw == 2 * PAIR and rows < LONGEST <= rows + SPAN <= 2 * rows
    z = lax.axis_index("mp")
    me = lax.axis_index("dp")
    core = lax.rem(me, 2)
    x = lax.rem(me // 2, 2)
    y = me // 4
    f32 = lambda v: v.astype(F32)

    near = -(-LONGEST // rows)
    own = (near - 1) * rows
    win = own + rows + 2 * HALO
    is_near = z < near
    seg_parts = [
        jnp.where(is_near, lax.dynamic_slice_in_dim(segments, lax.rem(z + j, near) * rows, rows), -1)
        for j in range(1, near)
    ]
    seg_own = lax.dynamic_slice_in_dim(segments, z * rows, rows)
    seg_prev = lax.dynamic_slice_in_dim(segments, jnp.maximum(z * rows - HALO, 0), HALO)
    seg_next = lax.dynamic_slice_in_dim(segments, jnp.minimum((z + 1) * rows, segments.shape[0] - HALO), HALO)
    seg_far = jnp.concatenate(seg_parts)
    seg_far = jnp.concatenate([seg_far[:-HALO], jnp.where(is_near, seg_far[-HALO:], seg_prev)])
    has_next = jnp.logical_and(z >= near - 1, z < mp - 1)
    seg_win = jnp.concatenate(
        [seg_far, seg_own, jnp.where(has_next, seg_next, -1), jnp.full((HALO,), -1, segments.dtype)]
    )
    kseg, qseg = seg_win[None, :], seg_own[:, None]
    info = jnp.stack([is_near.astype(jnp.int32), core]).astype(jnp.int32)

    pack = jnp.concatenate([w_query, w_key, w_value, w_out.T], axis=1)
    hw = mp * ffw // 2
    if fast:
        small = jnp.concatenate([ln1_gain, ln1_bias, ln2_gain, ln2_bias, b_out, b_down, b_query, b_value, b_up])
        small = f32(small)[None]
        (
            packed, n1_t, n2_t, cot_t, ghb_t, q, k, v, attn, attn_2, g_attn, active, g_upper, g_hidden, lse, output, vec
        ) = front_call(tokens, cotangent, pack, w_up, w_down, small, qseg, kseg, own)
        done_d, done_u, done_p, g_in, vec = back_call(
            cot_t, active, n2_t, g_upper, ghb_t, n1_t, attn_2, packed, tokens, q, k, v, attn, g_attn, lse, qseg, kseg, ln1_gain, vec, own
        )
        vec = vec[0]
        g_tokens = g_in + g_hidden
        coords = jnp.stack([y, x, core]).astype(jnp.int32)
        (g_w_down,) = place_grads(coords, done_d, "down")
        (g_w_up,) = place_grads(coords, done_u, "up")
        g_w_query, g_w_key, g_w_value, g_w_out = place_grads(coords, done_p, "pack")
    else:
        halo = [
            lax.ppermute(tokens, "mp", [((i + j) % near, i) for i in range(near)]) for j in range(1, near)
        ]
        before = lax.ppermute(tokens[-HALO:], "mp", [(i - 1, i) for i in range(near, mp)])
        behind = lax.ppermute(tokens[:HALO], "mp", [(i + 1, i) for i in range(near - 1, mp - 1)])
        small_vec = jnp.concatenate([b_query, b_value, b_up])
        vecs = relative(lax.all_gather(small_vec, "mp", axis=0, tiled=False), z)
        bq_all, bv_all = vecs[:, :cw], vecs[:, cw : 2 * cw]
        bu_all = vecs[:, 2 * cw :].reshape(mp, 2, ffw // 2).transpose(1, 0, 2)
        bu_all = core_first(bu_all, core, 0).reshape(mp * ffw)

        packed, up_all, down_all = (gather_any(w, z) for w in (pack, w_up, w_down))

        far = jnp.concatenate(halo, axis=0)
        far = jnp.concatenate([far[:-HALO], far[-HALO:] + before], axis=0)
        tok_win = jnp.concatenate([far, tokens, behind, jnp.zeros((HALO, dm), tokens.dtype)], axis=0)
        hat_win, inv_win = norm_rows(f32(tok_win))
        n1w = (hat_win * f32(ln1_gain) + f32(ln1_bias)).astype(BF16)
        q, k, v = qkv_call(n1w, packed, bq_all, bv_all, own, rows, cw)
        attn, lse = attn_fwd_call(info, q, k, v, qseg, kseg, own)
        hidden, n2 = out_call(attn, packed, tokens, b_out, ln2_gain, ln2_bias)
        output, g_n2, active, g_upper, g_b_up = ffn_call(
            info[1:], n2, hidden, cotangent, up_all, down_all, bu_all, b_down, 2
        )

        gout = f32(cotangent)
        hat2, inv2 = norm_rows(hidden)

        def norm_back(g, hat, inv, gain):
            gg = g * gain
            first = jnp.mean(gg, axis=1, keepdims=True)
            second = jnp.mean(gg * hat, axis=1, keepdims=True)
            return inv * (gg - first - hat * second), jnp.sum(g * hat, axis=0), jnp.sum(g, axis=0)

        g_hidden, g_gain2, g_bias2 = norm_back(g_n2, hat2, inv2, f32(ln2_gain))
        g_hidden = g_hidden + gout
        ghb = g_hidden.astype(BF16)

        g_attn = jnp.stack([dot_nn(ghb, packed[d, :, 3 * cw :]).astype(BF16) for d in range(mp)])
        dq, dk, dv = attn_bwd_call(info, q, k, v, attn, g_attn, lse, qseg, kseg, own)
        n1 = n1w[own : own + rows]
        sums = [jnp.sum(g_hidden, axis=0), g_gain2, g_bias2, jnp.sum(gout, axis=0)]
        halves = dq.shape[0]

        def shards(v, width):
            if v.shape[0] == 2:
                v = core_first(v.reshape(2, mp, width // 2), core, 0).transpose(1, 0, 2)
            return jnp.roll(v.reshape(mp, width), z, axis=0).reshape(mp * width)

        gbq = shards(jnp.sum(f32(dq), axis=1), cw)
        gbv = shards(jnp.sum(f32(dv), axis=1), cw)
        gbu = core_first(g_b_up.reshape(2, mp, ffw // 2), core, 0).transpose(1, 0, 2)
        gbu = jnp.roll(gbu.reshape(mp, ffw), z, axis=0).reshape(-1)
        sums = sums + [gbq, gbv, gbu]
        g_own, g_far, g_next = norm1_back_call(dq, dk, dv, packed, info, own)
        back = g_own
        for j in range(1, near):
            part = g_far[(j - 1) * rows : j * rows]
            back = back + f32(lax.ppermute(part, "mp", [(i, (i + j) % near) for i in range(near)]))
        to_prev = f32(lax.ppermute(g_far[-HALO:], "mp", [(i, i - 1) for i in range(near, mp)]))
        to_next = f32(lax.ppermute(g_next, "mp", [(i, i + 1) for i in range(near - 1, mp - 1)]))
        back = jnp.concatenate([back[:HALO] + to_next, back[HALO:-HALO], back[-HALO:] + to_prev], axis=0)
        hat1 = hat_win[own : own + rows]
        inv1 = inv_win[own : own + rows]
        g_in, g_gain1, g_bias1 = norm_back(back, hat1, inv1, f32(ln1_gain))
        g_tokens = g_in + g_hidden

        other = lambda v: lax.ppermute(v, "dp", [(i, i - i % 2 + (i + 1) % 2) for i in range(dp)])
        hw = mp * ffw // 2

        def pair_grad(left, right):
            return (dot_tn(left, right[:, :hw]) + dot_tn(other(left), other(right[:, hw:]))).astype(BF16)

        gd = pair_grad(cotangent, active)
        gu = pair_grad(n2, g_upper)
        g_w_up = reduce_any(gu.reshape(dm, mp, ffw // 2), z, core)
        g_w_down = reduce_any(gd.reshape(dm, mp, ffw // 2), z, core).T

        def whole_grad(left, right, name=None):
            v = dot_tn(left, right).astype(BF16).reshape(dm, mp, cw)
            v = jnp.roll(jnp.moveaxis(v, 1, 0), z, axis=0)
            v = lax.psum_scatter(v, "mp", scatter_dimension=0, tiled=True)[0]
            return lax.psum(v, "dp").astype(F32)

        def whole(v):
            if halves == 1:
                return v[0]
            v = v.reshape(2, v.shape[1], mp, cw // 2).transpose(1, 2, 0, 3)
            return core_first(v, core, 2).reshape(v.shape[0], mp * cw)

        g_w_query = whole_grad(n1, whole(dq))
        g_w_key = whole_grad(n1w, whole(dk))
        g_w_value = whole_grad(n1w, whole(dv))
        g_w_out = whole_grad(ghb, attn.transpose(1, 0, 2).reshape(rows, mp * cw)).T

        vec = lax.psum(jnp.concatenate([g_gain1, g_bias1] + sums), ("dp", "mp"))
    g_gain1, g_bias1, g_b_out, g_gain2, g_bias2, g_b_down = (vec[i * dm : (i + 1) * dm] for i in range(6))
    at = 6 * dm
    g_b_query = lax.dynamic_slice_in_dim(vec, at + z * cw, cw)
    g_b_value = lax.dynamic_slice_in_dim(vec, at + mp * cw + z * cw, cw)
    g_b_up = lax.dynamic_slice_in_dim(vec, at + 2 * mp * cw + z * ffw, ffw)
    return (
        output,
        g_tokens,
        g_gain1,
        g_bias1,
        g_w_query,
        g_b_query,
        g_w_key,
        g_w_value,
        g_b_value,
        g_w_out,
        g_b_out,
        g_gain2,
        g_bias2,
        g_w_up,
        g_b_up,
        g_w_down,
        g_b_down,
    )


def solution(mesh):
    in_specs = (
        P(("dp", "mp"), None),
        P("dp"),
        P(),
        P(),
        P(None, "mp"),
        P("mp"),
        P(None, "mp"),
        P(None, "mp"),
        P("mp"),
        P("mp", None),
        P(),
        P(),
        P(),
        P(None, "mp"),
        P("mp"),
        P("mp", None),
        P(),
        P(("dp", "mp"), None),
    )
    out_specs = (
        P(("dp", "mp"), None),
        P(("dp", "mp"), None),
        P(),
        P(),
        P(None, "mp"),
        P("mp"),
        P(None, "mp"),
        P(None, "mp"),
        P("mp"),
        P("mp", None),
        P(),
        P(),
        P(),
        P(None, "mp"),
        P("mp"),
        P("mp", None),
        P(),
    )
    return jax.shard_map(local, mesh=mesh, in_specs=in_specs, out_specs=out_specs, check_vma=False)
```

```python
import functools

import jax
import jax.numpy as jnp
from jax import lax
from jax.experimental import pallas as pl
from jax.experimental.pallas import tpu as pltpu
from jax.sharding import PartitionSpec as P

HEAD_DIM = 64
LONGEST = 900
HALO = 64
PAIR = 128
SPAN = 400
EPS = 1e-06
NEG = -1e30
VMEM = 60 * 1024 * 1024
VMEM_ALL = 67043328
F32 = jnp.float32
BF16 = jnp.bfloat16


def dot_nn(a, b):
    return lax.dot_general(a, b, (((1,), (0,)), ((), ())), preferred_element_type=F32)


def dot_nt(a, b):
    return lax.dot_general(a, b, (((1,), (1,)), ((), ())), preferred_element_type=F32)


def dot_tn(a, b):
    return lax.dot_general(a, b, (((0,), (0,)), ((), ())), preferred_element_type=F32)


def barrier(*xs):
    return lax.optimization_barrier(xs)


def params(*sem, **kw):
    return pltpu.CompilerParams(dimension_semantics=sem, vmem_limit_bytes=VMEM, **kw)


def norm_rows(x):
    mean = jnp.mean(x, axis=1, keepdims=True)
    cent = x - mean
    inv = lax.rsqrt(jnp.mean(cent * cent, axis=1, keepdims=True) + EPS)
    return cent * inv, inv


def qkv_call(n1w, packed, b_q, b_v, own, rows, cw):
    n, dm, _ = packed.shape
    win = n1w.shape[0]

    def body(x_ref, w_ref, bq_ref, bv_ref, q_ref, k_ref, v_ref):
        x = x_ref[...]
        q_ref[0] = (dot_nn(x[own : own + rows], w_ref[0, :, 0:cw]) + bq_ref[0].astype(F32)).astype(BF16)
        k_ref[0] = dot_nn(x, w_ref[0, :, cw : 2 * cw]).astype(BF16)
        v_ref[0] = (dot_nn(x, w_ref[0, :, 2 * cw : 3 * cw]) + bv_ref[0].astype(F32)).astype(BF16)

    return pl.pallas_call(
        body,
        grid=(n,),
        in_specs=[
            pl.BlockSpec((win, dm), lambda d: (0, 0)),
            pl.BlockSpec((1, dm, 4 * cw), lambda d: (d, 0, 0)),
            pl.BlockSpec((1, 1, cw), lambda d: (d, 0, 0)),
            pl.BlockSpec((1, 1, cw), lambda d: (d, 0, 0)),
        ],
        out_specs=[
            pl.BlockSpec((1, rows, cw), lambda d: (d, 0, 0)),
            pl.BlockSpec((1, win, cw), lambda d: (d, 0, 0)),
            pl.BlockSpec((1, win, cw), lambda d: (d, 0, 0)),
        ],
        out_shape=[
            jax.ShapeDtypeStruct((n, rows, cw), BF16),
            jax.ShapeDtypeStruct((n, win, cw), BF16),
            jax.ShapeDtypeStruct((n, win, cw), BF16),
        ],
        compiler_params=params("arbitrary"),
        cost_estimate=pl.CostEstimate(
            flops=2 * n * dm * cw * (rows + 2 * win), bytes_accessed=2 * (n * dm * 4 * cw + win * dm), transcendentals=0
        ),
    )(n1w, packed, b_q[:, None, :], b_v[:, None, :])


def blocks_of(rows, own, win, big):
    if big:
        step = min(256, rows)
        return [(s, step, 0, win) for s in range(0, rows, step)]
    return [(s, 128, own + s - 128, 384) for s in range(0, rows, 128)]


def attn_fwd_call(is_big, q, k, v, qseg, kseg, own):
    n, rows, cw = q.shape
    win = k.shape[1]
    pairs = cw // PAIR

    def work(big, q_ref, k_ref, v_ref, qs_ref, ks_ref, o_ref, l_ref):
        for qs, qn, ks, kn in blocks_of(rows, own, win, big):
            mask = qs_ref[qs : qs + qn, :] == ks_ref[:, ks : ks + kn]
            for h in range(2):
                lanes = slice(h * HEAD_DIM, (h + 1) * HEAD_DIM)
                qh = q_ref[0, qs : qs + qn, lanes] * BF16(HEAD_DIM**-0.5)
                s = jnp.where(mask, dot_nt(qh, k_ref[0, ks : ks + kn, lanes]), NEG)
                top = jnp.max(s, axis=1, keepdims=True)
                p = jnp.exp(s - top)
                total = jnp.sum(p, axis=1, keepdims=True)
                o = dot_nn(p.astype(BF16), v_ref[0, ks : ks + kn, lanes])
                o_ref[0, qs : qs + qn, lanes] = (o / total).astype(BF16)
                l_ref[0, qs : qs + qn, h : h + 1] = top + jnp.log(total)

    def body(big_ref, *refs):
        @pl.when(big_ref[0] == 1)
        def _():
            work(True, *refs)

        @pl.when(big_ref[0] == 0)
        def _():
            work(False, *refs)

    return pl.pallas_call(
        body,
        grid_spec=pltpu.PrefetchScalarGridSpec(
            num_scalar_prefetch=1,
            grid=(n, pairs),
            in_specs=[
                pl.BlockSpec((1, rows, PAIR), lambda d, p, *_: (d, 0, p)),
                pl.BlockSpec((1, win, PAIR), lambda d, p, *_: (d, 0, p)),
                pl.BlockSpec((1, win, PAIR), lambda d, p, *_: (d, 0, p)),
                pl.BlockSpec((rows, 1), lambda d, p, *_: (0, 0)),
                pl.BlockSpec((1, win), lambda d, p, *_: (0, 0)),
            ],
            out_specs=[
                pl.BlockSpec((1, rows, PAIR), lambda d, p, *_: (d, 0, p)),
                pl.BlockSpec((1, rows, 2), lambda d, p, *_: (d * pairs + p, 0, 0)),
            ],
        ),
        out_shape=[
            jax.ShapeDtypeStruct((n, rows, cw), BF16),
            jax.ShapeDtypeStruct((n * pairs, rows, 2), F32),
        ],
        compiler_params=params("arbitrary", "arbitrary"),
        cost_estimate=pl.CostEstimate(
            flops=16 * n * rows * win * cw, bytes_accessed=2 * n * cw * (2 * rows + 2 * win), transcendentals=n * rows * win * 4
        ),
    )(is_big, q, k, v, qseg, kseg)


def attn_bwd_call(info, q, k, v, attn, gattn, lse, qseg, kseg, own):
    n, rows, cw = q.shape
    win = k.shape[1]
    pairs = cw // PAIR
    scale = HEAD_DIM**-0.5

    def work(big, q_ref, k_ref, v_ref, a_ref, g_ref, l_ref, qs_ref, ks_ref, dq_ref, dk_ref, dv_ref, dkt, dvt):
        if not big:
            dkt[...] = jnp.zeros_like(dkt)
            dvt[...] = jnp.zeros_like(dvt)
        for i, (qs, qn, ks, kn) in enumerate(blocks_of(rows, own, win, big)):
            mask = qs_ref[qs : qs + qn, :] == ks_ref[:, ks : ks + kn]
            for h in range(2):
                lanes = slice(h * HEAD_DIM, (h + 1) * HEAD_DIM)
                qh = q_ref[0, qs : qs + qn, lanes] * BF16(scale)
                kh = k_ref[0, ks : ks + kn, lanes]
                gh = g_ref[0, qs : qs + qn, lanes]
                s = jnp.where(mask, dot_nt(qh, kh) - l_ref[0, qs : qs + qn, h : h + 1], NEG)
                p = jnp.exp(s)
                dp = dot_nt(gh, v_ref[0, ks : ks + kn, lanes])
                delta = jnp.sum(
                    gh.astype(F32) * a_ref[0, qs : qs + qn, lanes].astype(F32), axis=1, keepdims=True
                )
                ds = (p * (dp - delta)).astype(BF16)
                dq_ref[0, qs : qs + qn, lanes] = (dot_nn(ds, kh) * scale).astype(BF16)
                dk = dot_tn(qh, ds)
                dv = dot_tn(gh, p.astype(BF16))
                if big and i == 0:
                    dkt[lanes, :] = dk
                    dvt[lanes, :] = dv
                else:
                    dkt[lanes, ks : ks + kn] += dk
                    dvt[lanes, ks : ks + kn] += dv
        dk_ref[0] = dkt[...].T.astype(BF16)
        dv_ref[0] = dvt[...].T.astype(BF16)

    def body(info_ref, *refs):
        @pl.when(info_ref[0] == 1)
        def _():
            work(True, *refs)

        @pl.when(info_ref[0] == 0)
        def _():
            work(False, *refs)

    if pairs > 1:

        def put(d, p, info):
            rel = lax.bitwise_xor(p // (pairs // 2), info[1])
            return (rel, 0, d * (pairs // 2) + p % (pairs // 2))

        half_shape = (2, rows, n * cw // 2)
        half_win = (2, win, n * cw // 2)
    else:

        def put(d, p, info):
            return (0, 0, d)

        half_shape = (1, rows, n * cw)
        half_win = (1, win, n * cw)
    return pl.pallas_call(
        body,
        grid_spec=pltpu.PrefetchScalarGridSpec(
            num_scalar_prefetch=1,
            grid=(n, pairs),
            in_specs=[
                pl.BlockSpec((1, rows, PAIR), lambda d, p, *_: (d, 0, p)),
                pl.BlockSpec((1, win, PAIR), lambda d, p, *_: (d, 0, p)),
                pl.BlockSpec((1, win, PAIR), lambda d, p, *_: (d, 0, p)),
                pl.BlockSpec((1, rows, PAIR), lambda d, p, *_: (d, 0, p)),
                pl.BlockSpec((1, rows, PAIR), lambda d, p, *_: (d, 0, p)),
                pl.BlockSpec((1, rows, 2), lambda d, p, *_: (d * pairs + p, 0, 0)),
                pl.BlockSpec((rows, 1), lambda d, p, *_: (0, 0)),
                pl.BlockSpec((1, win), lambda d, p, *_: (0, 0)),
            ],
            out_specs=[
                pl.BlockSpec((1, rows, PAIR), put),
                pl.BlockSpec((1, win, PAIR), put),
                pl.BlockSpec((1, win, PAIR), put),
            ],
            scratch_shapes=[pltpu.VMEM((PAIR, win), F32), pltpu.VMEM((PAIR, win), F32)],
        ),
        out_shape=[
            jax.ShapeDtypeStruct(half_shape, BF16),
            jax.ShapeDtypeStruct(half_win, BF16),
            jax.ShapeDtypeStruct(half_win, BF16),
        ],
        compiler_params=params("arbitrary", "arbitrary"),
        cost_estimate=pl.CostEstimate(
            flops=40 * n * rows * win * cw, bytes_accessed=2 * n * cw * (4 * rows + 4 * win), transcendentals=n * rows * win * 4
        ),
    )(info, q, k, v, attn, gattn, lse, qseg, kseg)


def out_call(attn, packed, resid, b_out, gain, bias):
    n, rows, cw = attn.shape
    dm = packed.shape[1]

    def body(a_ref, w_ref, x_ref, bo_ref, g_ref, b_ref, h_ref, n_ref):
        d = pl.program_id(0)
        part = dot_nt(a_ref[0], w_ref[0])

        @pl.when(d == 0)
        def _():
            h_ref[...] = part + x_ref[...].astype(F32) + bo_ref[...].astype(F32)

        @pl.when(d > 0)
        def _():
            h_ref[...] += part

        @pl.when(d == n - 1)
        def _():
            hat, _ = norm_rows(h_ref[...])
            n_ref[...] = (hat * g_ref[...].astype(F32) + b_ref[...].astype(F32)).astype(BF16)

    full = lambda d: (0, 0)
    return pl.pallas_call(
        body,
        grid=(n,),
        in_specs=[
            pl.BlockSpec((1, rows, cw), lambda d: (d, 0, 0)),
            pl.BlockSpec((1, dm, cw), lambda d: (d, 0, 3)),
            pl.BlockSpec((rows, dm), full),
            pl.BlockSpec((1, dm), full),
            pl.BlockSpec((1, dm), full),
            pl.BlockSpec((1, dm), full),
        ],
        out_specs=[pl.BlockSpec((rows, dm), full), pl.BlockSpec((rows, dm), full)],
        out_shape=[jax.ShapeDtypeStruct((rows, dm), F32), jax.ShapeDtypeStruct((rows, dm), BF16)],
        compiler_params=params("arbitrary"),
        cost_estimate=pl.CostEstimate(flops=2 * n * rows * cw * dm, bytes_accessed=2 * n * dm * cw, transcendentals=0),
    )(attn, packed, resid, b_out[None], gain[None], bias[None])


def ffn_call(core, n2, hidden, cot, w_up, w_down, b_up, b_down, halves):
    rows, dm = n2.shape
    n, _, ffw = w_up.shape
    tile = ffw // halves

    def body(core_ref, x_ref, h_ref, c_ref, wu_ref, wd_ref, bu_ref, bd_ref, o_ref, gn_ref, a_ref, gu_ref, gb_ref, acc):
        t = pl.program_id(0)
        u = dot_nn(x_ref[...], wu_ref[0]) + bu_ref[...].astype(F32)
        cdf = 0.5 * (1.0 + lax.erf(u * 0.7071067811865476))
        act = (u * cdf).astype(BF16)
        slope = cdf + u * jnp.exp(-0.5 * u * u) * 0.3989422804014327
        a_ref[...] = act
        grad = dot_nt(c_ref[...], wd_ref[0]) * slope
        gu = grad.astype(BF16)
        gu_ref[...] = gu
        gb_ref[...] = jnp.sum(gu.astype(F32), axis=0, keepdims=True)
        out = dot_nn(act, wd_ref[0])
        gn = dot_nt(gu, wu_ref[0])

        @pl.when(t == 0)
        def _():
            acc[...] = h_ref[...] + bd_ref[...].astype(F32) + out
            gn_ref[...] = gn

        @pl.when(t > 0)
        def _():
            acc[...] += out
            gn_ref[...] += gn

        @pl.when(t == n * halves - 1)
        def _():
            o_ref[...] = acc[...].astype(BF16)

    full = lambda t, c: (0, 0)

    def part(t, c):
        return lax.bitwise_xor(t // n, c[0]) if halves > 1 else 0

    return pl.pallas_call(
        body,
        grid_spec=pltpu.PrefetchScalarGridSpec(
            num_scalar_prefetch=1,
            grid=(n * halves,),
            in_specs=[
                pl.BlockSpec((rows, dm), full),
                pl.BlockSpec((rows, dm), full),
                pl.BlockSpec((rows, dm), full),
                pl.BlockSpec((1, dm, tile), lambda t, c: (t % n, 0, part(t, c))),
                pl.BlockSpec((1, tile, dm), lambda t, c: (t % n, part(t, c), 0)),
                pl.BlockSpec((1, tile), lambda t, c: (0, t)),
                pl.BlockSpec((1, dm), full),
            ],
            out_specs=[
                pl.BlockSpec((rows, dm), full),
                pl.BlockSpec((rows, dm), full),
                pl.BlockSpec((rows, tile), lambda t, c: (0, t)),
                pl.BlockSpec((rows, tile), lambda t, c: (0, t)),
                pl.BlockSpec((1, tile), lambda t, c: (0, t)),
            ],
            scratch_shapes=[pltpu.VMEM((rows, dm), F32)],
        ),
        out_shape=[
            jax.ShapeDtypeStruct((rows, dm), BF16),
            jax.ShapeDtypeStruct((rows, dm), F32),
            jax.ShapeDtypeStruct((rows, n * ffw), BF16),
            jax.ShapeDtypeStruct((rows, n * ffw), BF16),
            jax.ShapeDtypeStruct((1, n * ffw), F32),
        ],
        compiler_params=params("arbitrary"),
        cost_estimate=pl.CostEstimate(
            flops=8 * rows * dm * n * ffw, bytes_accessed=4 * n * dm * ffw, transcendentals=2 * rows * n * ffw
        ),
    )(core, n2, hidden, cot, w_up, w_down, b_up[None], b_down[None])


def norm1_back_call(dq, dk, dv, packed, info, own):
    halves, rows, _ = dq.shape
    n, dm, four = packed.shape
    cw = four // 4
    win = dk.shape[1]
    width = cw // halves

    def body(info_ref, dq_ref, dk_ref, dv_ref, w_ref, o_ref, h_ref, t_ref, acc):
        step = pl.program_id(0)

        def weight(which, j):
            at = lax.bitwise_xor(j, info_ref[1]) if halves > 1 else 0
            return w_ref[0, :, pl.ds(pl.multiple_of(which * cw + at * width, width), width)]

        left = jnp.concatenate([r[j] for r in (dk_ref, dv_ref) for j in range(halves)], axis=1)
        right = jnp.concatenate([weight(m, j) for m in (1, 2) for j in range(halves)], axis=1)
        part = dot_nt(left, right)
        left = jnp.concatenate([dq_ref[j] for j in range(halves)], axis=1)
        right = jnp.concatenate([weight(0, j) for j in range(halves)], axis=1)
        mine = dot_nt(left, right)

        @pl.when(step == 0)
        def _():
            acc[...] = part

        @pl.when(step > 0)
        def _():
            acc[...] += part

        acc[own : own + rows, :] += mine

        @pl.when(step == n - 1)
        def _():
            o_ref[...] = acc[own : own + rows, :]
            h_ref[...] = acc[0:own, :].astype(BF16)
            t_ref[...] = acc[own + rows : own + rows + HALO, :].astype(BF16)

    full = lambda s, info: (0, 0)
    return pl.pallas_call(
        body,
        grid_spec=pltpu.PrefetchScalarGridSpec(
            num_scalar_prefetch=1,
            grid=(n,),
            in_specs=[
                pl.BlockSpec((halves, rows, width), lambda s, info: (0, 0, s)),
                pl.BlockSpec((halves, win, width), lambda s, info: (0, 0, s)),
                pl.BlockSpec((halves, win, width), lambda s, info: (0, 0, s)),
                pl.BlockSpec((1, dm, four), lambda s, info: (s, 0, 0)),
            ],
            out_specs=[
                pl.BlockSpec((rows, dm), full),
                pl.BlockSpec((own, dm), full),
                pl.BlockSpec((HALO, dm), full),
            ],
            scratch_shapes=[pltpu.VMEM((win, dm), F32)],
        ),
        out_shape=[
            jax.ShapeDtypeStruct((rows, dm), F32),
            jax.ShapeDtypeStruct((own, dm), BF16),
            jax.ShapeDtypeStruct((HALO, dm), BF16),
        ],
        compiler_params=params("arbitrary"),
        cost_estimate=pl.CostEstimate(
            flops=2 * n * cw * dm * (rows + 2 * win), bytes_accessed=2 * n * cw * (3 * dm + rows + 2 * win), transcendentals=0
        ),
    )(info, dq, dk, dv, packed)


MESH = pl.DeviceIdType.MESH


class Place:
    def __init__(self):
        self.me = lax.axis_index("dp")
        self.z = lax.axis_index("mp")
        self.k = lax.rem(self.me, 2)
        self.x = lax.rem(self.me // 2, 2)
        self.y = self.me // 4
        self.me_k = self.me + 1 - 2 * self.k
        self.me_x = self.me + 2 - 4 * self.x
        self.me_y = self.me + 4 - 8 * self.y
        self.me_xy = self.me_x + 4 - 8 * self.y
        self.core = {"dp": self.me_k, "mp": self.z}
        self.by_x = {"dp": self.me_x, "mp": self.z}
        self.by_y = {"dp": self.me_y, "mp": self.z}

    def along(self, d):
        return {"dp": self.me, "mp": lax.rem(self.z + d, 4)}

    def meet(self):
        sem = pltpu.get_barrier_semaphore()
        for dev in (self.core, self.by_x, self.by_y, self.along(1), self.along(2), self.along(3)):
            pl.semaphore_signal(sem, inc=1, device_id=dev, device_id_type=MESH)
        pl.semaphore_wait(sem, 6)


class Wire:
    def __init__(self, send, recv, dev):
        self.send, self.recv, self.dev = send, recv, dev

    def start(self, slot, src, dst, dev):
        copy = pltpu.make_async_remote_copy(
            src_ref=src, dst_ref=dst, send_sem=self.send.at[slot], recv_sem=self.recv.at[slot],
            device_id=dev, device_id_type=MESH,
        )
        copy.start()

    def sent(self, slot, ref):
        pltpu.make_async_remote_copy(
            src_ref=ref, dst_ref=ref, send_sem=self.send.at[slot], recv_sem=self.recv.at[slot],
            device_id=dict(self.dev), device_id_type=MESH,
        ).wait_send()

    def landed(self, slot, ref, dev):
        pltpu.make_async_remote_copy(
            src_ref=ref, dst_ref=ref, send_sem=self.send.at[slot], recv_sem=self.recv.at[slot],
            device_id=dev, device_id_type=MESH,
        ).wait_recv()


def gather_steps(place, wire, base, shard, whole):
    step = shard.shape[0] // 8
    half = step // 2

    def rows(who, at=0, size=step):
        return pl.ds(pl.multiple_of(who * step + at, half), size)

    def slot(d, kind):
        return base + (d - 1) * 10 + kind

    lower, upper = place.along(3), place.along(1)

    def begin():
        mine = shard.at[rows(place.me)]

        @pl.when(place.z > 0)
        def _():
            wire.start(slot(1, 0), mine, whole.at[1, rows(place.me)], lower)

        @pl.when(place.z < 3)
        def _():
            wire.start(slot(3, 0), mine, whole.at[3, rows(place.me)], upper)

    def goes_down(d):
        return jnp.logical_and(place.z + d < 4, place.z > 0)

    def goes_up(d):
        return jnp.logical_and(place.z + d > 3, place.z < 3)

    def onward(src, dst, d, to, dev):
        pltpu.make_async_remote_copy(
            src_ref=src, dst_ref=dst, send_sem=wire.send.at[slot(d, 9)], recv_sem=wire.recv.at[slot(to, 0)],
            device_id=dev, device_id_type=MESH,
        ).start()

    def first(d):
        mine = whole.at[d, rows(place.me)]
        wire.landed(slot(d, 0), mine, place.along(d))

        @pl.when(goes_down(d))
        def _():
            onward(mine, whole.at[d + 1, rows(place.me)], d, d + 1, lower)

        @pl.when(goes_up(d))
        def _():
            onward(mine, whole.at[d - 1, rows(place.me)], d, d - 1, upper)

        wire.start(slot(d, 2), mine, mine, place.by_x)
        wire.start(slot(d, 3), mine, mine, place.by_y)
        wire.start(slot(d, 1), mine, mine, place.core)

    def second(d):
        got = whole.at[d, rows(place.me_x)]
        wire.landed(slot(d, 2), got, place.by_x)
        part = whole.at[d, rows(place.me_x, 0, half)]
        wire.start(slot(d, 4), part, part, place.by_y)
        wire.start(slot(d, 6), got, got, place.core)
        got = whole.at[d, rows(place.me_y)]
        wire.landed(slot(d, 3), got, place.by_y)
        part = whole.at[d, rows(place.me_y, half, half)]
        wire.start(slot(d, 5), part, part, place.by_x)
        wire.start(slot(d, 7), got, got, place.core)

    def third(d):
        wire.landed(slot(d, 4), whole.at[d, rows(place.me_xy, 0, half)], place.by_y)
        wire.landed(slot(d, 5), whole.at[d, rows(place.me_xy, half, half)], place.by_x)
        got = whole.at[d, rows(place.me_xy)]
        wire.start(slot(d, 8), got, got, place.core)

    def done(d):
        flip = 1 - 2 * place.k
        for kind, who in ((1, place.me), (6, place.me_x), (7, place.me_y), (8, place.me_xy)):
            wire.landed(slot(d, kind), whole.at[d, rows(who + flip)], place.core)

    def drain():
        piece = whole.at[0, pl.ds(0, step)]

        @pl.when(place.z > 0)
        def _():
            wire.sent(slot(1, 0), piece)

        @pl.when(place.z < 3)
        def _():
            wire.sent(slot(3, 0), piece)

        for d in (1, 2, 3):

            @pl.when(jnp.logical_or(goes_down(d), goes_up(d)))
            def _():
                wire.sent(slot(d, 9), piece)

            for kind in range(1, 9):
                wire.sent(slot(d, kind), whole.at[0, pl.ds(0, half if kind in (4, 5) else step)])

    return begin, first, second, third, done, drain


def front_call(tokens, cot, pack, w_up, w_down, small, qseg, kseg, own):
    rows, dm = tokens.shape
    cw = pack.shape[1] // 4
    ffw = w_up.shape[1]
    n = 4
    tile = ffw // 2
    hw = n * tile
    win = own + rows + 2 * HALO
    pairs = cw // PAIR
    strip = 128
    per = rows // strip
    scale = HEAD_DIM**-0.5
    length = small.shape[1] - 6 * dm
    give = 6
    base = give + 3 + 3 * n

    def body(
        tok_ref, cot_ref, pack_ref, up_ref, down_ref, small_ref, qs_ref, ks_ref,
        packed_out, n1t_out, n2t_out, cott_out, ghbt_out, q_out, k_out, v_out, a_out, at_out, ga_out, act_out, gup_out, gh_out,
        l_ref, o_ref, vec_ref,
        up, down, n1, hid, n2, acc, act, gup, biases,
        packed, n1t, n2t, cott, ghbt, q_ref, k_ref, v_ref, a_ref, ga_ref, gh_ref, xs, xr, ls, fs, os,
    ):
        place = Place()
        core, z = place.k, place.z
        long, takes_prev, takes_next = z < 2, z >= 2, jnp.logical_and(z >= 1, z < 3)
        swap = {"dp": place.me, "mp": lax.rem(z + 1, 2)}
        left_dev = {"dp": place.me, "mp": lax.rem(z + 3, 4)}
        right_dev = {"dp": place.me, "mp": lax.rem(z + 1, 4)}
        wire = Wire(xs, xr, place.core)
        local = [
            pltpu.make_async_copy(src, dst, ls.at[i])
            for i, (src, dst) in enumerate(
                ((tok_ref, n1.at[own : own + rows]), (pack_ref, packed.at[0]), (up_ref, up.at[0]), (down_ref, down.at[0]))
            )
        ]
        for c in local:
            c.start()
        place.meet()
        bias_ref = small_ref.at[:, 6 * dm : 6 * dm + length]
        for d in (1, 2, 3):
            wire.start(d - 1, bias_ref, biases.at[d], place.along(4 - d))

        groups = [
            gather_steps(place, wire, base + 30 * g, src, dst)
            for g, (src, dst) in enumerate(((pack_ref, packed), (up_ref, up), (down_ref, down)))
        ]
        groups[0][0]()

        @pl.when(z == 0)
        def _():
            wire.start(3, tok_ref, n1.at[0:own], swap)

        @pl.when(takes_next)
        def _():
            wire.start(4, tok_ref.at[rows - HALO : rows], n1.at[own - HALO : own], right_dev)

        @pl.when(takes_prev)
        def _():
            wire.start(5, tok_ref.at[0:HALO], n1.at[own + rows : own + rows + HALO], left_dev)

        def near_shard(i):
            upper, odd = z // 2, lax.rem(z, 2)
            place_z = (1 + 3 * odd) * (1 + 15 * upper)
            place_i = 1 + 255 * i + (i * (i - 1) // 2) * 65025
            return lax.rem(7053045 // (place_z * place_i), 4)

        items = [(0, 0), (0, 1), (0, 2), (1, 0), (2, 0), (1, 1), (2, 1), (1, 2), (2, 2)]

        def relay(i):
            for lag in range(3):
                if 0 <= i - lag < len(items):
                    g, j = items[i - lag]
                    groups[g][1 + lag](near_shard(j))

        def arrived(j, *which):
            for g in which:
                groups[g][4](near_shard(j))

        def turns(i, table):
            for t, f in table.items():

                @pl.when(i == t)
                def _():
                    f()

        def shard_at(k):
            return near_shard(lax.rem(k + 2, 3)) * ((k + 3) // 4)

        def strip_at(i, start=0):
            return pl.ds(pl.multiple_of(start + i * strip, strip), strip)

        row = lambda i: small_ref[:, i * dm : (i + 1) * dm]

        whole = [
            (n1t, n1t_out.at[:, 0:win]), (n2t, n2t_out.at[:, 0:rows]), (cott, cott_out.at[:, 0:rows]), (ghbt, ghbt_out),
            (q_ref, q_out), (k_ref, k_out), (v_ref, v_out), (a_ref, a_out), (ga_ref, ga_out), (gh_ref, gh_out), (packed, packed_out),
        ]
        leaving = [pltpu.make_async_copy(src, dst, os.at[i]) for i, (src, dst) in enumerate(whole)]
        shared = ((n1t, n1t_out.at[:, win : 2 * win]), (n2t, n2t_out.at[:, rows : 2 * rows]), (cott, cott_out.at[:, rows : 2 * rows]))

        def leave(i):
            leaving[i].start()
            if i < len(shared):
                wire.start(give + i, *shared[i], place.core)

        @pl.when(z == 0)
        def _():
            n1[SPAN:own, :] = jnp.zeros((own - SPAN, dm), BF16)

        @pl.when(takes_prev)
        def _():
            n1[0 : own - HALO, :] = jnp.zeros((own - HALO, dm), BF16)

        @pl.when(jnp.logical_not(takes_next))
        def _():
            n1[own + rows : own + rows + HALO, :] = jnp.zeros((HALO, dm), BF16)

        n1[own + rows + HALO :, :] = jnp.zeros((HALO, dm), BF16)
        biases[0] = bias_ref[...]
        l_ref[...] = jnp.zeros_like(l_ref)
        vec_ref[...] = jnp.zeros_like(vec_ref)

        def turn_cot(i, carry):
            cott[:, strip_at(i)] = cot_ref[strip_at(i), :].astype(F32).T.astype(BF16)
            return carry

        lax.fori_loop(0, per, turn_cot, 0)
        leave(2)

        def norm1(i):
            at = strip_at(i)
            x = n1[at, :].astype(F32)
            hat, _ = norm_rows(x)
            val = hat * row(0) + row(1)
            n1[at, :] = val.astype(BF16)
            n1t[:, at] = val.T.astype(BF16)
            return x

        def norm_own(i, carry):
            hid[strip_at(i), :] = norm1(own // strip + i) + row(4)
            return carry

        def norm_far(i, carry):
            norm1(i)
            return carry

        local[0].wait()
        lax.fori_loop(0, per, norm_own, 0)
        for c in local[1:]:
            c.wait()
        relay(0)
        relay(1)
        relay(2)

        @pl.when(z == 1)
        def _():
            wire.start(3, tok_ref.at[0:SPAN], n1.at[0:SPAN], swap)

        groups[1][0]()
        groups[2][0]()

        @pl.when(z == 0)
        def _():
            wire.landed(3, n1.at[0:SPAN], swap)

        @pl.when(z == 1)
        def _():
            wire.landed(3, n1.at[0:own], swap)

        @pl.when(takes_prev)
        def _():
            wire.landed(4, n1.at[own - HALO : own], left_dev)

        @pl.when(takes_next)
        def _():
            wire.landed(5, n1.at[own + rows : own + rows + HALO], right_dev)

        lax.fori_loop(0, own // strip, norm_far, 0)
        norm1((own + rows) // strip)
        leave(0)
        for d in (1, 2, 3):
            wire.landed(d - 1, biases.at[d], place.along(d))
        relay(3)

        def attend(big, d, p):
            at = pl.ds(pl.multiple_of(p * PAIR, PAIR), PAIR)
            for qs, qn, ks, kn in blocks_of(rows, own, win, big):
                mask = qs_ref[qs : qs + qn, :] == ks_ref[:, ks : ks + kn]
                qq, kk, vv = q_ref[d, qs : qs + qn, at], k_ref[d, ks : ks + kn, at], v_ref[d, ks : ks + kn, at]
                outs = []
                for h in range(2):
                    lanes = slice(h * HEAD_DIM, (h + 1) * HEAD_DIM)
                    s = jnp.where(mask, dot_nt(qq[:, lanes] * BF16(scale), kk[:, lanes]), NEG)
                    top = jnp.max(s, axis=1, keepdims=True)
                    pr = jnp.exp(s - top)
                    total = jnp.sum(pr, axis=1, keepdims=True)
                    outs.append(dot_nn(pr.astype(BF16), vv[:, lanes]) / total)
                    lane = lax.broadcasted_iota(jnp.int32, (qn, 2 * n * pairs), 1)
                    seen = l_ref[qs : qs + qn, :]
                    l_ref[qs : qs + qn, :] = jnp.where(lane == (d * pairs + p) * 2 + h, top + jnp.log(total), seen)
                a_ref[d, qs : qs + qn, at] = jnp.concatenate(outs, axis=1).astype(BF16)

        def head_lanes(d):
            return pl.ds(pl.multiple_of(d * PAIR, PAIR), PAIR)

        def half_of_attn(d):
            mine = pl.ds(pl.multiple_of(core * PAIR, PAIR), PAIR)
            theirs = pl.ds(pl.multiple_of((1 - core) * PAIR, PAIR), PAIR)
            keep = pltpu.make_async_copy(a_ref.at[d, :, mine], at_out.at[0:rows, head_lanes(d)], fs.at[2 * n + d])
            return keep, a_ref.at[d, :, theirs]

        def heads(kk, carry):
            turns(kk, {j + 1: functools.partial(arrived, j, 0) for j in range(3)})
            d = shard_at(kk)
            q_ref[d] = (dot_nn(n1[own : own + rows, :], packed[d, :, 0:cw]) + biases[d, :, 0:cw]).astype(BF16)
            k_ref[d] = dot_nn(n1[...], packed[d, :, cw : 2 * cw]).astype(BF16)
            v_ref[d] = (dot_nn(n1[...], packed[d, :, 2 * cw : 3 * cw]) + biases[d, :, cw : 2 * cw]).astype(BF16)

            def one(p, inner):
                @pl.when(long)
                def _():
                    attend(True, d, p)

                @pl.when(jnp.logical_not(long))
                def _():
                    attend(False, d, p)

                turns(kk * pairs + p, {pairs * j: functools.partial(relay, 4 + j) for j in range(4)})
                return inner

            lax.fori_loop(0, pairs, one, 0)
            hid[...] += dot_nt(a_ref[d], packed[d, :, 3 * cw : 4 * cw])
            halves = half_of_attn(d)
            halves[0].start()
            wire.start(give + 3 + d, halves[1], at_out.at[rows : 2 * rows, head_lanes(d)], place.core)
            return carry

        lax.fori_loop(0, n, heads, 0)
        for i in (4, 5, 6, 7, 10):
            leave(i)

        def norm2(i, carry):
            at = strip_at(i)
            hidden = hid[at, :]
            hat, _ = norm_rows(hidden)
            val = hat * row(2) + row(3)
            n2[at, :] = val.astype(BF16)
            n2t[:, at] = val.T.astype(BF16)
            acc[at, :] = hidden + row(5)
            return carry

        lax.fori_loop(0, per, norm2, 0)
        leave(1)

        def kept(d):
            at = pl.ds(pl.multiple_of(d * tile, tile), tile)
            return (
                pltpu.make_async_copy(act.at[:, at], act_out.at[0:rows, at], fs.at[d]),
                pltpu.make_async_copy(gup.at[:, at], gup_out.at[0:rows, at], fs.at[n + d]),
            )

        def feed(i, carry):
            turns(
                i,
                {
                    2: lambda: (arrived(0, 1, 2), relay(8)),
                    4: lambda: (arrived(1, 1, 2), relay(9)),
                    5: lambda: relay(10),
                    6: lambda: arrived(2, 1, 2),
                },
            )
            d = shard_at(i // 2)
            rel = 1 - lax.rem(i, 2)
            part = lax.rem(rel + core, 2) * tile
            at = pl.ds(pl.multiple_of(part, tile), tile)
            to = pl.ds(pl.multiple_of(rel * hw + d * tile, tile), tile)
            u = dot_nn(n2[...], up[d, :, at]) + biases[d, :, pl.ds(pl.multiple_of(2 * cw + part, PAIR), tile)]
            cdf = 0.5 * (1.0 + lax.erf(u * 0.7071067811865476))
            val = (u * cdf).astype(BF16)
            slope = cdf + u * jnp.exp(-0.5 * u * u) * 0.3989422804014327
            act[:, to] = val
            gu = (dot_nt(cot_ref[...], down[d, at, :]) * slope).astype(BF16)
            gup[:, to] = gu
            unit = 8 * dm + lax.rem(z + d, n) * ffw + part
            vec_ref[:, pl.ds(pl.multiple_of(unit, tile), tile)] = jnp.sum(gu.astype(F32), axis=0, keepdims=True)

            @pl.when(rel == 0)
            def _():
                for c in kept(d):
                    c.start()

            @pl.when(rel == 1)
            def _():
                theirs = pl.ds(pl.multiple_of(d * tile, tile), tile)
                for j, (src, dst) in enumerate(((act, act_out), (gup, gup_out))):
                    wire.start(give + 3 + (j + 1) * n + d, src.at[:, to], dst.at[rows : 2 * rows, theirs], place.core)

            acc[...] += dot_nn(val, down[d, at, :])
            gn = dot_nt(gu, up[d, :, at])

            @pl.when(i == 0)
            def _():
                gh_ref[...] = gn

            @pl.when(i > 0)
            def _():
                gh_ref[...] += gn

            return carry

        lax.fori_loop(0, 2 * n, feed, 0)

        def back2(i, carry):
            at = strip_at(i)
            o_ref[at, :] = acc[at, :].astype(BF16)
            hat, inv = norm_rows(hid[at, :])
            g = gh_ref[at, :]
            gout = cot_ref[at, :].astype(F32)
            gg = g * row(2)
            first = jnp.mean(gg, axis=1, keepdims=True)
            second = jnp.mean(gg * hat, axis=1, keepdims=True)
            val = inv * (gg - first - hat * second) + gout
            gh_ref[at, :] = val
            n2[at, :] = val.astype(BF16)
            ghbt[:, at] = val.T.astype(BF16)
            for j, v in enumerate((val, g * hat, g, gout)):
                vec_ref[:, (2 + j) * dm : (3 + j) * dm] += jnp.sum(v, axis=0, keepdims=True)
            return carry

        lax.fori_loop(0, per, back2, 0)
        leave(9)
        leave(3)

        def back_attn(d, carry):
            ga_ref[d] = dot_nn(n2[...], packed[d, :, 3 * cw : 4 * cw]).astype(BF16)
            return carry

        lax.fori_loop(0, n, back_attn, 0)
        leave(8)
        for d in range(n):
            for c in (*kept(d), half_of_attn(d)[0]):
                c.wait()
        for i, (src, dst) in enumerate(shared):
            wire.landed(give + i, dst, place.core)
            wire.sent(give + i, src)
        for d in range(n):
            wire.landed(give + 3 + d, at_out.at[rows : 2 * rows, d * PAIR : (d + 1) * PAIR], place.core)
            wire.sent(give + 3 + d, at_out.at[0:rows, 0:PAIR])
            for j, dst in enumerate((act_out, gup_out)):
                wire.landed(give + 3 + (j + 1) * n + d, dst.at[rows : 2 * rows, d * tile : (d + 1) * tile], place.core)
                wire.sent(give + 3 + (j + 1) * n + d, dst.at[0:rows, 0:tile])
        for c in leaving:
            c.wait()
        for group in groups:
            group[5]()
        for d in (1, 2, 3):
            wire.sent(d - 1, biases.at[d])

        @pl.when(z == 0)
        def _():
            wire.sent(3, n1.at[0:own])

        @pl.when(z == 1)
        def _():
            wire.sent(3, n1.at[0:SPAN])

        @pl.when(takes_next)
        def _():
            wire.sent(4, n1.at[0:HALO])

        @pl.when(takes_prev)
        def _():
            wire.sent(5, n1.at[0:HALO])

    hbm = pl.BlockSpec(memory_space=pl.ANY)
    vmem = pl.BlockSpec(memory_space=pltpu.VMEM)
    half = lambda *shape: jax.ShapeDtypeStruct(shape, BF16)
    full = lambda *shape: jax.ShapeDtypeStruct(shape, F32)
    b16 = lambda *shape: pltpu.VMEM(shape, BF16)
    b32 = lambda *shape: pltpu.VMEM(shape, F32)
    slots = base + 30 * 3
    return pl.pallas_call(
        body,
        in_specs=[hbm, vmem, hbm, hbm, hbm, vmem, vmem, vmem],
        out_specs=[hbm] * 14 + [vmem] * 3,
        out_shape=[
            half(n, dm, 4 * cw), half(dm, 2 * win), half(dm, 2 * rows), half(dm, 2 * rows), half(dm, rows),
            half(n, rows, cw), half(n, win, cw), half(n, win, cw), half(n, rows, cw), half(2 * rows, n * PAIR), half(n, rows, cw),
            half(2 * rows, hw), half(2 * rows, hw), full(rows, dm),
            full(rows, 2 * n * pairs), half(rows, dm), full(1, 8 * dm + 2 * hw),
        ],
        scratch_shapes=[
            b16(n, dm, ffw), b16(n, ffw, dm), b16(win, dm), b32(rows, dm), b16(rows, dm), b32(rows, dm),
            b16(rows, 2 * hw), b16(rows, 2 * hw), b32(n, 1, length),
            b16(n, dm, 4 * cw), b16(dm, win), b16(dm, rows), b16(dm, rows), b16(dm, rows),
            b16(n, rows, cw), b16(n, win, cw), b16(n, win, cw), b16(n, rows, cw), b16(n, rows, cw), b32(rows, dm),
            pltpu.SemaphoreType.DMA((slots,)), pltpu.SemaphoreType.DMA((slots,)), pltpu.SemaphoreType.DMA((4,)),
            pltpu.SemaphoreType.DMA((3 * n,)), pltpu.SemaphoreType.DMA((11,)),
        ],
        compiler_params=pltpu.CompilerParams(collective_id=0, has_side_effects=True, vmem_limit_bytes=VMEM_ALL),
    )(tokens, cot, pack, w_up, w_down, small, qseg, kseg)


class Reduce:
    SLOTS = 32

    @staticmethod
    def scratch(dm, w):
        q = dm // 4
        e = q // 2
        return [
            pltpu.VMEM((4, q, w), BF16),
            pltpu.VMEM((4, q, w), BF16),
            pltpu.VMEM((4, e, w), BF16),
            pltpu.VMEM((4, e, w), BF16),
            pltpu.VMEM((3, q, w), BF16),
            pltpu.SemaphoreType.DMA((Reduce.SLOTS,)),
            pltpu.SemaphoreType.DMA((Reduce.SLOTS,)),
        ]

    def __init__(self, place, grad, landing, views, zb, send, recv):
        self.place, self.g, self.f = place, grad, landing
        self.ra1, self.rb1, self.ra2, self.rb2 = views
        self.zb = zb
        self.wire = Wire(send, recv, place.core)
        self.q = grad.shape[0] // 4
        self.e = self.q // 2
        self.w = grad.shape[1] // 4

    @staticmethod
    def of(place, grad, landing, scratch):
        views = [lambda d, ref=ref: ref.at[d] for ref in scratch[:4]]
        return Reduce(place, grad, landing, views, *scratch[4:])

    @staticmethod
    def within(place, grad, landing, spare, zb, send, recv):
        q, w = grad.shape[0] // 4, grad.shape[1] // 4
        bounds = (0, q, 2 * q, 2 * q + q // 2, 3 * q)
        views = [
            lambda d, a=a, b=b: spare.at[a:b, pl.ds(pl.multiple_of(d * w, w), w)] for a, b in zip(bounds[:-1], bounds[1:])
        ]
        return Reduce(place, grad, landing, views, zb, send, recv)

    def at(self, base, big, small=None):
        start = base * 2 * self.q + big * self.q + (0 if small is None else small * self.e)
        return pl.ds(pl.multiple_of(start, self.e), self.q if small is None else self.e)

    def eighth(self, small):
        return pl.ds(pl.multiple_of(small * self.e, self.e), self.e)

    def cols(self, d):
        return pl.ds(pl.multiple_of(d * self.w, self.w), self.w)

    def one(self, d):
        p, wire = self.place, self.wire
        wire.start(d, self.g.at[self.at(0, 1 - p.x), self.cols(d)], self.ra1(d), p.by_x)
        wire.start(4 + d, self.g.at[self.at(1, 1 - p.y), self.cols(d)], self.rb1(d), p.by_y)

    def two(self, d):
        p, wire, c = self.place, self.wire, self.cols(d)
        for slot, buf, to, at, mine, dev, nxt in (
            (0, self.ra1, self.ra2, self.at(0, p.x, 1 - p.y), self.eighth(1 - p.y), p.by_x, p.by_y),
            (4, self.rb1, self.rb2, self.at(1, p.y, 1 - p.x), self.eighth(1 - p.x), p.by_y, p.by_x),
        ):
            wire.landed(slot + d, buf(d), dev)
            self.g[at, c] = (self.g[at, c].astype(F32) + buf(d)[mine, :].astype(F32)).astype(BF16)
            wire.start(8 + slot + d, self.g.at[at, c], to(d), nxt)

    def sums(self, d):
        p, wire, c = self.place, self.wire, self.cols(d)
        wire.landed(8 + d, self.ra2(d), p.by_y)
        wire.landed(12 + d, self.rb2(d), p.by_x)
        up = (
            self.g[self.at(0, p.x, p.y), c].astype(F32)
            + self.ra1(d)[self.eighth(p.y), :].astype(F32)
            + self.ra2(d)[...].astype(F32)
        )
        low = (
            self.g[self.at(1, p.y, p.x), c].astype(F32)
            + self.rb1(d)[self.eighth(p.x), :].astype(F32)
            + self.rb2(d)[...].astype(F32)
        )
        return up, low

    def three(self, d):
        p, wire, c, e = self.place, self.wire, self.cols(d), self.e
        up, low = self.sums(d)
        for part, (at, val) in enumerate(((self.at(0, p.x, p.y), up), (self.at(1, p.y, p.x), low))):
            self.g[at, c] = val.astype(BF16)
            wire.start(
                16 + 12 * part + d, self.g.at[at, c], self.zb.at[d - 1, part * e : (part + 1) * e], p.along(d)
            )

    def last(self):
        p, wire, e = self.place, self.wire, self.e
        up, low = self.sums(0)
        for s in (1, 2, 3):
            wire.landed(16 + s, self.zb.at[s - 1, 0:e], p.along(4 - s))
            wire.landed(28 + s, self.zb.at[s - 1, e : 2 * e], p.along(4 - s))
            up = up + self.zb[s - 1, 0:e].astype(F32)
            low = low + self.zb[s - 1, e : 2 * e].astype(F32)
        ready = self.ra1(0)
        ready[0:e, :] = up.astype(BF16)
        ready[e : 2 * e, :] = low.astype(BF16)
        wire.start(20, ready, self.f.at[2], p.by_x)
        wire.start(21, ready, self.f.at[4], p.by_y)
        wire.start(22, ready, self.f.at[1], p.core)
        self.keep().start()

    def keep(self):
        return pltpu.make_async_copy(self.ra1(0), self.f.at[0], self.wire.send.at[16])

    def four(self):
        p, wire, e = self.place, self.wire, self.e
        wire.landed(20, self.f.at[2], p.by_x)
        wire.start(23, self.f.at[2, 0:e], self.f.at[6, 0:e], p.by_y)
        wire.start(25, self.f.at[2], self.f.at[3], p.core)
        wire.landed(21, self.f.at[4], p.by_y)
        wire.start(24, self.f.at[4, e : 2 * e], self.f.at[6, e : 2 * e], p.by_x)
        wire.start(26, self.f.at[4], self.f.at[5], p.core)

    def five(self):
        p, wire, e = self.place, self.wire, self.e
        wire.landed(23, self.f.at[6, 0:e], p.by_y)
        wire.landed(24, self.f.at[6, e : 2 * e], p.by_x)
        wire.start(27, self.f.at[6], self.f.at[7], p.core)

    def six(self):
        for slot, to in ((22, 1), (25, 3), (26, 5), (27, 7)):
            self.wire.landed(slot, self.f.at[to], self.place.core)
        e, sent = self.e, self.wire.sent
        for d in range(4):
            sent(d, self.ra1(d))
            sent(4 + d, self.rb1(d))
            sent(8 + d, self.ra2(d))
            sent(12 + d, self.rb2(d))
        for d in range(1, 4):
            sent(16 + d, self.zb.at[d - 1, 0:e])
            sent(28 + d, self.zb.at[d - 1, 0:e])
        for slot in (20, 21, 22, 25, 26, 27):
            sent(slot, self.f.at[0])
        for slot in (23, 24):
            sent(slot, self.f.at[0, 0:e])
        self.keep().wait()


def back_call(cot, act, n2, gup, ghb, n1w, attn2, packed, tokens, q, k, v, attn, gattn, lse, qseg, kseg, gain, vec, own):
    n, rows, cw = q.shape
    win = k.shape[1]
    dm = cot.shape[0]
    hw = act.shape[1]
    half = n * cw // 2
    w = hw // 4
    pairs = cw // PAIR
    scale = HEAD_DIM**-0.5
    each = len(Reduce.scratch(dm, w))
    length = vec.shape[1]
    strip = 128

    def body(
        cot_in, act_in, n2_in, gup_in, ghb_in, n1_in, at_in, w_ref, x_ref, q_in, k_in, v_in, a_in, g_in,
        l_ref, qs_ref, ks_ref, gain_ref, vec_ref,
        fd, fu, fp, gi_ref, sum_ref,
        wbuf, act2, gup2, n12, gd, gu, dq_o, dk_o, dv_o, at2, dq, dk, dv, dkt, dvt,
        far_in, prev_in, next_in, nxt, va, vr, vz, zb, q_ref, k_ref, v_ref, a_ref, g_ref, ps, pr_sem, xs, xr, ls, ws, *scr,
    ):
        place = Place()
        core, z = place.k, place.z
        long, gives_prev, gives_next = z < 2, z >= 2, jnp.logical_and(z >= 1, z < 3)
        swap = {"dp": place.me, "mp": lax.rem(z + 1, 2)}
        left_dev = {"dp": place.me, "mp": lax.rem(z + 3, 4)}
        right_dev = {"dp": place.me, "mp": lax.rem(z + 1, 4)}
        wire = Wire(xs, xr, place.core)
        cot2, n22, ghb2 = wbuf.at[0], wbuf.at[1], wbuf.at[2]
        loads = (
            (cot_in, cot2), (act_in, act2), (n2_in, n22), (gup_in, gup2), (q_in, q_ref), (k_in, k_ref), (v_in, v_ref),
            (a_in, a_ref), (g_in, g_ref), (ghb_in, ghb2.at[:, 0:rows]), (n1_in, n12), (at_in, at2),
        )
        local = [pltpu.make_async_copy(src, dst, ls.at[1 + i]) for i, (src, dst) in enumerate(loads)]
        for c in local:
            c.start()
        place.meet()
        wire.start(0, ghb_in, ghb2.at[:, rows : 2 * rows], place.core)

        def take(*which):
            for i in which:
                local[i].wait()

        down = Reduce.of(place, gd, fd, scr[:each])
        up = Reduce.of(place, gu, fu, scr[each : 2 * each])
        heads = Reduce.within(place, act2, fp, gup2, zb, ps, pr_sem)

        def make(red, grad, left, right):
            def step(i, carry):
                d = lax.rem(i + 1, 4)
                c = pl.ds(pl.multiple_of(d * w, w), w)
                grad[:, c] = dot_nn(left[...], right[:, c]).astype(BF16)
                red.one(d)
                return carry

            lax.fori_loop(0, 4, step, 0)

        take(0, 1)
        make(down, gd, cot2, act2)
        take(2, 3)
        make(up, gu, n22, gup2)

        def weights(t):
            at = lax.rem(t, 3)
            return pltpu.make_async_copy(w_ref.at[lax.rem(t, n)], wbuf.at[at], ws.at[at])

        weights(0).start()
        weights(1).start()

        def turns(i, table):
            for t, f in table.items():

                @pl.when(i == t)
                def _():
                    f()

        def work(big, d, p):
            at = pl.ds(pl.multiple_of(p * PAIR, PAIR), PAIR)
            to = pl.ds(pl.multiple_of(d * PAIR, PAIR), PAIR)
            rel = lax.rem(p + core, 2)
            if not big:
                dkt[...] = jnp.zeros_like(dkt)
                dvt[...] = jnp.zeros_like(dvt)
            for i, (qs, qn, ks, kn) in enumerate(blocks_of(rows, own, win, big)):
                mask = qs_ref[qs : qs + qn, :] == ks_ref[:, ks : ks + kn]
                qq, kk, vv = q_ref[d, qs : qs + qn, at], k_ref[d, ks : ks + kn, at], v_ref[d, ks : ks + kn, at]
                gg = g_ref[d, qs : qs + qn, at]
                prod = gg.astype(F32) * a_ref[d, qs : qs + qn, at].astype(F32)
                dqs = []
                for h in range(2):
                    lanes = slice(h * HEAD_DIM, (h + 1) * HEAD_DIM)
                    qh, kh, gh = qq[:, lanes] * BF16(scale), kk[:, lanes], gg[:, lanes]
                    lane = lax.broadcasted_iota(jnp.int32, (qn, 2 * n * pairs), 1)
                    picked = jnp.where(lane == (d * pairs + p) * 2 + h, l_ref[qs : qs + qn, :], 0.0)
                    s = jnp.where(mask, dot_nt(qh, kh) - jnp.sum(picked, axis=1, keepdims=True), NEG)
                    pr = jnp.exp(s)
                    dp = dot_nt(gh, vv[:, lanes])
                    delta = jnp.sum(prod[:, lanes], axis=1, keepdims=True)
                    ds = (pr * (dp - delta)).astype(BF16)
                    dqs.append(dot_nn(ds, kh) * scale)
                    gk = dot_tn(qh, ds)
                    gv = dot_tn(gh, pr.astype(BF16))
                    if big and i == 0:
                        dkt[lanes, :] = gk
                        dvt[lanes, :] = gv
                    else:
                        dkt[lanes, ks : ks + kn] += gk
                        dvt[lanes, ks : ks + kn] += gv
                dq[rel, qs : qs + qn, to] = jnp.concatenate(dqs, axis=1).astype(BF16)
            dk[rel, :, to] = dkt[...].T.astype(BF16)
            dv[rel, :, to] = dvt[...].T.astype(BF16)

        def head_pair(i, carry):
            d, p = i // pairs, lax.rem(i, pairs)

            @pl.when(long)
            def _():
                work(True, d, p)

            @pl.when(jnp.logical_not(long))
            def _():
                work(False, d, p)

            order = [(down, 1), (down, 2), (down, 3), (down, 0), (up, 1), (up, 2)]
            turns(i, {t + 2: functools.partial(red.two, shard) for t, (red, shard) in enumerate(order)})
            return carry

        take(4, 5, 6, 7, 8)
        lax.fori_loop(0, n * pairs, head_pair, 0)
        halves = ((dq, dq_o), (dk, dk_o), (dv, dv_o))
        for i, (src, dst) in enumerate(halves):
            wire.start(10 + i, src.at[1], dst, place.core)
        take(9, 10, 11)
        wire.landed(0, ghb2.at[:, rows : 2 * rows], place.core)

        def put(m, val):
            for d in range(n):
                at = d * w + m * PAIR
                act2[:, at : at + PAIR] = val[:, d * PAIR : (d + 1) * PAIR].astype(BF16)

        put(3, dot_nn(ghb2[...], at2[...]))
        weights(2).start()
        wire.landed(10, dq_o, place.core)
        put(0, dot_nn(n12[:, own : own + rows], dq[0]) + dot_nn(n12[:, win + own : win + own + rows], dq_o[...]))
        up.two(3)
        wire.landed(11, dk_o, place.core)
        put(1, dot_nn(n12[:, 0:win], dk[0]) + dot_nn(n12[:, win : 2 * win], dk_o[...]))
        up.two(0)
        wire.landed(12, dv_o, place.core)
        put(2, dot_nn(n12[:, 0:win], dv[0]) + dot_nn(n12[:, win : 2 * win], dv_o[...]))
        for d in (1, 2, 3, 0):
            heads.one(d)

        far_out, x_buf, next_out = n12.at[0:own, 0:dm], n12.at[0:rows, dm : 2 * dm], n12.at[own : own + HALO, 0:dm]
        tokens_in = pltpu.make_async_copy(x_ref, x_buf, ls.at[0])
        tokens_in.start()

        def dots(t, carry):
            weights(t).wait()
            slot = lax.rem(t, 3)
            to = pl.ds(pl.multiple_of(lax.rem(t, n) * PAIR, PAIR), PAIR)

            def weight(which, j):
                at = which * cw + lax.rem(j + core, 2) * PAIR
                return wbuf[slot, :, pl.ds(pl.multiple_of(at, PAIR), PAIR)]

            def add(ref, val, first):
                @pl.when(t == first)
                def _():
                    ref[...] = val

                @pl.when(t > first)
                def _():
                    ref[...] += val

            right = jnp.concatenate([weight(m, j) for m in (1, 2) for j in range(2)], axis=1)

            @pl.when(t < n)
            def _():
                left = jnp.concatenate([r[j, 0:own, to] for r in (dk, dv) for j in range(2)], axis=1)
                add(gi_ref, dot_nt(left, right), 0)

            @pl.when(t >= n)
            def _():
                left = jnp.concatenate([r[j, own : own + rows, to] for r in (dk, dv) for j in range(2)], axis=1)
                mine = jnp.concatenate([dq[j, :, to] for j in range(2)], axis=1)
                other = jnp.concatenate([weight(0, j) for j in range(2)], axis=1)
                add(gi_ref, dot_nt(left, right) + dot_nt(mine, other), n)
                left = jnp.concatenate(
                    [r[j, own + rows : own + rows + HALO, to] for r in (dk, dv) for j in range(2)], axis=1
                )
                add(nxt, dot_nt(left, right), n)

            @pl.when(t < 2 * n - 3)
            def _():
                weights(t + 3).start()

            @pl.when(t == n - 1)
            def _():
                far_out[...] = gi_ref[...].astype(BF16)

                @pl.when(z == 0)
                def _():
                    wire.start(13, far_out.at[0:SPAN], far_in.at[0:SPAN], swap)

                @pl.when(z == 1)
                def _():
                    wire.start(13, far_out, far_in, swap)

                @pl.when(gives_prev)
                def _():
                    wire.start(14, far_out.at[own - HALO : own], prev_in, left_dev)

            turns(t, {2 * i + 1: functools.partial(down.three, i + 1) for i in range(3)})
            return carry

        lax.fori_loop(0, 2 * n, dots, 0)
        next_out[...] = nxt[...].astype(BF16)

        @pl.when(gives_next)
        def _():
            wire.start(15, next_out, next_in, right_dev)

        up.three(1)
        up.three(2)
        up.three(3)
        heads.two(1)
        heads.two(2)
        down.last()
        heads.two(3)
        heads.two(0)
        heads.three(1)

        @pl.when(z == 0)
        def _():
            wire.landed(13, far_in, swap)
            gi_ref[...] += far_in[...].astype(F32)

        @pl.when(z == 1)
        def _():
            wire.landed(13, far_in.at[0:SPAN], swap)
            gi_ref[0:SPAN, :] += far_in[0:SPAN, :].astype(F32)

        @pl.when(gives_next)
        def _():
            wire.landed(14, prev_in, right_dev)
            gi_ref[rows - HALO : rows, :] += prev_in[...].astype(F32)

        @pl.when(gives_prev)
        def _():
            wire.landed(15, next_in, left_dev)
            gi_ref[0:HALO, :] += next_in[...].astype(F32)

        up.last()
        heads.three(2)
        heads.three(3)
        va[0] = vec_ref[...]
        for base, grad in ((6, dq), (7, dv)):
            for j in range(2):
                total = jnp.sum(grad[j].astype(F32), axis=0, keepdims=True)
                for d in range(n):
                    at = base * dm + lax.rem(z + d, n) * cw + lax.rem(j + core, 2) * PAIR
                    va[0, :, pl.ds(pl.multiple_of(at, PAIR), PAIR)] = total[:, d * PAIR : (d + 1) * PAIR]
        tokens_in.wait()
        gains = gain_ref[...].astype(F32)

        def norm(i, carry):
            at = pl.ds(pl.multiple_of(i * strip, strip), strip)
            hat, inv = norm_rows(x_buf[at, :].astype(F32))
            grad = gi_ref[at, :]
            gg = grad * gains
            first = jnp.mean(gg, axis=1, keepdims=True)
            second = jnp.mean(gg * hat, axis=1, keepdims=True)
            gi_ref[at, :] = inv * (gg - first - hat * second)
            va[0, :, 0:dm] += jnp.sum(grad * hat, axis=0, keepdims=True)
            va[0, :, dm : 2 * dm] += jnp.sum(grad, axis=0, keepdims=True)
            return carry

        lax.fori_loop(0, rows // strip, norm, 0)

        hops = (place.core, place.by_x, place.by_y)
        between = (down.four, up.four, down.five)
        for i, dev in enumerate(hops):
            wire.start(16 + i, va.at[i], vr.at[i], dev)
            between[i]()
            wire.landed(16 + i, vr.at[i], dev)
            if i < 2:
                va[i + 1] = va[i] + vr[i]
            else:
                vz[0] = va[i] + vr[i]
        for d in (1, 2, 3):
            wire.start(18 + d, vz.at[0], vz.at[d], place.along(d))
        up.five()
        heads.last()
        heads.four()
        for d in (1, 2, 3):
            wire.landed(18 + d, vz.at[d], place.along(4 - d))
        terms = [vz[lax.rem(z - a + 4, 4)] for a in range(4)]
        sum_ref[...] = (terms[0] + terms[1]) + (terms[2] + terms[3])
        heads.five()
        down.six()
        up.six()
        heads.six()
        wire.sent(0, ghb2.at[:, 0:rows])
        for i in range(3):
            wire.sent(10 + i, halves[i][1])

        @pl.when(z == 0)
        def _():
            wire.sent(13, far_in.at[0:SPAN])

        @pl.when(z == 1)
        def _():
            wire.sent(13, far_in)

        @pl.when(gives_prev)
        def _():
            wire.sent(14, prev_in)

        @pl.when(gives_next)
        def _():
            wire.sent(15, next_in)

        for i in range(3):
            wire.sent(16 + i, va.at[i])
        for d in (1, 2, 3):
            wire.sent(18 + d, vz.at[0])

    hbm = pl.BlockSpec(memory_space=pl.ANY)
    vmem = pl.BlockSpec(memory_space=pltpu.VMEM)
    shaped = lambda *shape: jax.ShapeDtypeStruct(shape, BF16)
    buf = lambda *shape: pltpu.VMEM(shape, BF16)
    wide = lambda *shape: pltpu.VMEM(shape, F32)
    sem = lambda count: pltpu.SemaphoreType.DMA((count,))
    q4 = dm // 4
    return pl.pallas_call(
        body,
        in_specs=[hbm] * 14 + [vmem] * 5,
        out_specs=[hbm] * 3 + [vmem] * 2,
        out_shape=[shaped(8, q4, w)] * 3 + [jax.ShapeDtypeStruct((rows, dm), F32), jax.ShapeDtypeStruct((1, length), F32)],
        scratch_shapes=[
            buf(3, dm, 2 * rows), buf(2 * rows, hw), buf(2 * rows, hw), buf(dm, 2 * win), buf(dm, hw), buf(dm, hw),
            buf(rows, half), buf(win, half), buf(win, half), buf(2 * rows, half), buf(2, rows, half), buf(2, win, half), buf(2, win, half),
            wide(PAIR, win), wide(PAIR, win), buf(own, dm), buf(HALO, dm), buf(HALO, dm), wide(HALO, dm),
            wide(3, 1, length), wide(3, 1, length), wide(4, 1, length), buf(3, q4, w),
            buf(n, rows, cw), buf(n, win, cw), buf(n, win, cw), buf(n, rows, cw), buf(n, rows, cw),
            sem(Reduce.SLOTS), sem(Reduce.SLOTS), sem(22), sem(22), sem(13), sem(3),
        ]
        + Reduce.scratch(dm, w) * 2,
        compiler_params=pltpu.CompilerParams(collective_id=1, has_side_effects=True, vmem_limit_bytes=VMEM_ALL),
    )(cot, act, n2, gup, ghb, n1w, attn2, packed, tokens, q, k, v, attn, gattn, lse, qseg, kseg, gain[None], vec)


def place_grads(coords, down, up, pack, g_in, g_hidden):
    _, q, w = up.shape
    e = q // 2
    dm = 4 * q
    lanes = w // 4
    rows = g_in.shape[0]
    shapes = [(rows, dm), (2 * w, dm), (dm, 2 * w), (dm, w // 2), (dm, w // 2), (dm, w // 2), (w // 2, dm)]
    count = len(shapes)
    strip = 128

    def body(c_ref, *refs):
        ins, outs, bufs, more = refs[:5], refs[5 : 5 + count], refs[5 + count : 5 + 2 * count], refs[5 + 2 * count :]
        d_buf, u_buf, p_buf, h_buf, ls, os = more
        pieces = (d_buf, u_buf, p_buf)
        loads = [
            pltpu.make_async_copy(src, dst, ls.at[i])
            for i, (src, dst) in enumerate(zip(ins, (*pieces, bufs[0], h_buf)))
        ]
        stores = [pltpu.make_async_copy(bufs[i], outs[i], os.at[i]) for i in range(count)]
        for i in (1, 3, 4, 0, 2):
            loads[i].start()

        def spread(ref, put):
            def one(off, carry):
                y = lax.rem(c_ref[0] + off // 4, 2)
                x = lax.rem(c_ref[1] + lax.rem(off // 2, 2), 2)
                k = lax.rem(c_ref[2] + lax.rem(off, 2), 2)
                for part, block in enumerate((2 * x + y, 4 + 2 * y + x)):
                    val = ref[off, part * e : (part + 1) * e, :].astype(F32)
                    put(val, pl.ds(pl.multiple_of(block * e, e), e), k)
                return carry

            lax.fori_loop(0, 8, one, 0)

        def put_up(val, at, k):
            bufs[2][at, pl.ds(pl.multiple_of(k * w, w), w)] = val

        def put_down(val, at, k):
            bufs[1][pl.ds(pl.multiple_of(k * w, w), w), at] = val.T

        def put_pack(val, at, k):
            half = pl.ds(pl.multiple_of(k * lanes, lanes), lanes)
            for m in range(3):
                bufs[3 + m][at, half] = val[:, m * lanes : (m + 1) * lanes]
            bufs[6][half, at] = val[:, 3 * lanes :].T

        loads[1].wait()
        spread(u_buf, put_up)
        stores[2].start()
        loads[3].wait()
        loads[4].wait()

        def add(i, carry):
            at = pl.ds(pl.multiple_of(i * strip, strip), strip)
            bufs[0][at, :] += h_buf[at, :]
            return carry

        lax.fori_loop(0, rows // strip, add, 0)
        stores[0].start()
        loads[0].wait()
        spread(d_buf, put_down)
        stores[1].start()
        loads[2].wait()
        spread(p_buf, put_pack)
        for i in range(3, count):
            stores[i].start()
        for c in stores:
            c.wait()

    hbm = pl.BlockSpec(memory_space=pl.ANY)
    return pl.pallas_call(
        body,
        in_specs=[pl.BlockSpec(memory_space=pltpu.SMEM)] + [hbm] * 5,
        out_specs=[hbm] * count,
        out_shape=[jax.ShapeDtypeStruct(shape, F32) for shape in shapes],
        scratch_shapes=[pltpu.VMEM(shape, F32) for shape in shapes]
        + [pltpu.VMEM((8, q, w), BF16)] * 3
        + [pltpu.VMEM((rows, dm), F32), pltpu.SemaphoreType.DMA((5,)), pltpu.SemaphoreType.DMA((count,))],
        compiler_params=pltpu.CompilerParams(vmem_limit_bytes=VMEM),
        cost_estimate=pl.CostEstimate(flops=0, bytes_accessed=36 * dm * w, transcendentals=0),
    )(coords, down, up, pack, g_in, g_hidden)


def relative(stack, z):
    return jnp.roll(stack, -z, axis=0)


def core_first(v, core, axis):
    return jnp.where(core == 0, v, jnp.flip(v, axis))


def gather_any(shard, z):
    return relative(lax.all_gather(shard, "mp", axis=0, tiled=False), z)


def reduce_any(half, z, core):
    zero = jnp.zeros_like(half)
    v = jnp.stack([jnp.where(core == 0, half, zero), jnp.where(core == 1, half, zero)], axis=2)
    v = jnp.roll(jnp.moveaxis(v, 1, 0), z, axis=0)
    v = lax.psum_scatter(v, "mp", scatter_dimension=0, tiled=True)[0]
    return lax.psum(v, "dp").astype(F32).reshape(half.shape[0], -1)


def local(
    tokens,
    segments,
    ln1_gain,
    ln1_bias,
    w_query,
    b_query,
    w_key,
    w_value,
    b_value,
    w_out,
    b_out,
    ln2_gain,
    ln2_bias,
    w_up,
    b_up,
    w_down,
    b_down,
    cotangent,
):
    rows, dm = tokens.shape
    cw = w_query.shape[1]
    ffw = w_up.shape[1]
    mp = lax.axis_size("mp")
    dp = lax.axis_size("dp")
    fast = mp == 4 and dp == 8 and rows % 256 == 0 and cw == 2 * PAIR and rows < LONGEST <= rows + SPAN <= 2 * rows
    z = lax.axis_index("mp")
    me = lax.axis_index("dp")
    core = lax.rem(me, 2)
    x = lax.rem(me // 2, 2)
    y = me // 4
    f32 = lambda v: v.astype(F32)

    near = -(-LONGEST // rows)
    own = (near - 1) * rows
    win = own + rows + 2 * HALO
    is_near = z < near
    seg_parts = [
        jnp.where(is_near, lax.dynamic_slice_in_dim(segments, lax.rem(z + j, near) * rows, rows), -1)
        for j in range(1, near)
    ]
    seg_own = lax.dynamic_slice_in_dim(segments, z * rows, rows)
    seg_prev = lax.dynamic_slice_in_dim(segments, jnp.maximum(z * rows - HALO, 0), HALO)
    seg_next = lax.dynamic_slice_in_dim(segments, jnp.minimum((z + 1) * rows, segments.shape[0] - HALO), HALO)
    seg_far = jnp.concatenate(seg_parts)
    seg_far = jnp.concatenate([seg_far[:-HALO], jnp.where(is_near, seg_far[-HALO:], seg_prev)])
    has_next = jnp.logical_and(z >= near - 1, z < mp - 1)
    seg_win = jnp.concatenate(
        [seg_far, seg_own, jnp.where(has_next, seg_next, -1), jnp.full((HALO,), -1, segments.dtype)]
    )
    kseg, qseg = seg_win[None, :], seg_own[:, None]
    info = jnp.stack([is_near.astype(jnp.int32), core]).astype(jnp.int32)

    pack = jnp.concatenate([w_query, w_key, w_value, w_out.T], axis=1)
    hw = mp * ffw // 2
    if fast:
        small = jnp.concatenate([ln1_gain, ln1_bias, ln2_gain, ln2_bias, b_out, b_down, b_query, b_value, b_up])
        small = f32(small)[None]
        (
            packed, n1_t, n2_t, cot_t, ghb_t, q, k, v, attn, attn_2, g_attn, active, g_upper, g_hidden, lse, output, vec
        ) = front_call(tokens, cotangent, pack, w_up, w_down, small, qseg, kseg, own)
        done_d, done_u, done_p, g_in, vec = back_call(
            cot_t, active, n2_t, g_upper, ghb_t, n1_t, attn_2, packed, tokens, q, k, v, attn, g_attn, lse, qseg, kseg, ln1_gain, vec, own
        )
        vec = vec[0]
        coords = jnp.stack([y, x, core]).astype(jnp.int32)
        g_tokens, g_w_down, g_w_up, g_w_query, g_w_key, g_w_value, g_w_out = place_grads(
            coords, done_d, done_u, done_p, g_in, g_hidden
        )
    else:
        halo = [
            lax.ppermute(tokens, "mp", [((i + j) % near, i) for i in range(near)]) for j in range(1, near)
        ]
        before = lax.ppermute(tokens[-HALO:], "mp", [(i - 1, i) for i in range(near, mp)])
        behind = lax.ppermute(tokens[:HALO], "mp", [(i + 1, i) for i in range(near - 1, mp - 1)])
        small_vec = jnp.concatenate([b_query, b_value, b_up])
        vecs = relative(lax.all_gather(small_vec, "mp", axis=0, tiled=False), z)
        bq_all, bv_all = vecs[:, :cw], vecs[:, cw : 2 * cw]
        bu_all = vecs[:, 2 * cw :].reshape(mp, 2, ffw // 2).transpose(1, 0, 2)
        bu_all = core_first(bu_all, core, 0).reshape(mp * ffw)

        packed, up_all, down_all = (gather_any(w, z) for w in (pack, w_up, w_down))

        far = jnp.concatenate(halo, axis=0)
        far = jnp.concatenate([far[:-HALO], far[-HALO:] + before], axis=0)
        tok_win = jnp.concatenate([far, tokens, behind, jnp.zeros((HALO, dm), tokens.dtype)], axis=0)
        hat_win, inv_win = norm_rows(f32(tok_win))
        n1w = (hat_win * f32(ln1_gain) + f32(ln1_bias)).astype(BF16)
        q, k, v = qkv_call(n1w, packed, bq_all, bv_all, own, rows, cw)
        attn, lse = attn_fwd_call(info, q, k, v, qseg, kseg, own)
        hidden, n2 = out_call(attn, packed, tokens, b_out, ln2_gain, ln2_bias)
        output, g_n2, active, g_upper, g_b_up = ffn_call(
            info[1:], n2, hidden, cotangent, up_all, down_all, bu_all, b_down, 2
        )

        gout = f32(cotangent)
        hat2, inv2 = norm_rows(hidden)

        def norm_back(g, hat, inv, gain):
            gg = g * gain
            first = jnp.mean(gg, axis=1, keepdims=True)
            second = jnp.mean(gg * hat, axis=1, keepdims=True)
            return inv * (gg - first - hat * second), jnp.sum(g * hat, axis=0), jnp.sum(g, axis=0)

        g_hidden, g_gain2, g_bias2 = norm_back(g_n2, hat2, inv2, f32(ln2_gain))
        g_hidden = g_hidden + gout
        ghb = g_hidden.astype(BF16)

        g_attn = jnp.stack([dot_nn(ghb, packed[d, :, 3 * cw :]).astype(BF16) for d in range(mp)])
        dq, dk, dv = attn_bwd_call(info, q, k, v, attn, g_attn, lse, qseg, kseg, own)
        n1 = n1w[own : own + rows]
        sums = [jnp.sum(g_hidden, axis=0), g_gain2, g_bias2, jnp.sum(gout, axis=0)]
        halves = dq.shape[0]

        def shards(v, width):
            if v.shape[0] == 2:
                v = core_first(v.reshape(2, mp, width // 2), core, 0).transpose(1, 0, 2)
            return jnp.roll(v.reshape(mp, width), z, axis=0).reshape(mp * width)

        gbq = shards(jnp.sum(f32(dq), axis=1), cw)
        gbv = shards(jnp.sum(f32(dv), axis=1), cw)
        gbu = core_first(g_b_up.reshape(2, mp, ffw // 2), core, 0).transpose(1, 0, 2)
        gbu = jnp.roll(gbu.reshape(mp, ffw), z, axis=0).reshape(-1)
        sums = sums + [gbq, gbv, gbu]
        g_own, g_far, g_next = norm1_back_call(dq, dk, dv, packed, info, own)
        back = g_own
        for j in range(1, near):
            part = g_far[(j - 1) * rows : j * rows]
            back = back + f32(lax.ppermute(part, "mp", [(i, (i + j) % near) for i in range(near)]))
        to_prev = f32(lax.ppermute(g_far[-HALO:], "mp", [(i, i - 1) for i in range(near, mp)]))
        to_next = f32(lax.ppermute(g_next, "mp", [(i, i + 1) for i in range(near - 1, mp - 1)]))
        back = jnp.concatenate([back[:HALO] + to_next, back[HALO:-HALO], back[-HALO:] + to_prev], axis=0)
        hat1 = hat_win[own : own + rows]
        inv1 = inv_win[own : own + rows]
        g_in, g_gain1, g_bias1 = norm_back(back, hat1, inv1, f32(ln1_gain))
        g_tokens = g_in + g_hidden

        other = lambda v: lax.ppermute(v, "dp", [(i, i - i % 2 + (i + 1) % 2) for i in range(dp)])
        hw = mp * ffw // 2

        def pair_grad(left, right):
            return (dot_tn(left, right[:, :hw]) + dot_tn(other(left), other(right[:, hw:]))).astype(BF16)

        gd = pair_grad(cotangent, active)
        gu = pair_grad(n2, g_upper)
        g_w_up = reduce_any(gu.reshape(dm, mp, ffw // 2), z, core)
        g_w_down = reduce_any(gd.reshape(dm, mp, ffw // 2), z, core).T

        def whole_grad(left, right, name=None):
            v = dot_tn(left, right).astype(BF16).reshape(dm, mp, cw)
            v = jnp.roll(jnp.moveaxis(v, 1, 0), z, axis=0)
            v = lax.psum_scatter(v, "mp", scatter_dimension=0, tiled=True)[0]
            return lax.psum(v, "dp").astype(F32)

        def whole(v):
            if halves == 1:
                return v[0]
            v = v.reshape(2, v.shape[1], mp, cw // 2).transpose(1, 2, 0, 3)
            return core_first(v, core, 2).reshape(v.shape[0], mp * cw)

        g_w_query = whole_grad(n1, whole(dq))
        g_w_key = whole_grad(n1w, whole(dk))
        g_w_value = whole_grad(n1w, whole(dv))
        g_w_out = whole_grad(ghb, attn.transpose(1, 0, 2).reshape(rows, mp * cw)).T

        vec = lax.psum(jnp.concatenate([g_gain1, g_bias1] + sums), ("dp", "mp"))
    g_gain1, g_bias1, g_b_out, g_gain2, g_bias2, g_b_down = (vec[i * dm : (i + 1) * dm] for i in range(6))
    at = 6 * dm
    g_b_query = lax.dynamic_slice_in_dim(vec, at + z * cw, cw)
    g_b_value = lax.dynamic_slice_in_dim(vec, at + mp * cw + z * cw, cw)
    g_b_up = lax.dynamic_slice_in_dim(vec, at + 2 * mp * cw + z * ffw, ffw)
    return (
        output,
        g_tokens,
        g_gain1,
        g_bias1,
        g_w_query,
        g_b_query,
        g_w_key,
        g_w_value,
        g_b_value,
        g_w_out,
        g_b_out,
        g_gain2,
        g_bias2,
        g_w_up,
        g_b_up,
        g_w_down,
        g_b_down,
    )


def solution(mesh):
    in_specs = (
        P(("dp", "mp"), None),
        P("dp"),
        P(),
        P(),
        P(None, "mp"),
        P("mp"),
        P(None, "mp"),
        P(None, "mp"),
        P("mp"),
        P("mp", None),
        P(),
        P(),
        P(),
        P(None, "mp"),
        P("mp"),
        P("mp", None),
        P(),
        P(("dp", "mp"), None),
    )
    out_specs = (
        P(("dp", "mp"), None),
        P(("dp", "mp"), None),
        P(),
        P(),
        P(None, "mp"),
        P("mp"),
        P(None, "mp"),
        P(None, "mp"),
        P("mp"),
        P("mp", None),
        P(),
        P(),
        P(),
        P(None, "mp"),
        P("mp"),
        P("mp", None),
        P(),
    )
    return jax.shard_map(local, mesh=mesh, in_specs=in_specs, out_specs=out_specs, check_vma=False)
```

```python
import functools

import jax
import jax.numpy as jnp
from jax import lax
from jax.experimental import pallas as pl
from jax.experimental.pallas import tpu as pltpu
from jax.sharding import PartitionSpec as P

HEAD_DIM = 64
LONGEST = 900
HALO = 64
PAIR = 128
SPAN = 400
EPS = 1e-06
NEG = -1e30
VMEM = 60 * 1024 * 1024
VMEM_ALL = 67043328
F32 = jnp.float32
BF16 = jnp.bfloat16


def dot_nn(a, b):
    return lax.dot_general(a, b, (((1,), (0,)), ((), ())), preferred_element_type=F32)


def dot_nt(a, b):
    return lax.dot_general(a, b, (((1,), (1,)), ((), ())), preferred_element_type=F32)


def dot_tn(a, b):
    return lax.dot_general(a, b, (((0,), (0,)), ((), ())), preferred_element_type=F32)


def barrier(*xs):
    return lax.optimization_barrier(xs)


def params(*sem, **kw):
    return pltpu.CompilerParams(dimension_semantics=sem, vmem_limit_bytes=VMEM, **kw)


def norm_rows(x):
    mean = jnp.mean(x, axis=1, keepdims=True)
    cent = x - mean
    inv = lax.rsqrt(jnp.mean(cent * cent, axis=1, keepdims=True) + EPS)
    return cent * inv, inv


def qkv_call(n1w, packed, b_q, b_v, own, rows, cw):
    n, dm, _ = packed.shape
    win = n1w.shape[0]

    def body(x_ref, w_ref, bq_ref, bv_ref, q_ref, k_ref, v_ref):
        x = x_ref[...]
        q_ref[0] = (dot_nn(x[own : own + rows], w_ref[0, :, 0:cw]) + bq_ref[0].astype(F32)).astype(BF16)
        k_ref[0] = dot_nn(x, w_ref[0, :, cw : 2 * cw]).astype(BF16)
        v_ref[0] = (dot_nn(x, w_ref[0, :, 2 * cw : 3 * cw]) + bv_ref[0].astype(F32)).astype(BF16)

    return pl.pallas_call(
        body,
        grid=(n,),
        in_specs=[
            pl.BlockSpec((win, dm), lambda d: (0, 0)),
            pl.BlockSpec((1, dm, 4 * cw), lambda d: (d, 0, 0)),
            pl.BlockSpec((1, 1, cw), lambda d: (d, 0, 0)),
            pl.BlockSpec((1, 1, cw), lambda d: (d, 0, 0)),
        ],
        out_specs=[
            pl.BlockSpec((1, rows, cw), lambda d: (d, 0, 0)),
            pl.BlockSpec((1, win, cw), lambda d: (d, 0, 0)),
            pl.BlockSpec((1, win, cw), lambda d: (d, 0, 0)),
        ],
        out_shape=[
            jax.ShapeDtypeStruct((n, rows, cw), BF16),
            jax.ShapeDtypeStruct((n, win, cw), BF16),
            jax.ShapeDtypeStruct((n, win, cw), BF16),
        ],
        compiler_params=params("arbitrary"),
        cost_estimate=pl.CostEstimate(
            flops=2 * n * dm * cw * (rows + 2 * win), bytes_accessed=2 * (n * dm * 4 * cw + win * dm), transcendentals=0
        ),
    )(n1w, packed, b_q[:, None, :], b_v[:, None, :])


def blocks_of(rows, own, win, big):
    if big:
        step = min(256, rows)
        return [(s, step, 0, win) for s in range(0, rows, step)]
    return [(s, 128, own + s - 128, 384) for s in range(0, rows, 128)]


def attn_fwd_call(is_big, q, k, v, qseg, kseg, own):
    n, rows, cw = q.shape
    win = k.shape[1]
    pairs = cw // PAIR

    def work(big, q_ref, k_ref, v_ref, qs_ref, ks_ref, o_ref, l_ref):
        for qs, qn, ks, kn in blocks_of(rows, own, win, big):
            mask = qs_ref[qs : qs + qn, :] == ks_ref[:, ks : ks + kn]
            for h in range(2):
                lanes = slice(h * HEAD_DIM, (h + 1) * HEAD_DIM)
                qh = q_ref[0, qs : qs + qn, lanes] * BF16(HEAD_DIM**-0.5)
                s = jnp.where(mask, dot_nt(qh, k_ref[0, ks : ks + kn, lanes]), NEG)
                top = jnp.max(s, axis=1, keepdims=True)
                p = jnp.exp(s - top)
                total = jnp.sum(p, axis=1, keepdims=True)
                o = dot_nn(p.astype(BF16), v_ref[0, ks : ks + kn, lanes])
                o_ref[0, qs : qs + qn, lanes] = (o / total).astype(BF16)
                l_ref[0, qs : qs + qn, h : h + 1] = top + jnp.log(total)

    def body(big_ref, *refs):
        @pl.when(big_ref[0] == 1)
        def _():
            work(True, *refs)

        @pl.when(big_ref[0] == 0)
        def _():
            work(False, *refs)

    return pl.pallas_call(
        body,
        grid_spec=pltpu.PrefetchScalarGridSpec(
            num_scalar_prefetch=1,
            grid=(n, pairs),
            in_specs=[
                pl.BlockSpec((1, rows, PAIR), lambda d, p, *_: (d, 0, p)),
                pl.BlockSpec((1, win, PAIR), lambda d, p, *_: (d, 0, p)),
                pl.BlockSpec((1, win, PAIR), lambda d, p, *_: (d, 0, p)),
                pl.BlockSpec((rows, 1), lambda d, p, *_: (0, 0)),
                pl.BlockSpec((1, win), lambda d, p, *_: (0, 0)),
            ],
            out_specs=[
                pl.BlockSpec((1, rows, PAIR), lambda d, p, *_: (d, 0, p)),
                pl.BlockSpec((1, rows, 2), lambda d, p, *_: (d * pairs + p, 0, 0)),
            ],
        ),
        out_shape=[
            jax.ShapeDtypeStruct((n, rows, cw), BF16),
            jax.ShapeDtypeStruct((n * pairs, rows, 2), F32),
        ],
        compiler_params=params("arbitrary", "arbitrary"),
        cost_estimate=pl.CostEstimate(
            flops=16 * n * rows * win * cw, bytes_accessed=2 * n * cw * (2 * rows + 2 * win), transcendentals=n * rows * win * 4
        ),
    )(is_big, q, k, v, qseg, kseg)


def attn_bwd_call(info, q, k, v, attn, gattn, lse, qseg, kseg, own):
    n, rows, cw = q.shape
    win = k.shape[1]
    pairs = cw // PAIR
    scale = HEAD_DIM**-0.5

    def work(big, q_ref, k_ref, v_ref, a_ref, g_ref, l_ref, qs_ref, ks_ref, dq_ref, dk_ref, dv_ref, dkt, dvt):
        if not big:
            dkt[...] = jnp.zeros_like(dkt)
            dvt[...] = jnp.zeros_like(dvt)
        for i, (qs, qn, ks, kn) in enumerate(blocks_of(rows, own, win, big)):
            mask = qs_ref[qs : qs + qn, :] == ks_ref[:, ks : ks + kn]
            for h in range(2):
                lanes = slice(h * HEAD_DIM, (h + 1) * HEAD_DIM)
                qh = q_ref[0, qs : qs + qn, lanes] * BF16(scale)
                kh = k_ref[0, ks : ks + kn, lanes]
                gh = g_ref[0, qs : qs + qn, lanes]
                s = jnp.where(mask, dot_nt(qh, kh) - l_ref[0, qs : qs + qn, h : h + 1], NEG)
                p = jnp.exp(s)
                dp = dot_nt(gh, v_ref[0, ks : ks + kn, lanes])
                delta = jnp.sum(
                    gh.astype(F32) * a_ref[0, qs : qs + qn, lanes].astype(F32), axis=1, keepdims=True
                )
                ds = (p * (dp - delta)).astype(BF16)
                dq_ref[0, qs : qs + qn, lanes] = (dot_nn(ds, kh) * scale).astype(BF16)
                dk = dot_tn(qh, ds)
                dv = dot_tn(gh, p.astype(BF16))
                if big and i == 0:
                    dkt[lanes, :] = dk
                    dvt[lanes, :] = dv
                else:
                    dkt[lanes, ks : ks + kn] += dk
                    dvt[lanes, ks : ks + kn] += dv
        dk_ref[0] = dkt[...].T.astype(BF16)
        dv_ref[0] = dvt[...].T.astype(BF16)

    def body(info_ref, *refs):
        @pl.when(info_ref[0] == 1)
        def _():
            work(True, *refs)

        @pl.when(info_ref[0] == 0)
        def _():
            work(False, *refs)

    if pairs > 1:

        def put(d, p, info):
            rel = lax.bitwise_xor(p // (pairs // 2), info[1])
            return (rel, 0, d * (pairs // 2) + p % (pairs // 2))

        half_shape = (2, rows, n * cw // 2)
        half_win = (2, win, n * cw // 2)
    else:

        def put(d, p, info):
            return (0, 0, d)

        half_shape = (1, rows, n * cw)
        half_win = (1, win, n * cw)
    return pl.pallas_call(
        body,
        grid_spec=pltpu.PrefetchScalarGridSpec(
            num_scalar_prefetch=1,
            grid=(n, pairs),
            in_specs=[
                pl.BlockSpec((1, rows, PAIR), lambda d, p, *_: (d, 0, p)),
                pl.BlockSpec((1, win, PAIR), lambda d, p, *_: (d, 0, p)),
                pl.BlockSpec((1, win, PAIR), lambda d, p, *_: (d, 0, p)),
                pl.BlockSpec((1, rows, PAIR), lambda d, p, *_: (d, 0, p)),
                pl.BlockSpec((1, rows, PAIR), lambda d, p, *_: (d, 0, p)),
                pl.BlockSpec((1, rows, 2), lambda d, p, *_: (d * pairs + p, 0, 0)),
                pl.BlockSpec((rows, 1), lambda d, p, *_: (0, 0)),
                pl.BlockSpec((1, win), lambda d, p, *_: (0, 0)),
            ],
            out_specs=[
                pl.BlockSpec((1, rows, PAIR), put),
                pl.BlockSpec((1, win, PAIR), put),
                pl.BlockSpec((1, win, PAIR), put),
            ],
            scratch_shapes=[pltpu.VMEM((PAIR, win), F32), pltpu.VMEM((PAIR, win), F32)],
        ),
        out_shape=[
            jax.ShapeDtypeStruct(half_shape, BF16),
            jax.ShapeDtypeStruct(half_win, BF16),
            jax.ShapeDtypeStruct(half_win, BF16),
        ],
        compiler_params=params("arbitrary", "arbitrary"),
        cost_estimate=pl.CostEstimate(
            flops=40 * n * rows * win * cw, bytes_accessed=2 * n * cw * (4 * rows + 4 * win), transcendentals=n * rows * win * 4
        ),
    )(info, q, k, v, attn, gattn, lse, qseg, kseg)


def out_call(attn, packed, resid, b_out, gain, bias):
    n, rows, cw = attn.shape
    dm = packed.shape[1]

    def body(a_ref, w_ref, x_ref, bo_ref, g_ref, b_ref, h_ref, n_ref):
        d = pl.program_id(0)
        part = dot_nt(a_ref[0], w_ref[0])

        @pl.when(d == 0)
        def _():
            h_ref[...] = part + x_ref[...].astype(F32) + bo_ref[...].astype(F32)

        @pl.when(d > 0)
        def _():
            h_ref[...] += part

        @pl.when(d == n - 1)
        def _():
            hat, _ = norm_rows(h_ref[...])
            n_ref[...] = (hat * g_ref[...].astype(F32) + b_ref[...].astype(F32)).astype(BF16)

    full = lambda d: (0, 0)
    return pl.pallas_call(
        body,
        grid=(n,),
        in_specs=[
            pl.BlockSpec((1, rows, cw), lambda d: (d, 0, 0)),
            pl.BlockSpec((1, dm, cw), lambda d: (d, 0, 3)),
            pl.BlockSpec((rows, dm), full),
            pl.BlockSpec((1, dm), full),
            pl.BlockSpec((1, dm), full),
            pl.BlockSpec((1, dm), full),
        ],
        out_specs=[pl.BlockSpec((rows, dm), full), pl.BlockSpec((rows, dm), full)],
        out_shape=[jax.ShapeDtypeStruct((rows, dm), F32), jax.ShapeDtypeStruct((rows, dm), BF16)],
        compiler_params=params("arbitrary"),
        cost_estimate=pl.CostEstimate(flops=2 * n * rows * cw * dm, bytes_accessed=2 * n * dm * cw, transcendentals=0),
    )(attn, packed, resid, b_out[None], gain[None], bias[None])


def ffn_call(core, n2, hidden, cot, w_up, w_down, b_up, b_down, halves):
    rows, dm = n2.shape
    n, _, ffw = w_up.shape
    tile = ffw // halves

    def body(core_ref, x_ref, h_ref, c_ref, wu_ref, wd_ref, bu_ref, bd_ref, o_ref, gn_ref, a_ref, gu_ref, gb_ref, acc):
        t = pl.program_id(0)
        u = dot_nn(x_ref[...], wu_ref[0]) + bu_ref[...].astype(F32)
        cdf = 0.5 * (1.0 + lax.erf(u * 0.7071067811865476))
        act = (u * cdf).astype(BF16)
        slope = cdf + u * jnp.exp(-0.5 * u * u) * 0.3989422804014327
        a_ref[...] = act
        grad = dot_nt(c_ref[...], wd_ref[0]) * slope
        gu = grad.astype(BF16)
        gu_ref[...] = gu
        gb_ref[...] = jnp.sum(gu.astype(F32), axis=0, keepdims=True)
        out = dot_nn(act, wd_ref[0])
        gn = dot_nt(gu, wu_ref[0])

        @pl.when(t == 0)
        def _():
            acc[...] = h_ref[...] + bd_ref[...].astype(F32) + out
            gn_ref[...] = gn

        @pl.when(t > 0)
        def _():
            acc[...] += out
            gn_ref[...] += gn

        @pl.when(t == n * halves - 1)
        def _():
            o_ref[...] = acc[...].astype(BF16)

    full = lambda t, c: (0, 0)

    def part(t, c):
        return lax.bitwise_xor(t // n, c[0]) if halves > 1 else 0

    return pl.pallas_call(
        body,
        grid_spec=pltpu.PrefetchScalarGridSpec(
            num_scalar_prefetch=1,
            grid=(n * halves,),
            in_specs=[
                pl.BlockSpec((rows, dm), full),
                pl.BlockSpec((rows, dm), full),
                pl.BlockSpec((rows, dm), full),
                pl.BlockSpec((1, dm, tile), lambda t, c: (t % n, 0, part(t, c))),
                pl.BlockSpec((1, tile, dm), lambda t, c: (t % n, part(t, c), 0)),
                pl.BlockSpec((1, tile), lambda t, c: (0, t)),
                pl.BlockSpec((1, dm), full),
            ],
            out_specs=[
                pl.BlockSpec((rows, dm), full),
                pl.BlockSpec((rows, dm), full),
                pl.BlockSpec((rows, tile), lambda t, c: (0, t)),
                pl.BlockSpec((rows, tile), lambda t, c: (0, t)),
                pl.BlockSpec((1, tile), lambda t, c: (0, t)),
            ],
            scratch_shapes=[pltpu.VMEM((rows, dm), F32)],
        ),
        out_shape=[
            jax.ShapeDtypeStruct((rows, dm), BF16),
            jax.ShapeDtypeStruct((rows, dm), F32),
            jax.ShapeDtypeStruct((rows, n * ffw), BF16),
            jax.ShapeDtypeStruct((rows, n * ffw), BF16),
            jax.ShapeDtypeStruct((1, n * ffw), F32),
        ],
        compiler_params=params("arbitrary"),
        cost_estimate=pl.CostEstimate(
            flops=8 * rows * dm * n * ffw, bytes_accessed=4 * n * dm * ffw, transcendentals=2 * rows * n * ffw
        ),
    )(core, n2, hidden, cot, w_up, w_down, b_up[None], b_down[None])


def norm1_back_call(dq, dk, dv, packed, info, own):
    halves, rows, _ = dq.shape
    n, dm, four = packed.shape
    cw = four // 4
    win = dk.shape[1]
    width = cw // halves

    def body(info_ref, dq_ref, dk_ref, dv_ref, w_ref, o_ref, h_ref, t_ref, acc):
        step = pl.program_id(0)

        def weight(which, j):
            at = lax.bitwise_xor(j, info_ref[1]) if halves > 1 else 0
            return w_ref[0, :, pl.ds(pl.multiple_of(which * cw + at * width, width), width)]

        left = jnp.concatenate([r[j] for r in (dk_ref, dv_ref) for j in range(halves)], axis=1)
        right = jnp.concatenate([weight(m, j) for m in (1, 2) for j in range(halves)], axis=1)
        part = dot_nt(left, right)
        left = jnp.concatenate([dq_ref[j] for j in range(halves)], axis=1)
        right = jnp.concatenate([weight(0, j) for j in range(halves)], axis=1)
        mine = dot_nt(left, right)

        @pl.when(step == 0)
        def _():
            acc[...] = part

        @pl.when(step > 0)
        def _():
            acc[...] += part

        acc[own : own + rows, :] += mine

        @pl.when(step == n - 1)
        def _():
            o_ref[...] = acc[own : own + rows, :]
            h_ref[...] = acc[0:own, :].astype(BF16)
            t_ref[...] = acc[own + rows : own + rows + HALO, :].astype(BF16)

    full = lambda s, info: (0, 0)
    return pl.pallas_call(
        body,
        grid_spec=pltpu.PrefetchScalarGridSpec(
            num_scalar_prefetch=1,
            grid=(n,),
            in_specs=[
                pl.BlockSpec((halves, rows, width), lambda s, info: (0, 0, s)),
                pl.BlockSpec((halves, win, width), lambda s, info: (0, 0, s)),
                pl.BlockSpec((halves, win, width), lambda s, info: (0, 0, s)),
                pl.BlockSpec((1, dm, four), lambda s, info: (s, 0, 0)),
            ],
            out_specs=[
                pl.BlockSpec((rows, dm), full),
                pl.BlockSpec((own, dm), full),
                pl.BlockSpec((HALO, dm), full),
            ],
            scratch_shapes=[pltpu.VMEM((win, dm), F32)],
        ),
        out_shape=[
            jax.ShapeDtypeStruct((rows, dm), F32),
            jax.ShapeDtypeStruct((own, dm), BF16),
            jax.ShapeDtypeStruct((HALO, dm), BF16),
        ],
        compiler_params=params("arbitrary"),
        cost_estimate=pl.CostEstimate(
            flops=2 * n * cw * dm * (rows + 2 * win), bytes_accessed=2 * n * cw * (3 * dm + rows + 2 * win), transcendentals=0
        ),
    )(info, dq, dk, dv, packed)


MESH = pl.DeviceIdType.MESH


class Place:
    def __init__(self):
        self.me = lax.axis_index("dp")
        self.z = lax.axis_index("mp")
        self.k = lax.rem(self.me, 2)
        self.x = lax.rem(self.me // 2, 2)
        self.y = self.me // 4
        self.me_k = self.me + 1 - 2 * self.k
        self.me_x = self.me + 2 - 4 * self.x
        self.me_y = self.me + 4 - 8 * self.y
        self.me_xy = self.me_x + 4 - 8 * self.y
        self.core = {"dp": self.me_k, "mp": self.z}
        self.by_x = {"dp": self.me_x, "mp": self.z}
        self.by_y = {"dp": self.me_y, "mp": self.z}

    def along(self, d):
        return {"dp": self.me, "mp": lax.rem(self.z + d, 4)}

    def meet(self):
        sem = pltpu.get_barrier_semaphore()
        for dev in (self.core, self.by_x, self.by_y, self.along(1), self.along(2), self.along(3)):
            pl.semaphore_signal(sem, inc=1, device_id=dev, device_id_type=MESH)
        pl.semaphore_wait(sem, 6)


class Wire:
    def __init__(self, send, recv, dev):
        self.send, self.recv, self.dev = send, recv, dev

    def start(self, slot, src, dst, dev):
        copy = pltpu.make_async_remote_copy(
            src_ref=src, dst_ref=dst, send_sem=self.send.at[slot], recv_sem=self.recv.at[slot],
            device_id=dev, device_id_type=MESH,
        )
        copy.start()

    def sent(self, slot, ref):
        pltpu.make_async_remote_copy(
            src_ref=ref, dst_ref=ref, send_sem=self.send.at[slot], recv_sem=self.recv.at[slot],
            device_id=dict(self.dev), device_id_type=MESH,
        ).wait_send()

    def landed(self, slot, ref, dev):
        pltpu.make_async_remote_copy(
            src_ref=ref, dst_ref=ref, send_sem=self.send.at[slot], recv_sem=self.recv.at[slot],
            device_id=dev, device_id_type=MESH,
        ).wait_recv()


def gather_steps(place, wire, base, shard, whole):
    step = shard.shape[0] // 8
    half = step // 2

    def rows(who, at=0, size=step):
        return pl.ds(pl.multiple_of(who * step + at, half), size)

    def slot(d, kind):
        return base + (d - 1) * 10 + kind

    lower, upper = place.along(3), place.along(1)

    def begin():
        mine = shard.at[rows(place.me)]

        @pl.when(place.z > 0)
        def _():
            wire.start(slot(1, 0), mine, whole.at[1, rows(place.me)], lower)

        @pl.when(place.z < 3)
        def _():
            wire.start(slot(3, 0), mine, whole.at[3, rows(place.me)], upper)

    def goes_down(d):
        return jnp.logical_and(place.z + d < 4, place.z > 0)

    def goes_up(d):
        return jnp.logical_and(place.z + d > 3, place.z < 3)

    def onward(src, dst, d, to, dev):
        pltpu.make_async_remote_copy(
            src_ref=src, dst_ref=dst, send_sem=wire.send.at[slot(d, 9)], recv_sem=wire.recv.at[slot(to, 0)],
            device_id=dev, device_id_type=MESH,
        ).start()

    def first(d):
        mine = whole.at[d, rows(place.me)]
        wire.landed(slot(d, 0), mine, place.along(d))

        @pl.when(goes_down(d))
        def _():
            onward(mine, whole.at[d + 1, rows(place.me)], d, d + 1, lower)

        @pl.when(goes_up(d))
        def _():
            onward(mine, whole.at[d - 1, rows(place.me)], d, d - 1, upper)

        wire.start(slot(d, 2), mine, mine, place.by_x)
        wire.start(slot(d, 3), mine, mine, place.by_y)
        wire.start(slot(d, 1), mine, mine, place.core)

    def second(d):
        got = whole.at[d, rows(place.me_x)]
        wire.landed(slot(d, 2), got, place.by_x)
        part = whole.at[d, rows(place.me_x, 0, half)]
        wire.start(slot(d, 4), part, part, place.by_y)
        wire.start(slot(d, 6), got, got, place.core)
        got = whole.at[d, rows(place.me_y)]
        wire.landed(slot(d, 3), got, place.by_y)
        part = whole.at[d, rows(place.me_y, half, half)]
        wire.start(slot(d, 5), part, part, place.by_x)
        wire.start(slot(d, 7), got, got, place.core)

    def third(d):
        wire.landed(slot(d, 4), whole.at[d, rows(place.me_xy, 0, half)], place.by_y)
        wire.landed(slot(d, 5), whole.at[d, rows(place.me_xy, half, half)], place.by_x)
        got = whole.at[d, rows(place.me_xy)]
        wire.start(slot(d, 8), got, got, place.core)

    def done(d):
        flip = 1 - 2 * place.k
        for kind, who in ((1, place.me), (6, place.me_x), (7, place.me_y), (8, place.me_xy)):
            wire.landed(slot(d, kind), whole.at[d, rows(who + flip)], place.core)

    def drain():
        piece = whole.at[0, pl.ds(0, step)]

        @pl.when(place.z > 0)
        def _():
            wire.sent(slot(1, 0), piece)

        @pl.when(place.z < 3)
        def _():
            wire.sent(slot(3, 0), piece)

        for d in (1, 2, 3):

            @pl.when(jnp.logical_or(goes_down(d), goes_up(d)))
            def _():
                wire.sent(slot(d, 9), piece)

            for kind in range(1, 9):
                wire.sent(slot(d, kind), whole.at[0, pl.ds(0, half if kind in (4, 5) else step)])

    return begin, first, second, third, done, drain


def front_call(tokens, cot, pack, w_up, w_down, small, qseg, kseg, own):
    rows, dm = tokens.shape
    cw = pack.shape[1] // 4
    ffw = w_up.shape[1]
    n = 4
    tile = ffw // 2
    hw = n * tile
    win = own + rows + 2 * HALO
    pairs = cw // PAIR
    strip = 128
    per = rows // strip
    scale = HEAD_DIM**-0.5
    length = small.shape[1] - 6 * dm
    give = 6
    base = give + 3 + 3 * n

    def body(
        tok_ref, cot_ref, pack_ref, up_ref, down_ref, small_ref, qs_ref, ks_ref,
        packed_out, n1t_out, n2t_out, cott_out, ghbt_out, q_out, k_out, v_out, a_out, at_out, ga_out, act_out, gup_out, gh_out,
        l_ref, o_ref, vec_ref,
        up, down, n1, hid, n2, acc, act, gup, biases,
        packed, n1t, n2t, cott, ghbt, q_ref, k_ref, v_ref, a_ref, ga_ref, gh_ref, xs, xr, ls, fs, os,
    ):
        place = Place()
        core, z = place.k, place.z
        long, takes_prev, takes_next = z < 2, z >= 2, jnp.logical_and(z >= 1, z < 3)
        swap = {"dp": place.me, "mp": lax.rem(z + 1, 2)}
        left_dev = {"dp": place.me, "mp": lax.rem(z + 3, 4)}
        right_dev = {"dp": place.me, "mp": lax.rem(z + 1, 4)}
        wire = Wire(xs, xr, place.core)
        local = [
            pltpu.make_async_copy(src, dst, ls.at[i])
            for i, (src, dst) in enumerate(
                ((tok_ref, n1.at[own : own + rows]), (pack_ref, packed.at[0]), (up_ref, up.at[0]), (down_ref, down.at[0]))
            )
        ]
        for c in local:
            c.start()
        place.meet()
        bias_ref = small_ref.at[:, 6 * dm : 6 * dm + length]
        for d in (1, 2, 3):
            wire.start(d - 1, bias_ref, biases.at[d], place.along(4 - d))

        groups = [
            gather_steps(place, wire, base + 30 * g, src, dst)
            for g, (src, dst) in enumerate(((pack_ref, packed), (up_ref, up), (down_ref, down)))
        ]
        groups[0][0]()

        @pl.when(z == 0)
        def _():
            wire.start(3, tok_ref, n1.at[0:own], swap)

        @pl.when(takes_next)
        def _():
            wire.start(4, tok_ref.at[rows - HALO : rows], n1.at[own - HALO : own], right_dev)

        @pl.when(takes_prev)
        def _():
            wire.start(5, tok_ref.at[0:HALO], n1.at[own + rows : own + rows + HALO], left_dev)

        def near_shard(i):
            upper, odd = z // 2, lax.rem(z, 2)
            place_z = (1 + 3 * odd) * (1 + 15 * upper)
            place_i = 1 + 255 * i + (i * (i - 1) // 2) * 65025
            return lax.rem(7053045 // (place_z * place_i), 4)

        items = [(0, 0), (0, 1), (0, 2), (1, 0), (2, 0), (1, 1), (2, 1), (1, 2), (2, 2)]

        def relay(i):
            for lag in range(3):
                if 0 <= i - lag < len(items):
                    g, j = items[i - lag]
                    groups[g][1 + lag](near_shard(j))

        def arrived(j, *which):
            for g in which:
                groups[g][4](near_shard(j))

        def turns(i, table):
            for t, f in table.items():

                @pl.when(i == t)
                def _():
                    f()

        def shard_at(k):
            return near_shard(lax.rem(k + 2, 3)) * ((k + 3) // 4)

        def strip_at(i, start=0):
            return pl.ds(pl.multiple_of(start + i * strip, strip), strip)

        row = lambda i: small_ref[:, i * dm : (i + 1) * dm]

        whole = [
            (n1t, n1t_out.at[:, 0:win]), (n2t, n2t_out.at[:, 0:rows]), (cott, cott_out.at[:, 0:rows]), (ghbt, ghbt_out),
            (q_ref, q_out), (k_ref, k_out), (v_ref, v_out), (a_ref, a_out), (ga_ref, ga_out), (gh_ref, gh_out), (packed, packed_out),
        ]
        leaving = [pltpu.make_async_copy(src, dst, os.at[i]) for i, (src, dst) in enumerate(whole)]
        shared = ((n1t, n1t_out.at[:, win : 2 * win]), (n2t, n2t_out.at[:, rows : 2 * rows]), (cott, cott_out.at[:, rows : 2 * rows]))

        def leave(i):
            leaving[i].start()
            if i < len(shared):
                wire.start(give + i, *shared[i], place.core)

        @pl.when(z == 0)
        def _():
            n1[SPAN:own, :] = jnp.zeros((own - SPAN, dm), BF16)

        @pl.when(takes_prev)
        def _():
            n1[0 : own - HALO, :] = jnp.zeros((own - HALO, dm), BF16)

        @pl.when(jnp.logical_not(takes_next))
        def _():
            n1[own + rows : own + rows + HALO, :] = jnp.zeros((HALO, dm), BF16)

        n1[own + rows + HALO :, :] = jnp.zeros((HALO, dm), BF16)
        biases[0] = bias_ref[...]
        l_ref[...] = jnp.zeros_like(l_ref)
        vec_ref[...] = jnp.zeros_like(vec_ref)

        def turn_cot(i, carry):
            cott[:, strip_at(i)] = cot_ref[strip_at(i), :].astype(F32).T.astype(BF16)
            return carry

        lax.fori_loop(0, per, turn_cot, 0)
        leave(2)

        def norm1(i):
            at = strip_at(i)
            x = n1[at, :].astype(F32)
            hat, _ = norm_rows(x)
            val = hat * row(0) + row(1)
            n1[at, :] = val.astype(BF16)
            n1t[:, at] = val.T.astype(BF16)
            return x

        def norm_own(i, carry):
            hid[strip_at(i), :] = norm1(own // strip + i) + row(4)
            return carry

        def norm_far(i, carry):
            norm1(i)
            return carry

        local[0].wait()
        lax.fori_loop(0, per, norm_own, 0)
        for c in local[1:]:
            c.wait()
        relay(0)
        relay(1)
        relay(2)

        @pl.when(z == 1)
        def _():
            wire.start(3, tok_ref.at[0:SPAN], n1.at[0:SPAN], swap)

        groups[1][0]()
        groups[2][0]()

        @pl.when(z == 0)
        def _():
            wire.landed(3, n1.at[0:SPAN], swap)

        @pl.when(z == 1)
        def _():
            wire.landed(3, n1.at[0:own], swap)

        @pl.when(takes_prev)
        def _():
            wire.landed(4, n1.at[own - HALO : own], left_dev)

        @pl.when(takes_next)
        def _():
            wire.landed(5, n1.at[own + rows : own + rows + HALO], right_dev)

        lax.fori_loop(0, own // strip, norm_far, 0)
        norm1((own + rows) // strip)
        leave(0)
        for d in (1, 2, 3):
            wire.landed(d - 1, biases.at[d], place.along(d))
        relay(3)

        def attend(big, d, p):
            at = pl.ds(pl.multiple_of(p * PAIR, PAIR), PAIR)
            for qs, qn, ks, kn in blocks_of(rows, own, win, big):
                mask = qs_ref[qs : qs + qn, :] == ks_ref[:, ks : ks + kn]
                qq, kk, vv = q_ref[d, qs : qs + qn, at], k_ref[d, ks : ks + kn, at], v_ref[d, ks : ks + kn, at]
                outs = []
                for h in range(2):
                    lanes = slice(h * HEAD_DIM, (h + 1) * HEAD_DIM)
                    s = jnp.where(mask, dot_nt(qq[:, lanes] * BF16(scale), kk[:, lanes]), NEG)
                    top = jnp.max(s, axis=1, keepdims=True)
                    pr = jnp.exp(s - top)
                    total = jnp.sum(pr, axis=1, keepdims=True)
                    outs.append(dot_nn(pr.astype(BF16), vv[:, lanes]) / total)
                    lane = lax.broadcasted_iota(jnp.int32, (qn, 2 * n * pairs), 1)
                    seen = l_ref[qs : qs + qn, :]
                    l_ref[qs : qs + qn, :] = jnp.where(lane == (d * pairs + p) * 2 + h, top + jnp.log(total), seen)
                a_ref[d, qs : qs + qn, at] = jnp.concatenate(outs, axis=1).astype(BF16)

        def head_lanes(d):
            return pl.ds(pl.multiple_of(d * PAIR, PAIR), PAIR)

        def half_of_attn(d):
            mine = pl.ds(pl.multiple_of(core * PAIR, PAIR), PAIR)
            theirs = pl.ds(pl.multiple_of((1 - core) * PAIR, PAIR), PAIR)
            keep = pltpu.make_async_copy(a_ref.at[d, :, mine], at_out.at[0:rows, head_lanes(d)], fs.at[2 * n + d])
            return keep, a_ref.at[d, :, theirs]

        def heads(kk, carry):
            turns(kk, {j + 1: functools.partial(arrived, j, 0) for j in range(3)})
            d = shard_at(kk)
            q_ref[d] = (dot_nn(n1[own : own + rows, :], packed[d, :, 0:cw]) + biases[d, :, 0:cw]).astype(BF16)
            k_ref[d] = dot_nn(n1[...], packed[d, :, cw : 2 * cw]).astype(BF16)
            v_ref[d] = (dot_nn(n1[...], packed[d, :, 2 * cw : 3 * cw]) + biases[d, :, cw : 2 * cw]).astype(BF16)

            def one(p, inner):
                @pl.when(long)
                def _():
                    attend(True, d, p)

                @pl.when(jnp.logical_not(long))
                def _():
                    attend(False, d, p)

                turns(kk * pairs + p, {pairs * j: functools.partial(relay, 4 + j) for j in range(4)})
                return inner

            lax.fori_loop(0, pairs, one, 0)
            hid[...] += dot_nt(a_ref[d], packed[d, :, 3 * cw : 4 * cw])
            halves = half_of_attn(d)
            halves[0].start()
            wire.start(give + 3 + d, halves[1], at_out.at[rows : 2 * rows, head_lanes(d)], place.core)
            return carry

        lax.fori_loop(0, n, heads, 0)
        for i in (4, 5, 6, 7, 10):
            leave(i)

        def norm2(i, carry):
            at = strip_at(i)
            hidden = hid[at, :]
            hat, _ = norm_rows(hidden)
            val = hat * row(2) + row(3)
            n2[at, :] = val.astype(BF16)
            n2t[:, at] = val.T.astype(BF16)
            acc[at, :] = hidden + row(5)
            return carry

        lax.fori_loop(0, per, norm2, 0)
        leave(1)

        def kept(d):
            at = pl.ds(pl.multiple_of(d * tile, tile), tile)
            return (
                pltpu.make_async_copy(act.at[:, at], act_out.at[0:rows, at], fs.at[d]),
                pltpu.make_async_copy(gup.at[:, at], gup_out.at[0:rows, at], fs.at[n + d]),
            )

        def feed(i, carry):
            turns(
                i,
                {
                    2: lambda: (arrived(0, 1, 2), relay(8)),
                    4: lambda: (arrived(1, 1, 2), relay(9)),
                    5: lambda: relay(10),
                    6: lambda: arrived(2, 1, 2),
                },
            )
            d = shard_at(i // 2)
            rel = 1 - lax.rem(i, 2)
            part = lax.rem(rel + core, 2) * tile
            at = pl.ds(pl.multiple_of(part, tile), tile)
            to = pl.ds(pl.multiple_of(rel * hw + d * tile, tile), tile)
            u = dot_nn(n2[...], up[d, :, at]) + biases[d, :, pl.ds(pl.multiple_of(2 * cw + part, PAIR), tile)]
            cdf = 0.5 * (1.0 + lax.erf(u * 0.7071067811865476))
            val = (u * cdf).astype(BF16)
            slope = cdf + u * jnp.exp(-0.5 * u * u) * 0.3989422804014327
            act[:, to] = val
            gu = (dot_nt(cot_ref[...], down[d, at, :]) * slope).astype(BF16)
            gup[:, to] = gu
            unit = 8 * dm + lax.rem(z + d, n) * ffw + part
            vec_ref[:, pl.ds(pl.multiple_of(unit, tile), tile)] = jnp.sum(gu.astype(F32), axis=0, keepdims=True)

            @pl.when(rel == 0)
            def _():
                for c in kept(d):
                    c.start()

            @pl.when(rel == 1)
            def _():
                theirs = pl.ds(pl.multiple_of(d * tile, tile), tile)
                for j, (src, dst) in enumerate(((act, act_out), (gup, gup_out))):
                    wire.start(give + 3 + (j + 1) * n + d, src.at[:, to], dst.at[rows : 2 * rows, theirs], place.core)

            acc[...] += dot_nn(val, down[d, at, :])
            gn = dot_nt(gu, up[d, :, at])

            @pl.when(i == 0)
            def _():
                gh_ref[...] = gn

            @pl.when(i > 0)
            def _():
                gh_ref[...] += gn

            return carry

        lax.fori_loop(0, 2 * n, feed, 0)

        def back2(i, carry):
            at = strip_at(i)
            o_ref[at, :] = acc[at, :].astype(BF16)
            hat, inv = norm_rows(hid[at, :])
            g = gh_ref[at, :]
            gout = cot_ref[at, :].astype(F32)
            gg = g * row(2)
            first = jnp.mean(gg, axis=1, keepdims=True)
            second = jnp.mean(gg * hat, axis=1, keepdims=True)
            val = inv * (gg - first - hat * second) + gout
            gh_ref[at, :] = val
            n2[at, :] = val.astype(BF16)
            ghbt[:, at] = val.T.astype(BF16)
            for j, v in enumerate((val, g * hat, g, gout)):
                vec_ref[:, (2 + j) * dm : (3 + j) * dm] += jnp.sum(v, axis=0, keepdims=True)
            return carry

        lax.fori_loop(0, per, back2, 0)
        leave(9)
        leave(3)

        def back_attn(d, carry):
            ga_ref[d] = dot_nn(n2[...], packed[d, :, 3 * cw : 4 * cw]).astype(BF16)
            return carry

        lax.fori_loop(0, n, back_attn, 0)
        leave(8)
        for d in range(n):
            for c in (*kept(d), half_of_attn(d)[0]):
                c.wait()
        for i, (src, dst) in enumerate(shared):
            wire.landed(give + i, dst, place.core)
            wire.sent(give + i, src)
        for d in range(n):
            wire.landed(give + 3 + d, at_out.at[rows : 2 * rows, d * PAIR : (d + 1) * PAIR], place.core)
            wire.sent(give + 3 + d, at_out.at[0:rows, 0:PAIR])
            for j, dst in enumerate((act_out, gup_out)):
                wire.landed(give + 3 + (j + 1) * n + d, dst.at[rows : 2 * rows, d * tile : (d + 1) * tile], place.core)
                wire.sent(give + 3 + (j + 1) * n + d, dst.at[0:rows, 0:tile])
        for c in leaving:
            c.wait()
        for group in groups:
            group[5]()
        for d in (1, 2, 3):
            wire.sent(d - 1, biases.at[d])

        @pl.when(z == 0)
        def _():
            wire.sent(3, n1.at[0:own])

        @pl.when(z == 1)
        def _():
            wire.sent(3, n1.at[0:SPAN])

        @pl.when(takes_next)
        def _():
            wire.sent(4, n1.at[0:HALO])

        @pl.when(takes_prev)
        def _():
            wire.sent(5, n1.at[0:HALO])

    hbm = pl.BlockSpec(memory_space=pl.ANY)
    vmem = pl.BlockSpec(memory_space=pltpu.VMEM)
    half = lambda *shape: jax.ShapeDtypeStruct(shape, BF16)
    full = lambda *shape: jax.ShapeDtypeStruct(shape, F32)
    b16 = lambda *shape: pltpu.VMEM(shape, BF16)
    b32 = lambda *shape: pltpu.VMEM(shape, F32)
    slots = base + 30 * 3
    return pl.pallas_call(
        body,
        in_specs=[hbm, vmem, hbm, hbm, hbm, vmem, vmem, vmem],
        out_specs=[hbm] * 14 + [vmem] * 3,
        out_shape=[
            half(n, dm, 4 * cw), half(dm, 2 * win), half(dm, 2 * rows), half(dm, 2 * rows), half(dm, rows),
            half(n, rows, cw), half(n, win, cw), half(n, win, cw), half(n, rows, cw), half(2 * rows, n * PAIR), half(n, rows, cw),
            half(2 * rows, hw), half(2 * rows, hw), full(rows, dm),
            full(rows, 2 * n * pairs), half(rows, dm), full(1, 8 * dm + 2 * hw),
        ],
        scratch_shapes=[
            b16(n, dm, ffw), b16(n, ffw, dm), b16(win, dm), b32(rows, dm), b16(rows, dm), b32(rows, dm),
            b16(rows, 2 * hw), b16(rows, 2 * hw), b32(n, 1, length),
            b16(n, dm, 4 * cw), b16(dm, win), b16(dm, rows), b16(dm, rows), b16(dm, rows),
            b16(n, rows, cw), b16(n, win, cw), b16(n, win, cw), b16(n, rows, cw), b16(n, rows, cw), b32(rows, dm),
            pltpu.SemaphoreType.DMA((slots,)), pltpu.SemaphoreType.DMA((slots,)), pltpu.SemaphoreType.DMA((4,)),
            pltpu.SemaphoreType.DMA((3 * n,)), pltpu.SemaphoreType.DMA((11,)),
        ],
        compiler_params=pltpu.CompilerParams(collective_id=0, has_side_effects=True, vmem_limit_bytes=VMEM_ALL),
    )(tokens, cot, pack, w_up, w_down, small, qseg, kseg)


class Reduce:
    SLOTS = 32

    @staticmethod
    def scratch(dm, w):
        q = dm // 4
        e = q // 2
        return [
            pltpu.VMEM((4, q, w), BF16),
            pltpu.VMEM((4, q, w), BF16),
            pltpu.VMEM((4, e, w), BF16),
            pltpu.VMEM((4, e, w), BF16),
            pltpu.VMEM((3, q, w), BF16),
            pltpu.SemaphoreType.DMA((Reduce.SLOTS,)),
            pltpu.SemaphoreType.DMA((Reduce.SLOTS,)),
        ]

    def __init__(self, place, grad, landing, views, zb, send, recv):
        self.place, self.g, self.f = place, grad, landing
        self.ra1, self.rb1, self.ra2, self.rb2 = views
        self.zb = zb
        self.wire = Wire(send, recv, place.core)
        self.q = grad.shape[0] // 4
        self.e = self.q // 2
        self.w = grad.shape[1] // 4

    @staticmethod
    def of(place, grad, landing, scratch):
        views = [lambda d, ref=ref: ref.at[d] for ref in scratch[:4]]
        return Reduce(place, grad, landing, views, *scratch[4:])

    @staticmethod
    def within(place, grad, landing, spare, zb, send, recv):
        q, w = grad.shape[0] // 4, grad.shape[1] // 4
        bounds = (0, q, 2 * q, 2 * q + q // 2, 3 * q)
        views = [
            lambda d, a=a, b=b: spare.at[a:b, pl.ds(pl.multiple_of(d * w, w), w)] for a, b in zip(bounds[:-1], bounds[1:])
        ]
        return Reduce(place, grad, landing, views, zb, send, recv)

    def at(self, base, big, small=None):
        start = base * 2 * self.q + big * self.q + (0 if small is None else small * self.e)
        return pl.ds(pl.multiple_of(start, self.e), self.q if small is None else self.e)

    def eighth(self, small):
        return pl.ds(pl.multiple_of(small * self.e, self.e), self.e)

    def cols(self, d):
        return pl.ds(pl.multiple_of(d * self.w, self.w), self.w)

    def one(self, d):
        p, wire = self.place, self.wire
        wire.start(d, self.g.at[self.at(0, 1 - p.x), self.cols(d)], self.ra1(d), p.by_x)
        wire.start(4 + d, self.g.at[self.at(1, 1 - p.y), self.cols(d)], self.rb1(d), p.by_y)

    def two(self, d):
        p, wire, c = self.place, self.wire, self.cols(d)
        for slot, buf, to, at, mine, dev, nxt in (
            (0, self.ra1, self.ra2, self.at(0, p.x, 1 - p.y), self.eighth(1 - p.y), p.by_x, p.by_y),
            (4, self.rb1, self.rb2, self.at(1, p.y, 1 - p.x), self.eighth(1 - p.x), p.by_y, p.by_x),
        ):
            wire.landed(slot + d, buf(d), dev)
            self.g[at, c] = (self.g[at, c].astype(F32) + buf(d)[mine, :].astype(F32)).astype(BF16)
            wire.start(8 + slot + d, self.g.at[at, c], to(d), nxt)

    def sums(self, d):
        p, wire, c = self.place, self.wire, self.cols(d)
        wire.landed(8 + d, self.ra2(d), p.by_y)
        wire.landed(12 + d, self.rb2(d), p.by_x)
        up = (
            self.g[self.at(0, p.x, p.y), c].astype(F32)
            + self.ra1(d)[self.eighth(p.y), :].astype(F32)
            + self.ra2(d)[...].astype(F32)
        )
        low = (
            self.g[self.at(1, p.y, p.x), c].astype(F32)
            + self.rb1(d)[self.eighth(p.x), :].astype(F32)
            + self.rb2(d)[...].astype(F32)
        )
        return up, low

    def three(self, d):
        p, wire, c, e = self.place, self.wire, self.cols(d), self.e
        up, low = self.sums(d)
        for part, (at, val) in enumerate(((self.at(0, p.x, p.y), up), (self.at(1, p.y, p.x), low))):
            self.g[at, c] = val.astype(BF16)
            wire.start(
                16 + 12 * part + d, self.g.at[at, c], self.zb.at[d - 1, part * e : (part + 1) * e], p.along(d)
            )

    def last(self):
        p, wire, e = self.place, self.wire, self.e
        up, low = self.sums(0)
        for s in (1, 2, 3):
            wire.landed(16 + s, self.zb.at[s - 1, 0:e], p.along(4 - s))
            wire.landed(28 + s, self.zb.at[s - 1, e : 2 * e], p.along(4 - s))
            up = up + self.zb[s - 1, 0:e].astype(F32)
            low = low + self.zb[s - 1, e : 2 * e].astype(F32)
        ready = self.ra1(0)
        ready[0:e, :] = up.astype(BF16)
        ready[e : 2 * e, :] = low.astype(BF16)
        wire.start(20, ready, self.f.at[2], p.by_x)
        wire.start(21, ready, self.f.at[4], p.by_y)
        wire.start(22, ready, self.f.at[1], p.core)
        self.keep().start()

    def keep(self):
        return pltpu.make_async_copy(self.ra1(0), self.f.at[0], self.wire.send.at[16])

    def four(self):
        p, wire, e = self.place, self.wire, self.e
        wire.landed(20, self.f.at[2], p.by_x)
        wire.start(23, self.f.at[2, 0:e], self.f.at[6, 0:e], p.by_y)
        wire.start(25, self.f.at[2], self.f.at[3], p.core)
        wire.landed(21, self.f.at[4], p.by_y)
        wire.start(24, self.f.at[4, e : 2 * e], self.f.at[6, e : 2 * e], p.by_x)
        wire.start(26, self.f.at[4], self.f.at[5], p.core)

    def five(self):
        p, wire, e = self.place, self.wire, self.e
        wire.landed(23, self.f.at[6, 0:e], p.by_y)
        wire.landed(24, self.f.at[6, e : 2 * e], p.by_x)
        wire.start(27, self.f.at[6], self.f.at[7], p.core)

    def six(self):
        for slot, to in ((22, 1), (25, 3), (26, 5), (27, 7)):
            self.wire.landed(slot, self.f.at[to], self.place.core)
        e, sent = self.e, self.wire.sent
        for d in range(4):
            sent(d, self.ra1(d))
            sent(4 + d, self.rb1(d))
            sent(8 + d, self.ra2(d))
            sent(12 + d, self.rb2(d))
        for d in range(1, 4):
            sent(16 + d, self.zb.at[d - 1, 0:e])
            sent(28 + d, self.zb.at[d - 1, 0:e])
        for slot in (20, 21, 22, 25, 26, 27):
            sent(slot, self.f.at[0])
        for slot in (23, 24):
            sent(slot, self.f.at[0, 0:e])
        self.keep().wait()


def back_call(cot, act, n2, gup, ghb, n1w, attn2, packed, tokens, q, k, v, attn, gattn, lse, qseg, kseg, small, vec, own):
    n, rows, cw = q.shape
    win = k.shape[1]
    dm = cot.shape[0]
    hw = act.shape[1]
    half = n * cw // 2
    w = hw // 4
    pairs = cw // PAIR
    scale = HEAD_DIM**-0.5
    each = len(Reduce.scratch(dm, w))
    length = vec.shape[1]
    strip = 128

    def body(
        cot_in, act_in, n2_in, gup_in, ghb_in, n1_in, at_in, w_ref, x_ref, q_in, k_in, v_in, a_in, g_in,
        l_ref, qs_ref, ks_ref, gain_ref, vec_ref,
        fd, fu, fp, gi_ref, sum_ref,
        wbuf, act2, gup2, n12, gd, gu, dq_o, dk_o, dv_o, at2, dq, dk, dv, dkt, dvt,
        far_in, prev_in, next_in, nxt, va, vr, vz, zb, q_ref, k_ref, v_ref, a_ref, g_ref, ps, pr_sem, xs, xr, ls, ws, *scr,
    ):
        place = Place()
        core, z = place.k, place.z
        long, gives_prev, gives_next = z < 2, z >= 2, jnp.logical_and(z >= 1, z < 3)
        swap = {"dp": place.me, "mp": lax.rem(z + 1, 2)}
        left_dev = {"dp": place.me, "mp": lax.rem(z + 3, 4)}
        right_dev = {"dp": place.me, "mp": lax.rem(z + 1, 4)}
        wire = Wire(xs, xr, place.core)
        cot2, n22, ghb2 = wbuf.at[0], wbuf.at[1], wbuf.at[2]
        loads = (
            (cot_in, cot2), (act_in, act2), (n2_in, n22), (gup_in, gup2), (q_in, q_ref), (k_in, k_ref), (v_in, v_ref),
            (a_in, a_ref), (g_in, g_ref), (ghb_in, ghb2.at[:, 0:rows]), (n1_in, n12), (at_in, at2),
        )
        local = [pltpu.make_async_copy(src, dst, ls.at[1 + i]) for i, (src, dst) in enumerate(loads)]
        for c in local:
            c.start()
        place.meet()
        wire.start(0, ghb_in, ghb2.at[:, rows : 2 * rows], place.core)

        def take(*which):
            for i in which:
                local[i].wait()

        down = Reduce.of(place, gd, fd, scr[:each])
        up = Reduce.of(place, gu, fu, scr[each : 2 * each])
        heads = Reduce.within(place, act2, fp, gup2, zb, ps, pr_sem)

        def make(red, grad, left, right):
            def step(i, carry):
                d = lax.rem(i + 1, 4)
                c = pl.ds(pl.multiple_of(d * w, w), w)
                grad[:, c] = dot_nn(left[...], right[:, c]).astype(BF16)
                red.one(d)
                return carry

            lax.fori_loop(0, 4, step, 0)

        take(0, 1)
        make(down, gd, cot2, act2)
        take(2, 3)
        make(up, gu, n22, gup2)

        def weights(t):
            at = lax.rem(t, 3)
            return pltpu.make_async_copy(w_ref.at[lax.rem(t, n)], wbuf.at[at], ws.at[at])

        weights(0).start()
        weights(1).start()

        def turns(i, table):
            for t, f in table.items():

                @pl.when(i == t)
                def _():
                    f()

        def work(big, d, p):
            at = pl.ds(pl.multiple_of(p * PAIR, PAIR), PAIR)
            to = pl.ds(pl.multiple_of(d * PAIR, PAIR), PAIR)
            rel = lax.rem(p + core, 2)
            if not big:
                dkt[...] = jnp.zeros_like(dkt)
                dvt[...] = jnp.zeros_like(dvt)
            for i, (qs, qn, ks, kn) in enumerate(blocks_of(rows, own, win, big)):
                mask = qs_ref[qs : qs + qn, :] == ks_ref[:, ks : ks + kn]
                qq, kk, vv = q_ref[d, qs : qs + qn, at], k_ref[d, ks : ks + kn, at], v_ref[d, ks : ks + kn, at]
                gg = g_ref[d, qs : qs + qn, at]
                prod = gg.astype(F32) * a_ref[d, qs : qs + qn, at].astype(F32)
                dqs = []
                for h in range(2):
                    lanes = slice(h * HEAD_DIM, (h + 1) * HEAD_DIM)
                    qh, kh, gh = qq[:, lanes] * BF16(scale), kk[:, lanes], gg[:, lanes]
                    lane = lax.broadcasted_iota(jnp.int32, (qn, 2 * n * pairs), 1)
                    picked = jnp.where(lane == (d * pairs + p) * 2 + h, l_ref[qs : qs + qn, :], 0.0)
                    s = jnp.where(mask, dot_nt(qh, kh) - jnp.sum(picked, axis=1, keepdims=True), NEG)
                    pr = jnp.exp(s)
                    dp = dot_nt(gh, vv[:, lanes])
                    delta = jnp.sum(prod[:, lanes], axis=1, keepdims=True)
                    ds = (pr * (dp - delta)).astype(BF16)
                    dqs.append(dot_nn(ds, kh) * scale)
                    gk = dot_tn(qh, ds)
                    gv = dot_tn(gh, pr.astype(BF16))
                    if big and i == 0:
                        dkt[lanes, :] = gk
                        dvt[lanes, :] = gv
                    else:
                        dkt[lanes, ks : ks + kn] += gk
                        dvt[lanes, ks : ks + kn] += gv
                dq[rel, qs : qs + qn, to] = jnp.concatenate(dqs, axis=1).astype(BF16)
            dk[rel, :, to] = dkt[...].T.astype(BF16)
            dv[rel, :, to] = dvt[...].T.astype(BF16)

        def head_pair(i, carry):
            d, p = i // pairs, lax.rem(i, pairs)

            @pl.when(long)
            def _():
                work(True, d, p)

            @pl.when(jnp.logical_not(long))
            def _():
                work(False, d, p)

            order = [(down, 1), (down, 2), (down, 3), (down, 0), (up, 1), (up, 2)]
            turns(i, {t + 2: functools.partial(red.two, shard) for t, (red, shard) in enumerate(order)})
            return carry

        take(4, 5, 6, 7, 8)
        lax.fori_loop(0, n * pairs, head_pair, 0)
        halves = ((dq, dq_o), (dk, dk_o), (dv, dv_o))
        for i, (src, dst) in enumerate(halves):
            wire.start(10 + i, src.at[1], dst, place.core)
        take(9, 10, 11)
        wire.landed(0, ghb2.at[:, rows : 2 * rows], place.core)

        def put(m, val):
            for d in range(n):
                at = d * w + m * PAIR
                act2[:, at : at + PAIR] = val[:, d * PAIR : (d + 1) * PAIR].astype(BF16)

        put(3, dot_nn(ghb2[...], at2[...]))
        weights(2).start()
        wire.landed(10, dq_o, place.core)
        put(0, dot_nn(n12[:, own : own + rows], dq[0]) + dot_nn(n12[:, win + own : win + own + rows], dq_o[...]))
        up.two(3)
        wire.landed(11, dk_o, place.core)
        put(1, dot_nn(n12[:, 0:win], dk[0]) + dot_nn(n12[:, win : 2 * win], dk_o[...]))
        up.two(0)
        wire.landed(12, dv_o, place.core)
        put(2, dot_nn(n12[:, 0:win], dv[0]) + dot_nn(n12[:, win : 2 * win], dv_o[...]))
        for d in (1, 2, 3, 0):
            heads.one(d)

        far_out, x_buf, next_out = n12.at[0:own, 0:dm], n12.at[0:rows, dm : 2 * dm], n12.at[own : own + HALO, 0:dm]
        tokens_in = pltpu.make_async_copy(x_ref, x_buf, ls.at[0])
        tokens_in.start()

        def dots(t, carry):
            weights(t).wait()
            slot = lax.rem(t, 3)
            to = pl.ds(pl.multiple_of(lax.rem(t, n) * PAIR, PAIR), PAIR)

            def weight(which, j):
                at = which * cw + lax.rem(j + core, 2) * PAIR
                return wbuf[slot, :, pl.ds(pl.multiple_of(at, PAIR), PAIR)]

            def add(ref, val, first):
                @pl.when(t == first)
                def _():
                    ref[...] = val

                @pl.when(t > first)
                def _():
                    ref[...] += val

            right = jnp.concatenate([weight(m, j) for m in (1, 2) for j in range(2)], axis=1)

            @pl.when(t < n)
            def _():
                left = jnp.concatenate([r[j, 0:own, to] for r in (dk, dv) for j in range(2)], axis=1)
                add(gi_ref, dot_nt(left, right), 0)

            @pl.when(t >= n)
            def _():
                left = jnp.concatenate([r[j, own : own + rows, to] for r in (dk, dv) for j in range(2)], axis=1)
                mine = jnp.concatenate([dq[j, :, to] for j in range(2)], axis=1)
                other = jnp.concatenate([weight(0, j) for j in range(2)], axis=1)
                add(gi_ref, dot_nt(left, right) + dot_nt(mine, other), n)
                left = jnp.concatenate(
                    [r[j, own + rows : own + rows + HALO, to] for r in (dk, dv) for j in range(2)], axis=1
                )
                add(nxt, dot_nt(left, right), n)

            @pl.when(t < 2 * n - 3)
            def _():
                weights(t + 3).start()

            @pl.when(t == n - 1)
            def _():
                far_out[...] = gi_ref[...].astype(BF16)

                @pl.when(z == 0)
                def _():
                    wire.start(13, far_out.at[0:SPAN], far_in.at[0:SPAN], swap)

                @pl.when(z == 1)
                def _():
                    wire.start(13, far_out, far_in, swap)

                @pl.when(gives_prev)
                def _():
                    wire.start(14, far_out.at[own - HALO : own], prev_in, left_dev)

            turns(t, {2 * i + 1: functools.partial(down.three, i + 1) for i in range(3)})
            return carry

        lax.fori_loop(0, 2 * n, dots, 0)
        next_out[...] = nxt[...].astype(BF16)

        @pl.when(gives_next)
        def _():
            wire.start(15, next_out, next_in, right_dev)

        up.three(1)
        up.three(2)
        up.three(3)
        heads.two(1)
        heads.two(2)
        down.last()
        heads.two(3)
        heads.two(0)
        heads.three(1)

        @pl.when(z == 0)
        def _():
            wire.landed(13, far_in, swap)
            gi_ref[...] += far_in[...].astype(F32)

        @pl.when(z == 1)
        def _():
            wire.landed(13, far_in.at[0:SPAN], swap)
            gi_ref[0:SPAN, :] += far_in[0:SPAN, :].astype(F32)

        @pl.when(gives_next)
        def _():
            wire.landed(14, prev_in, right_dev)
            gi_ref[rows - HALO : rows, :] += prev_in[...].astype(F32)

        @pl.when(gives_prev)
        def _():
            wire.landed(15, next_in, left_dev)
            gi_ref[0:HALO, :] += next_in[...].astype(F32)

        up.last()
        heads.three(2)
        heads.three(3)
        va[0] = vec_ref[...]
        for base, grad in ((6, dq), (7, dv)):
            for j in range(2):
                total = jnp.sum(grad[j].astype(F32), axis=0, keepdims=True)
                for d in range(n):
                    at = base * dm + lax.rem(z + d, n) * cw + lax.rem(j + core, 2) * PAIR
                    va[0, :, pl.ds(pl.multiple_of(at, PAIR), PAIR)] = total[:, d * PAIR : (d + 1) * PAIR]
        tokens_in.wait()
        gains = gain_ref[:, 0:dm]

        def norm(i, carry):
            at = pl.ds(pl.multiple_of(i * strip, strip), strip)
            hat, inv = norm_rows(x_buf[at, :].astype(F32))
            grad = gi_ref[at, :]
            gg = grad * gains
            first = jnp.mean(gg, axis=1, keepdims=True)
            second = jnp.mean(gg * hat, axis=1, keepdims=True)
            gi_ref[at, :] = inv * (gg - first - hat * second)
            va[0, :, 0:dm] += jnp.sum(grad * hat, axis=0, keepdims=True)
            va[0, :, dm : 2 * dm] += jnp.sum(grad, axis=0, keepdims=True)
            return carry

        lax.fori_loop(0, rows // strip, norm, 0)

        hops = (place.core, place.by_x, place.by_y)
        between = (down.four, up.four, down.five)
        for i, dev in enumerate(hops):
            wire.start(16 + i, va.at[i], vr.at[i], dev)
            between[i]()
            wire.landed(16 + i, vr.at[i], dev)
            if i < 2:
                va[i + 1] = va[i] + vr[i]
            else:
                vz[0] = va[i] + vr[i]
        for d in (1, 2, 3):
            wire.start(18 + d, vz.at[0], vz.at[d], place.along(d))
        up.five()
        heads.last()
        heads.four()
        for d in (1, 2, 3):
            wire.landed(18 + d, vz.at[d], place.along(4 - d))
        terms = [vz[lax.rem(z - a + 4, 4)] for a in range(4)]
        sum_ref[...] = (terms[0] + terms[1]) + (terms[2] + terms[3])
        heads.five()
        down.six()
        up.six()
        heads.six()
        wire.sent(0, ghb2.at[:, 0:rows])
        for i in range(3):
            wire.sent(10 + i, halves[i][1])

        @pl.when(z == 0)
        def _():
            wire.sent(13, far_in.at[0:SPAN])

        @pl.when(z == 1)
        def _():
            wire.sent(13, far_in)

        @pl.when(gives_prev)
        def _():
            wire.sent(14, prev_in)

        @pl.when(gives_next)
        def _():
            wire.sent(15, next_in)

        for i in range(3):
            wire.sent(16 + i, va.at[i])
        for d in (1, 2, 3):
            wire.sent(18 + d, vz.at[0])

    hbm = pl.BlockSpec(memory_space=pl.ANY)
    vmem = pl.BlockSpec(memory_space=pltpu.VMEM)
    shaped = lambda *shape: jax.ShapeDtypeStruct(shape, BF16)
    buf = lambda *shape: pltpu.VMEM(shape, BF16)
    wide = lambda *shape: pltpu.VMEM(shape, F32)
    sem = lambda count: pltpu.SemaphoreType.DMA((count,))
    q4 = dm // 4
    return pl.pallas_call(
        body,
        in_specs=[hbm] * 14 + [vmem] * 5,
        out_specs=[hbm] * 3 + [vmem] * 2,
        out_shape=[shaped(8, q4, w)] * 3 + [jax.ShapeDtypeStruct((rows, dm), F32), jax.ShapeDtypeStruct((1, length), F32)],
        scratch_shapes=[
            buf(3, dm, 2 * rows), buf(2 * rows, hw), buf(2 * rows, hw), buf(dm, 2 * win), buf(dm, hw), buf(dm, hw),
            buf(rows, half), buf(win, half), buf(win, half), buf(2 * rows, half), buf(2, rows, half), buf(2, win, half), buf(2, win, half),
            wide(PAIR, win), wide(PAIR, win), buf(own, dm), buf(HALO, dm), buf(HALO, dm), wide(HALO, dm),
            wide(3, 1, length), wide(3, 1, length), wide(4, 1, length), buf(3, q4, w),
            buf(n, rows, cw), buf(n, win, cw), buf(n, win, cw), buf(n, rows, cw), buf(n, rows, cw),
            sem(Reduce.SLOTS), sem(Reduce.SLOTS), sem(22), sem(22), sem(13), sem(3),
        ]
        + Reduce.scratch(dm, w) * 2,
        compiler_params=pltpu.CompilerParams(collective_id=1, has_side_effects=True, vmem_limit_bytes=VMEM_ALL),
    )(cot, act, n2, gup, ghb, n1w, attn2, packed, tokens, q, k, v, attn, gattn, lse, qseg, kseg, small, vec)


def place_grads(coords, down, up, pack, g_in, g_hidden):
    _, q, w = up.shape
    e = q // 2
    dm = 4 * q
    lanes = w // 4
    rows = g_in.shape[0]
    shapes = [(rows, dm), (2 * w, dm), (dm, 2 * w), (dm, w // 2), (dm, w // 2), (dm, w // 2), (w // 2, dm)]
    count = len(shapes)
    strip = 128

    def body(c_ref, *refs):
        ins, outs, bufs, more = refs[:5], refs[5 : 5 + count], refs[5 + count : 5 + 2 * count], refs[5 + 2 * count :]
        d_buf, u_buf, p_buf, h_buf, ls, os = more
        pieces = (d_buf, u_buf, p_buf)
        loads = [
            pltpu.make_async_copy(src, dst, ls.at[i])
            for i, (src, dst) in enumerate(zip(ins, (*pieces, bufs[0], h_buf)))
        ]
        stores = [pltpu.make_async_copy(bufs[i], outs[i], os.at[i]) for i in range(count)]
        for i in (1, 3, 4, 0, 2):
            loads[i].start()

        def spread(ref, put):
            def one(off, carry):
                y = lax.rem(c_ref[0] + off // 4, 2)
                x = lax.rem(c_ref[1] + lax.rem(off // 2, 2), 2)
                k = lax.rem(c_ref[2] + lax.rem(off, 2), 2)
                for part, block in enumerate((2 * x + y, 4 + 2 * y + x)):
                    val = ref[off, part * e : (part + 1) * e, :].astype(F32)
                    put(val, pl.ds(pl.multiple_of(block * e, e), e), k)
                return carry

            lax.fori_loop(0, 8, one, 0)

        def put_up(val, at, k):
            bufs[2][at, pl.ds(pl.multiple_of(k * w, w), w)] = val

        def put_down(val, at, k):
            bufs[1][pl.ds(pl.multiple_of(k * w, w), w), at] = val.T

        def put_pack(val, at, k):
            half = pl.ds(pl.multiple_of(k * lanes, lanes), lanes)
            for m in range(3):
                bufs[3 + m][at, half] = val[:, m * lanes : (m + 1) * lanes]
            bufs[6][half, at] = val[:, 3 * lanes :].T

        loads[1].wait()
        spread(u_buf, put_up)
        stores[2].start()
        loads[3].wait()
        loads[4].wait()

        def add(i, carry):
            at = pl.ds(pl.multiple_of(i * strip, strip), strip)
            bufs[0][at, :] += h_buf[at, :]
            return carry

        lax.fori_loop(0, rows // strip, add, 0)
        stores[0].start()
        loads[0].wait()
        spread(d_buf, put_down)
        stores[1].start()
        loads[2].wait()
        spread(p_buf, put_pack)
        for i in range(3, count):
            stores[i].start()
        for c in stores:
            c.wait()

    hbm = pl.BlockSpec(memory_space=pl.ANY)
    return pl.pallas_call(
        body,
        in_specs=[pl.BlockSpec(memory_space=pltpu.SMEM)] + [hbm] * 5,
        out_specs=[hbm] * count,
        out_shape=[jax.ShapeDtypeStruct(shape, F32) for shape in shapes],
        scratch_shapes=[pltpu.VMEM(shape, F32) for shape in shapes]
        + [pltpu.VMEM((8, q, w), BF16)] * 3
        + [pltpu.VMEM((rows, dm), F32), pltpu.SemaphoreType.DMA((5,)), pltpu.SemaphoreType.DMA((count,))],
        compiler_params=pltpu.CompilerParams(vmem_limit_bytes=VMEM),
        cost_estimate=pl.CostEstimate(flops=0, bytes_accessed=36 * dm * w, transcendentals=0),
    )(coords, down, up, pack, g_in, g_hidden)


def relative(stack, z):
    return jnp.roll(stack, -z, axis=0)


def core_first(v, core, axis):
    return jnp.where(core == 0, v, jnp.flip(v, axis))


def gather_any(shard, z):
    return relative(lax.all_gather(shard, "mp", axis=0, tiled=False), z)


def reduce_any(half, z, core):
    zero = jnp.zeros_like(half)
    v = jnp.stack([jnp.where(core == 0, half, zero), jnp.where(core == 1, half, zero)], axis=2)
    v = jnp.roll(jnp.moveaxis(v, 1, 0), z, axis=0)
    v = lax.psum_scatter(v, "mp", scatter_dimension=0, tiled=True)[0]
    return lax.psum(v, "dp").astype(F32).reshape(half.shape[0], -1)


def local(
    tokens,
    segments,
    ln1_gain,
    ln1_bias,
    w_query,
    b_query,
    w_key,
    w_value,
    b_value,
    w_out,
    b_out,
    ln2_gain,
    ln2_bias,
    w_up,
    b_up,
    w_down,
    b_down,
    cotangent,
):
    rows, dm = tokens.shape
    cw = w_query.shape[1]
    ffw = w_up.shape[1]
    mp = lax.axis_size("mp")
    dp = lax.axis_size("dp")
    fast = mp == 4 and dp == 8 and rows % 256 == 0 and cw == 2 * PAIR and rows < LONGEST <= rows + SPAN <= 2 * rows
    z = lax.axis_index("mp")
    me = lax.axis_index("dp")
    core = lax.rem(me, 2)
    x = lax.rem(me // 2, 2)
    y = me // 4
    f32 = lambda v: v.astype(F32)

    near = -(-LONGEST // rows)
    own = (near - 1) * rows
    win = own + rows + 2 * HALO
    is_near = z < near
    seg_parts = [
        jnp.where(is_near, lax.dynamic_slice_in_dim(segments, lax.rem(z + j, near) * rows, rows), -1)
        for j in range(1, near)
    ]
    seg_own = lax.dynamic_slice_in_dim(segments, z * rows, rows)
    seg_prev = lax.dynamic_slice_in_dim(segments, jnp.maximum(z * rows - HALO, 0), HALO)
    seg_next = lax.dynamic_slice_in_dim(segments, jnp.minimum((z + 1) * rows, segments.shape[0] - HALO), HALO)
    seg_far = jnp.concatenate(seg_parts)
    seg_far = jnp.concatenate([seg_far[:-HALO], jnp.where(is_near, seg_far[-HALO:], seg_prev)])
    has_next = jnp.logical_and(z >= near - 1, z < mp - 1)
    seg_win = jnp.concatenate(
        [seg_far, seg_own, jnp.where(has_next, seg_next, -1), jnp.full((HALO,), -1, segments.dtype)]
    )
    kseg, qseg = seg_win[None, :], seg_own[:, None]
    info = jnp.stack([is_near.astype(jnp.int32), core]).astype(jnp.int32)

    pack = jnp.concatenate([w_query, w_key, w_value, w_out.T], axis=1)
    hw = mp * ffw // 2
    if fast:
        small = jnp.concatenate([ln1_gain, ln1_bias, ln2_gain, ln2_bias, b_out, b_down, b_query, b_value, b_up])
        small = f32(small)[None]
        (
            packed, n1_t, n2_t, cot_t, ghb_t, q, k, v, attn, attn_2, g_attn, active, g_upper, g_hidden, lse, output, vec
        ) = front_call(tokens, cotangent, pack, w_up, w_down, small, qseg, kseg, own)
        done_d, done_u, done_p, g_in, vec = back_call(
            cot_t, active, n2_t, g_upper, ghb_t, n1_t, attn_2, packed, tokens, q, k, v, attn, g_attn, lse, qseg, kseg, small, vec, own
        )
        vec = vec[0]
        coords = jnp.stack([y, x, core]).astype(jnp.int32)
        g_tokens, g_w_down, g_w_up, g_w_query, g_w_key, g_w_value, g_w_out = place_grads(
            coords, done_d, done_u, done_p, g_in, g_hidden
        )
    else:
        halo = [
            lax.ppermute(tokens, "mp", [((i + j) % near, i) for i in range(near)]) for j in range(1, near)
        ]
        before = lax.ppermute(tokens[-HALO:], "mp", [(i - 1, i) for i in range(near, mp)])
        behind = lax.ppermute(tokens[:HALO], "mp", [(i + 1, i) for i in range(near - 1, mp - 1)])
        small_vec = jnp.concatenate([b_query, b_value, b_up])
        vecs = relative(lax.all_gather(small_vec, "mp", axis=0, tiled=False), z)
        bq_all, bv_all = vecs[:, :cw], vecs[:, cw : 2 * cw]
        bu_all = vecs[:, 2 * cw :].reshape(mp, 2, ffw // 2).transpose(1, 0, 2)
        bu_all = core_first(bu_all, core, 0).reshape(mp * ffw)

        packed, up_all, down_all = (gather_any(w, z) for w in (pack, w_up, w_down))

        far = jnp.concatenate(halo, axis=0)
        far = jnp.concatenate([far[:-HALO], far[-HALO:] + before], axis=0)
        tok_win = jnp.concatenate([far, tokens, behind, jnp.zeros((HALO, dm), tokens.dtype)], axis=0)
        hat_win, inv_win = norm_rows(f32(tok_win))
        n1w = (hat_win * f32(ln1_gain) + f32(ln1_bias)).astype(BF16)
        q, k, v = qkv_call(n1w, packed, bq_all, bv_all, own, rows, cw)
        attn, lse = attn_fwd_call(info, q, k, v, qseg, kseg, own)
        hidden, n2 = out_call(attn, packed, tokens, b_out, ln2_gain, ln2_bias)
        output, g_n2, active, g_upper, g_b_up = ffn_call(
            info[1:], n2, hidden, cotangent, up_all, down_all, bu_all, b_down, 2
        )

        gout = f32(cotangent)
        hat2, inv2 = norm_rows(hidden)

        def norm_back(g, hat, inv, gain):
            gg = g * gain
            first = jnp.mean(gg, axis=1, keepdims=True)
            second = jnp.mean(gg * hat, axis=1, keepdims=True)
            return inv * (gg - first - hat * second), jnp.sum(g * hat, axis=0), jnp.sum(g, axis=0)

        g_hidden, g_gain2, g_bias2 = norm_back(g_n2, hat2, inv2, f32(ln2_gain))
        g_hidden = g_hidden + gout
        ghb = g_hidden.astype(BF16)

        g_attn = jnp.stack([dot_nn(ghb, packed[d, :, 3 * cw :]).astype(BF16) for d in range(mp)])
        dq, dk, dv = attn_bwd_call(info, q, k, v, attn, g_attn, lse, qseg, kseg, own)
        n1 = n1w[own : own + rows]
        sums = [jnp.sum(g_hidden, axis=0), g_gain2, g_bias2, jnp.sum(gout, axis=0)]
        halves = dq.shape[0]

        def shards(v, width):
            if v.shape[0] == 2:
                v = core_first(v.reshape(2, mp, width // 2), core, 0).transpose(1, 0, 2)
            return jnp.roll(v.reshape(mp, width), z, axis=0).reshape(mp * width)

        gbq = shards(jnp.sum(f32(dq), axis=1), cw)
        gbv = shards(jnp.sum(f32(dv), axis=1), cw)
        gbu = core_first(g_b_up.reshape(2, mp, ffw // 2), core, 0).transpose(1, 0, 2)
        gbu = jnp.roll(gbu.reshape(mp, ffw), z, axis=0).reshape(-1)
        sums = sums + [gbq, gbv, gbu]
        g_own, g_far, g_next = norm1_back_call(dq, dk, dv, packed, info, own)
        back = g_own
        for j in range(1, near):
            part = g_far[(j - 1) * rows : j * rows]
            back = back + f32(lax.ppermute(part, "mp", [(i, (i + j) % near) for i in range(near)]))
        to_prev = f32(lax.ppermute(g_far[-HALO:], "mp", [(i, i - 1) for i in range(near, mp)]))
        to_next = f32(lax.ppermute(g_next, "mp", [(i, i + 1) for i in range(near - 1, mp - 1)]))
        back = jnp.concatenate([back[:HALO] + to_next, back[HALO:-HALO], back[-HALO:] + to_prev], axis=0)
        hat1 = hat_win[own : own + rows]
        inv1 = inv_win[own : own + rows]
        g_in, g_gain1, g_bias1 = norm_back(back, hat1, inv1, f32(ln1_gain))
        g_tokens = g_in + g_hidden

        other = lambda v: lax.ppermute(v, "dp", [(i, i - i % 2 + (i + 1) % 2) for i in range(dp)])
        hw = mp * ffw // 2

        def pair_grad(left, right):
            return (dot_tn(left, right[:, :hw]) + dot_tn(other(left), other(right[:, hw:]))).astype(BF16)

        gd = pair_grad(cotangent, active)
        gu = pair_grad(n2, g_upper)
        g_w_up = reduce_any(gu.reshape(dm, mp, ffw // 2), z, core)
        g_w_down = reduce_any(gd.reshape(dm, mp, ffw // 2), z, core).T

        def whole_grad(left, right, name=None):
            v = dot_tn(left, right).astype(BF16).reshape(dm, mp, cw)
            v = jnp.roll(jnp.moveaxis(v, 1, 0), z, axis=0)
            v = lax.psum_scatter(v, "mp", scatter_dimension=0, tiled=True)[0]
            return lax.psum(v, "dp").astype(F32)

        def whole(v):
            if halves == 1:
                return v[0]
            v = v.reshape(2, v.shape[1], mp, cw // 2).transpose(1, 2, 0, 3)
            return core_first(v, core, 2).reshape(v.shape[0], mp * cw)

        g_w_query = whole_grad(n1, whole(dq))
        g_w_key = whole_grad(n1w, whole(dk))
        g_w_value = whole_grad(n1w, whole(dv))
        g_w_out = whole_grad(ghb, attn.transpose(1, 0, 2).reshape(rows, mp * cw)).T

        vec = lax.psum(jnp.concatenate([g_gain1, g_bias1] + sums), ("dp", "mp"))
    g_gain1, g_bias1, g_b_out, g_gain2, g_bias2, g_b_down = (vec[i * dm : (i + 1) * dm] for i in range(6))
    at = 6 * dm
    g_b_query = lax.dynamic_slice_in_dim(vec, at + z * cw, cw)
    g_b_value = lax.dynamic_slice_in_dim(vec, at + mp * cw + z * cw, cw)
    g_b_up = lax.dynamic_slice_in_dim(vec, at + 2 * mp * cw + z * ffw, ffw)
    return (
        output,
        g_tokens,
        g_gain1,
        g_bias1,
        g_w_query,
        g_b_query,
        g_w_key,
        g_w_value,
        g_b_value,
        g_w_out,
        g_b_out,
        g_gain2,
        g_bias2,
        g_w_up,
        g_b_up,
        g_w_down,
        g_b_down,
    )


def solution(mesh):
    in_specs = (
        P(("dp", "mp"), None),
        P("dp"),
        P(),
        P(),
        P(None, "mp"),
        P("mp"),
        P(None, "mp"),
        P(None, "mp"),
        P("mp"),
        P("mp", None),
        P(),
        P(),
        P(),
        P(None, "mp"),
        P("mp"),
        P("mp", None),
        P(),
        P(("dp", "mp"), None),
    )
    out_specs = (
        P(("dp", "mp"), None),
        P(("dp", "mp"), None),
        P(),
        P(),
        P(None, "mp"),
        P("mp"),
        P(None, "mp"),
        P(None, "mp"),
        P("mp"),
        P("mp", None),
        P(),
        P(),
        P(),
        P(None, "mp"),
        P("mp"),
        P("mp", None),
        P(),
    )
    return jax.shard_map(local, mesh=mesh, in_specs=in_specs, out_specs=out_specs, check_vma=False)
```
